32 devices in a mesh: dp: 16 (over z, y, core), tensor: 2 (over x).
Axes of the slice: x: 2, y: 2, z: 4, core: 2. Of those that a mesh axis runs over, the one named last changes fastest.
Arguments:
- hidden_in: bfloat16 [8192, 1536], P(('dp', 'tensor')), may hold values from -6 to 6
- prenorm_gain: float32 [1536], replicated, may hold values from 0.5 to 1.5
- w_zx: bfloat16 [1536, 2, 3072], P('dp', None, 'tensor'), may hold values from -0.15625 to 0.15625
- w_dt: bfloat16 [1536, 48], P('dp', 'tensor'), may hold values from -0.15625 to 0.15625
- w_bc: bfloat16 [1536, 256], P('dp'), may hold values from -0.15625 to 0.15625
- conv_x: float32 [5, 3072], P(None, 'tensor'), may hold values from -0.5 to 0.5
- conv_bc: float32 [5, 256], replicated, may hold values from -0.5 to 0.5
- dt_bias: float32 [48], P('tensor'), may hold values from -6 to -2
- a_log: float32 [48], P('tensor'), may hold values from 0 to 2.77
- d_skip: float32 [48], P('tensor'), may hold values from 0.1 to 1.9
- norm_gain: float32 [3072], P('tensor'), may hold values from 0.5 to 1.5
- w_out: bfloat16 [3072, 1536], P('tensor', 'dp'), may hold values from -0.109375 to 0.109375
- seg_ids: int32 [16, 512], P('dp'), may hold values from 0 to 2, never falling along the last dimension, each value on 1 to 256 neighbouring positions
- grad_out: bfloat16 [8192, 1536], P(('dp', 'tensor')), may hold values from -12 to 12
Outputs:
- block_out: bfloat16 [8192, 1536], P(('dp', 'tensor'))
- grad_in: bfloat16 [8192, 1536], P(('dp', 'tensor'))
- grad_prenorm: float32 [1536], P('tensor')
- grad_w_zx: float32 [1536, 2, 3072], P('dp', None, 'tensor')
- grad_w_dt: float32 [1536, 48], P('dp', 'tensor')
- grad_w_bc: float32 [1536, 256], P('dp', 'tensor')
- grad_conv_x: float32 [5, 3072], P(None, 'tensor')
- grad_conv_bc: float32 [5, 256], P(None, 'tensor')
- grad_dt_bias: float32 [48], P('tensor')
- grad_a_log: float32 [48], P('tensor')
- grad_d_skip: float32 [48], P('tensor')
- grad_norm_gain: float32 [3072], P('tensor')
- grad_w_out: float32 [3072, 1536], P('tensor', 'dp')
The draws below stay inside these ranges and needn't reach their ends.
Inputs may be any that keep to these rules, and one draw needn't show every extreme that they name: `seg_ids`: in each row the ids never fall and start at 0; every document holds 1 to 256 tokens, one exactly 256.
All inputs are finite; a program needn't handle non-finite values.
Results may differ from the reference program's by a relative error of at most 0.0073.
The reference program's roundings to bfloat16 on the way count: a program that leaves them out, or rounds other values in their place, can miss the bound.
Values may be sent and summed in bfloat16 or wider, within the bound.
A program may use at most 192 MiB of HBM per device.

```python
import math
import jax
import jax.numpy as jnp
import numpy as np
from jax import lax

D = 1536
HEADS = 48
STATE = 128
KCONV = 4
BLOCK_LEN = 256
INNER = 3072
GROUP = 512
LENGTH = 512
SEQS = 16
TOKENS = 8192
DOCS = 3
DOC_MAX = 256
N_DP = 16


def spiked(values, own_key, source, target, parts, factor):
    def block_of(dim):
        return (jnp.arange(values.shape[dim]) // (values.shape[dim] // parts)).reshape((-1,) + (1,) * (values.ndim - 1 - dim))

    one_side = jax.random.permutation(own_key, parts)[block_of(target)]
    far = (block_of(target) + parts // 2) % parts
    return jnp.where((block_of(source) == one_side) | (block_of(source) == far), factor * values, values)


def levels(key, extent, split, least, largest):
    loudness = 1.0
    for axis_at, shards_of in split:
        steps = jax.random.uniform(jax.random.fold_in(jax.random.fold_in(key, 6), axis_at), (shards_of,), jnp.float32, least / len(split), largest / len(split))
        loudness = loudness * jnp.repeat(jnp.exp(steps), extent[axis_at] // shards_of).reshape((-1,) + (1,) * (len(extent) - 1 - axis_at))
    return loudness


def profile(number_of, total, most, lean):
    loads = [(1 << 20) // math.isqrt(rank ** lean) + 1 for rank in range(2, number_of + 1)]
    surplus, given = total - most - (number_of - 1), [1] * (number_of - 1)
    while surplus > 0:
        free = [i for i in range(number_of - 1) if given[i] < most]
        whole, left = sum([loads[i] for i in free]), surplus
        for i in free:
            extra = min(most - given[i], max(1, left * loads[i] // whole), surplus)
            given[i] = given[i] + extra
            surplus = surplus - extra
    return np.array([most] + given)


def ragged(key, number_of, total, most, skew):
    if number_of == 2:
        one = jax.random.randint(key, (), max(1, total - most), min(most, total - 1) + 1)
        return jnp.stack([one, total - one])
    tallies = jnp.asarray(profile(number_of, total, most, skew), jnp.int32)
    twos = (number_of - 1) // 2
    donor, taker = tallies[1:1 + 2 * twos:2], tallies[2:2 + 2 * twos:2]
    room = jnp.minimum(donor - 1, most - taker)
    shifted = jax.random.randint(jax.random.fold_in(key, 1), (twos,), 0, 1 << 20) % (room + 1)
    tallies = tallies.at[1:1 + 2 * twos:2].set(donor - shifted).at[2:2 + 2 * twos:2].set(taker + shifted)
    return tallies[jax.random.permutation(jax.random.fold_in(key, 2), number_of)]


def gaussian(rng, shape, deviation, bound, cuts=(), held_as=jnp.bfloat16):
    values = deviation * jax.random.normal(rng, shape, jnp.float32)
    if cuts:
        values = values * levels(rng, shape, cuts, -0.22, 0.18)
    return jnp.clip(values, -bound, bound).astype(held_as)


def heavy_noise(rng, dims, scale, bound, shards, heavy, kind=jnp.bfloat16):
    array = scale * jax.random.normal(rng, dims, jnp.float32)
    if shards:
        array = array * levels(rng, dims, shards, -0.22, 0.18)
    return jnp.clip(spiked(array, jax.random.fold_in(rng, 3), *heavy), -bound, bound).astype(kind)


def setup_inputs(seed: int = 0) -> dict:
    splits = jax.random.split(jax.random.key(seed), 15)
    hidden_in = gaussian(splits[0], (TOKENS, D), 1.0, 6.0, ((0, 32),))
    prenorm_gain = jnp.clip(1.0 + 0.1 * jax.random.normal(splits[1], (D,), jnp.float32), 0.5, 1.5)
    w_zx = gaussian(splits[2], (D, 2, INNER), D ** -0.5, 0.15625, ((0, 16), (2, 2)))
    w_dt = gaussian(splits[3], (D, HEADS), D ** -0.5, 0.15625, ((0, 16), (1, 2)))
    w_bc = gaussian(splits[4], (D, 2 * STATE), D ** -0.5, 0.15625, ((0, 16),))
    conv_x = jnp.clip(jax.random.uniform(splits[5], (KCONV + 1, INNER), jnp.float32, -0.5, 0.5) * levels(splits[5], (KCONV + 1, INNER), ((1, 2),), -0.4, 0.0), -0.5, 0.5)
    conv_bc = jnp.clip(jax.random.uniform(splits[6], (KCONV + 1, 2 * STATE), jnp.float32, -0.5, 0.5), -0.5, 0.5)
    dt_bias = jnp.clip(-6.0 + 4.0 * jax.random.uniform(splits[7], (HEADS,), jnp.float32) ** levels(splits[7], (HEADS,), ((0, 2),), -0.2, 0.2), -6.0, -2.0)
    a_log = jnp.clip(2.77 * jax.random.uniform(splits[8], (HEADS,), jnp.float32) ** levels(splits[8], (HEADS,), ((0, 2),), -0.2, 0.2), 0.0, 2.77)
    d_skip = jnp.clip(1.0 + 0.18 * jax.random.normal(splits[9], (HEADS,), jnp.float32), 0.1, 1.9)
    norm_gain = jnp.clip(1.0 + 0.1 * jax.random.normal(splits[10], (INNER,), jnp.float32), 0.5, 1.5)
    w_out = gaussian(splits[11], (INNER, D), INNER ** -0.5, 0.109375, ((0, 2), (1, 16)))
    seg_ids = jax.vmap(lambda own: jnp.searchsorted(jnp.cumsum(ragged(own, DOCS, LENGTH, DOC_MAX, 1)), jnp.arange(LENGTH), side="right"))(jax.random.split(splits[12], SEQS)).reshape((SEQS, LENGTH)).astype(jnp.int32)
    grad_out = heavy_noise(splits[13], (TOKENS, D), 1.0, 12.0, ((0, 32),), (0, 1, 32, 2.75))
    return dict(hidden_in=hidden_in, prenorm_gain=prenorm_gain, w_zx=w_zx, w_dt=w_dt, w_bc=w_bc, conv_x=conv_x, conv_bc=conv_bc, dt_bias=dt_bias, a_log=a_log, d_skip=d_skip, norm_gain=norm_gain, w_out=w_out, seg_ids=seg_ids, grad_out=grad_out)


epsilon = 1e-05
highest = lax.Precision.HIGHEST

@jax.custom_vjp
def low(v):
    return lax.optimization_barrier(v.astype(jnp.bfloat16)).astype(jnp.float32)

@jax.custom_vjp
def low_back(v):
    return v

def low_keep(v):
    return (low(v), None)

def low_pass(kept, grad):
    return (grad,)

def back_keep(v):
    return (v, None)

def back_low(kept, grad):
    return (low(grad),)
low.defvjp(low_keep, low_pass)
low_back.defvjp(back_keep, back_low)

def causal_conv(signal, kernel, keep_mask):
    kernel_len = kernel.shape[0] - 1
    summed = kernel[kernel_len] + kernel[kernel_len - 1] * signal
    reach_mask = jnp.ones_like(keep_mask)
    for offset in range(1, kernel_len):
        reach_mask = reach_mask * jnp.pad(keep_mask, (offset - 1, 0))[:keep_mask.shape[0]]
        moved_rows = jnp.pad(signal, ((offset, 0), (0, 0)))[:signal.shape[0]]
        summed = summed + kernel[kernel_len - 1 - offset] * moved_rows * reach_mask[:, None]
    return summed

def block_scan(values, step_sizes, decay_rates, input_b, output_c, keep_mask, block_len):
    tokens = values.shape[0]
    blocks = tokens // block_len
    head_count = values.shape[1]
    head_dim = values.shape[2]
    state_dim = input_b.shape[1]
    lower_mask = jnp.arange(block_len)[:, None] >= jnp.arange(block_len)[None, :]
    lower_float = jnp.where(lower_mask, 1.0, 0.0).astype(values.dtype)

    def one_block(carry_state, pieces):
        block_vals, block_steps, block_b, block_c, block_keep = pieces
        counts = jnp.dot(lower_float, 1.0 - block_keep, precision=highest)
        log_decay = jnp.dot(lower_float, block_steps * decay_rates, precision=highest)
        same_run = jnp.where(lower_mask & (counts[:, None] == counts[None, :]), 1.0, 0.0).astype(values.dtype)
        carried = jnp.where(counts == 0.0, 1.0, 0.0).astype(values.dtype)
        differ = log_decay[:, None, :] - log_decay[None, :, :]
        decay = jnp.exp(jnp.where(same_run[:, :, None] > 0.0, differ, 0.0)) * same_run[:, :, None]
        inner_cb = jnp.dot(block_c, block_b.T, precision=highest)
        weights = decay * inner_cb[:, :, None] * block_steps[None, :, :]
        local_out = jnp.einsum('ijh,jhp->ihp', weights, block_vals, precision=highest)
        enter = carried[:, None] * jnp.exp(log_decay)
        from_state = jnp.einsum('in,hpn->ihp', block_c, carry_state, precision=highest) * enter[:, :, None]
        last_row = decay[block_len - 1] * block_steps
        new_state = carry_state * enter[block_len - 1][:, None, None] + jnp.einsum('jh,jhp,jn->hpn', last_row, block_vals, block_b, precision=highest)
        return (new_state, local_out + from_state)
    initial = jnp.zeros((head_count, head_dim, state_dim), values.dtype)
    pieces = (values.reshape(blocks, block_len, head_count, head_dim), step_sizes.reshape(blocks, block_len, head_count), input_b.reshape(blocks, block_len, state_dim), output_c.reshape(blocks, block_len, state_dim), keep_mask.reshape(blocks, block_len))
    final_state, outputs = lax.scan(jax.checkpoint(one_block), initial, pieces)
    return outputs.reshape(tokens, head_count, head_dim)

def mixer_core(proj_zx, dt_raw, proj_bc, conv_x, conv_bc, dt_bias, a_log, d_skip, keep_mask):
    gate_branch = proj_zx[:, 0, :]
    conv_in = jax.nn.silu(causal_conv(proj_zx[:, 1, :], conv_x, keep_mask))
    conv_bcs = jax.nn.silu(causal_conv(proj_bc, conv_bc, keep_mask))
    state_width = proj_bc.shape[1] // 2
    step_sizes = jax.nn.softplus(dt_raw + dt_bias)
    decay_rates = -jnp.exp(a_log)
    head_count = dt_raw.shape[1]
    values = conv_in.reshape(conv_in.shape[0], head_count, -1)
    scanned = block_scan(values, step_sizes, decay_rates, conv_bcs[:, :state_width], conv_bcs[:, state_width:], keep_mask, BLOCK_LEN)
    output = (scanned + d_skip[None, :, None] * values).reshape(conv_in.shape)
    return output * jax.nn.silu(gate_branch)

def block_forward(group_rows, params, keep_mask):
    prenorm_gain, w_zx, w_dt, w_bc, conv_x, conv_bc, dt_bias, a_log, d_skip, norm_gain, w_out = params
    scale_in = lax.rsqrt(lax.optimization_barrier(jnp.mean(group_rows * group_rows, axis=1, keepdims=True)) + epsilon)
    normed = low(group_rows * scale_in * prenorm_gain)
    proj_zx = low_back(jnp.einsum('td,dki->tki', normed, w_zx, precision=highest))
    dt_raw = low_back(jnp.dot(normed, w_dt, precision=highest))
    proj_bc = jnp.dot(normed, w_bc, precision=highest)
    mixed_in = mixer_core(proj_zx, dt_raw, proj_bc, conv_x, conv_bc, dt_bias, a_log, d_skip, keep_mask)
    scale_out = lax.rsqrt(lax.optimization_barrier(jnp.mean(mixed_in * mixed_in, axis=1, keepdims=True)) + epsilon)
    gated = low(mixed_in * scale_out * norm_gain)
    return group_rows + jnp.dot(gated, w_out, precision=highest)

def reference(hidden_in, prenorm_gain, w_zx, w_dt, w_bc, conv_x, conv_bc, dt_bias, a_log, d_skip, norm_gain, w_out, seg_ids, grad_out):
    weights = (prenorm_gain, w_zx.astype(jnp.float32), w_dt.astype(jnp.float32), w_bc.astype(jnp.float32), conv_x, conv_bc, dt_bias, a_log, d_skip, norm_gain, w_out.astype(jnp.float32))
    rows_all = hidden_in.astype(jnp.float32).reshape(N_DP, GROUP, D)
    cot_all = grad_out.astype(jnp.float32).reshape(N_DP, GROUP, D)
    seg_groups = seg_ids.reshape(N_DP, GROUP)
    position = jnp.arange(GROUP) % LENGTH

    def one_group(totals, pieces):
        group_rows, group_cot, seg_row = pieces
        previous = jnp.concatenate([seg_row[:1], seg_row[:-1]])
        keep_mask = jnp.where((position > 0) & (seg_row == previous), 1.0, 0.0).astype(jnp.float32)

        def forward(rows_in, params):
            return block_forward(rows_in, params, keep_mask)
        result, pullback = jax.vjp(forward, group_rows, weights)
        gradients = pullback(group_cot)
        totals = jax.tree.map(lambda earlier, later: earlier + later, totals, gradients[1])
        return (totals, (result, gradients[0]))
    initial = jax.tree.map(jnp.zeros_like, weights)
    totals, (results, row_grads) = lax.scan(one_group, initial, (rows_all, cot_all, seg_groups))
    block_out = results.reshape(TOKENS, D).astype(jnp.bfloat16)
    grad_in = row_grads.reshape(TOKENS, D).astype(jnp.bfloat16)
    return (block_out, grad_in, totals[0], totals[1], totals[2], totals[3], totals[4], totals[5], totals[6], totals[7], totals[8], totals[9], totals[10])
```

```python
import functools

import jax
import jax.numpy as jnp
from jax import lax
from jax.experimental import pallas as pl
from jax.experimental.pallas import tpu as pltpu
from jax.sharding import PartitionSpec as P

BLOCK_LEN = 256
EPS = 1e-05
NEG = -1e30
F32 = jnp.float32
BF16 = jnp.bfloat16
HIGHEST = lax.Precision.HIGHEST
VMEM_LIMIT = 60 * 1024 * 1024


def dot(a, b, dims=((1,), (0,)), precision=None):
    return lax.dot_general(a, b, (dims, ((), ())), preferred_element_type=F32, precision=precision)


NN, NT, TN = ((1,), (0,)), ((1,), (1,)), ((0,), (0,))


def sigmoid(w):
    return 1.0 / (1.0 + jnp.exp(-w))


def conv_of(signal, taps, masks):
    out = taps[4:5, :] + taps[3:4, :] * signal
    for back in range(1, 4):
        out = out + taps[3 - back : 4 - back, :] * (
            pltpu.roll(signal, back, 0) * masks[:, back - 1 : back]
        )
    return out


def conv_back(grad, signal, taps, masks):
    rows = signal.shape[0]
    grad_signal = taps[3:4, :] * grad
    tap_rows = [None] * 5
    tap_rows[4] = jnp.sum(grad, axis=0, keepdims=True)
    tap_rows[3] = jnp.sum(grad * signal, axis=0, keepdims=True)
    for back in range(1, 4):
        kept = grad * masks[:, back - 1 : back]
        tap_rows[3 - back] = jnp.sum(kept * pltpu.roll(signal, back, 0), axis=0, keepdims=True)
        grad_signal = grad_signal + taps[3 - back : 4 - back, :] * pltpu.roll(kept, rows - back, 0)
    return grad_signal, tap_rows


def expand(columns, width):
    rows, heads = columns.shape
    lane = lax.broadcasted_iota(jnp.int32, (rows, 2 * width), 1)
    pieces = [
        jnp.where(lane < width, columns[:, h : h + 1], columns[:, h + 1 : h + 2])
        for h in range(0, heads, 2)
    ]
    return pieces[0] if len(pieces) == 1 else jnp.concatenate(pieces, axis=1)


def block_rows(block, size):
    return pl.ds(pl.multiple_of(block * size, size), size)


def fwd_kernel(
    q, heads, width,
    nm_ref, w_ref, bcraw_ref, kx_ref, kbc_ref, la_ref, lat_ref, dt_ref, msk_ref, segc_ref, segr_ref, dsk_ref,
    s_ref, y_ref, st_ref,
    bcc, mneg, cb, xs, state,
):
    tokens = nm_ref.shape[0]
    blocks = tokens // q
    n = bcc.shape[1] // 2
    lanes = heads * width

    @pl.when(pl.program_id(0) == 0)
    def _():
        c = conv_of(bcraw_ref[...], kbc_ref[...], msk_ref[...])
        bcc[...] = c * sigmoid(c)
        later = lax.broadcasted_iota(jnp.int32, (q, q), 0) >= lax.broadcasted_iota(jnp.int32, (q, q), 1)

        def prepare(b, carry):
            rows = block_rows(b, q)
            same = segc_ref[rows, :] == segr_ref[:, rows]
            mneg[rows, :] = jnp.where(later & same, 0.0, NEG)
            cb[rows, :] = dot(bcc[rows, n:], bcc[rows, :n], NT, HIGHEST)
            return carry

        lax.fori_loop(0, blocks, prepare, 0)

    s = dot(nm_ref[...], w_ref[...])
    s_ref[...] = s
    c = conv_of(s, kx_ref[...], msk_ref[...])
    xs[...] = c * sigmoid(c)
    state[...] = jnp.zeros_like(state)
    lane_head = lax.broadcasted_iota(jnp.int32, (q, lanes), 1) // width

    def one_block(b, carry):
        rows = block_rows(b, q)
        x = xs[rows, :]
        la = la_ref[0, rows, :]
        u = x * expand(dt_ref[0, rows, :], width)
        ub = u.astype(BF16)
        enter = expand(jnp.exp(la) * msk_ref[rows, 3:4], width)
        last = expand(jnp.exp(la[q - 1 : q, :] - la) * msk_ref[rows, 4:5], width)
        st = state[...]
        st_ref[b] = st
        base = mneg[rows, :]
        cb_b = cb[rows, :]
        weights, values = [], []
        for h in range(heads):
            decay = jnp.exp(la[:, h : h + 1] - lat_ref[0, h : h + 1, rows] + base)
            weights.append((decay * cb_b).astype(BF16))
            values.append(jnp.where(lane_head == h, ub, jnp.zeros_like(ub)))
        local = dot(jnp.concatenate(weights, axis=1), jnp.concatenate(values, axis=0))
        carried = dot(bcc[rows, n:].astype(BF16), st.astype(BF16))
        y_ref[rows, :] = local + carried * enter + dsk_ref[...] * x
        state[...] = st * enter[q - 1 : q, :] + dot(
            bcc[rows, :n].astype(BF16), (u * last).astype(BF16), TN
        )
        return carry

    lax.fori_loop(0, blocks, one_block, 0, unroll=blocks <= 2)


def bwd_kernel(
    q, heads, width,
    s_ref, dy_ref, bcraw_ref, kx_ref, kbc_ref, la_ref, lat_ref, dt_ref, msk_ref, segc_ref, segr_ref, dsk_ref, st_ref,
    ds_ref, gk_ref, row_ref, col_ref, dbc_ref, gkbc_ref,
    bcc, mnegt, cbt, xs, dxs, dtt, gt,
):
    tokens = s_ref.shape[0]
    blocks = tokens // q
    n = bcc.shape[1] // 2
    lanes = heads * width
    step = pl.program_id(0)

    @pl.when(step == 0)
    def _():
        c = conv_of(bcraw_ref[...], kbc_ref[...], msk_ref[...])
        bcc[...] = c * sigmoid(c)
        dtt[...] = jnp.zeros_like(dtt)
        dbc_ref[...] = jnp.zeros_like(dbc_ref)
        col_ref[...] = jnp.zeros_like(col_ref)
        earlier = lax.broadcasted_iota(jnp.int32, (q, q), 0) <= lax.broadcasted_iota(jnp.int32, (q, q), 1)

        def prepare(b, carry):
            rows = block_rows(b, q)
            same = segc_ref[rows, :] == segr_ref[:, rows]
            mnegt[rows, :] = jnp.where(earlier & same, 0.0, NEG)
            cbt[rows, :] = dot(bcc[rows, :n], bcc[rows, n:], NT, HIGHEST)
            return carry

        lax.fori_loop(0, blocks, prepare, 0)

    c = conv_of(s_ref[...], kx_ref[...], msk_ref[...])
    xs[...] = c * sigmoid(c)
    gt[...] = jnp.zeros_like(gt)
    lane_head = lax.broadcasted_iota(jnp.int32, (q, lanes), 1) // width
    pick = jnp.where(
        lax.broadcasted_iota(jnp.int32, (8, lanes), 1) // width
        == lax.broadcasted_iota(jnp.int32, (8, lanes), 0),
        1.0,
        0.0,
    )
    token_lane = lax.broadcasted_iota(jnp.int32, (1, q), 1)
    col_lane = lax.broadcasted_iota(jnp.int32, (q, col_ref.shape[1]), 1)

    def one_block(i, carry):
        b = blocks - 1 - i
        rows = block_rows(b, q)
        x = xs[rows, :]
        dy = dy_ref[rows, :]
        la = la_ref[0, rows, :]
        dtx = expand(dt_ref[0, rows, :], width)
        u = x * dtx
        ub, dyb = u.astype(BF16), dy.astype(BF16)
        enter = expand(jnp.exp(la) * msk_ref[rows, 3:4], width)
        last = expand(jnp.exp(la[q - 1 : q, :] - la) * msk_ref[rows, 4:5], width)
        base = mnegt[rows, :]
        cb_b = cbt[rows, :]
        weights, values, row_sums = [], [], []
        d_cb = jnp.zeros((q, q), F32)
        col_sums = jnp.zeros((q, col_ref.shape[1]), F32)
        for h in range(heads):
            own = lane_head == h
            decay = jnp.exp(lat_ref[0, h : h + 1, rows] - la[:, h : h + 1] + base)
            dyh = jnp.where(own, dyb, jnp.zeros_like(dyb))
            pair = dot(ub, dyh, NT)
            weight = decay * cb_b
            d_cb = d_cb + decay * pair
            both = weight * pair
            row_sums.append(jnp.sum(both, axis=0, keepdims=True))
            col_sums = jnp.where(
                col_lane == step * heads + h, jnp.sum(both, axis=1, keepdims=True), col_sums
            )
            weights.append(weight.astype(BF16))
            values.append(dyh)
        dtt[rows, :] += d_cb
        col_ref[rows, :] += col_sums
        g = gt[...]
        gb16 = g.astype(BF16)
        st = st_ref[b]
        stb = st.astype(BF16)
        c16 = bcc[rows, n:].astype(BF16)
        b16 = bcc[rows, :n].astype(BF16)
        gb = dot(b16, gb16) * last
        du = dot(jnp.concatenate(weights, axis=1), jnp.concatenate(values, axis=0)) + gb
        dye = (dy * enter).astype(BF16)
        from_state = dot(c16, stb) * enter
        dbc_ref[rows, n:] += dot(dye, stb, NT)
        dbc_ref[rows, :n] += dot((u * last).astype(BF16), gb16, NT)
        ug = u * gb
        dla = dot(pick, dy * from_state - ug, NT, HIGHEST)
        ddt = dot(pick, x * du, NT, HIGHEST)
        tail = jnp.sum(ug, axis=0, keepdims=True) + enter[q - 1 : q, :] * jnp.sum(
            g * st, axis=0, keepdims=True
        )
        for h in range(heads):
            end = jnp.sum(
                jnp.where(lane_head[0:1, :] == h, tail, 0.0), axis=1, keepdims=True
            )
            row_ref[0, h : h + 1, rows] = (
                row_sums[h] + dla[h : h + 1, :] + jnp.where(token_lane == q - 1, end, 0.0)
            )
            row_ref[0, heads + h : heads + h + 1, rows] = ddt[h : h + 1, :]
        gt[...] = g * enter[q - 1 : q, :] + dot(c16, dye, TN)
        dxs[rows, :] = dtx * du + dsk_ref[...] * dy
        return carry

    lax.fori_loop(0, blocks, one_block, 0, unroll=blocks <= 2)

    s = s_ref[...]
    taps = kx_ref[...]
    masks = msk_ref[...]
    c = conv_of(s, taps, masks)
    sig = sigmoid(c)
    grad = dxs[...] * sig * (1.0 + c * (1.0 - sig))
    d_s, tap_rows = conv_back(grad, s, taps, masks)
    ds_ref[...] = d_s.astype(BF16)
    skip_row = jnp.sum(dy_ref[...] * xs[...], axis=0, keepdims=True)
    gk_ref[...] = jnp.concatenate(
        tap_rows + [skip_row, jnp.zeros_like(skip_row), jnp.zeros_like(skip_row)], axis=0
    )

    @pl.when(step == pl.num_programs(0) - 1)
    def _():
        def finish(b, carry):
            rows = block_rows(b, q)
            d_cb = dtt[rows, :]
            dbc_ref[rows, :n] += dot(d_cb, bcc[rows, n:], NN, HIGHEST)
            dbc_ref[rows, n:] += dot(d_cb, bcc[rows, :n], TN, HIGHEST)
            return carry

        lax.fori_loop(0, blocks, finish, 0)
        raw = bcraw_ref[...]
        taps_bc = kbc_ref[...]
        c_bc = conv_of(raw, taps_bc, masks)
        sig_bc = sigmoid(c_bc)
        grad_bc = dbc_ref[...] * sig_bc * (1.0 + c_bc * (1.0 - sig_bc))
        d_bc, bc_rows = conv_back(grad_bc, raw, taps_bc, masks)
        dbc_ref[...] = d_bc
        zero_row = jnp.zeros_like(bc_rows[0])
        gkbc_ref[...] = jnp.concatenate(bc_rows + [zero_row] * 3, axis=0)


def full(shape):
    return pl.BlockSpec(shape, lambda i: (0,) * len(shape))


def lane_block(rows, lanes):
    return pl.BlockSpec((rows, lanes), lambda i: (0, i))


def lead_block(shape):
    return pl.BlockSpec((1,) + shape, lambda i: (i, 0, 0))


def heads_per_step(head_count):
    return 4 if head_count % 4 == 0 else 2


def grouped(per_head, heads):
    tokens, head_count = per_head.shape
    return per_head.reshape(tokens, head_count // heads, heads).transpose(1, 0, 2)


def grouped_rows(per_head, heads):
    tokens, head_count = per_head.shape
    return per_head.T.reshape(head_count // heads, heads, tokens)


def scan_forward(normed, w_s, common, conv_x, la, dt, skip_lanes, q):
    bcraw, conv_bc, masks, seg_col, seg_row = common
    tokens, depth = normed.shape
    inner = w_s.shape[1]
    head_count = la.shape[1]
    width = inner // head_count
    heads = heads_per_step(head_count)
    lanes = heads * width
    n = bcraw.shape[1] // 2
    blocks = tokens // q
    groups = head_count // heads
    return pl.pallas_call(
        functools.partial(fwd_kernel, q, heads, width),
        grid=(groups,),
        in_specs=[
            full((tokens, depth)), lane_block(depth, lanes), full((tokens, 2 * n)), lane_block(5, lanes),
            full((5, 2 * n)), lead_block((tokens, heads)), lead_block((heads, tokens)), lead_block((tokens, heads)),
            full((tokens, 8)), full((tokens, 1)), full((1, tokens)), lane_block(1, lanes),
        ],
        out_specs=[
            lane_block(tokens, lanes), lane_block(tokens, lanes),
            pl.BlockSpec((blocks, n, lanes), lambda i: (0, 0, i)),
        ],
        out_shape=[
            jax.ShapeDtypeStruct((tokens, inner), F32), jax.ShapeDtypeStruct((tokens, inner), F32),
            jax.ShapeDtypeStruct((blocks, n, inner), F32),
        ],
        scratch_shapes=[
            pltpu.VMEM((tokens, 2 * n), F32), pltpu.VMEM((tokens, q), F32), pltpu.VMEM((tokens, q), F32),
            pltpu.VMEM((tokens, lanes), F32), pltpu.VMEM((n, lanes), F32),
        ],
        compiler_params=pltpu.CompilerParams(
            dimension_semantics=("arbitrary",), vmem_limit_bytes=VMEM_LIMIT
        ),
        cost_estimate=pl.CostEstimate(
            flops=2 * tokens * inner * (depth + q + 4 * n),
            bytes_accessed=2 * (depth * inner + tokens * depth) + 8 * tokens * inner,
            transcendentals=tokens * q * head_count,
        ),
        name="scan_forward",
    )(
        normed, w_s, bcraw, conv_x, conv_bc, grouped(la, heads), grouped_rows(la, heads), grouped(dt, heads),
        masks, seg_col, seg_row, skip_lanes,
    )


def scan_backward(s, dy, common, conv_x, la, dt, skip_lanes, states, q):
    bcraw, conv_bc, masks, seg_col, seg_row = common
    tokens, inner = s.shape
    head_count = la.shape[1]
    width = inner // head_count
    heads = heads_per_step(head_count)
    lanes = heads * width
    n = bcraw.shape[1] // 2
    blocks = tokens // q
    groups = head_count // heads
    return pl.pallas_call(
        functools.partial(bwd_kernel, q, heads, width),
        grid=(groups,),
        in_specs=[
            lane_block(tokens, lanes), lane_block(tokens, lanes), full((tokens, 2 * n)), lane_block(5, lanes),
            full((5, 2 * n)), lead_block((tokens, heads)), lead_block((heads, tokens)), lead_block((tokens, heads)),
            full((tokens, 8)), full((tokens, 1)), full((1, tokens)), lane_block(1, lanes),
            pl.BlockSpec((blocks, n, lanes), lambda i: (0, 0, i)),
        ],
        out_specs=[
            lane_block(tokens, lanes), lane_block(8, lanes), lead_block((2 * heads, tokens)),
            full((tokens, 128)), full((tokens, 2 * n)), full((8, 2 * n)),
        ],
        out_shape=[
            jax.ShapeDtypeStruct((tokens, inner), BF16), jax.ShapeDtypeStruct((8, inner), F32),
            jax.ShapeDtypeStruct((groups, 2 * heads, tokens), F32), jax.ShapeDtypeStruct((tokens, 128), F32),
            jax.ShapeDtypeStruct((tokens, 2 * n), F32), jax.ShapeDtypeStruct((8, 2 * n), F32),
        ],
        scratch_shapes=[
            pltpu.VMEM((tokens, 2 * n), F32), pltpu.VMEM((tokens, q), F32), pltpu.VMEM((tokens, q), F32),
            pltpu.VMEM((tokens, lanes), F32), pltpu.VMEM((tokens, lanes), F32), pltpu.VMEM((tokens, q), F32),
            pltpu.VMEM((n, lanes), F32),
        ],
        compiler_params=pltpu.CompilerParams(
            dimension_semantics=("arbitrary",), vmem_limit_bytes=VMEM_LIMIT
        ),
        cost_estimate=pl.CostEstimate(
            flops=2 * tokens * inner * (8 * q + 8 * n),
            bytes_accessed=12 * tokens * inner,
            transcendentals=tokens * q * head_count,
        ),
        name="scan_backward",
    )(
        s, dy, bcraw, conv_x, conv_bc, grouped(la, heads), grouped_rows(la, heads), grouped(dt, heads),
        masks, seg_col, seg_row, skip_lanes, states,
    )


class Links:
    def __init__(self, dp, tp):
        self.dp, self.tp = dp, tp
        self.staged = dp == 16 and tp == 2

    def place(self):
        me = lax.axis_index("dp")
        return me // 4, (me // 2) % 2, me % 2

    def along_z(self, value, by):
        pairs = [(i, (i // 4 + by) % 4 * 4 + i % 4) for i in range(16)]
        return lax.ppermute(value, "dp", pairs)

    def along_y(self, value):
        return lax.ppermute(value, "dp", [(i, i ^ 2) for i in range(16)])

    def to_core(self, value):
        return lax.ppermute(value, "dp", [(i, i ^ 1) for i in range(16)])

    def along_x(self, value):
        return lax.ppermute(value, "tensor", [(0, 1), (1, 0)])

    def gather_rows(self, value):
        if not self.staged:
            return lax.all_gather(value, "tensor", axis=0, tiled=True)
        other = self.along_x(value)
        first = lax.axis_index("tensor") == 0
        return jnp.concatenate(
            [jnp.where(first, value, other), jnp.where(first, other, value)], axis=0
        )

    def add_rows(self, make):
        if not self.staged:
            parts = jnp.concatenate([make(i) for i in range(self.tp)], axis=0)
            return lax.psum_scatter(parts, "tensor", scatter_dimension=0, tiled=True)
        me = lax.axis_index("tensor")
        away = self.along_x(make(1 - me).astype(BF16))
        return make(me) + away.astype(F32)

    def sum_tensor(self, value):
        if not self.staged:
            return lax.psum(value, "tensor")
        return value + self.along_x(value)

    def gather_weight(self, value, after=None):
        if not self.staged:
            return lax.all_gather(value, "dp", axis=0, tiled=True), None
        if after is not None:
            value, after = lax.optimization_barrier((value, after))
        z, y, c = self.place()
        by = [value] + [self.along_z(value, d) for d in (1, 2, 3)]
        line = jnp.stack([lax.select_n((z - k) % 4, *by) for k in range(4)])
        other = self.along_y(line)
        low = y == 0
        plane = jnp.stack([jnp.where(low, line, other), jnp.where(low, other, line)], axis=1)
        other = self.to_core(plane)
        low = c == 0
        whole = jnp.stack([jnp.where(low, plane, other), jnp.where(low, other, plane)], axis=2)
        return whole.reshape((16 * value.shape[0],) + value.shape[1:]), line

    def split_rows(self, left):
        if not self.staged:
            return left
        z, y, c = self.place()
        parts = left.reshape(4, 2, 2, left.shape[0] // 16, left.shape[1])
        own = lax.dynamic_index_in_dim(parts, c, 2, keepdims=False)
        away = lax.dynamic_index_in_dim(parts, 1 - c, 2, keepdims=False)
        pick = lambda i: lax.dynamic_index_in_dim(own, i, 1, keepdims=False)
        return away, pick(y), pick(1 - y)

    def scatter_product(self, split, right):
        if not self.staged:
            return lax.psum_scatter(dot(split, right), "dp", scatter_dimension=0, tiled=True)
        away, own, across = split
        z, y, c = self.place()
        rows, columns = own.shape[1], right.shape[1]
        product = lambda part: dot(part.reshape(-1, part.shape[-1]), right).reshape(
            part.shape[:-1] + (columns,)
        )
        came = self.to_core(product(away).astype(BF16))
        pick = lambda i: lax.dynamic_index_in_dim(came, i, 1, keepdims=False).astype(F32)
        far = self.along_y((product(across) + pick(1 - y)).astype(BF16))
        near = product(own) + pick(y) + far.astype(F32)
        part = lambda i: lax.dynamic_index_in_dim(near, i, 0, keepdims=False)
        total = part(z)
        for d in (1, 2, 3):
            total = total + self.along_z(part((z + d) % 4).astype(BF16), d).astype(F32)
        return total

    def sum_dp(self, value):
        if not self.staged:
            return lax.psum(value, "dp")
        value = value + self.to_core(value)
        value = value + self.along_y(value)
        return value + self.along_z(value, 1) + self.along_z(value, 2) + self.along_z(value, 3)

    def own_half(self, value):
        if not self.staged:
            return lax.psum_scatter(
                value, "tensor", scatter_dimension=value.ndim - 1, tiled=True
            )
        me = lax.axis_index("tensor")
        size = value.shape[-1] // 2
        half = lambda i: lax.dynamic_slice_in_dim(value, i * size, size, value.ndim - 1)
        return half(me) + self.along_x(half(1 - me))


def body(
    links,
    hidden_in,
    prenorm_gain,
    w_zx,
    w_dt,
    w_bc,
    conv_x,
    conv_bc,
    dt_bias,
    a_log,
    d_skip,
    norm_gain,
    w_out,
    seg_ids,
    grad_out,
):
    q = BLOCK_LEN
    inner = w_out.shape[0]
    head_count = dt_bias.shape[0]
    width = inner // head_count
    bc_width = w_bc.shape[1]
    shard = w_bc.shape[0]
    tp = links.tp
    inner_total = inner * tp

    small, line = links.gather_weight(jnp.concatenate([w_bc, w_dt], axis=1))
    halves = 2 if head_count % 8 == 0 else 1
    part = inner // halves
    w_s = []
    for i in range(halves):
        gathered, line = links.gather_weight(w_zx[:, 1, i * part : (i + 1) * part], line)
        w_s.append(gathered)
    w_z, line = links.gather_weight(w_zx[:, 0, :], line)
    w_out_t, line = links.gather_weight(w_out.T, line)

    full_rows = links.gather_rows(hidden_in)
    rows_float = full_rows.astype(F32)
    mean_square = jnp.mean(rows_float * rows_float, axis=1, keepdims=True)
    scale_in = lax.rsqrt(mean_square + EPS)
    normed = (rows_float * scale_in * prenorm_gain).astype(BF16)
    cot_rows = links.gather_rows(grad_out)
    tokens = normed.shape[0]
    blocks = tokens // q

    flat_ids = seg_ids + seg_ids.shape[1] * lax.broadcasted_iota(jnp.int32, seg_ids.shape, 0)
    flat_ids = flat_ids.reshape(-1)
    shifted = lambda l: jnp.concatenate([jnp.full((l,), -1, jnp.int32), flat_ids[:-l]])
    by_block = flat_ids.reshape(blocks, q)
    before = jnp.concatenate([jnp.full((1,), -1, jnp.int32), by_block[:-1, -1]])
    carried = (by_block == before[:, None]).reshape(-1)
    run_last = (by_block == by_block[:, -1:]).reshape(-1)
    never = jnp.zeros_like(carried)
    masks = jnp.stack(
        [flat_ids == shifted(1), flat_ids == shifted(2), flat_ids == shifted(3), carried, run_last]
        + [never] * 3,
        axis=1,
    ).astype(F32)
    seg_float = flat_ids.astype(F32)

    small_proj = dot(normed, small)
    bcraw = small_proj[:, :bc_width]
    dt_in = small_proj[:, bc_width:] + dt_bias
    dt = jax.nn.softplus(dt_in)
    rate = -jnp.exp(a_log)
    lower = jnp.where(jnp.arange(q)[:, None] >= jnp.arange(q)[None, :], 1.0, 0.0)
    la = jnp.einsum(
        "ij,bjh->bih", lower, (dt * rate).reshape(blocks, q, head_count), precision=HIGHEST
    ).reshape(tokens, head_count)
    common = (bcraw, conv_bc, masks, seg_float[:, None], seg_float[None, :])
    skip_lanes = jnp.repeat(d_skip, width)[None, :]

    outs = []
    for i in range(halves):
        cut, hcut = slice(i * part, (i + 1) * part), slice(i * part // width, (i + 1) * part // width)
        outs.append(
            scan_forward(
                normed, w_s[i], common, conv_x[:, cut], la[:, hcut], dt[:, hcut], skip_lanes[:, cut], q
            )
        )
    s, y, states = [
        outs[0][k] if halves == 1 else jnp.concatenate([o[k] for o in outs], axis=-1) for k in range(3)
    ]

    z = dot(normed, w_z)
    gate_sig = sigmoid(z)
    gate = z * gate_sig
    v = y * gate
    grad_gated = dot(cot_rows, w_out_t)
    scaled_grad = grad_gated * norm_gain
    sums = links.sum_tensor(
        jnp.stack([jnp.sum(v * v, axis=1), jnp.sum(scaled_grad * v, axis=1)])
    )
    scale_out = lax.rsqrt(sums[0] / inner_total + EPS)[:, None]
    pull = sums[1][:, None] * scale_out**3 / inner_total
    gated = (v * scale_out * norm_gain).astype(BF16)
    grad_norm_gain = jnp.sum(grad_gated * v * scale_out, axis=0)
    d_v = scaled_grad * scale_out - pull * v
    d_y = d_v * gate
    d_z = (d_v * y * gate_sig * (1.0 + z * (1.0 - gate_sig))).astype(BF16)

    cot_split = links.split_rows(cot_rows.T)
    grad_w_out = links.scatter_product(cot_split, gated).T
    norm_split = links.split_rows(normed.T)
    grad_w_z = links.scatter_product(norm_split, d_z)

    own_rows = tokens // tp
    rows_of = lambda array, i: lax.dynamic_slice_in_dim(array, i * own_rows, own_rows, 0)
    projected = links.add_rows(lambda i: dot(rows_of(gated, i), w_out_t, NT))
    block_out = (hidden_in.astype(F32) + projected).astype(BF16)

    d_s, grad_taps, row_terms, col_terms, d_bc, grad_taps_bc = scan_backward(
        s, d_y, common, conv_x, la, dt, skip_lanes, states, q
    )
    heads = row_terms.shape[1] // 2
    d_la = row_terms[:, :heads].reshape(head_count, tokens).T - col_terms[:, :head_count]
    d_dt = row_terms[:, heads:].reshape(head_count, tokens).T
    d_exponent = jnp.einsum(
        "ji,bjh->bih", lower, d_la.reshape(blocks, q, head_count), precision=HIGHEST
    ).reshape(tokens, head_count)
    d_dt = d_dt + rate * d_exponent
    d_dt_raw = d_dt * jax.nn.sigmoid(dt_in)
    grad_a_log = rate * jnp.sum(dt * d_exponent, axis=0)
    grad_dt_bias = jnp.sum(d_dt_raw, axis=0)
    grad_d_skip = jnp.sum(grad_taps[5].reshape(head_count, width), axis=1)
    low_dt = d_dt_raw.astype(BF16)
    high_bc = d_bc.astype(BF16)
    low_bc = (d_bc - high_bc.astype(F32)).astype(BF16)

    d_small = jnp.concatenate([high_bc, low_dt], axis=1)
    grad_last = links.scatter_product(norm_split, jnp.concatenate([d_s, d_small], axis=1))
    grad_w_zx = jnp.stack([grad_w_z, grad_last[:, :inner]], axis=1)
    grad_w_bc = links.own_half(grad_last[:, inner : inner + bc_width])
    grad_w_dt = grad_last[:, inner + bc_width :]

    w_s_whole = w_s[0] if halves == 1 else jnp.concatenate(w_s, axis=1)

    def column_grad(i):
        return (
            dot(rows_of(d_z, i), w_z, NT)
            + dot(rows_of(d_s, i), w_s_whole, NT)
            + dot(rows_of(d_small, i), small, NT)
            + dot(rows_of(low_bc, i), small[:, :bc_width], NT)
        )

    def back_rows(i, columns):
        unit = rows_of(rows_float, i) * rows_of(scale_in, i)
        grad_unit = columns * prenorm_gain
        return rows_of(scale_in, i) * (
            grad_unit - unit * jnp.mean(grad_unit * unit, axis=1, keepdims=True)
        )

    prenorm_terms = []

    def grad_rows(i):
        columns = column_grad(i)
        prenorm_terms.append(jnp.sum(columns * (rows_of(rows_float, i) * rows_of(scale_in, i)), axis=0))
        return back_rows(i, columns)

    own_grad = links.add_rows(grad_rows)
    grad_in = (grad_out.astype(F32) + own_grad).astype(BF16)
    grad_prenorm = sum(prenorm_terms)

    pieces = [
        grad_taps[:5].reshape(-1),
        grad_taps_bc[:5].reshape(-1),
        grad_norm_gain,
        grad_prenorm,
        grad_dt_bias,
        grad_a_log,
        grad_d_skip,
    ]
    flat = jnp.concatenate(pieces)
    flat = jnp.pad(flat, (0, -flat.shape[0] % 1024)).reshape(-1, 128)
    flat = links.sum_dp(flat).reshape(-1)
    at, cut_out = 0, []
    for piece in pieces:
        cut_out.append(flat[at : at + piece.shape[0]])
        at += piece.shape[0]
    grad_conv_bc = links.own_half(cut_out[1].reshape(5, bc_width))
    grad_prenorm = links.own_half(cut_out[3][None, :])[0]
    return (
        block_out,
        grad_in,
        grad_prenorm,
        grad_w_zx,
        grad_w_dt,
        grad_w_bc,
        cut_out[0].reshape(5, inner),
        grad_conv_bc,
        cut_out[4],
        cut_out[5],
        cut_out[6],
        cut_out[2],
        grad_w_out,
    )


def solution(mesh):
    links = Links(mesh.shape["dp"], mesh.shape["tensor"])
    in_specs = (
        P(("dp", "tensor"), None),
        P(),
        P("dp", None, "tensor"),
        P("dp", "tensor"),
        P("dp", None),
        P(None, "tensor"),
        P(),
        P("tensor"),
        P("tensor"),
        P("tensor"),
        P("tensor"),
        P("tensor", "dp"),
        P("dp", None),
        P(("dp", "tensor"), None),
    )
    out_specs = (
        P(("dp", "tensor"), None),
        P(("dp", "tensor"), None),
        P("tensor"),
        P("dp", None, "tensor"),
        P("dp", "tensor"),
        P("dp", "tensor"),
        P(None, "tensor"),
        P(None, "tensor"),
        P("tensor"),
        P("tensor"),
        P("tensor"),
        P("tensor"),
        P("tensor", "dp"),
    )
    return jax.shard_map(
        functools.partial(body, links),
        mesh=mesh,
        in_specs=in_specs,
        out_specs=out_specs,
        check_vma=False,
    )
```

```python
import functools

import jax
import jax.numpy as jnp
from jax import lax
from jax.experimental import pallas as pl
from jax.experimental.pallas import tpu as pltpu
from jax.sharding import PartitionSpec as P

BLOCK_LEN = 256
EPS = 1e-05
NEG = -1e30
F32 = jnp.float32
BF16 = jnp.bfloat16
HIGHEST = lax.Precision.HIGHEST
VMEM_LIMIT = 60 * 1024 * 1024


def dot(a, b, dims=((1,), (0,)), precision=None):
    return lax.dot_general(a, b, (dims, ((), ())), preferred_element_type=F32, precision=precision)


NN, NT, TN = ((1,), (0,)), ((1,), (1,)), ((0,), (0,))


def sigmoid(w):
    return 1.0 / (1.0 + jnp.exp(-w))


def conv_of(signal, taps, masks):
    out = taps[4:5, :] + taps[3:4, :] * signal
    for back in range(1, 4):
        out = out + taps[3 - back : 4 - back, :] * (
            pltpu.roll(signal, back, 0) * masks[:, back - 1 : back]
        )
    return out


def conv_back(grad, signal, taps, masks):
    rows = signal.shape[0]
    grad_signal = taps[3:4, :] * grad
    tap_rows = [None] * 5
    tap_rows[4] = jnp.sum(grad, axis=0, keepdims=True)
    tap_rows[3] = jnp.sum(grad * signal, axis=0, keepdims=True)
    for back in range(1, 4):
        kept = grad * masks[:, back - 1 : back]
        tap_rows[3 - back] = jnp.sum(kept * pltpu.roll(signal, back, 0), axis=0, keepdims=True)
        grad_signal = grad_signal + taps[3 - back : 4 - back, :] * pltpu.roll(kept, rows - back, 0)
    return grad_signal, tap_rows


def expand(columns, width):
    rows, heads = columns.shape
    lane = lax.broadcasted_iota(jnp.int32, (rows, 2 * width), 1)
    pieces = [
        jnp.where(lane < width, columns[:, h : h + 1], columns[:, h + 1 : h + 2])
        for h in range(0, heads, 2)
    ]
    return pieces[0] if len(pieces) == 1 else jnp.concatenate(pieces, axis=1)


def block_rows(block, size):
    return pl.ds(pl.multiple_of(block * size, size), size)


def head_lanes(array, step, heads):
    return pltpu.roll(array, lax.rem(128 - step * heads, 128), 1)


def fwd_kernel(
    q, heads, width,
    nm_ref, w_ref, bcraw_ref, kx_ref, kbc_ref, la_ref, dt_ref, msk_ref, segr_ref, dsk_ref,
    s_ref, y_ref, st_ref,
    bcc, mneg, cb, xs, state, la4, lat4, dt4,
):
    tokens = nm_ref.shape[0]
    blocks = tokens // q
    n = bcc.shape[1] // 2
    lanes = heads * width
    step = pl.program_id(0)

    @pl.when(step == 0)
    def _():
        c = conv_of(bcraw_ref[...], kbc_ref[...], msk_ref[...])
        bcc[...] = c * sigmoid(c)
        later = lax.broadcasted_iota(jnp.int32, (q, q), 0) >= lax.broadcasted_iota(jnp.int32, (q, q), 1)

        def prepare(b, carry):
            rows = block_rows(b, q)
            same = msk_ref[rows, 5:6] == segr_ref[:, rows]
            mneg[rows, :] = jnp.where(later & same, 0.0, NEG)
            cb[rows, :] = dot(bcc[rows, n:], bcc[rows, :n], NT, HIGHEST)
            return carry

        lax.fori_loop(0, blocks, prepare, 0)

    la_here = head_lanes(la_ref[...], step, heads)
    la4[...] = la_here
    lat4[...] = la_here.T[0:8, :]
    dt4[...] = head_lanes(dt_ref[...], step, heads)
    s = dot(nm_ref[...], w_ref[...])
    s_ref[...] = s
    c = conv_of(s, kx_ref[...], msk_ref[...])
    xs[...] = c * sigmoid(c)
    state[...] = jnp.zeros_like(state)
    lane_head = lax.broadcasted_iota(jnp.int32, (q, lanes), 1) // width

    def one_block(b, carry):
        rows = block_rows(b, q)
        x = xs[rows, :]
        la = la4[rows, 0:heads]
        u = x * expand(dt4[rows, 0:heads], width)
        ub = u.astype(BF16)
        enter = expand(jnp.exp(la) * msk_ref[rows, 3:4], width)
        last = expand(jnp.exp(la[q - 1 : q, :] - la) * msk_ref[rows, 4:5], width)
        st = state[...]
        st_ref[b] = st
        base = mneg[rows, :]
        cb_b = cb[rows, :]
        weights, values = [], []
        for h in range(heads):
            decay = jnp.exp(la[:, h : h + 1] - lat4[h : h + 1, rows] + base)
            weights.append((decay * cb_b).astype(BF16))
            values.append(jnp.where(lane_head == h, ub, jnp.zeros_like(ub)))
        local = dot(jnp.concatenate(weights, axis=1), jnp.concatenate(values, axis=0))
        carried = dot(bcc[rows, n:].astype(BF16), st.astype(BF16))
        y_ref[rows, :] = local + carried * enter + dsk_ref[...] * x
        state[...] = st * enter[q - 1 : q, :] + dot(
            bcc[rows, :n].astype(BF16), (u * last).astype(BF16), TN
        )
        return carry

    lax.fori_loop(0, blocks, one_block, 0, unroll=blocks <= 2)


def bwd_kernel(
    q, heads, width,
    s_ref, dy_ref, bcraw_ref, kx_ref, kbc_ref, la_ref, dt_ref, msk_ref, segr_ref, dsk_ref, st_ref, dtin_ref, rate_ref,
    ds_ref, gk_ref, small_ref, dbc_ref, gkbc_ref, ghead_ref,
    bcc, mnegt, cbt, xs, dxs, dtt, gt, la4, lat4, dt4, dla_acc, ddt_acc, dbc_acc,
):
    tokens = s_ref.shape[0]
    blocks = tokens // q
    n = bcc.shape[1] // 2
    lanes = heads * width
    step = pl.program_id(0)

    @pl.when(step == 0)
    def _():
        c = conv_of(bcraw_ref[...], kbc_ref[...], msk_ref[...])
        bcc[...] = c * sigmoid(c)
        dtt[...] = jnp.zeros_like(dtt)
        dbc_acc[...] = jnp.zeros_like(dbc_acc)
        dla_acc[...] = jnp.zeros_like(dla_acc)
        ddt_acc[...] = jnp.zeros_like(ddt_acc)
        earlier = lax.broadcasted_iota(jnp.int32, (q, q), 0) <= lax.broadcasted_iota(jnp.int32, (q, q), 1)

        def prepare(b, carry):
            rows = block_rows(b, q)
            same = msk_ref[rows, 5:6] == segr_ref[:, rows]
            mnegt[rows, :] = jnp.where(earlier & same, 0.0, NEG)
            cbt[rows, :] = dot(bcc[rows, :n], bcc[rows, n:], NT, HIGHEST)
            return carry

        lax.fori_loop(0, blocks, prepare, 0)

    la_here = head_lanes(la_ref[...], step, heads)
    la4[...] = la_here
    lat4[...] = la_here.T[0:8, :]
    dt4[...] = head_lanes(dt_ref[...], step, heads)
    c = conv_of(s_ref[...], kx_ref[...], msk_ref[...])
    xs[...] = c * sigmoid(c)
    gt[...] = jnp.zeros_like(gt)
    lane_head = lax.broadcasted_iota(jnp.int32, (q, lanes), 1) // width
    pick = jnp.where(
        lax.broadcasted_iota(jnp.int32, (8, lanes), 1) // width
        == lax.broadcasted_iota(jnp.int32, (8, lanes), 0),
        1.0,
        0.0,
    )
    token_lane = lax.broadcasted_iota(jnp.int32, (1, q), 1)
    col_lane = lax.broadcasted_iota(jnp.int32, (q, 128), 1)

    def one_block(i, carry):
        b = blocks - 1 - i
        rows = block_rows(b, q)
        x = xs[rows, :]
        dy = dy_ref[rows, :]
        la = la4[rows, 0:heads]
        dtx = expand(dt4[rows, 0:heads], width)
        u = x * dtx
        ub, dyb = u.astype(BF16), dy.astype(BF16)
        enter = expand(jnp.exp(la) * msk_ref[rows, 3:4], width)
        last = expand(jnp.exp(la[q - 1 : q, :] - la) * msk_ref[rows, 4:5], width)
        base = mnegt[rows, :]
        cb_b = cbt[rows, :]
        weights, values, row_sums = [], [], []
        d_cb = jnp.zeros((q, q), F32)
        col_sums = jnp.zeros((q, 128), F32)
        for h in range(heads):
            own = lane_head == h
            decay = jnp.exp(lat4[h : h + 1, rows] - la[:, h : h + 1] + base)
            dyh = jnp.where(own, dyb, jnp.zeros_like(dyb))
            pair = dot(ub, dyh, NT)
            weight = decay * cb_b
            d_cb = d_cb + decay * pair
            both = weight * pair
            row_sums.append(jnp.sum(both, axis=0, keepdims=True))
            col_sums = jnp.where(col_lane == h, jnp.sum(both, axis=1, keepdims=True), col_sums)
            weights.append(weight.astype(BF16))
            values.append(dyh)
        dtt[rows, :] += d_cb
        g = gt[...]
        gb16 = g.astype(BF16)
        st = st_ref[b]
        stb = st.astype(BF16)
        c16 = bcc[rows, n:].astype(BF16)
        b16 = bcc[rows, :n].astype(BF16)
        gb = dot(b16, gb16) * last
        du = dot(jnp.concatenate(weights, axis=1), jnp.concatenate(values, axis=0)) + gb
        dye = (dy * enter).astype(BF16)
        from_state = dot(c16, stb) * enter
        dbc_acc[rows, n:] += dot(dye, stb, NT)
        dbc_acc[rows, :n] += dot((u * last).astype(BF16), gb16, NT)
        ug = u * gb
        dla = dot(pick, dy * from_state - ug, NT, HIGHEST)
        ddt = dot(pick, x * du, NT, HIGHEST)
        tail = jnp.sum(ug, axis=0, keepdims=True) + enter[q - 1 : q, :] * jnp.sum(
            g * st, axis=0, keepdims=True
        )
        la_rows = []
        for h in range(heads):
            end = jnp.sum(jnp.where(lane_head[0:1, :] == h, tail, 0.0), axis=1, keepdims=True)
            la_rows.append(
                row_sums[h] + dla[h : h + 1, :] + jnp.where(token_lane == q - 1, end, 0.0)
            )
        dt_rows = [ddt[h : h + 1, :] for h in range(heads)]
        rest = jnp.zeros((128 - 2 * heads, q), F32)
        columns = jnp.concatenate(la_rows + dt_rows + [rest], axis=0).T
        la_part = jnp.where(col_lane < heads, columns, 0.0) - col_sums
        dt_part = jnp.where(col_lane >= heads, columns, 0.0)
        dla_acc[rows, :] += pltpu.roll(la_part, step * heads, 1)
        ddt_acc[rows, :] += pltpu.roll(dt_part, lax.rem(128 + (step - 1) * heads, 128), 1)
        gt[...] = g * enter[q - 1 : q, :] + dot(c16, dye, TN)
        dxs[rows, :] = dtx * du + dsk_ref[...] * dy
        return carry

    lax.fori_loop(0, blocks, one_block, 0, unroll=blocks <= 2)

    s = s_ref[...]
    taps = kx_ref[...]
    masks = msk_ref[...]
    c = conv_of(s, taps, masks)
    sig = sigmoid(c)
    grad = dxs[...] * sig * (1.0 + c * (1.0 - sig))
    d_s, tap_rows = conv_back(grad, s, taps, masks)
    ds_ref[...] = d_s.astype(BF16)
    skip_row = jnp.sum(dy_ref[...] * xs[...], axis=0, keepdims=True)
    gk_ref[...] = jnp.concatenate(
        tap_rows + [skip_row, jnp.zeros_like(skip_row), jnp.zeros_like(skip_row)], axis=0
    )

    @pl.when(step == pl.num_programs(0) - 1)
    def _():
        upper = jnp.where(
            lax.broadcasted_iota(jnp.int32, (q, q), 0) <= lax.broadcasted_iota(jnp.int32, (q, q), 1), 1.0, 0.0
        )

        def finish(b, carry):
            rows = block_rows(b, q)
            d_cb = dtt[rows, :]
            dbc_acc[rows, :n] += dot(d_cb, bcc[rows, n:], NN, HIGHEST)
            dbc_acc[rows, n:] += dot(d_cb, bcc[rows, :n], TN, HIGHEST)
            dla_acc[rows, :] = dot(upper, dla_acc[rows, :], NN, HIGHEST)
            return carry

        lax.fori_loop(0, blocks, finish, 0)
        rate = rate_ref[...]
        d_exponent = dla_acc[...]
        d_raw = (ddt_acc[...] + rate * d_exponent) * sigmoid(dtin_ref[...])
        d_rate = rate * jnp.sum(dt_ref[...] * d_exponent, axis=0, keepdims=True)
        d_bias = jnp.sum(d_raw, axis=0, keepdims=True)
        ghead_ref[...] = jnp.concatenate([d_bias, d_rate, jnp.zeros((6, 128), F32)], axis=0)
        raw = bcraw_ref[...]
        taps_bc = kbc_ref[...]
        c_bc = conv_of(raw, taps_bc, masks)
        sig_bc = sigmoid(c_bc)
        grad_bc = dbc_acc[...] * sig_bc * (1.0 + c_bc * (1.0 - sig_bc))
        d_bc, bc_rows = conv_back(grad_bc, raw, taps_bc, masks)
        high = d_bc.astype(BF16)
        small_ref[:, : 2 * n] = high
        small_ref[:, 2 * n :] = d_raw.astype(BF16)
        dbc_ref[...] = (d_bc - high.astype(F32)).astype(BF16)
        zero_row = jnp.zeros_like(bc_rows[0])
        gkbc_ref[...] = jnp.concatenate(bc_rows + [zero_row] * 3, axis=0)


def full(shape):
    return pl.BlockSpec(shape, lambda i: (0,) * len(shape))


def lane_block(rows, lanes):
    return pl.BlockSpec((rows, lanes), lambda i: (0, i))


def heads_per_step(head_count):
    return 4 if head_count % 4 == 0 else 2


def scan_forward(normed, w_s, prep, conv_x, conv_bc, skip_lanes, width, q):
    bcraw, la, dt, masks, seg_row = (prep[k] for k in ("bcraw", "la", "dt", "masks", "seg_row"))
    tokens, depth = normed.shape
    inner = w_s.shape[1]
    head_count = inner // width
    heads = heads_per_step(head_count)
    lanes = heads * width
    n = bcraw.shape[1] // 2
    blocks = tokens // q
    return pl.pallas_call(
        functools.partial(fwd_kernel, q, heads, width),
        grid=(head_count // heads,),
        in_specs=[
            full((tokens, depth)), lane_block(depth, lanes), full((tokens, 2 * n)), lane_block(5, lanes),
            full((5, 2 * n)), full((tokens, 128)), full((tokens, 128)), full((tokens, 128)),
            full((1, tokens)), lane_block(1, lanes),
        ],
        out_specs=[
            lane_block(tokens, lanes), lane_block(tokens, lanes),
            pl.BlockSpec((blocks, n, lanes), lambda i: (0, 0, i)),
        ],
        out_shape=[
            jax.ShapeDtypeStruct((tokens, inner), F32), jax.ShapeDtypeStruct((tokens, inner), F32),
            jax.ShapeDtypeStruct((blocks, n, inner), F32),
        ],
        scratch_shapes=[
            pltpu.VMEM((tokens, 2 * n), F32), pltpu.VMEM((tokens, q), F32), pltpu.VMEM((tokens, q), F32),
            pltpu.VMEM((tokens, lanes), F32), pltpu.VMEM((n, lanes), F32), pltpu.VMEM((tokens, 128), F32),
            pltpu.VMEM((8, tokens), F32), pltpu.VMEM((tokens, 128), F32),
        ],
        compiler_params=pltpu.CompilerParams(
            dimension_semantics=("arbitrary",), vmem_limit_bytes=VMEM_LIMIT
        ),
        cost_estimate=pl.CostEstimate(
            flops=2 * tokens * inner * (depth + q + 4 * n),
            bytes_accessed=2 * (depth * inner + tokens * depth) + 8 * tokens * inner,
            transcendentals=tokens * q * head_count,
        ),
        name="scan_forward",
    )(normed, w_s, bcraw, conv_x, conv_bc, la, dt, masks, seg_row, skip_lanes)


def scan_backward(s, dy, prep, conv_x, conv_bc, skip_lanes, states, width, q):
    bcraw, la, dt, masks, seg_row = (prep[k] for k in ("bcraw", "la", "dt", "masks", "seg_row"))
    tokens, inner = s.shape
    head_count = inner // width
    heads = heads_per_step(head_count)
    lanes = heads * width
    n = bcraw.shape[1] // 2
    blocks = tokens // q
    return pl.pallas_call(
        functools.partial(bwd_kernel, q, heads, width),
        grid=(head_count // heads,),
        in_specs=[
            lane_block(tokens, lanes), lane_block(tokens, lanes), full((tokens, 2 * n)), lane_block(5, lanes),
            full((5, 2 * n)), full((tokens, 128)), full((tokens, 128)), full((tokens, 128)),
            full((1, tokens)), lane_block(1, lanes), pl.BlockSpec((blocks, n, lanes), lambda i: (0, 0, i)),
            full((tokens, 128)), full((1, 128)),
        ],
        out_specs=[
            lane_block(tokens, lanes), lane_block(8, lanes), full((tokens, 2 * n + 128)),
            full((tokens, 2 * n)), full((8, 2 * n)), full((8, 128)),
        ],
        out_shape=[
            jax.ShapeDtypeStruct((tokens, inner), BF16), jax.ShapeDtypeStruct((8, inner), F32),
            jax.ShapeDtypeStruct((tokens, 2 * n + 128), BF16), jax.ShapeDtypeStruct((tokens, 2 * n), BF16),
            jax.ShapeDtypeStruct((8, 2 * n), F32), jax.ShapeDtypeStruct((8, 128), F32),
        ],
        scratch_shapes=[
            pltpu.VMEM((tokens, 2 * n), F32), pltpu.VMEM((tokens, q), F32), pltpu.VMEM((tokens, q), F32),
            pltpu.VMEM((tokens, lanes), F32), pltpu.VMEM((tokens, lanes), F32), pltpu.VMEM((tokens, q), F32),
            pltpu.VMEM((n, lanes), F32), pltpu.VMEM((tokens, 128), F32), pltpu.VMEM((8, tokens), F32),
            pltpu.VMEM((tokens, 128), F32), pltpu.VMEM((tokens, 128), F32), pltpu.VMEM((tokens, 128), F32),
            pltpu.VMEM((tokens, 2 * n), F32),
        ],
        compiler_params=pltpu.CompilerParams(
            dimension_semantics=("arbitrary",), vmem_limit_bytes=VMEM_LIMIT
        ),
        cost_estimate=pl.CostEstimate(
            flops=2 * tokens * inner * (8 * q + 8 * n),
            bytes_accessed=12 * tokens * inner,
            transcendentals=tokens * q * head_count,
        ),
        name="scan_backward",
    )(
        s, dy, bcraw, conv_x, conv_bc, la, dt, masks, seg_row, skip_lanes, states, prep["dt_in"], prep["rate"],
    )


MESH = pl.DeviceIdType.MESH


class Here:
    def __init__(self):
        self.me = lax.axis_index("dp")
        self.t = lax.axis_index("tensor")
        self.z = self.me // 4
        self.y = (self.me // 2) % 2
        self.c = self.me % 2

    def slot(self, z, y, c):
        return z * 4 + y * 2 + c

    def z_plus(self, d):
        return (self.z + d) % 4

    def at_z(self, d):
        return (self.slot(self.z_plus(d), self.y, self.c), self.t)

    def across_y(self):
        return (self.slot(self.z, 1 - self.y, self.c), self.t)

    def other_core(self):
        return (self.slot(self.z, self.y, 1 - self.c), self.t)

    def across_x(self):
        return (self.me, 1 - self.t)

    def greet(self):
        barrier = pltpu.get_barrier_semaphore()
        for peer in (self.at_z(1), self.at_z(2), self.at_z(3), self.across_y(), self.other_core(), self.across_x()):
            pl.semaphore_signal(barrier, inc=1, device_id=peer, device_id_type=MESH)
        pl.semaphore_wait(barrier, 6)


def send(src, dst, sems, index, peer):
    return pltpu.make_async_remote_copy(
        src_ref=src, dst_ref=dst, send_sem=sems.at[0, index], recv_sem=sems.at[1, index],
        device_id=peer, device_id_type=MESH,
    )


class Gather:
    COPIES = 15

    def __init__(self, here, src, dst, sems, local_sem):
        self.here, self.src, self.dst, self.sems = here, src, dst, sems
        self.local = pltpu.make_async_copy(src, dst.at[here.me], local_sem)

    def slot_of(self, d, far):
        here = self.here
        return here.slot(here.z_plus(4 - d), 1 - here.y if far else here.y, here.c)

    def z_copy(self, d):
        return send(self.src, self.dst.at[self.here.me], self.sems, d - 1, self.here.at_z(d))

    def y_copy(self, d):
        slot = self.slot_of(d, False)
        src = self.src if d == 0 else self.dst.at[slot]
        return send(src, self.dst.at[slot], self.sems, 3 + d, self.here.across_y())

    def core_copy(self, k):
        slot = self.slot_of(k % 4, k >= 4)
        src = self.src if k == 0 else self.dst.at[slot]
        return send(src, self.dst.at[slot], self.sems, 7 + k, self.here.other_core())

    def start(self):
        for d in (1, 2, 3):
            self.z_copy(d).start()
        self.y_copy(0).start()
        self.core_copy(0).start()
        self.local.start()

    def pass_z(self):
        for d in (1, 2, 3):
            self.z_copy(d).wait_recv()
            self.y_copy(d).start()
            self.core_copy(d).start()

    def pass_y(self):
        for d in range(4):
            self.y_copy(d).wait_recv()
            self.core_copy(4 + d).start()

    def arrived(self):
        self.local.wait()
        for k in range(8):
            self.core_copy(k).wait_recv()

    def sent(self):
        for d in (1, 2, 3):
            self.z_copy(d).wait_send()
        for d in range(4):
            self.y_copy(d).wait_send()
        for k in range(8):
            self.core_copy(k).wait_send()


def softplus(w):
    return jnp.maximum(w, 0.0) + jnp.log1p(jnp.exp(-jnp.abs(w)))


def gather_kernel(
    q,
    hid_ref, cot_ref, small_ref, ws_ref, wz_ref, wo_ref, gain_ref, bias_ref, rate_ref, seg_ref,
    rows_out, cot_out, small_out, ws_out, wz_out, wo_out,
    normed_out, scale_out, bcraw_out, dtin_out, dt_out, la_out, masks_out,
    small_sems, ws_sems, wz_sems, wo_sems, x_sems, local_sems,
):
    here = Here()
    tokens = normed_out.shape[0]
    half = tokens // 2
    here.greet()
    hidden = send(hid_ref, rows_out.at[here.t], x_sems, 0, here.across_x())
    cotangent = send(cot_ref, cot_out.at[here.t], x_sems, 1, here.across_x())
    gathers = [
        Gather(here, src, dst, sems, local_sems.at[i])
        for i, (src, dst, sems) in enumerate(
            [
                (small_ref, small_out, small_sems),
                (ws_ref, ws_out, ws_sems),
                (wz_ref, wz_out, wz_sems),
                (wo_ref, wo_out, wo_sems),
            ]
        )
    ]
    small, ws, wz, wo = gathers
    hidden.start()
    for gather in gathers:
        gather.start()
    cotangent.start()
    own_hidden = pltpu.make_async_copy(hid_ref, rows_out.at[here.t], local_sems.at[4])
    own_cot = pltpu.make_async_copy(cot_ref, cot_out.at[here.t], local_sems.at[5])
    own_hidden.start()
    own_cot.start()

    seg = jnp.broadcast_to(seg_ref[...], (128, tokens)).T
    row = lax.broadcasted_iota(jnp.int32, (tokens, 128), 0)
    lane = lax.broadcasted_iota(jnp.int32, (tokens, 128), 1)
    masks = jnp.where(lane == 5, seg, 0.0)
    for back in (1, 2, 3):
        same = (pltpu.roll(seg, back, 0) == seg) & (row >= back)
        masks = jnp.where((lane == back - 1) & same, 1.0, masks)
    for b in range(tokens // q):
        inside = (row >= b * q) & (row < (b + 1) * q)
        if b:
            carried = inside & (seg == seg[b * q - 1 : b * q, :])
            masks = jnp.where((lane == 3) & carried, 1.0, masks)
        run_last = inside & (seg == seg[(b + 1) * q - 1 : (b + 1) * q, :])
        masks = jnp.where((lane == 4) & run_last, 1.0, masks)
    masks_out[...] = masks

    small.pass_z()
    ws.pass_z()
    small.pass_y()

    own_hidden.wait()
    hidden.wait_recv()
    gain = gain_ref[...]
    chunk = 64

    def norm(i, carry):
        side, at = i // (half // chunk), i % (half // chunk)
        rows = pl.ds(pl.multiple_of(at * chunk, chunk), chunk)
        values = rows_out[side, rows, :].astype(F32)
        scale = lax.rsqrt(jnp.mean(values * values, axis=1, keepdims=True) + EPS)
        out_rows = pl.ds(pl.multiple_of(i * chunk, chunk), chunk)
        normed_out[out_rows, :] = (values * scale * gain).astype(BF16)
        scale_out[out_rows, :] = jnp.broadcast_to(scale, (chunk, 128))
        return carry

    lax.fori_loop(0, tokens // chunk, norm, 0)
    wz.pass_z()
    ws.pass_y()
    small.arrived()
    pieces, shard, columns = small_out.shape
    proj = dot(normed_out[...], small_out[...].reshape(pieces * shard, columns))
    bc_width = columns - 128
    bcraw_out[...] = proj[:, :bc_width]
    dt_in = proj[:, bc_width:] + bias_ref[...]
    dtin_out[...] = dt_in
    dt = softplus(dt_in)
    dt_out[...] = dt
    lower = jnp.where(
        lax.broadcasted_iota(jnp.int32, (q, q), 0) >= lax.broadcasted_iota(jnp.int32, (q, q), 1), 1.0, 0.0
    )
    exponent = dt * rate_ref[...]
    for b in range(tokens // q):
        la_out[b * q : (b + 1) * q, :] = dot(lower, exponent[b * q : (b + 1) * q, :], NN, HIGHEST)
    wo.pass_z()
    wz.pass_y()
    wo.pass_y()
    own_cot.wait()
    cotangent.wait_recv()
    for gather in gathers[1:]:
        gather.arrived()
    hidden.wait_send()
    cotangent.wait_send()
    for gather in gathers:
        gather.sent()


def in_vmem():
    return pl.BlockSpec(memory_space=pltpu.VMEM)


def in_any():
    return pl.BlockSpec(memory_space=pl.ANY)


def gather_all(hidden, cot, small, ws, wz, wo, gain, bias, rate, seg_row, q):
    half, depth = hidden.shape
    tokens = 2 * half
    shard, inner = ws.shape
    columns = small.shape[1]
    shape = jax.ShapeDtypeStruct
    sems = pltpu.SemaphoreType.DMA
    outs = pl.pallas_call(
        functools.partial(gather_kernel, q),
        in_specs=[in_vmem()] * 10,
        out_specs=[in_vmem()] * 3 + [in_any()] * 3 + [in_vmem()] * 7,
        out_shape=[
            shape((2, half, depth), BF16), shape((2, half, depth), BF16), shape((16, shard, columns), BF16),
            shape((16, shard, inner), BF16), shape((16, shard, inner), BF16), shape((16, shard, wo.shape[1]), BF16),
            shape((tokens, depth), BF16), shape((tokens, 128), F32), shape((tokens, columns - 128), F32),
            shape((tokens, 128), F32), shape((tokens, 128), F32), shape((tokens, 128), F32), shape((tokens, 128), F32),
        ],
        scratch_shapes=[sems((2, 15))] * 4 + [sems((2, 2)), sems((6,))],
        compiler_params=pltpu.CompilerParams(
            collective_id=0, has_side_effects=True, vmem_limit_bytes=VMEM_LIMIT
        ),
        name="gather_all",
    )(hidden, cot, small, ws, wz, wo, gain, bias, rate, seg_row)
    flat = lambda a: a.reshape((-1, a.shape[-1]))
    return [flat(a) for a in outs]


class Scatter:
    COPIES = 15

    def __init__(self, here, product, out, own, from_core, from_y, from_z, sems, local_sems):
        self.here, self.product, self.out, self.own = here, product, out, own
        self.from_core, self.from_y, self.from_z = from_core, from_y, from_z
        self.sems, self.local_sems = sems, local_sems

    def piece(self, k, core):
        here = self.here
        return here.slot(k % 4, 1 - here.y if k < 4 else here.y, core)

    def load(self, k):
        return pltpu.make_async_copy(
            self.product.at[self.piece(k, self.here.c)], self.own.at[k], self.local_sems.at[k]
        )

    def core_copy(self, k):
        src = self.product.at[self.piece(k, 1 - self.here.c)]
        return send(src, self.from_core.at[k], self.sems, k, self.here.other_core())

    def y_copy(self, k):
        return send(self.own.at[k], self.from_y.at[k], self.sems, 8 + k, self.here.across_y())

    def z_copy(self, d):
        src = self.own.at[4 + self.here.z_plus(d)]
        return send(src, self.from_z.at[d - 1], self.sems, 11 + d, self.here.at_z(d))

    def start(self):
        for k in range(8):
            self.core_copy(k).start()
            self.load(k).start()

    def by_rows(self, step):
        rows = self.own.shape[1]

        def one(i, carry):
            step(pl.ds(pl.multiple_of(i * 16, 16), 16))
            return carry

        lax.fori_loop(0, rows // 16, one, 0)

    def to_y(self):
        for k in range(4):
            self.load(k).wait()
            self.core_copy(k).wait_recv()

            def add(rows, k=k):
                total = self.own[k, rows, :].astype(F32) + self.from_core[k, rows, :].astype(F32)
                self.own[k, rows, :] = total.astype(BF16)

            self.by_rows(add)
            self.y_copy(k).start()

    def to_z(self):
        for k in range(4, 8):
            self.load(k).wait()
            self.core_copy(k).wait_recv()
        for k in range(4):
            self.y_copy(k).wait_recv()
        for d in (1, 2, 3):
            at = self.here.z_plus(d)

            def add(rows, at=at):
                total = (
                    self.own[4 + at, rows, :].astype(F32)
                    + self.from_core[4 + at, rows, :].astype(F32)
                    + self.from_y[at, rows, :].astype(F32)
                )
                self.own[4 + at, rows, :] = total.astype(BF16)

            self.by_rows(add)
            self.z_copy(d).start()

    def finish(self):
        at = self.here.z
        for d in (1, 2, 3):
            self.z_copy(d).wait_recv()

        def add(rows):
            total = (
                self.own[4 + at, rows, :].astype(F32)
                + self.from_core[4 + at, rows, :].astype(F32)
                + self.from_y[at, rows, :].astype(F32)
            )
            for d in range(3):
                total = total + self.from_z[d, rows, :].astype(F32)
            self.out[rows, :] = total

        self.by_rows(add)

    def sent(self):
        for k in range(8):
            self.core_copy(k).wait_send()
        for k in range(4):
            self.y_copy(k).wait_send()
        for d in (1, 2, 3):
            self.z_copy(d).wait_send()


def scatter_kernel(
    matrices, x_rows, *refs
):
    refs = list(refs)
    take = lambda count: [refs.pop(0) for _ in range(count)]
    products, (xa_ref, xb_ref, sums_ref) = take(matrices), take(3)
    outs, (xa_out, xb_out, sums_out) = take(matrices), take(3)
    buffers = [take(4) for _ in range(matrices)]
    sems, local_sems = take(matrices), take(matrices)
    x_sems, sum_sems, sum_own, sum_came = take(4)
    here = Here()
    here.greet()
    scatters = [
        Scatter(here, products[i], outs[i], *buffers[i], sems[i], local_sems[i]) for i in range(matrices)
    ]
    core_sum = send(sums_ref, sum_came.at[0], sum_sems, 0, here.other_core())
    y_sum = send(sum_own.at[0], sum_came.at[1], sum_sems, 1, here.across_y())
    z_sums = [send(sum_own.at[1], sum_came.at[1 + d], sum_sems, 1 + d, here.at_z(d)) for d in (1, 2, 3)]
    x_part = pl.ds(0, x_rows)
    x_sum = send(sum_own.at[2, x_part], sum_came.at[5, x_part], sum_sems, 5, here.across_x())
    xa = send(xa_ref, xa_out, x_sems, 0, here.across_x())
    xb = send(xb_ref, xb_out, x_sems, 1, here.across_x())
    core_sum.start()
    for scatter in scatters:
        scatter.start()
    core_sum.wait_recv()
    sum_own[0] = sums_ref[...] + sum_came[0]
    y_sum.start()
    for scatter in scatters:
        scatter.to_y()
    y_sum.wait_recv()
    sum_own[1] = sum_own[0] + sum_came[1]
    for copy in z_sums:
        copy.start()
    scatters[0].to_z()
    for copy in z_sums:
        copy.wait_recv()
    sum_own[2] = sum_own[1] + sum_came[2] + sum_came[3] + sum_came[4]
    x_sum.start()
    xa.start()
    xb.start()
    for i in range(1, matrices):
        scatters[i].to_z()
        scatters[i - 1].finish()
    x_sum.wait_recv()
    sums_out[...] = sum_own[2]
    sums_out[0:x_rows, :] = sum_own[2, 0:x_rows, :] + sum_came[5, 0:x_rows, :]
    scatters[-1].finish()
    for copy in (xa, xb):
        copy.wait()
    for copy in [core_sum, y_sum, x_sum] + z_sums:
        copy.wait_send()
    for scatter in scatters:
        scatter.sent()


def scatter_all(products, xa, xb, sums, x_rows):
    shape = jax.ShapeDtypeStruct
    sems = pltpu.SemaphoreType.DMA
    matrices = len(products)
    scratch = []
    for product in products:
        piece = product.shape[1:]
        scratch += [pltpu.VMEM((count,) + piece, BF16) for count in (8, 8, 4, 3)]
    scratch += [sems((2, 15))] * matrices + [sems((8,))] * matrices
    scratch += [sems((2, 2)), sems((2, 6)), pltpu.VMEM((3,) + sums.shape, F32), pltpu.VMEM((6,) + sums.shape, F32)]
    return pl.pallas_call(
        functools.partial(scatter_kernel, matrices, x_rows),
        in_specs=[in_any()] * (matrices + 2) + [in_vmem()],
        out_specs=[in_vmem()] * matrices + [in_any()] * 2 + [in_vmem()],
        out_shape=[shape(product.shape[1:], F32) for product in products]
        + [shape(xa.shape, BF16), shape(xb.shape, BF16), shape(sums.shape, F32)],
        scratch_shapes=scratch,
        compiler_params=pltpu.CompilerParams(
            collective_id=1, has_side_effects=True, vmem_limit_bytes=VMEM_LIMIT
        ),
        name="scatter_all",
    )(*products, xa, xb, sums)


def lanes_of(per_head):
    return jnp.pad(per_head, [(0, 0)] * (per_head.ndim - 1) + [(0, 128 - per_head.shape[-1])])


def prepare_plain(normed, small, bias, rate, flat_ids, q):
    tokens = normed.shape[0]
    blocks = tokens // q
    proj = dot(normed, small)
    bc_width = small.shape[1] - 128
    dt_in = proj[:, bc_width:] + bias
    dt = jax.nn.softplus(dt_in)
    lower = jnp.where(jnp.arange(q)[:, None] >= jnp.arange(q)[None, :], 1.0, 0.0)
    la = jnp.einsum("ij,bjh->bih", lower, (dt * rate).reshape(blocks, q, 128), precision=HIGHEST)
    shifted = lambda l: jnp.concatenate([jnp.full((l,), -1, jnp.int32), flat_ids[:-l]])
    by_block = flat_ids.reshape(blocks, q)
    before = jnp.concatenate([jnp.full((1,), -1, jnp.int32), by_block[:-1, -1]])
    carried = (by_block == before[:, None]).reshape(-1)
    run_last = (by_block == by_block[:, -1:]).reshape(-1)
    masks = [flat_ids == shifted(1), flat_ids == shifted(2), flat_ids == shifted(3), carried, run_last, flat_ids]
    return proj[:, :bc_width], dt_in, dt, la.reshape(tokens, 128), lanes_of(jnp.stack(masks, axis=1).astype(F32))


def body(
    dp,
    tp,
    hidden_in,
    prenorm_gain,
    w_zx,
    w_dt,
    w_bc,
    conv_x,
    conv_bc,
    dt_bias,
    a_log,
    d_skip,
    norm_gain,
    w_out,
    seg_ids,
    grad_out,
):
    q = BLOCK_LEN
    staged = dp == 16 and tp == 2
    inner = w_out.shape[0]
    head_count = dt_bias.shape[0]
    width = inner // head_count
    bc_width = w_bc.shape[1]
    shard = w_bc.shape[0]
    depth = hidden_in.shape[1]
    inner_total = inner * tp
    tensor = lax.axis_index("tensor")

    bias = lanes_of(dt_bias)[None, :]
    rate = lanes_of(-jnp.exp(a_log))[None, :]
    small_shard = jnp.concatenate([w_bc, lanes_of(w_dt)], axis=1)
    flat_ids = (seg_ids + seg_ids.shape[1] * lax.broadcasted_iota(jnp.int32, seg_ids.shape, 0)).reshape(-1)
    seg_row = flat_ids.astype(F32)[None, :]
    skip_lanes = jnp.repeat(d_skip, width)[None, :]
    prep = dict(rate=rate, seg_row=seg_row)

    if staged:
        (
            full_rows, cot_rows, small, w_s, w_z, w_out_t, normed, scale_in,
            prep["bcraw"], prep["dt_in"], prep["dt"], prep["la"], prep["masks"],
        ) = gather_all(
            hidden_in, grad_out, small_shard, w_zx[:, 1, :], w_zx[:, 0, :], w_out.T,
            prenorm_gain[None, :], bias, rate, seg_row, q,
        )
        scale_in = scale_in[:, :1]
        rows_float = full_rows.astype(F32)
    else:
        over_dp = lambda value: lax.all_gather(value, "dp", axis=0, tiled=True)
        small = over_dp(small_shard)
        w_s, w_z, w_out_t = over_dp(w_zx[:, 1, :]), over_dp(w_zx[:, 0, :]), over_dp(w_out.T)
        rows_float = lax.all_gather(hidden_in, "tensor", axis=0, tiled=True).astype(F32)
        cot_rows = lax.all_gather(grad_out, "tensor", axis=0, tiled=True)
        scale_in = lax.rsqrt(jnp.mean(rows_float * rows_float, axis=1, keepdims=True) + EPS)
        normed = (rows_float * scale_in * prenorm_gain).astype(BF16)
        prep["bcraw"], prep["dt_in"], prep["dt"], prep["la"], prep["masks"] = prepare_plain(
            normed, small, bias, rate, flat_ids, q
        )
    tokens = normed.shape[0]

    s, y, states = scan_forward(normed, w_s, prep, conv_x, conv_bc, skip_lanes, width, q)

    z = dot(normed, w_z)
    gate_sig = sigmoid(z)
    gate = z * gate_sig
    v = y * gate
    grad_gated = dot(cot_rows, w_out_t)
    scaled_grad = grad_gated * norm_gain
    sums = jnp.stack([jnp.sum(v * v, axis=1), jnp.sum(scaled_grad * v, axis=1)])
    if staged:
        sums = sums + lax.ppermute(sums, "tensor", [(0, 1), (1, 0)])
    else:
        sums = lax.psum(sums, "tensor")
    scale_out = lax.rsqrt(sums[0] / inner_total + EPS)[:, None]
    pull = sums[1][:, None] * scale_out**3 / inner_total
    gated = (v * scale_out * norm_gain).astype(BF16)
    grad_norm_gain = jnp.sum(grad_gated * v * scale_out, axis=0)
    d_v = scaled_grad * scale_out - pull * v
    d_y = d_v * gate
    d_z = (d_v * y * gate_sig * (1.0 + z * (1.0 - gate_sig))).astype(BF16)

    d_s, grad_taps, d_small, low_bc, grad_taps_bc, grad_heads = scan_backward(
        s, d_y, prep, conv_x, conv_bc, skip_lanes, states, width, q
    )
    grad_d_skip = jnp.sum(grad_taps[5].reshape(head_count, width), axis=1)

    own_rows = tokens // tp
    rows_of = lambda array, i: lax.dynamic_slice_in_dim(array, i * own_rows, own_rows, 0)
    project = lambda i: dot(rows_of(gated, i), w_out_t, NT)
    prenorm_terms = []

    def grad_rows(i):
        columns = (
            dot(rows_of(d_z, i), w_z, NT)
            + dot(rows_of(d_s, i), w_s, NT)
            + dot(rows_of(d_small, i), small, NT)
            + dot(rows_of(low_bc, i), small[:, :bc_width], NT)
        )
        unit = rows_of(rows_float, i) * rows_of(scale_in, i)
        prenorm_terms.append(jnp.sum(columns * unit, axis=0))
        grad_unit = columns * prenorm_gain
        return rows_of(scale_in, i) * (
            grad_unit - unit * jnp.mean(grad_unit * unit, axis=1, keepdims=True)
        )

    products = [
        dot(cot_rows, gated, TN),
        dot(normed, d_z, TN),
        dot(normed, jnp.concatenate([d_s, d_small], axis=1), TN),
    ]
    if staged:
        projected, own_grad = project(tensor), grad_rows(tensor)
        away_projected, away_grad = project(1 - tensor).astype(BF16), grad_rows(1 - tensor).astype(BF16)
    else:
        every = lambda make: jnp.concatenate([make(i) for i in range(tp)], axis=0)
        onto = lambda value, dim: lax.psum_scatter(value, "tensor", scatter_dimension=dim, tiled=True)
        projected, own_grad = onto(every(project), 0), onto(every(grad_rows), 0)

    pieces = [
        sum(prenorm_terms),
        grad_taps_bc[:5].reshape(-1),
        grad_taps[:5].reshape(-1),
        grad_norm_gain,
        grad_heads[0],
        grad_heads[1],
        lanes_of(grad_d_skip),
    ]
    gap = -(pieces[0].shape[0] + pieces[1].shape[0]) % 1024
    pieces.insert(2, jnp.zeros((gap,), F32))
    x_rows = sum(piece.shape[0] for piece in pieces[:3]) // 128
    flat = jnp.concatenate(pieces)
    flat = jnp.pad(flat, (0, -flat.shape[0] % 1024)).reshape(-1, 128)
    half_of = lambda value: lax.dynamic_slice_in_dim(
        value, tensor * (value.shape[-1] // tp), value.shape[-1] // tp, value.ndim - 1
    )
    if staged:
        grad_w_out, grad_w_z, grad_last, came_projected, came_grad, flat = scatter_all(
            [p.astype(BF16).reshape(16, shard, -1) for p in products],
            away_projected, away_grad, flat, x_rows,
        )
        projected = projected + came_projected.astype(F32)
        own_grad = own_grad + came_grad.astype(F32)
        bc_sum = grad_last[:, inner : inner + bc_width]
        bc_half = bc_width // 2
        away_bc = lax.dynamic_slice_in_dim(bc_sum, (1 - tensor) * bc_half, bc_half, 1)
        grad_w_bc = half_of(bc_sum) + lax.ppermute(away_bc, "tensor", [(0, 1), (1, 0)])
    else:
        grad_w_out, grad_w_z, grad_last = [
            lax.psum_scatter(p, "dp", scatter_dimension=0, tiled=True) for p in products
        ]
        grad_w_bc = onto(grad_last[:, inner : inner + bc_width], 1)
        flat = lax.psum(flat, "dp")
        flat = jnp.concatenate([lax.psum(flat[:x_rows], "tensor"), flat[x_rows:]], axis=0)
    block_out = (hidden_in.astype(F32) + projected).astype(BF16)
    grad_in = (grad_out.astype(F32) + own_grad).astype(BF16)
    grad_w_zx = jnp.stack([grad_w_z, grad_last[:, :inner]], axis=1)
    grad_w_dt = grad_last[:, inner + bc_width : inner + bc_width + head_count]

    flat = flat.reshape(-1)
    at, cut_out = 0, []
    for piece in pieces:
        cut_out.append(flat[at : at + piece.shape[0]])
        at += piece.shape[0]
    return (
        block_out,
        grad_in,
        half_of(cut_out[0]),
        grad_w_zx,
        grad_w_dt,
        grad_w_bc,
        cut_out[3].reshape(5, inner),
        half_of(cut_out[1].reshape(5, bc_width)),
        cut_out[5][:head_count],
        cut_out[6][:head_count],
        cut_out[7][:head_count],
        cut_out[4],
        grad_w_out.T,
    )


def solution(mesh):
    in_specs = (
        P(("dp", "tensor"), None),
        P(),
        P("dp", None, "tensor"),
        P("dp", "tensor"),
        P("dp", None),
        P(None, "tensor"),
        P(),
        P("tensor"),
        P("tensor"),
        P("tensor"),
        P("tensor"),
        P("tensor", "dp"),
        P("dp", None),
        P(("dp", "tensor"), None),
    )
    out_specs = (
        P(("dp", "tensor"), None),
        P(("dp", "tensor"), None),
        P("tensor"),
        P("dp", None, "tensor"),
        P("dp", "tensor"),
        P("dp", "tensor"),
        P(None, "tensor"),
        P(None, "tensor"),
        P("tensor"),
        P("tensor"),
        P("tensor"),
        P("tensor"),
        P("tensor", "dp"),
    )
    return jax.shard_map(
        functools.partial(body, mesh.shape["dp"], mesh.shape["tensor"]),
        mesh=mesh,
        in_specs=in_specs,
        out_specs=out_specs,
        check_vma=False,
    )
```

```python
import functools

import jax
import jax.numpy as jnp
from jax import lax
from jax.experimental import pallas as pl
from jax.experimental.pallas import tpu as pltpu
from jax.sharding import PartitionSpec as P

BLOCK_LEN = 256
EPS = 1e-05
NEG = -1e30
F32 = jnp.float32
BF16 = jnp.bfloat16
HIGHEST = lax.Precision.HIGHEST
VMEM_LIMIT = 60 * 1024 * 1024


def dot(a, b, dims=((1,), (0,)), precision=None):
    return lax.dot_general(a, b, (dims, ((), ())), preferred_element_type=F32, precision=precision)


NN, NT, TN = ((1,), (0,)), ((1,), (1,)), ((0,), (0,))


def sigmoid(w):
    return 1.0 / (1.0 + jnp.exp(-w))


def conv_of(signal, taps, masks):
    out = taps[4:5, :] + taps[3:4, :] * signal
    for back in range(1, 4):
        out = out + taps[3 - back : 4 - back, :] * (
            pltpu.roll(signal, back, 0) * masks[:, back - 1 : back]
        )
    return out


def conv_back(grad, signal, taps, masks):
    rows = signal.shape[0]
    grad_signal = taps[3:4, :] * grad
    tap_rows = [None] * 5
    tap_rows[4] = jnp.sum(grad, axis=0, keepdims=True)
    tap_rows[3] = jnp.sum(grad * signal, axis=0, keepdims=True)
    for back in range(1, 4):
        kept = grad * masks[:, back - 1 : back]
        tap_rows[3 - back] = jnp.sum(kept * pltpu.roll(signal, back, 0), axis=0, keepdims=True)
        grad_signal = grad_signal + taps[3 - back : 4 - back, :] * pltpu.roll(kept, rows - back, 0)
    return grad_signal, tap_rows


def expand(columns, width):
    rows, heads = columns.shape
    lane = lax.broadcasted_iota(jnp.int32, (rows, 2 * width), 1)
    pieces = [
        jnp.where(lane < width, columns[:, h : h + 1], columns[:, h + 1 : h + 2])
        for h in range(0, heads, 2)
    ]
    return pieces[0] if len(pieces) == 1 else jnp.concatenate(pieces, axis=1)


def block_rows(block, size):
    return pl.ds(pl.multiple_of(block * size, size), size)


def head_lanes(array, step, heads):
    return pltpu.roll(array, lax.rem(128 - step * heads, 128), 1)


def block_tables(q, bcraw_ref, kbc_ref, msk_ref, segr_ref, bcc, mneg, cb):
    n = bcc.shape[1] // 2
    c = conv_of(bcraw_ref[...], kbc_ref[...], msk_ref[...])
    bcc[...] = c * sigmoid(c)
    later = lax.broadcasted_iota(jnp.int32, (q, q), 0) >= lax.broadcasted_iota(jnp.int32, (q, q), 1)

    def prepare(b, carry):
        rows = block_rows(b, q)
        same = msk_ref[rows, 5:6] == segr_ref[:, rows]
        mneg[rows, :] = jnp.where(later & same, 0.0, NEG)
        cb[rows, :] = dot(bcc[rows, n:], bcc[rows, :n], NT, HIGHEST)
        return carry

    lax.fori_loop(0, bcc.shape[0] // q, prepare, 0)


def fwd_group(
    q, heads, width, step, at, s, taps, skip, la_ref, dt_ref, msk_ref, s_ref, y_ref, st_ref,
    bcc, mneg, cb, xs, state, la4, lat4, dt4,
):
    tokens = s.shape[0]
    blocks = tokens // q
    n = bcc.shape[1] // 2
    lanes = heads * width
    la_here = head_lanes(la_ref[...], step, heads)
    la4[...] = la_here
    lat4[...] = la_here.T[0:8, :]
    dt4[...] = head_lanes(dt_ref[...], step, heads)
    s_ref[:, at] = s
    c = conv_of(s, taps, msk_ref[...])
    xs[...] = c * sigmoid(c)
    state[...] = jnp.zeros_like(state)
    lane_head = lax.broadcasted_iota(jnp.int32, (q, lanes), 1) // width

    def one_block(b, carry):
        rows = block_rows(b, q)
        x = xs[rows, :]
        la = la4[rows, 0:heads]
        u = x * expand(dt4[rows, 0:heads], width)
        ub = u.astype(BF16)
        enter = expand(jnp.exp(la) * msk_ref[rows, 3:4], width)
        last = expand(jnp.exp(la[q - 1 : q, :] - la) * msk_ref[rows, 4:5], width)
        st = state[...]
        st_ref[b, :, at] = st
        base = mneg[rows, :]
        cb_b = cb[rows, :]
        weights, values = [], []
        for h in range(heads):
            decay = jnp.exp(la[:, h : h + 1] - lat4[h : h + 1, rows] + base)
            weights.append((decay * cb_b).astype(BF16))
            values.append(jnp.where(lane_head == h, ub, jnp.zeros_like(ub)))
        local = dot(jnp.concatenate(weights, axis=1), jnp.concatenate(values, axis=0))
        carried = dot(bcc[rows, n:].astype(BF16), st.astype(BF16))
        y_ref[rows, at] = local + carried * enter + skip * x
        state[...] = st * enter[q - 1 : q, :] + dot(
            bcc[rows, :n].astype(BF16), (u * last).astype(BF16), TN
        )
        return carry

    lax.fori_loop(0, blocks, one_block, 0, unroll=blocks <= 2)


def fwd_kernel(
    q, heads, width,
    nm_ref, w_ref, bcraw_ref, kx_ref, kbc_ref, la_ref, dt_ref, msk_ref, segr_ref, dsk_ref,
    s_ref, y_ref, st_ref,
    bcc, mneg, cb, *scratch,
):
    step = pl.program_id(0)

    @pl.when(step == 0)
    def _():
        block_tables(q, bcraw_ref, kbc_ref, msk_ref, segr_ref, bcc, mneg, cb)

    s = dot(nm_ref[...], w_ref[...])
    fwd_group(
        q, heads, width, step, slice(None), s, kx_ref[...], dsk_ref[...], la_ref, dt_ref, msk_ref,
        s_ref, y_ref, st_ref, bcc, mneg, cb, *scratch,
    )


def bwd_kernel(
    q, heads, width,
    s_ref, dy_ref, bcraw_ref, kx_ref, kbc_ref, la_ref, dt_ref, msk_ref, segr_ref, dsk_ref, st_ref, dtin_ref, rate_ref,
    ds_ref, gk_ref, small_ref, dbc_ref, gkbc_ref, ghead_ref,
    bcc, mnegt, cbt, xs, dxs, dtt, gt, la4, lat4, dt4, dla_acc, ddt_acc, dbc_acc,
):
    tokens = s_ref.shape[0]
    blocks = tokens // q
    n = bcc.shape[1] // 2
    lanes = heads * width
    step = pl.program_id(0)

    @pl.when(step == 0)
    def _():
        c = conv_of(bcraw_ref[...], kbc_ref[...], msk_ref[...])
        bcc[...] = c * sigmoid(c)
        dtt[...] = jnp.zeros_like(dtt)
        dbc_acc[...] = jnp.zeros_like(dbc_acc)
        dla_acc[...] = jnp.zeros_like(dla_acc)
        ddt_acc[...] = jnp.zeros_like(ddt_acc)
        earlier = lax.broadcasted_iota(jnp.int32, (q, q), 0) <= lax.broadcasted_iota(jnp.int32, (q, q), 1)

        def prepare(b, carry):
            rows = block_rows(b, q)
            same = msk_ref[rows, 5:6] == segr_ref[:, rows]
            mnegt[rows, :] = jnp.where(earlier & same, 0.0, NEG)
            cbt[rows, :] = dot(bcc[rows, :n], bcc[rows, n:], NT, HIGHEST)
            return carry

        lax.fori_loop(0, blocks, prepare, 0)

    la_here = head_lanes(la_ref[...], step, heads)
    la4[...] = la_here
    lat4[...] = la_here.T[0:8, :]
    dt4[...] = head_lanes(dt_ref[...], step, heads)
    c = conv_of(s_ref[...], kx_ref[...], msk_ref[...])
    xs[...] = c * sigmoid(c)
    gt[...] = jnp.zeros_like(gt)
    lane_head = lax.broadcasted_iota(jnp.int32, (q, lanes), 1) // width
    pick = jnp.where(
        lax.broadcasted_iota(jnp.int32, (8, lanes), 1) // width
        == lax.broadcasted_iota(jnp.int32, (8, lanes), 0),
        1.0,
        0.0,
    )
    token_lane = lax.broadcasted_iota(jnp.int32, (1, q), 1)
    col_lane = lax.broadcasted_iota(jnp.int32, (q, 128), 1)

    def one_block(i, carry):
        b = blocks - 1 - i
        rows = block_rows(b, q)
        x = xs[rows, :]
        dy = dy_ref[rows, :]
        la = la4[rows, 0:heads]
        dtx = expand(dt4[rows, 0:heads], width)
        u = x * dtx
        ub, dyb = u.astype(BF16), dy.astype(BF16)
        enter = expand(jnp.exp(la) * msk_ref[rows, 3:4], width)
        last = expand(jnp.exp(la[q - 1 : q, :] - la) * msk_ref[rows, 4:5], width)
        base = mnegt[rows, :]
        cb_b = cbt[rows, :]
        weights, values, row_sums = [], [], []
        d_cb = jnp.zeros((q, q), F32)
        col_sums = jnp.zeros((q, 128), F32)
        for h in range(heads):
            own = lane_head == h
            decay = jnp.exp(lat4[h : h + 1, rows] - la[:, h : h + 1] + base)
            dyh = jnp.where(own, dyb, jnp.zeros_like(dyb))
            pair = dot(ub, dyh, NT)
            weight = decay * cb_b
            d_cb = d_cb + decay * pair
            both = weight * pair
            row_sums.append(jnp.sum(both, axis=0, keepdims=True))
            col_sums = jnp.where(col_lane == h, jnp.sum(both, axis=1, keepdims=True), col_sums)
            weights.append(weight.astype(BF16))
            values.append(dyh)
        dtt[rows, :] += d_cb
        g = gt[...]
        gb16 = g.astype(BF16)
        st = st_ref[b]
        stb = st.astype(BF16)
        c16 = bcc[rows, n:].astype(BF16)
        b16 = bcc[rows, :n].astype(BF16)
        gb = dot(b16, gb16) * last
        du = dot(jnp.concatenate(weights, axis=1), jnp.concatenate(values, axis=0)) + gb
        dye = (dy * enter).astype(BF16)
        from_state = dot(c16, stb) * enter
        dbc_acc[rows, n:] += dot(dye, stb, NT)
        dbc_acc[rows, :n] += dot((u * last).astype(BF16), gb16, NT)
        ug = u * gb
        dla = dot(pick, dy * from_state - ug, NT, HIGHEST)
        ddt = dot(pick, x * du, NT, HIGHEST)
        tail = jnp.sum(ug, axis=0, keepdims=True) + enter[q - 1 : q, :] * jnp.sum(
            g * st, axis=0, keepdims=True
        )
        la_rows = []
        for h in range(heads):
            end = jnp.sum(jnp.where(lane_head[0:1, :] == h, tail, 0.0), axis=1, keepdims=True)
            la_rows.append(
                row_sums[h] + dla[h : h + 1, :] + jnp.where(token_lane == q - 1, end, 0.0)
            )
        dt_rows = [ddt[h : h + 1, :] for h in range(heads)]
        rest = jnp.zeros((128 - 2 * heads, q), F32)
        columns = jnp.concatenate(la_rows + dt_rows + [rest], axis=0).T
        la_part = jnp.where(col_lane < heads, columns, 0.0) - col_sums
        dt_part = jnp.where(col_lane >= heads, columns, 0.0)
        dla_acc[rows, :] += pltpu.roll(la_part, step * heads, 1)
        ddt_acc[rows, :] += pltpu.roll(dt_part, lax.rem(128 + (step - 1) * heads, 128), 1)
        gt[...] = g * enter[q - 1 : q, :] + dot(c16, dye, TN)
        dxs[rows, :] = dtx * du + dsk_ref[...] * dy
        return carry

    lax.fori_loop(0, blocks, one_block, 0, unroll=blocks <= 2)

    s = s_ref[...]
    taps = kx_ref[...]
    masks = msk_ref[...]
    c = conv_of(s, taps, masks)
    sig = sigmoid(c)
    grad = dxs[...] * sig * (1.0 + c * (1.0 - sig))
    d_s, tap_rows = conv_back(grad, s, taps, masks)
    ds_ref[...] = d_s.astype(BF16)
    skip_row = jnp.sum(dy_ref[...] * xs[...], axis=0, keepdims=True)
    gk_ref[...] = jnp.concatenate(
        tap_rows + [skip_row, jnp.zeros_like(skip_row), jnp.zeros_like(skip_row)], axis=0
    )

    @pl.when(step == pl.num_programs(0) - 1)
    def _():
        upper = jnp.where(
            lax.broadcasted_iota(jnp.int32, (q, q), 0) <= lax.broadcasted_iota(jnp.int32, (q, q), 1), 1.0, 0.0
        )

        def finish(b, carry):
            rows = block_rows(b, q)
            d_cb = dtt[rows, :]
            dbc_acc[rows, :n] += dot(d_cb, bcc[rows, n:], NN, HIGHEST)
            dbc_acc[rows, n:] += dot(d_cb, bcc[rows, :n], TN, HIGHEST)
            dla_acc[rows, :] = dot(upper, dla_acc[rows, :], NN, HIGHEST)
            return carry

        lax.fori_loop(0, blocks, finish, 0)
        rate = rate_ref[...]
        d_exponent = dla_acc[...]
        d_raw = (ddt_acc[...] + rate * d_exponent) * sigmoid(dtin_ref[...])
        d_rate = rate * jnp.sum(dt_ref[...] * d_exponent, axis=0, keepdims=True)
        d_bias = jnp.sum(d_raw, axis=0, keepdims=True)
        ghead_ref[...] = jnp.concatenate([d_bias, d_rate, jnp.zeros((6, 128), F32)], axis=0)
        raw = bcraw_ref[...]
        taps_bc = kbc_ref[...]
        c_bc = conv_of(raw, taps_bc, masks)
        sig_bc = sigmoid(c_bc)
        grad_bc = dbc_acc[...] * sig_bc * (1.0 + c_bc * (1.0 - sig_bc))
        d_bc, bc_rows = conv_back(grad_bc, raw, taps_bc, masks)
        high = d_bc.astype(BF16)
        small_ref[:, : 2 * n] = high
        small_ref[:, 2 * n :] = d_raw.astype(BF16)
        dbc_ref[...] = (d_bc - high.astype(F32)).astype(BF16)
        zero_row = jnp.zeros_like(bc_rows[0])
        gkbc_ref[...] = jnp.concatenate(bc_rows + [zero_row] * 3, axis=0)


def full(shape):
    return pl.BlockSpec(shape, lambda i: (0,) * len(shape))


def lane_block(rows, lanes):
    return pl.BlockSpec((rows, lanes), lambda i: (0, i))


def heads_per_step(head_count):
    return 4 if head_count % 4 == 0 else 2


def forward_scratch(tokens, q, n, lanes):
    return [
        pltpu.VMEM((tokens, 2 * n), F32), pltpu.VMEM((tokens, q), F32), pltpu.VMEM((tokens, q), F32),
        pltpu.VMEM((tokens, lanes), F32), pltpu.VMEM((n, lanes), F32), pltpu.VMEM((tokens, 128), F32),
        pltpu.VMEM((8, tokens), F32), pltpu.VMEM((tokens, 128), F32),
    ]


def scan_forward(normed, w_s, prep, conv_x, conv_bc, skip_lanes, width, q):
    bcraw, la, dt, masks, seg_row = (prep[k] for k in ("bcraw", "la", "dt", "masks", "seg_row"))
    tokens, depth = normed.shape
    inner = w_s.shape[1]
    head_count = inner // width
    heads = heads_per_step(head_count)
    lanes = heads * width
    n = bcraw.shape[1] // 2
    blocks = tokens // q
    return pl.pallas_call(
        functools.partial(fwd_kernel, q, heads, width),
        grid=(head_count // heads,),
        in_specs=[
            full((tokens, depth)), lane_block(depth, lanes), full((tokens, 2 * n)), lane_block(5, lanes),
            full((5, 2 * n)), full((tokens, 128)), full((tokens, 128)), full((tokens, 128)),
            full((1, tokens)), lane_block(1, lanes),
        ],
        out_specs=[
            lane_block(tokens, lanes), lane_block(tokens, lanes),
            pl.BlockSpec((blocks, n, lanes), lambda i: (0, 0, i)),
        ],
        out_shape=[
            jax.ShapeDtypeStruct((tokens, inner), F32), jax.ShapeDtypeStruct((tokens, inner), F32),
            jax.ShapeDtypeStruct((blocks, n, inner), F32),
        ],
        scratch_shapes=forward_scratch(tokens, q, n, lanes),
        compiler_params=pltpu.CompilerParams(
            dimension_semantics=("arbitrary",), vmem_limit_bytes=VMEM_LIMIT
        ),
        cost_estimate=pl.CostEstimate(
            flops=2 * tokens * inner * (depth + q + 4 * n),
            bytes_accessed=2 * (depth * inner + tokens * depth) + 8 * tokens * inner,
            transcendentals=tokens * q * head_count,
        ),
        name="scan_forward",
    )(normed, w_s, bcraw, conv_x, conv_bc, la, dt, masks, seg_row, skip_lanes)


def scan_backward(s, dy, prep, conv_x, conv_bc, skip_lanes, states, width, q):
    bcraw, la, dt, masks, seg_row = (prep[k] for k in ("bcraw", "la", "dt", "masks", "seg_row"))
    tokens, inner = s.shape
    head_count = inner // width
    heads = heads_per_step(head_count)
    lanes = heads * width
    n = bcraw.shape[1] // 2
    blocks = tokens // q
    return pl.pallas_call(
        functools.partial(bwd_kernel, q, heads, width),
        grid=(head_count // heads,),
        in_specs=[
            lane_block(tokens, lanes), lane_block(tokens, lanes), full((tokens, 2 * n)), lane_block(5, lanes),
            full((5, 2 * n)), full((tokens, 128)), full((tokens, 128)), full((tokens, 128)),
            full((1, tokens)), lane_block(1, lanes), pl.BlockSpec((blocks, n, lanes), lambda i: (0, 0, i)),
            full((tokens, 128)), full((1, 128)),
        ],
        out_specs=[
            lane_block(tokens, lanes), lane_block(8, lanes), full((tokens, 2 * n + 128)),
            full((tokens, 2 * n)), full((8, 2 * n)), full((8, 128)),
        ],
        out_shape=[
            jax.ShapeDtypeStruct((tokens, inner), BF16), jax.ShapeDtypeStruct((8, inner), F32),
            jax.ShapeDtypeStruct((tokens, 2 * n + 128), BF16), jax.ShapeDtypeStruct((tokens, 2 * n), BF16),
            jax.ShapeDtypeStruct((8, 2 * n), F32), jax.ShapeDtypeStruct((8, 128), F32),
        ],
        scratch_shapes=[
            pltpu.VMEM((tokens, 2 * n), F32), pltpu.VMEM((tokens, q), F32), pltpu.VMEM((tokens, q), F32),
            pltpu.VMEM((tokens, lanes), F32), pltpu.VMEM((tokens, lanes), F32), pltpu.VMEM((tokens, q), F32),
            pltpu.VMEM((n, lanes), F32), pltpu.VMEM((tokens, 128), F32), pltpu.VMEM((8, tokens), F32),
            pltpu.VMEM((tokens, 128), F32), pltpu.VMEM((tokens, 128), F32), pltpu.VMEM((tokens, 128), F32),
            pltpu.VMEM((tokens, 2 * n), F32),
        ],
        compiler_params=pltpu.CompilerParams(
            dimension_semantics=("arbitrary",), vmem_limit_bytes=VMEM_LIMIT
        ),
        cost_estimate=pl.CostEstimate(
            flops=2 * tokens * inner * (8 * q + 8 * n),
            bytes_accessed=12 * tokens * inner,
            transcendentals=tokens * q * head_count,
        ),
        name="scan_backward",
    )(
        s, dy, bcraw, conv_x, conv_bc, la, dt, masks, seg_row, skip_lanes, states, prep["dt_in"], prep["rate"],
    )


MESH = pl.DeviceIdType.MESH


class Here:
    def __init__(self):
        self.me = lax.axis_index("dp")
        self.t = lax.axis_index("tensor")
        self.z = self.me // 4
        self.y = (self.me // 2) % 2
        self.c = self.me % 2

    def slot(self, z, y, c):
        return z * 4 + y * 2 + c

    def z_plus(self, d):
        return (self.z + d) % 4

    def at_z(self, d):
        return (self.slot(self.z_plus(d), self.y, self.c), self.t)

    def across_y(self):
        return (self.slot(self.z, 1 - self.y, self.c), self.t)

    def other_core(self):
        return (self.slot(self.z, self.y, 1 - self.c), self.t)

    def across_x(self):
        return (self.me, 1 - self.t)

    def greet(self):
        barrier = pltpu.get_barrier_semaphore()
        for peer in (self.at_z(1), self.at_z(2), self.at_z(3), self.across_y(), self.other_core(), self.across_x()):
            pl.semaphore_signal(barrier, inc=1, device_id=peer, device_id_type=MESH)
        pl.semaphore_wait(barrier, 6)


def send(src, dst, sems, index, peer):
    return pltpu.make_async_remote_copy(
        src_ref=src, dst_ref=dst, send_sem=sems.at[0, index], recv_sem=sems.at[1, index],
        device_id=peer, device_id_type=MESH,
    )


class Gather:
    COPIES = 27

    def __init__(self, here, src, dst, sems, local_sem):
        self.here, self.src, self.dst, self.sems = here, src, dst, sems
        self.local = pltpu.make_async_copy(src, dst.at[here.me], local_sem)

    def holds(self, i):
        z = self.here.z
        return z >= 0 if i == 0 else z >= i if i <= 3 else z + i - 3 <= 3

    def slot_of(self, i, far=False):
        here = self.here
        z = here.z - i if i <= 3 else here.z + i - 3
        return here.slot(z, 1 - here.y if far else here.y, here.c)

    def from_here(self, i, far=False):
        return self.src if i == 0 and not far else self.dst.at[self.slot_of(i, far)]

    def up(self, d):
        i = d - 1
        return send(self.from_here(i), self.dst.at[self.slot_of(i)], self.sems, i, self.here.at_z(1))

    def down(self, d):
        i = d + 2 if d > 1 else 0
        return send(self.from_here(i), self.dst.at[self.slot_of(i)], self.sems, 2 + d, self.here.at_z(3))

    def across(self, i):
        return send(self.from_here(i), self.dst.at[self.slot_of(i)], self.sems, 6 + i, self.here.across_y())

    def to_core(self, k):
        i, far = k % 7, k >= 7
        src = self.from_here(i, far)
        return send(src, self.dst.at[self.slot_of(i, far)], self.sems, 13 + k, self.here.other_core())

    def sends_up(self, d):
        return (self.here.z < 3) & (self.here.z >= d - 1)

    def sends_down(self, d):
        return (self.here.z > 0) & (self.here.z + d <= 4)

    def start(self):
        pl.when(self.sends_up(1))(lambda: self.up(1).start())
        pl.when(self.sends_down(1))(lambda: self.down(1).start())
        self.across(0).start()
        self.to_core(0).start()
        self.local.start()

    def pass_z(self, *hops):
        for d in hops:

            @pl.when(self.holds(d))
            def _(d=d):
                self.up(d).wait_recv()
                if d < 3:
                    pl.when(self.here.z < 3)(lambda: self.up(d + 1).start())
                self.across(d).start()
                self.to_core(d).start()

            @pl.when(self.holds(3 + d))
            def _(d=d):
                self.down(d).wait_recv()
                if d < 3:
                    pl.when(self.here.z > 0)(lambda: self.down(d + 1).start())
                self.across(3 + d).start()
                self.to_core(3 + d).start()

    def pass_y(self):
        for i in range(7):

            @pl.when(self.holds(i))
            def _(i=i):
                self.across(i).wait_recv()
                self.to_core(7 + i).start()

    def arrived(self):
        self.local.wait()
        for k in range(14):
            pl.when(self.holds(k % 7))(lambda k=k: self.to_core(k).wait_recv())

    def sent(self):
        for d in (1, 2, 3):
            pl.when(self.sends_up(d))(lambda d=d: self.up(d).wait_send())
            pl.when(self.sends_down(d))(lambda d=d: self.down(d).wait_send())
        for i in range(7):
            pl.when(self.holds(i))(lambda i=i: self.across(i).wait_send())
        for k in range(14):
            pl.when(self.holds(k % 7))(lambda k=k: self.to_core(k).wait_send())


def softplus(w):
    return jnp.maximum(w, 0.0) + jnp.log1p(jnp.exp(-jnp.abs(w)))


def forward_kernel(
    q, heads, width, inner_total,
    hid_ref, cot_ref, small_ref, ws_ref, wz_ref, wo_ref, gain_ref, bias_ref, rate_ref, seg_ref,
    kx_ref, kbc_ref, dsk_ref, ngain_ref,
    rows_out, cot_out, small_out, ws_out, wz_out, wo_out, s_out, normed_out,
    scale_out, bcraw_out, dtin_out, dt_out, la_out, masks_out, st_out, dy_out, gated_out, dz_out, gngain_out,
    small_sems, ws_sems, wz_sems, wo_sems, x_sems, local_sems,
    rows_v, cot_v, ws_v, wz_v, wo_v, s_v, normed_v, y_v, z_v, dg_v, sum_v, sum_own, sum_came,
    bcc, mneg, cb, *group_scratch,
):
    here = Here()
    tokens = normed_v.shape[0]
    half = tokens // 2
    inner = y_v.shape[1]
    lanes = heads * width
    groups = inner // lanes
    here.greet()
    hidden = send(hid_ref, rows_v.at[here.t], x_sems, 0, here.across_x())
    cotangent = send(cot_ref, cot_v.at[here.t], x_sems, 1, here.across_x())
    sums_x = send(sum_own, sum_came, x_sems, 2, here.across_x())
    gathers = [
        Gather(here, src, dst, sems, local_sems.at[i])
        for i, (src, dst, sems) in enumerate(
            [
                (small_ref, small_out, small_sems),
                (ws_ref, ws_out, ws_sems),
                (wz_ref, wz_out, wz_sems),
                (wo_ref, wo_out, wo_sems),
            ]
        )
    ]
    small, ws, wz, wo = gathers
    local = lambda src, dst, i: pltpu.make_async_copy(src, dst, local_sems.at[i])
    own_hidden = local(hid_ref, rows_v.at[here.t], 4)
    own_cot = local(cot_ref, cot_v.at[here.t], 5)
    load_ws, load_wz, load_wo = local(ws_out, ws_v, 6), local(wz_out, wz_v, 7), local(wo_out, wo_v, 8)
    store_rows, store_cot = local(rows_v, rows_out, 9), local(cot_v, cot_out, 10)
    store_normed, store_s = local(normed_v, normed_out, 11), local(s_v, s_out, 12)
    hidden.start()
    small.start()
    ws.start()
    cotangent.start()
    own_hidden.start()
    own_cot.start()

    seg = jnp.broadcast_to(seg_ref[...], (128, tokens)).T
    row = lax.broadcasted_iota(jnp.int32, (tokens, 128), 0)
    lane = lax.broadcasted_iota(jnp.int32, (tokens, 128), 1)
    masks = jnp.where(lane == 5, seg, 0.0)
    for back in (1, 2, 3):
        same = (pltpu.roll(seg, back, 0) == seg) & (row >= back)
        masks = jnp.where((lane == back - 1) & same, 1.0, masks)
    for b in range(tokens // q):
        inside = (row >= b * q) & (row < (b + 1) * q)
        if b:
            carried = inside & (seg == seg[b * q - 1 : b * q, :])
            masks = jnp.where((lane == 3) & carried, 1.0, masks)
        run_last = inside & (seg == seg[(b + 1) * q - 1 : (b + 1) * q, :])
        masks = jnp.where((lane == 4) & run_last, 1.0, masks)
    masks_out[...] = masks

    small.pass_z(1, 2, 3)
    ws.pass_z(1, 2)
    small.pass_y()
    own_hidden.wait()
    hidden.wait_recv()
    store_rows.start()
    gain = gain_ref[...]
    chunk = 64

    def norm(i, carry):
        side, at = i // (half // chunk), i % (half // chunk)
        rows = pl.ds(pl.multiple_of(at * chunk, chunk), chunk)
        values = rows_v[side, rows, :].astype(F32)
        scale = lax.rsqrt(jnp.mean(values * values, axis=1, keepdims=True) + EPS)
        out_rows = pl.ds(pl.multiple_of(i * chunk, chunk), chunk)
        normed_v[out_rows, :] = (values * scale * gain).astype(BF16)
        scale_out[out_rows, :] = jnp.broadcast_to(scale, (chunk, 128))
        return carry

    lax.fori_loop(0, tokens // chunk, norm, 0)
    store_normed.start()
    ws.pass_z(3)
    wz.start()
    small.arrived()
    pieces, shard, columns = small_out.shape
    proj = dot(normed_v[...], small_out[...].reshape(pieces * shard, columns))
    bc_width = columns - 128
    bcraw_out[...] = proj[:, :bc_width]
    dt_in = proj[:, bc_width:] + bias_ref[...]
    dtin_out[...] = dt_in
    dt = softplus(dt_in)
    dt_out[...] = dt
    lower = jnp.where(
        lax.broadcasted_iota(jnp.int32, (q, q), 0) >= lax.broadcasted_iota(jnp.int32, (q, q), 1), 1.0, 0.0
    )
    exponent = dt * rate_ref[...]
    for b in range(tokens // q):
        la_out[b * q : (b + 1) * q, :] = dot(lower, exponent[b * q : (b + 1) * q, :], NN, HIGHEST)
    block_tables(q, bcraw_out, kbc_ref, masks_out, seg_ref, bcc, mneg, cb)
    ws.pass_y()
    ws.arrived()
    load_ws.start()
    load_ws.wait()

    def weight_block(ref, at):
        return ref[:, :, at].reshape(pieces * shard, lanes)

    def lane_range(g):
        return pl.ds(pl.multiple_of(g * lanes, lanes), lanes)

    def scan_group(g, carry):
        pl.when(g == 0)(lambda: wz.pass_z(1))
        pl.when(g == 1)(lambda: wz.pass_z(2))

        @pl.when(g == 2)
        def _():
            wz.pass_z(3)
            wo.start()

        pl.when(g == 4)(lambda: wo.pass_z(1))
        pl.when(g == 5)(lambda: wo.pass_z(2))
        at = lane_range(g)
        s = dot(normed_v[...], weight_block(ws_v, at))
        fwd_group(
            q, heads, width, g, at, s, kx_ref[:, at], dsk_ref[:, at], la_out, dt_out, masks_out,
            s_v, y_v, st_out, bcc, mneg, cb, *group_scratch,
        )
        return carry

    lax.fori_loop(0, groups, scan_group, 0)
    store_s.start()
    wo.pass_z(3)
    wz.pass_y()
    wz.arrived()
    load_wz.start()
    own_cot.wait()
    cotangent.wait_recv()
    store_cot.start()
    sum_v[...] = jnp.zeros_like(sum_v)
    load_wz.wait()

    def gate_group(g, carry):
        at = lane_range(g)
        z = dot(normed_v[...], weight_block(wz_v, at))
        z_v[:, at] = z
        v = y_v[:, at] * (z * sigmoid(z))
        square = v * v
        for piece in range(lanes // 128):
            sum_v[0] += square[:, piece * 128 : (piece + 1) * 128]
        return carry

    lax.fori_loop(0, groups, gate_group, 0)
    wo.pass_y()
    wo.arrived()
    load_wo.start()
    load_wo.wait()

    def pull_group(g, carry):
        at = lane_range(g)
        side = cot_v[...].reshape(tokens, cot_v.shape[2])
        pulled = dot(side, weight_block(wo_v, at))
        dg_v[:, at] = pulled
        z = z_v[:, at]
        product = pulled * ngain_ref[:, at] * (y_v[:, at] * (z * sigmoid(z)))
        for piece in range(lanes // 128):
            sum_v[1] += product[:, piece * 128 : (piece + 1) * 128]
        return carry

    lax.fori_loop(0, groups, pull_group, 0)
    row_of = lambda array: jnp.sum(array.T, axis=0, keepdims=True)
    sum_own[...] = jnp.concatenate(
        [row_of(sum_v[0]), row_of(sum_v[1]), jnp.zeros((6, tokens), F32)], axis=0
    )
    sums_x.start()
    sums_x.wait_recv()
    both = sum_own[...] + sum_came[...]
    scale_row = lax.rsqrt(both[0:1, :] / inner_total + EPS)
    pull_row = both[1:2, :] * (scale_row * scale_row * scale_row) / inner_total
    column_of = lambda array: jnp.broadcast_to(array, (128, tokens)).T
    sum_v[0] = column_of(scale_row)
    sum_v[1] = column_of(pull_row)

    def grad_group(g, carry):
        at = lane_range(g)
        scale, pull = sum_v[0][:, 0:1], sum_v[1][:, 0:1]
        z, y, pulled = z_v[:, at], y_v[:, at], dg_v[:, at]
        sig = sigmoid(z)
        gate = z * sig
        v = y * gate
        unit = v * scale
        gngain_out[:, at] = jnp.sum(pulled * unit, axis=0, keepdims=True)
        gated_out[:, at] = (unit * ngain_ref[:, at]).astype(BF16)
        d_v = pulled * ngain_ref[:, at] * scale - pull * v
        dy_out[:, at] = d_v * gate
        dz_out[:, at] = (d_v * y * sig * (1.0 + z * (1.0 - sig))).astype(BF16)
        return carry

    lax.fori_loop(0, groups, grad_group, 0)
    for gather in gathers:
        gather.sent()
    for copy in (hidden, cotangent, sums_x):
        copy.wait_send()
    for copy in (store_rows, store_cot, store_normed, store_s):
        copy.wait()


def in_vmem():
    return pl.BlockSpec(memory_space=pltpu.VMEM)


def in_any():
    return pl.BlockSpec(memory_space=pl.ANY)


def forward_all(
    hidden, cot, small, ws, wz, wo, gain, bias, rate, seg_row, conv_x, conv_bc, skip_lanes, norm_gain, width, inner_total, q
):
    half, depth = hidden.shape
    tokens = 2 * half
    shard, inner = ws.shape
    columns = small.shape[1]
    heads = heads_per_step(inner // width)
    lanes = heads * width
    n = (columns - 128) // 2
    blocks = tokens // q
    shape = jax.ShapeDtypeStruct
    sems = pltpu.SemaphoreType.DMA
    weight, rows = (16, shard, inner), (2, half, depth)
    per_head = shape((tokens, 128), F32)
    outs = pl.pallas_call(
        functools.partial(forward_kernel, q, heads, width, inner_total),
        in_specs=[in_vmem()] * 14,
        out_specs=[in_any()] * 2 + [in_vmem()] + [in_any()] * 5 + [in_vmem()] * 11,
        out_shape=[
            shape(rows, BF16), shape(rows, BF16), shape((16, shard, columns), BF16),
            shape(weight, BF16), shape(weight, BF16), shape(weight, BF16),
            shape((tokens, inner), F32), shape((tokens, depth), BF16),
            per_head, shape((tokens, columns - 128), F32), per_head, per_head, per_head, per_head,
            shape((blocks, n, inner), F32), shape((tokens, inner), F32), shape((tokens, inner), BF16),
            shape((tokens, inner), BF16), shape((1, inner), F32),
        ],
        scratch_shapes=[sems((2, Gather.COPIES))] * 4 + [sems((2, 3)), sems((13,))]
        + [pltpu.VMEM(rows, BF16)] * 2 + [pltpu.VMEM(weight, BF16)] * 3
        + [
            pltpu.VMEM((tokens, inner), F32), pltpu.VMEM((tokens, depth), BF16), pltpu.VMEM((tokens, inner), F32),
            pltpu.VMEM((tokens, inner), F32), pltpu.VMEM((tokens, inner), F32), pltpu.VMEM((2, tokens, 128), F32),
            pltpu.VMEM((8, tokens), F32), pltpu.VMEM((8, tokens), F32),
        ]
        + forward_scratch(tokens, q, n, lanes),
        compiler_params=pltpu.CompilerParams(
            collective_id=0, has_side_effects=True, vmem_limit_bytes=VMEM_LIMIT
        ),
        name="forward_all",
    )(
        hidden, cot, small, ws, wz, wo, gain, bias, rate, seg_row, conv_x, conv_bc, skip_lanes, norm_gain,
    )
    flat = lambda a: a.reshape((-1, a.shape[-1]))
    return [flat(a) for a in outs[:14]] + list(outs[14:])


class Scatter:
    COPIES = 18

    def __init__(self, here, product, out, own, from_core, from_y, from_z, sems, local_sems):
        self.here, self.product, self.out, self.own = here, product, out, own
        self.from_core, self.from_y, self.from_z = from_core, from_y, from_z
        self.sems, self.local_sems = sems, local_sems

    def piece(self, k, core):
        here = self.here
        return here.slot(k % 4, 1 - here.y if k < 4 else here.y, core)

    def load(self, k):
        return pltpu.make_async_copy(
            self.product.at[self.piece(k, self.here.c)], self.own.at[k], self.local_sems.at[k]
        )

    def core_copy(self, k):
        src = self.product.at[self.piece(k, 1 - self.here.c)]
        return send(src, self.from_core.at[k], self.sems, k, self.here.other_core())

    def y_copy(self, k):
        return send(self.own.at[k], self.from_y.at[k], self.sems, 8 + k, self.here.across_y())

    def up(self, k):
        return send(self.own.at[4 + k], self.from_z.at[k - 1], self.sems, 11 + k, self.here.at_z(1))

    def down(self, k):
        return send(self.own.at[4 + k], self.from_z.at[3 + k], self.sems, 15 + k, self.here.at_z(3))

    def start(self):
        for k in range(8):
            self.core_copy(k).start()
            self.load(k).start()

    def by_rows(self, step):
        rows = self.own.shape[1]

        def one(i, carry):
            step(pl.ds(pl.multiple_of(i * 16, 16), 16))
            return carry

        lax.fori_loop(0, rows // 16, one, 0)

    def to_y(self):
        for k in range(4):
            self.load(k).wait()
            self.core_copy(k).wait_recv()

            def add(rows, k=k):
                total = self.own[k, rows, :].astype(F32) + self.from_core[k, rows, :].astype(F32)
                self.own[k, rows, :] = total.astype(BF16)

            self.by_rows(add)
            self.y_copy(k).start()

    def local_sum(self, k, rows):
        return (
            self.own[4 + k, rows, :].astype(F32)
            + self.from_core[4 + k, rows, :].astype(F32)
            + self.from_y[k, rows, :].astype(F32)
        )

    def pass_on(self, k, copy, came, first):
        @pl.when(first)
        def _():
            def add(rows):
                self.own[4 + k, rows, :] = self.local_sum(k, rows).astype(BF16)

            self.by_rows(add)

        @pl.when(jnp.logical_not(first))
        def _():
            copy.wait_recv()

            def add(rows):
                total = self.local_sum(k, rows) + self.from_z[came, rows, :].astype(F32)
                self.own[4 + k, rows, :] = total.astype(BF16)

            self.by_rows(add)

        copy.start()

    def ready_z(self):
        for k in range(4, 8):
            self.load(k).wait()
            self.core_copy(k).wait_recv()
        for k in range(4):
            self.y_copy(k).wait_recv()

    def to_z(self, turn):
        z = self.here.z
        k = 3 - turn
        pl.when(z < k)(lambda: self.pass_on(k, self.up(k), k - 1, z == 0))
        j = turn
        pl.when(z > j)(lambda: self.pass_on(j, self.down(j), 3 + j, z == 3))

    def finish(self):
        at = self.here.z
        for k in range(4):

            @pl.when(at == k)
            def _(k=k):
                if k > 0:
                    self.up(k).wait_recv()
                if k < 3:
                    self.down(k).wait_recv()

                def add(rows):
                    total = self.local_sum(k, rows)
                    if k > 0:
                        total = total + self.from_z[k - 1, rows, :].astype(F32)
                    if k < 3:
                        total = total + self.from_z[3 + k, rows, :].astype(F32)
                    self.out[rows, :] = total

                self.by_rows(add)

    def sent(self):
        z = self.here.z
        for k in range(8):
            self.core_copy(k).wait_send()
        for k in range(4):
            self.y_copy(k).wait_send()
        for k in (1, 2, 3):
            pl.when(z < k)(lambda k=k: self.up(k).wait_send())
        for k in (0, 1, 2):
            pl.when(z > k)(lambda k=k: self.down(k).wait_send())


def scatter_kernel(
    matrices, x_rows, *refs
):
    refs = list(refs)
    take = lambda count: [refs.pop(0) for _ in range(count)]
    products, (xa_ref, xb_ref, sums_ref) = take(matrices), take(3)
    outs, (xa_out, xb_out, sums_out) = take(matrices), take(3)
    buffers = [take(4) for _ in range(matrices)]
    sems, local_sems = take(matrices), take(matrices)
    x_sems, sum_sems, sum_own, sum_came = take(4)
    here = Here()
    here.greet()
    scatters = [
        Scatter(here, products[i], outs[i], *buffers[i], sems[i], local_sems[i]) for i in range(matrices)
    ]
    core_sum = send(sums_ref, sum_came.at[0], sum_sems, 0, here.other_core())
    y_sum = send(sum_own.at[0], sum_came.at[1], sum_sems, 1, here.across_y())
    z_sums = [send(sum_own.at[1], sum_came.at[1 + d], sum_sems, 1 + d, here.at_z(d)) for d in (1, 2, 3)]
    x_part = pl.ds(0, x_rows)
    x_sum = send(sum_own.at[2, x_part], sum_came.at[5, x_part], sum_sems, 5, here.across_x())
    xa = send(xa_ref, xa_out, x_sems, 0, here.across_x())
    xb = send(xb_ref, xb_out, x_sems, 1, here.across_x())
    core_sum.start()
    for scatter in scatters:
        scatter.start()
    core_sum.wait_recv()
    sum_own[0] = sums_ref[...] + sum_came[0]
    y_sum.start()
    for scatter in scatters:
        scatter.to_y()
    y_sum.wait_recv()
    sum_own[1] = sum_own[0] + sum_came[1]
    for copy in z_sums:
        copy.start()
    scatters[0].ready_z()
    for turn in range(3):
        scatters[0].to_z(turn)
    for copy in z_sums:
        copy.wait_recv()
    sum_own[2] = sum_own[1] + sum_came[2] + sum_came[3] + sum_came[4]
    x_sum.start()
    xa.start()
    xb.start()
    for i in range(1, matrices):
        scatters[i].ready_z()
        for turn in range(3):
            scatters[i].to_z(turn)
        scatters[i - 1].finish()
    x_sum.wait_recv()
    sums_out[...] = sum_own[2]
    sums_out[0:x_rows, :] = sum_own[2, 0:x_rows, :] + sum_came[5, 0:x_rows, :]
    scatters[-1].finish()
    for copy in (xa, xb):
        copy.wait()
    for copy in [core_sum, y_sum, x_sum] + z_sums:
        copy.wait_send()
    for scatter in scatters:
        scatter.sent()


def scatter_all(products, xa, xb, sums, x_rows):
    shape = jax.ShapeDtypeStruct
    sems = pltpu.SemaphoreType.DMA
    matrices = len(products)
    scratch = []
    for product in products:
        piece = product.shape[1:]
        scratch += [pltpu.VMEM((count,) + piece, BF16) for count in (8, 8, 4, 6)]
    scratch += [sems((2, Scatter.COPIES))] * matrices + [sems((8,))] * matrices
    scratch += [sems((2, 2)), sems((2, 6)), pltpu.VMEM((3,) + sums.shape, F32), pltpu.VMEM((6,) + sums.shape, F32)]
    return pl.pallas_call(
        functools.partial(scatter_kernel, matrices, x_rows),
        in_specs=[in_any()] * (matrices + 2) + [in_vmem()],
        out_specs=[in_vmem()] * matrices + [in_any()] * 2 + [in_vmem()],
        out_shape=[shape(product.shape[1:], F32) for product in products]
        + [shape(xa.shape, BF16), shape(xb.shape, BF16), shape(sums.shape, F32)],
        scratch_shapes=scratch,
        compiler_params=pltpu.CompilerParams(
            collective_id=1, has_side_effects=True, vmem_limit_bytes=VMEM_LIMIT
        ),
        name="scatter_all",
    )(*products, xa, xb, sums)


def lanes_of(per_head):
    return jnp.pad(per_head, [(0, 0)] * (per_head.ndim - 1) + [(0, 128 - per_head.shape[-1])])


def prepare_plain(normed, small, bias, rate, flat_ids, q):
    tokens = normed.shape[0]
    blocks = tokens // q
    proj = dot(normed, small)
    bc_width = small.shape[1] - 128
    dt_in = proj[:, bc_width:] + bias
    dt = jax.nn.softplus(dt_in)
    lower = jnp.where(jnp.arange(q)[:, None] >= jnp.arange(q)[None, :], 1.0, 0.0)
    la = jnp.einsum("ij,bjh->bih", lower, (dt * rate).reshape(blocks, q, 128), precision=HIGHEST)
    shifted = lambda l: jnp.concatenate([jnp.full((l,), -1, jnp.int32), flat_ids[:-l]])
    by_block = flat_ids.reshape(blocks, q)
    before = jnp.concatenate([jnp.full((1,), -1, jnp.int32), by_block[:-1, -1]])
    carried = (by_block == before[:, None]).reshape(-1)
    run_last = (by_block == by_block[:, -1:]).reshape(-1)
    masks = [flat_ids == shifted(1), flat_ids == shifted(2), flat_ids == shifted(3), carried, run_last, flat_ids]
    return proj[:, :bc_width], dt_in, dt, la.reshape(tokens, 128), lanes_of(jnp.stack(masks, axis=1).astype(F32))


def body(
    dp,
    tp,
    hidden_in,
    prenorm_gain,
    w_zx,
    w_dt,
    w_bc,
    conv_x,
    conv_bc,
    dt_bias,
    a_log,
    d_skip,
    norm_gain,
    w_out,
    seg_ids,
    grad_out,
):
    q = BLOCK_LEN
    staged = dp == 16 and tp == 2
    inner = w_out.shape[0]
    head_count = dt_bias.shape[0]
    width = inner // head_count
    bc_width = w_bc.shape[1]
    shard = w_bc.shape[0]
    depth = hidden_in.shape[1]
    inner_total = inner * tp
    tensor = lax.axis_index("tensor")

    bias = lanes_of(dt_bias)[None, :]
    rate = lanes_of(-jnp.exp(a_log))[None, :]
    small_shard = jnp.concatenate([w_bc, lanes_of(w_dt)], axis=1)
    flat_ids = (seg_ids + seg_ids.shape[1] * lax.broadcasted_iota(jnp.int32, seg_ids.shape, 0)).reshape(-1)
    seg_row = flat_ids.astype(F32)[None, :]
    skip_lanes = jnp.repeat(d_skip, width)[None, :]
    prep = dict(rate=rate, seg_row=seg_row)

    if staged:
        (
            full_rows, cot_rows, small, w_s, w_z, w_out_t, s, normed, scale_in,
            prep["bcraw"], prep["dt_in"], prep["dt"], prep["la"], prep["masks"],
            states, d_y, gated, d_z, grad_norm_gain,
        ) = forward_all(
            hidden_in, grad_out, small_shard, w_zx[:, 1, :], w_zx[:, 0, :], w_out.T,
            prenorm_gain[None, :], bias, rate, seg_row, conv_x, conv_bc, skip_lanes, norm_gain[None, :],
            width, inner_total, q,
        )
        grad_norm_gain = grad_norm_gain[0]
        scale_in = scale_in[:, :1]
        rows_float = full_rows.astype(F32)
    else:
        over_dp = lambda value: lax.all_gather(value, "dp", axis=0, tiled=True)
        small = over_dp(small_shard)
        w_s, w_z, w_out_t = over_dp(w_zx[:, 1, :]), over_dp(w_zx[:, 0, :]), over_dp(w_out.T)
        rows_float = lax.all_gather(hidden_in, "tensor", axis=0, tiled=True).astype(F32)
        cot_rows = lax.all_gather(grad_out, "tensor", axis=0, tiled=True)
        scale_in = lax.rsqrt(jnp.mean(rows_float * rows_float, axis=1, keepdims=True) + EPS)
        normed = (rows_float * scale_in * prenorm_gain).astype(BF16)
        prep["bcraw"], prep["dt_in"], prep["dt"], prep["la"], prep["masks"] = prepare_plain(
            normed, small, bias, rate, flat_ids, q
        )
        s, y, states = scan_forward(normed, w_s, prep, conv_x, conv_bc, skip_lanes, width, q)
        z = dot(normed, w_z)
        gate_sig = sigmoid(z)
        gate = z * gate_sig
        v = y * gate
        grad_gated = dot(cot_rows, w_out_t)
        scaled_grad = grad_gated * norm_gain
        sums = jnp.stack([jnp.sum(v * v, axis=1), jnp.sum(scaled_grad * v, axis=1)])
        sums = lax.psum(sums, "tensor")
        scale_out = lax.rsqrt(sums[0] / inner_total + EPS)[:, None]
        pull = sums[1][:, None] * scale_out**3 / inner_total
        gated = (v * scale_out * norm_gain).astype(BF16)
        grad_norm_gain = jnp.sum(grad_gated * v * scale_out, axis=0)
        d_v = scaled_grad * scale_out - pull * v
        d_y = d_v * gate
        d_z = (d_v * y * gate_sig * (1.0 + z * (1.0 - gate_sig))).astype(BF16)
    tokens = normed.shape[0]

    d_s, grad_taps, d_small, low_bc, grad_taps_bc, grad_heads = scan_backward(
        s, d_y, prep, conv_x, conv_bc, skip_lanes, states, width, q
    )
    grad_d_skip = jnp.sum(grad_taps[5].reshape(head_count, width), axis=1)

    own_rows = tokens // tp
    rows_of = lambda array, i: lax.dynamic_slice_in_dim(array, i * own_rows, own_rows, 0)
    project = lambda i: dot(rows_of(gated, i), w_out_t, NT)
    prenorm_terms = []

    def grad_rows(i):
        columns = (
            dot(rows_of(d_z, i), w_z, NT)
            + dot(rows_of(d_s, i), w_s, NT)
            + dot(rows_of(d_small, i), small, NT)
            + dot(rows_of(low_bc, i), small[:, :bc_width], NT)
        )
        unit = rows_of(rows_float, i) * rows_of(scale_in, i)
        prenorm_terms.append(jnp.sum(columns * unit, axis=0))
        grad_unit = columns * prenorm_gain
        return rows_of(scale_in, i) * (
            grad_unit - unit * jnp.mean(grad_unit * unit, axis=1, keepdims=True)
        )

    products = [
        dot(cot_rows, gated, TN),
        dot(normed, d_z, TN),
        dot(normed, jnp.concatenate([d_s, d_small], axis=1), TN),
    ]
    if staged:
        projected, own_grad = project(tensor), grad_rows(tensor)
        away_projected, away_grad = project(1 - tensor).astype(BF16), grad_rows(1 - tensor).astype(BF16)
    else:
        every = lambda make: jnp.concatenate([make(i) for i in range(tp)], axis=0)
        onto = lambda value, dim: lax.psum_scatter(value, "tensor", scatter_dimension=dim, tiled=True)
        projected, own_grad = onto(every(project), 0), onto(every(grad_rows), 0)

    pieces = [
        sum(prenorm_terms),
        grad_taps_bc[:5].reshape(-1),
        grad_taps[:5].reshape(-1),
        grad_norm_gain,
        grad_heads[0],
        grad_heads[1],
        lanes_of(grad_d_skip),
    ]
    gap = -(pieces[0].shape[0] + pieces[1].shape[0]) % 1024
    pieces.insert(2, jnp.zeros((gap,), F32))
    x_rows = sum(piece.shape[0] for piece in pieces[:3]) // 128
    flat = jnp.concatenate(pieces)
    flat = jnp.pad(flat, (0, -flat.shape[0] % 1024)).reshape(-1, 128)
    half_of = lambda value: lax.dynamic_slice_in_dim(
        value, tensor * (value.shape[-1] // tp), value.shape[-1] // tp, value.ndim - 1
    )
    if staged:
        grad_w_out, grad_w_z, grad_last, came_projected, came_grad, flat = scatter_all(
            [p.astype(BF16).reshape(16, shard, -1) for p in products],
            away_projected, away_grad, flat, x_rows,
        )
        projected = projected + came_projected.astype(F32)
        own_grad = own_grad + came_grad.astype(F32)
        bc_sum = grad_last[:, inner : inner + bc_width]
        bc_half = bc_width // 2
        away_bc = lax.dynamic_slice_in_dim(bc_sum, (1 - tensor) * bc_half, bc_half, 1)
        grad_w_bc = half_of(bc_sum) + lax.ppermute(away_bc, "tensor", [(0, 1), (1, 0)])
    else:
        grad_w_out, grad_w_z, grad_last = [
            lax.psum_scatter(p, "dp", scatter_dimension=0, tiled=True) for p in products
        ]
        grad_w_bc = onto(grad_last[:, inner : inner + bc_width], 1)
        flat = lax.psum(flat, "dp")
        flat = jnp.concatenate([lax.psum(flat[:x_rows], "tensor"), flat[x_rows:]], axis=0)
    block_out = (hidden_in.astype(F32) + projected).astype(BF16)
    grad_in = (grad_out.astype(F32) + own_grad).astype(BF16)
    grad_w_zx = jnp.stack([grad_w_z, grad_last[:, :inner]], axis=1)
    grad_w_dt = grad_last[:, inner + bc_width : inner + bc_width + head_count]

    flat = flat.reshape(-1)
    at, cut_out = 0, []
    for piece in pieces:
        cut_out.append(flat[at : at + piece.shape[0]])
        at += piece.shape[0]
    return (
        block_out,
        grad_in,
        half_of(cut_out[0]),
        grad_w_zx,
        grad_w_dt,
        grad_w_bc,
        cut_out[3].reshape(5, inner),
        half_of(cut_out[1].reshape(5, bc_width)),
        cut_out[5][:head_count],
        cut_out[6][:head_count],
        cut_out[7][:head_count],
        cut_out[4],
        grad_w_out.T,
    )


def solution(mesh):
    in_specs = (
        P(("dp", "tensor"), None),
        P(),
        P("dp", None, "tensor"),
        P("dp", "tensor"),
        P("dp", None),
        P(None, "tensor"),
        P(),
        P("tensor"),
        P("tensor"),
        P("tensor"),
        P("tensor"),
        P("tensor", "dp"),
        P("dp", None),
        P(("dp", "tensor"), None),
    )
    out_specs = (
        P(("dp", "tensor"), None),
        P(("dp", "tensor"), None),
        P("tensor"),
        P("dp", None, "tensor"),
        P("dp", "tensor"),
        P("dp", "tensor"),
        P(None, "tensor"),
        P(None, "tensor"),
        P("tensor"),
        P("tensor"),
        P("tensor"),
        P("tensor"),
        P("tensor", "dp"),
    )
    return jax.shard_map(
        functools.partial(body, mesh.shape["dp"], mesh.shape["tensor"]),
        mesh=mesh,
        in_specs=in_specs,
        out_specs=out_specs,
        check_vma=False,
    )
```

```python
import functools

import jax
import jax.numpy as jnp
from jax import lax
from jax.experimental import pallas as pl
from jax.experimental.pallas import tpu as pltpu
from jax.sharding import PartitionSpec as P

BLOCK_LEN = 256
EPS = 1e-05
NEG = -1e30
F32 = jnp.float32
BF16 = jnp.bfloat16
HIGHEST = lax.Precision.HIGHEST
VMEM_LIMIT = 60 * 1024 * 1024


def dot(a, b, dims=((1,), (0,)), precision=None):
    return lax.dot_general(a, b, (dims, ((), ())), preferred_element_type=F32, precision=precision)


NN, NT, TN = ((1,), (0,)), ((1,), (1,)), ((0,), (0,))


def sigmoid(w):
    return 1.0 / (1.0 + jnp.exp(-w))


def conv_of(signal, taps, masks):
    out = taps[4:5, :] + taps[3:4, :] * signal
    for back in range(1, 4):
        out = out + taps[3 - back : 4 - back, :] * (
            pltpu.roll(signal, back, 0) * masks[:, back - 1 : back]
        )
    return out


def conv_back(grad, signal, taps, masks):
    rows = signal.shape[0]
    grad_signal = taps[3:4, :] * grad
    tap_rows = [None] * 5
    tap_rows[4] = jnp.sum(grad, axis=0, keepdims=True)
    tap_rows[3] = jnp.sum(grad * signal, axis=0, keepdims=True)
    for back in range(1, 4):
        kept = grad * masks[:, back - 1 : back]
        tap_rows[3 - back] = jnp.sum(kept * pltpu.roll(signal, back, 0), axis=0, keepdims=True)
        grad_signal = grad_signal + taps[3 - back : 4 - back, :] * pltpu.roll(kept, rows - back, 0)
    return grad_signal, tap_rows


def expand(columns, width):
    rows, heads = columns.shape
    lane = lax.broadcasted_iota(jnp.int32, (rows, 2 * width), 1)
    pieces = [
        jnp.where(lane < width, columns[:, h : h + 1], columns[:, h + 1 : h + 2])
        for h in range(0, heads, 2)
    ]
    return pieces[0] if len(pieces) == 1 else jnp.concatenate(pieces, axis=1)


def block_rows(block, size):
    return pl.ds(pl.multiple_of(block * size, size), size)


def head_lanes(array, step, heads):
    return pltpu.roll(array, lax.rem(128 - step * heads, 128), 1)


def block_tables(q, bcraw_ref, kbc_ref, msk_ref, segr_ref, bcc, mneg, cb):
    n = bcc.shape[1] // 2
    c = conv_of(bcraw_ref[...], kbc_ref[...], msk_ref[...])
    bcc[...] = c * sigmoid(c)
    later = lax.broadcasted_iota(jnp.int32, (q, q), 0) >= lax.broadcasted_iota(jnp.int32, (q, q), 1)

    def prepare(b, carry):
        rows = block_rows(b, q)
        same = msk_ref[rows, 5:6] == segr_ref[:, rows]
        mneg[rows, :] = jnp.where(later & same, 0.0, NEG)
        cb[rows, :] = dot(bcc[rows, n:], bcc[rows, :n], NT, HIGHEST)
        return carry

    lax.fori_loop(0, bcc.shape[0] // q, prepare, 0)


def fwd_group(
    q, heads, width, step, at, s, taps, skip, la_ref, dt_ref, msk_ref, s_ref, y_ref, st_ref,
    bcc, mneg, cb, xs, state, la4, lat4, dt4,
):
    tokens = s.shape[0]
    blocks = tokens // q
    n = bcc.shape[1] // 2
    lanes = heads * width
    la_here = head_lanes(la_ref[...], step, heads)
    la4[...] = la_here
    lat4[...] = la_here.T[0:8, :]
    dt4[...] = head_lanes(dt_ref[...], step, heads)
    s_ref[:, at] = s
    c = conv_of(s, taps, msk_ref[...])
    xs[...] = c * sigmoid(c)
    state[...] = jnp.zeros_like(state)
    lane_head = lax.broadcasted_iota(jnp.int32, (q, lanes), 1) // width

    def one_block(b, carry):
        rows = block_rows(b, q)
        x = xs[rows, :]
        la = la4[rows, 0:heads]
        u = x * expand(dt4[rows, 0:heads], width)
        ub = u.astype(BF16)
        enter = expand(jnp.exp(la) * msk_ref[rows, 3:4], width)
        last = expand(jnp.exp(la[q - 1 : q, :] - la) * msk_ref[rows, 4:5], width)
        st = state[...]
        st_ref[b, :, at] = st
        base = mneg[rows, :]
        cb_b = cb[rows, :]
        weights, values = [], []
        for h in range(heads):
            decay = jnp.exp(la[:, h : h + 1] - lat4[h : h + 1, rows] + base)
            weights.append((decay * cb_b).astype(BF16))
            values.append(jnp.where(lane_head == h, ub, jnp.zeros_like(ub)))
        local = dot(jnp.concatenate(weights, axis=1), jnp.concatenate(values, axis=0))
        carried = dot(bcc[rows, n:].astype(BF16), st.astype(BF16))
        y_ref[rows, at] = local + carried * enter + skip * x
        state[...] = st * enter[q - 1 : q, :] + dot(
            bcc[rows, :n].astype(BF16), (u * last).astype(BF16), TN
        )
        return carry

    lax.fori_loop(0, blocks, one_block, 0, unroll=blocks <= 2)


def fwd_kernel(
    q, heads, width,
    nm_ref, w_ref, bcraw_ref, kx_ref, kbc_ref, la_ref, dt_ref, msk_ref, segr_ref, dsk_ref,
    s_ref, y_ref, st_ref,
    bcc, mneg, cb, *scratch,
):
    step = pl.program_id(0)

    @pl.when(step == 0)
    def _():
        block_tables(q, bcraw_ref, kbc_ref, msk_ref, segr_ref, bcc, mneg, cb)

    s = dot(nm_ref[...], w_ref[...])
    fwd_group(
        q, heads, width, step, slice(None), s, kx_ref[...], dsk_ref[...], la_ref, dt_ref, msk_ref,
        s_ref, y_ref, st_ref, bcc, mneg, cb, *scratch,
    )


def bwd_tables(q, bcraw_ref, kbc_ref, msk_ref, segr_ref, bcc, mnegt, cbt, *zeroed):
    n = bcc.shape[1] // 2
    c = conv_of(bcraw_ref[...], kbc_ref[...], msk_ref[...])
    bcc[...] = c * sigmoid(c)
    for ref in zeroed:
        ref[...] = jnp.zeros_like(ref)
    earlier = lax.broadcasted_iota(jnp.int32, (q, q), 0) <= lax.broadcasted_iota(jnp.int32, (q, q), 1)

    def prepare(b, carry):
        rows = block_rows(b, q)
        same = msk_ref[rows, 5:6] == segr_ref[:, rows]
        mnegt[rows, :] = jnp.where(earlier & same, 0.0, NEG)
        cbt[rows, :] = dot(bcc[rows, :n], bcc[rows, n:], NT, HIGHEST)
        return carry

    lax.fori_loop(0, bcc.shape[0] // q, prepare, 0)


def bwd_group(
    q, heads, width, step,
    s_ref, dy_ref, kx_ref, la_ref, dt_ref, msk_ref, dsk_ref, st_ref, ds_ref, gk_ref,
    bcc, mnegt, cbt, xs, dxs, dtt, gt, la4, lat4, dt4, dla_acc, ddt_acc, dbc_acc,
    between=None,
):
    tokens = s_ref.shape[0]
    blocks = tokens // q
    n = bcc.shape[1] // 2
    lanes = heads * width
    la_here = head_lanes(la_ref[...], step, heads)
    la4[...] = la_here
    lat4[...] = la_here.T[0:8, :]
    dt4[...] = head_lanes(dt_ref[...], step, heads)
    c = conv_of(s_ref[...], kx_ref[...], msk_ref[...])
    xs[...] = c * sigmoid(c)
    gt[...] = jnp.zeros_like(gt)
    lane_head = lax.broadcasted_iota(jnp.int32, (q, lanes), 1) // width
    pick = jnp.where(
        lax.broadcasted_iota(jnp.int32, (8, lanes), 1) // width
        == lax.broadcasted_iota(jnp.int32, (8, lanes), 0),
        1.0,
        0.0,
    )
    token_lane = lax.broadcasted_iota(jnp.int32, (1, q), 1)
    col_lane = lax.broadcasted_iota(jnp.int32, (q, 128), 1)

    def one_block(i, carry):
        b = blocks - 1 - i
        rows = block_rows(b, q)
        x = xs[rows, :]
        dy = dy_ref[rows, :]
        la = la4[rows, 0:heads]
        dtx = expand(dt4[rows, 0:heads], width)
        u = x * dtx
        ub, dyb = u.astype(BF16), dy.astype(BF16)
        enter = expand(jnp.exp(la) * msk_ref[rows, 3:4], width)
        last = expand(jnp.exp(la[q - 1 : q, :] - la) * msk_ref[rows, 4:5], width)
        base = mnegt[rows, :]
        cb_b = cbt[rows, :]
        weights, values, row_sums = [], [], []
        d_cb = jnp.zeros((q, q), F32)
        col_sums = jnp.zeros((q, 128), F32)
        for h in range(heads):
            own = lane_head == h
            decay = jnp.exp(lat4[h : h + 1, rows] - la[:, h : h + 1] + base)
            dyh = jnp.where(own, dyb, jnp.zeros_like(dyb))
            pair = dot(ub, dyh, NT)
            weight = decay * cb_b
            d_cb = d_cb + decay * pair
            both = weight * pair
            row_sums.append(jnp.sum(both, axis=0, keepdims=True))
            col_sums = jnp.where(col_lane == h, jnp.sum(both, axis=1, keepdims=True), col_sums)
            weights.append(weight.astype(BF16))
            values.append(dyh)
        dtt[rows, :] += d_cb
        g = gt[...]
        gb16 = g.astype(BF16)
        st = st_ref[b]
        stb = st.astype(BF16)
        c16 = bcc[rows, n:].astype(BF16)
        b16 = bcc[rows, :n].astype(BF16)
        gb = dot(b16, gb16) * last
        du = dot(jnp.concatenate(weights, axis=1), jnp.concatenate(values, axis=0)) + gb
        dye = (dy * enter).astype(BF16)
        from_state = dot(c16, stb) * enter
        dbc_acc[rows, n:] += dot(dye, stb, NT)
        dbc_acc[rows, :n] += dot((u * last).astype(BF16), gb16, NT)
        ug = u * gb
        dla = dot(pick, dy * from_state - ug, NT, HIGHEST)
        ddt = dot(pick, x * du, NT, HIGHEST)
        tail = jnp.sum(ug, axis=0, keepdims=True) + enter[q - 1 : q, :] * jnp.sum(
            g * st, axis=0, keepdims=True
        )
        la_rows = []
        for h in range(heads):
            end = jnp.sum(jnp.where(lane_head[0:1, :] == h, tail, 0.0), axis=1, keepdims=True)
            la_rows.append(
                row_sums[h] + dla[h : h + 1, :] + jnp.where(token_lane == q - 1, end, 0.0)
            )
        dt_rows = [ddt[h : h + 1, :] for h in range(heads)]
        rest = jnp.zeros((128 - 2 * heads, q), F32)
        columns = jnp.concatenate(la_rows + dt_rows + [rest], axis=0).T
        la_part = jnp.where(col_lane < heads, columns, 0.0) - col_sums
        dt_part = jnp.where(col_lane >= heads, columns, 0.0)
        dla_acc[rows, :] += pltpu.roll(la_part, step * heads, 1)
        ddt_acc[rows, :] += pltpu.roll(dt_part, lax.rem(128 + (step - 1) * heads, 128), 1)
        gt[...] = g * enter[q - 1 : q, :] + dot(c16, dye, TN)
        dxs[rows, :] = dtx * du + dsk_ref[...] * dy
        return carry

    if between is None:
        lax.fori_loop(0, blocks, one_block, 0, unroll=blocks <= 2)
    else:
        for i in range(blocks):
            one_block(i, 0)
            between(i)

    s = s_ref[...]
    taps = kx_ref[...]
    masks = msk_ref[...]
    c = conv_of(s, taps, masks)
    sig = sigmoid(c)
    grad = dxs[...] * sig * (1.0 + c * (1.0 - sig))
    d_s, tap_rows = conv_back(grad, s, taps, masks)
    ds_ref[...] = d_s.astype(BF16)
    skip_row = jnp.sum(dy_ref[...] * xs[...], axis=0, keepdims=True)
    gk_ref[...] = jnp.concatenate(
        tap_rows + [skip_row, jnp.zeros_like(skip_row), jnp.zeros_like(skip_row)], axis=0
    )


def bwd_finish(
    q, bcraw_ref, kbc_ref, dt_ref, msk_ref, dtin_ref, rate_ref, small_ref, low_ref, gkbc_ref, ghead_ref,
    bcc, dtt, dla_acc, ddt_acc, dbc_acc,
):
    n = bcc.shape[1] // 2
    upper = jnp.where(
        lax.broadcasted_iota(jnp.int32, (q, q), 0) <= lax.broadcasted_iota(jnp.int32, (q, q), 1), 1.0, 0.0
    )

    def finish(b, carry):
        rows = block_rows(b, q)
        d_cb = dtt[rows, :]
        dbc_acc[rows, :n] += dot(d_cb, bcc[rows, n:], NN, HIGHEST)
        dbc_acc[rows, n:] += dot(d_cb, bcc[rows, :n], TN, HIGHEST)
        dla_acc[rows, :] = dot(upper, dla_acc[rows, :], NN, HIGHEST)
        return carry

    lax.fori_loop(0, bcc.shape[0] // q, finish, 0)
    rate = rate_ref[...]
    d_exponent = dla_acc[...]
    d_raw = (ddt_acc[...] + rate * d_exponent) * sigmoid(dtin_ref[...])
    d_rate = rate * jnp.sum(dt_ref[...] * d_exponent, axis=0, keepdims=True)
    d_bias = jnp.sum(d_raw, axis=0, keepdims=True)
    ghead_ref[...] = jnp.concatenate([d_bias, d_rate, jnp.zeros((6, 128), F32)], axis=0)
    raw = bcraw_ref[...]
    taps = kbc_ref[...]
    masks = msk_ref[...]
    c = conv_of(raw, taps, masks)
    sig = sigmoid(c)
    grad = dbc_acc[...] * sig * (1.0 + c * (1.0 - sig))
    d_bc, rows_bc = conv_back(grad, raw, taps, masks)
    high = d_bc.astype(BF16)
    small_ref[:, : 2 * n] = high
    small_ref[:, 2 * n : 2 * n + 128] = d_raw.astype(BF16)
    low_ref[...] = (d_bc - high.astype(F32)).astype(BF16)
    zero_row = jnp.zeros_like(rows_bc[0])
    gkbc_ref[...] = jnp.concatenate(rows_bc + [zero_row] * 3, axis=0)


def bwd_kernel(
    q, heads, width,
    s_ref, dy_ref, bcraw_ref, kx_ref, kbc_ref, la_ref, dt_ref, msk_ref, segr_ref, dsk_ref, st_ref, dtin_ref, rate_ref,
    ds_ref, gk_ref, small_ref, low_ref, gkbc_ref, ghead_ref,
    bcc, mnegt, cbt, xs, dxs, dtt, gt, la4, lat4, dt4, dla_acc, ddt_acc, dbc_acc,
):
    step = pl.program_id(0)

    @pl.when(step == 0)
    def _():
        bwd_tables(
            q, bcraw_ref, kbc_ref, msk_ref, segr_ref, bcc, mnegt, cbt, dtt, dbc_acc, dla_acc, ddt_acc
        )

    bwd_group(
        q, heads, width, step, s_ref, dy_ref, kx_ref, la_ref, dt_ref, msk_ref, dsk_ref, st_ref, ds_ref, gk_ref,
        bcc, mnegt, cbt, xs, dxs, dtt, gt, la4, lat4, dt4, dla_acc, ddt_acc, dbc_acc,
    )

    @pl.when(step == pl.num_programs(0) - 1)
    def _():
        bwd_finish(
            q, bcraw_ref, kbc_ref, dt_ref, msk_ref, dtin_ref, rate_ref, small_ref, low_ref, gkbc_ref, ghead_ref,
            bcc, dtt, dla_acc, ddt_acc, dbc_acc,
        )


def full(shape):
    return pl.BlockSpec(shape, lambda i: (0,) * len(shape))


def lane_block(rows, lanes):
    return pl.BlockSpec((rows, lanes), lambda i: (0, i))


def heads_per_step(head_count):
    return 4 if head_count % 4 == 0 else 2


def forward_scratch(tokens, q, n, lanes):
    return [
        pltpu.VMEM((tokens, 2 * n), F32), pltpu.VMEM((tokens, q), F32), pltpu.VMEM((tokens, q), F32),
        pltpu.VMEM((tokens, lanes), F32), pltpu.VMEM((n, lanes), F32), pltpu.VMEM((tokens, 128), F32),
        pltpu.VMEM((8, tokens), F32), pltpu.VMEM((tokens, 128), F32),
    ]


def scan_forward(normed, w_s, prep, conv_x, conv_bc, skip_lanes, width, q):
    bcraw, la, dt, masks, seg_row = (prep[k] for k in ("bcraw", "la", "dt", "masks", "seg_row"))
    tokens, depth = normed.shape
    inner = w_s.shape[1]
    head_count = inner // width
    heads = heads_per_step(head_count)
    lanes = heads * width
    n = bcraw.shape[1] // 2
    blocks = tokens // q
    return pl.pallas_call(
        functools.partial(fwd_kernel, q, heads, width),
        grid=(head_count // heads,),
        in_specs=[
            full((tokens, depth)), lane_block(depth, lanes), full((tokens, 2 * n)), lane_block(5, lanes),
            full((5, 2 * n)), full((tokens, 128)), full((tokens, 128)), full((tokens, 128)),
            full((1, tokens)), lane_block(1, lanes),
        ],
        out_specs=[
            lane_block(tokens, lanes), lane_block(tokens, lanes),
            pl.BlockSpec((blocks, n, lanes), lambda i: (0, 0, i)),
        ],
        out_shape=[
            jax.ShapeDtypeStruct((tokens, inner), F32), jax.ShapeDtypeStruct((tokens, inner), F32),
            jax.ShapeDtypeStruct((blocks, n, inner), F32),
        ],
        scratch_shapes=forward_scratch(tokens, q, n, lanes),
        compiler_params=pltpu.CompilerParams(
            dimension_semantics=("arbitrary",), vmem_limit_bytes=VMEM_LIMIT
        ),
        cost_estimate=pl.CostEstimate(
            flops=2 * tokens * inner * (depth + q + 4 * n),
            bytes_accessed=2 * (depth * inner + tokens * depth) + 8 * tokens * inner,
            transcendentals=tokens * q * head_count,
        ),
        name="scan_forward",
    )(normed, w_s, bcraw, conv_x, conv_bc, la, dt, masks, seg_row, skip_lanes)


def backward_scratch(tokens, q, n, lanes):
    return [
        pltpu.VMEM((tokens, 2 * n), F32), pltpu.VMEM((tokens, q), F32), pltpu.VMEM((tokens, q), F32),
        pltpu.VMEM((tokens, lanes), F32), pltpu.VMEM((tokens, lanes), F32), pltpu.VMEM((tokens, q), F32),
        pltpu.VMEM((n, lanes), F32), pltpu.VMEM((tokens, 128), F32), pltpu.VMEM((8, tokens), F32),
        pltpu.VMEM((tokens, 128), F32), pltpu.VMEM((tokens, 128), F32), pltpu.VMEM((tokens, 128), F32),
        pltpu.VMEM((tokens, 2 * n), F32),
    ]


def scan_backward(s, dy, prep, conv_x, conv_bc, skip_lanes, states, width, q):
    bcraw, la, dt, masks, seg_row = (prep[k] for k in ("bcraw", "la", "dt", "masks", "seg_row"))
    tokens, inner = s.shape
    head_count = inner // width
    heads = heads_per_step(head_count)
    lanes = heads * width
    n = bcraw.shape[1] // 2
    blocks = tokens // q
    return pl.pallas_call(
        functools.partial(bwd_kernel, q, heads, width),
        grid=(head_count // heads,),
        in_specs=[
            lane_block(tokens, lanes), lane_block(tokens, lanes), full((tokens, 2 * n)), lane_block(5, lanes),
            full((5, 2 * n)), full((tokens, 128)), full((tokens, 128)), full((tokens, 128)),
            full((1, tokens)), lane_block(1, lanes), pl.BlockSpec((blocks, n, lanes), lambda i: (0, 0, i)),
            full((tokens, 128)), full((1, 128)),
        ],
        out_specs=[
            lane_block(tokens, lanes), lane_block(8, lanes), full((tokens, 2 * n + 128)),
            full((tokens, 2 * n)), full((8, 2 * n)), full((8, 128)),
        ],
        out_shape=[
            jax.ShapeDtypeStruct((tokens, inner), BF16), jax.ShapeDtypeStruct((8, inner), F32),
            jax.ShapeDtypeStruct((tokens, 2 * n + 128), BF16), jax.ShapeDtypeStruct((tokens, 2 * n), BF16),
            jax.ShapeDtypeStruct((8, 2 * n), F32), jax.ShapeDtypeStruct((8, 128), F32),
        ],
        scratch_shapes=backward_scratch(tokens, q, n, lanes),
        compiler_params=pltpu.CompilerParams(
            dimension_semantics=("arbitrary",), vmem_limit_bytes=VMEM_LIMIT
        ),
        cost_estimate=pl.CostEstimate(
            flops=2 * tokens * inner * (8 * q + 8 * n),
            bytes_accessed=12 * tokens * inner,
            transcendentals=tokens * q * head_count,
        ),
        name="scan_backward",
    )(
        s, dy, bcraw, conv_x, conv_bc, la, dt, masks, seg_row, skip_lanes, states, prep["dt_in"], prep["rate"],
    )


MESH = pl.DeviceIdType.MESH


class Here:
    def __init__(self):
        self.me = lax.axis_index("dp")
        self.t = lax.axis_index("tensor")
        self.z = self.me // 4
        self.y = (self.me // 2) % 2
        self.c = self.me % 2

    def slot(self, z, y, c):
        return z * 4 + y * 2 + c

    def z_plus(self, d):
        return (self.z + d) % 4

    def owner(self, k):
        core = self.c if k < 8 else 1 - self.c
        return self.slot(k % 4, 1 - self.y if k % 8 < 4 else self.y, core)

    def at_z(self, d):
        return (self.slot(self.z_plus(d), self.y, self.c), self.t)

    def across_y(self):
        return (self.slot(self.z, 1 - self.y, self.c), self.t)

    def other_core(self):
        return (self.slot(self.z, self.y, 1 - self.c), self.t)

    def across_x(self):
        return (self.me, 1 - self.t)

    def greet(self):
        barrier = pltpu.get_barrier_semaphore()
        for peer in (self.at_z(1), self.at_z(2), self.at_z(3), self.across_y(), self.other_core(), self.across_x()):
            pl.semaphore_signal(barrier, inc=1, device_id=peer, device_id_type=MESH)
        pl.semaphore_wait(barrier, 6)


def send(src, dst, sems, index, peer):
    return pltpu.make_async_remote_copy(
        src_ref=src, dst_ref=dst, send_sem=sems.at[0, index], recv_sem=sems.at[1, index],
        device_id=peer, device_id_type=MESH,
    )


class Gather:
    COPIES = 27

    def __init__(self, here, src, dst, sems, local_sem):
        self.here, self.src, self.dst, self.sems = here, src, dst, sems
        self.local = pltpu.make_async_copy(src, dst.at[here.me], local_sem)

    def holds(self, i):
        z = self.here.z
        return z >= 0 if i == 0 else z >= i if i <= 3 else z + i - 3 <= 3

    def slot_of(self, i, far=False):
        here = self.here
        z = here.z - i if i <= 3 else here.z + i - 3
        return here.slot(z, 1 - here.y if far else here.y, here.c)

    def from_here(self, i, far=False):
        return self.src if i == 0 and not far else self.dst.at[self.slot_of(i, far)]

    def up(self, d):
        i = d - 1
        return send(self.from_here(i), self.dst.at[self.slot_of(i)], self.sems, i, self.here.at_z(1))

    def down(self, d):
        i = d + 2 if d > 1 else 0
        return send(self.from_here(i), self.dst.at[self.slot_of(i)], self.sems, 2 + d, self.here.at_z(3))

    def across(self, i):
        return send(self.from_here(i), self.dst.at[self.slot_of(i)], self.sems, 6 + i, self.here.across_y())

    def to_core(self, k):
        i, far = k % 7, k >= 7
        src = self.from_here(i, far)
        return send(src, self.dst.at[self.slot_of(i, far)], self.sems, 13 + k, self.here.other_core())

    def sends_up(self, d):
        return (self.here.z < 3) & (self.here.z >= d - 1)

    def sends_down(self, d):
        return (self.here.z > 0) & (self.here.z + d <= 4)

    def start(self):
        pl.when(self.sends_up(1))(lambda: self.up(1).start())
        pl.when(self.sends_down(1))(lambda: self.down(1).start())
        self.across(0).start()
        self.to_core(0).start()
        self.local.start()

    def pass_z(self, *hops):
        for d in hops:

            @pl.when(self.holds(d))
            def _(d=d):
                self.up(d).wait_recv()
                if d < 3:
                    pl.when(self.here.z < 3)(lambda: self.up(d + 1).start())
                self.across(d).start()
                self.to_core(d).start()

            @pl.when(self.holds(3 + d))
            def _(d=d):
                self.down(d).wait_recv()
                if d < 3:
                    pl.when(self.here.z > 0)(lambda: self.down(d + 1).start())
                self.across(3 + d).start()
                self.to_core(3 + d).start()

    def pass_y(self):
        for i in range(7):

            @pl.when(self.holds(i))
            def _(i=i):
                self.across(i).wait_recv()
                self.to_core(7 + i).start()

    def arrived(self):
        self.local.wait()
        for k in range(14):
            pl.when(self.holds(k % 7))(lambda k=k: self.to_core(k).wait_recv())

    def sent(self):
        for d in (1, 2, 3):
            pl.when(self.sends_up(d))(lambda d=d: self.up(d).wait_send())
            pl.when(self.sends_down(d))(lambda d=d: self.down(d).wait_send())
        for i in range(7):
            pl.when(self.holds(i))(lambda i=i: self.across(i).wait_send())
        for k in range(14):
            pl.when(self.holds(k % 7))(lambda k=k: self.to_core(k).wait_send())


def softplus(w):
    return jnp.maximum(w, 0.0) + jnp.log1p(jnp.exp(-jnp.abs(w)))


def forward_kernel(
    q, heads, width, inner_total,
    hid_ref, cot_ref, small_ref, ws_ref, wz_ref, wo_ref, gain_ref, bias_ref, rate_ref, seg_ref,
    kx_ref, kbc_ref, dsk_ref, ngain_ref,
    rows_out, small_out, ws_out, wz_out, wo_out, s_out, normt_out, cott_out,
    scale_out, bcraw_out, dtin_out, dt_out, la_out, masks_out, st_out, dy_out, gated_out, dz_out, gngain_out,
    small_sems, ws_sems, wz_sems, wo_sems, x_sems, local_sems,
    rows_v, cot_v, ws_v, wz_v, wo_v, s_v, normed_v, y_v, z_v, dg_v, sum_v, sum_own, sum_came, normt_v, cott_v,
    t_sems,
    bcc, mneg, cb, *group_scratch,
):
    here = Here()
    tokens = normed_v.shape[0]
    half = tokens // 2
    inner = y_v.shape[1]
    lanes = heads * width
    groups = inner // lanes
    here.greet()
    hidden = send(hid_ref, rows_v.at[here.t], x_sems, 0, here.across_x())
    cotangent = send(cot_ref, cot_v.at[here.t], x_sems, 1, here.across_x())
    sums_x = send(sum_own, sum_came, x_sems, 2, here.across_x())
    gathers = [
        Gather(here, src, dst, sems, local_sems.at[i])
        for i, (src, dst, sems) in enumerate(
            [
                (small_ref, small_out, small_sems),
                (ws_ref, ws_out, ws_sems),
                (wz_ref, wz_out, wz_sems),
                (wo_ref, wo_out, wo_sems),
            ]
        )
    ]
    small, ws, wz, wo = gathers
    local = lambda src, dst, i: pltpu.make_async_copy(src, dst, local_sems.at[i])
    own_hidden = local(hid_ref, rows_v.at[here.t], 4)
    own_cot = local(cot_ref, cot_v.at[here.t], 5)
    load_ws, load_wz, load_wo = local(ws_out, ws_v, 6), local(wz_out, wz_v, 7), local(wo_out, wo_v, 8)
    store_rows, store_s = local(rows_v, rows_out, 9), local(s_v, s_out, 10)

    def by_piece(src, dst, row):
        return [
            pltpu.make_async_copy(src.at[here.owner(k)], dst.at[k], t_sems.at[row, k]) for k in range(16)
        ]

    store_normt, store_cott = by_piece(normt_v, normt_out, 0), by_piece(cott_v, cott_out, 1)

    def turn(values, at, dst):
        shard_rows = dst.shape[1]
        flipped = values.astype(F32).T.astype(BF16)
        dst[pl.ds(at * (384 // shard_rows), 384 // shard_rows)] = flipped.reshape(
            384 // shard_rows, shard_rows, flipped.shape[1]
        )
    hidden.start()
    small.start()
    ws.start()
    cotangent.start()
    own_hidden.start()
    own_cot.start()

    seg = jnp.broadcast_to(seg_ref[...], (128, tokens)).T
    row = lax.broadcasted_iota(jnp.int32, (tokens, 128), 0)
    lane = lax.broadcasted_iota(jnp.int32, (tokens, 128), 1)
    masks = jnp.where(lane == 5, seg, 0.0)
    for back in (1, 2, 3):
        same = (pltpu.roll(seg, back, 0) == seg) & (row >= back)
        masks = jnp.where((lane == back - 1) & same, 1.0, masks)
    for b in range(tokens // q):
        inside = (row >= b * q) & (row < (b + 1) * q)
        if b:
            carried = inside & (seg == seg[b * q - 1 : b * q, :])
            masks = jnp.where((lane == 3) & carried, 1.0, masks)
        run_last = inside & (seg == seg[(b + 1) * q - 1 : (b + 1) * q, :])
        masks = jnp.where((lane == 4) & run_last, 1.0, masks)
    masks_out[...] = masks

    small.pass_z(1, 2, 3)
    ws.pass_z(1, 2)
    small.pass_y()
    own_hidden.wait()
    hidden.wait_recv()
    store_rows.start()
    gain = gain_ref[...]
    chunk = 64

    def norm(i, carry):
        side, at = i // (half // chunk), i % (half // chunk)
        rows = pl.ds(pl.multiple_of(at * chunk, chunk), chunk)
        values = rows_v[side, rows, :].astype(F32)
        scale = lax.rsqrt(jnp.mean(values * values, axis=1, keepdims=True) + EPS)
        out_rows = pl.ds(pl.multiple_of(i * chunk, chunk), chunk)
        normed_v[out_rows, :] = (values * scale * gain).astype(BF16)
        scale_out[out_rows, :] = jnp.broadcast_to(scale, (chunk, 128))
        return carry

    lax.fori_loop(0, tokens // chunk, norm, 0)

    def turn_normed(i, carry):
        turn(normed_v[:, pl.ds(pl.multiple_of(i * 384, 384), 384)], i, normt_v)
        return carry

    lax.fori_loop(0, normed_v.shape[1] // 384, turn_normed, 0)
    for copy in store_normt:
        copy.start()
    ws.pass_z(3)
    wz.start()
    small.arrived()
    pieces, shard, columns = small_out.shape
    proj = dot(normed_v[...], small_out[...].reshape(pieces * shard, columns))
    bc_width = columns - 128
    bcraw_out[...] = proj[:, :bc_width]
    dt_in = proj[:, bc_width:] + bias_ref[...]
    dtin_out[...] = dt_in
    dt = softplus(dt_in)
    dt_out[...] = dt
    lower = jnp.where(
        lax.broadcasted_iota(jnp.int32, (q, q), 0) >= lax.broadcasted_iota(jnp.int32, (q, q), 1), 1.0, 0.0
    )
    exponent = dt * rate_ref[...]
    for b in range(tokens // q):
        la_out[b * q : (b + 1) * q, :] = dot(lower, exponent[b * q : (b + 1) * q, :], NN, HIGHEST)
    block_tables(q, bcraw_out, kbc_ref, masks_out, seg_ref, bcc, mneg, cb)
    ws.pass_y()
    ws.arrived()
    load_ws.start()
    load_ws.wait()

    def weight_block(ref, at):
        return ref[:, :, at].reshape(pieces * shard, lanes)

    def lane_range(g):
        return pl.ds(pl.multiple_of(g * lanes, lanes), lanes)

    def scan_group(g, carry):
        pl.when(g == 0)(lambda: wz.pass_z(1))
        pl.when(g == 1)(lambda: wz.pass_z(2))

        @pl.when(g == 2)
        def _():
            wz.pass_z(3)
            wo.start()

        pl.when(g == 4)(lambda: wo.pass_z(1))
        pl.when(g == 5)(lambda: wo.pass_z(2))
        at = lane_range(g)
        s = dot(normed_v[...], weight_block(ws_v, at))
        fwd_group(
            q, heads, width, g, at, s, kx_ref[:, at], dsk_ref[:, at], la_out, dt_out, masks_out,
            s_v, y_v, st_out, bcc, mneg, cb, *group_scratch,
        )
        return carry

    lax.fori_loop(0, groups, scan_group, 0)
    store_s.start()
    wo.pass_z(3)
    wz.pass_y()
    wz.arrived()
    load_wz.start()
    own_cot.wait()
    cotangent.wait_recv()

    def turn_cot(i, carry):
        turn(
            cot_v[:, :, pl.ds(pl.multiple_of(i * 384, 384), 384)].reshape(tokens, 384), i, cott_v
        )
        return carry

    lax.fori_loop(0, cot_v.shape[2] // 384, turn_cot, 0)
    for copy in store_cott:
        copy.start()
    sum_v[...] = jnp.zeros_like(sum_v)
    load_wz.wait()

    def gate_group(g, carry):
        at = lane_range(g)
        z = dot(normed_v[...], weight_block(wz_v, at))
        z_v[:, at] = z
        v = y_v[:, at] * (z * sigmoid(z))
        square = v * v
        for piece in range(lanes // 128):
            sum_v[0] += square[:, piece * 128 : (piece + 1) * 128]
        return carry

    lax.fori_loop(0, groups, gate_group, 0)
    wo.pass_y()
    wo.arrived()
    load_wo.start()
    load_wo.wait()

    def pull_group(g, carry):
        at = lane_range(g)
        side = cot_v[...].reshape(tokens, cot_v.shape[2])
        pulled = dot(side, weight_block(wo_v, at))
        dg_v[:, at] = pulled
        z = z_v[:, at]
        product = pulled * ngain_ref[:, at] * (y_v[:, at] * (z * sigmoid(z)))
        for piece in range(lanes // 128):
            sum_v[1] += product[:, piece * 128 : (piece + 1) * 128]
        return carry

    lax.fori_loop(0, groups, pull_group, 0)
    row_of = lambda array: jnp.sum(array.T, axis=0, keepdims=True)
    sum_own[...] = jnp.concatenate(
        [row_of(sum_v[0]), row_of(sum_v[1]), jnp.zeros((6, tokens), F32)], axis=0
    )
    sums_x.start()
    sums_x.wait_recv()
    both = sum_own[...] + sum_came[...]
    scale_row = lax.rsqrt(both[0:1, :] / inner_total + EPS)
    pull_row = both[1:2, :] * (scale_row * scale_row * scale_row) / inner_total
    column_of = lambda array: jnp.broadcast_to(array, (128, tokens)).T
    sum_v[0] = column_of(scale_row)
    sum_v[1] = column_of(pull_row)

    def grad_group(g, carry):
        at = lane_range(g)
        scale, pull = sum_v[0][:, 0:1], sum_v[1][:, 0:1]
        z, y, pulled = z_v[:, at], y_v[:, at], dg_v[:, at]
        sig = sigmoid(z)
        gate = z * sig
        v = y * gate
        unit = v * scale
        gngain_out[:, at] = jnp.sum(pulled * unit, axis=0, keepdims=True)
        gated_out[:, at] = (unit * ngain_ref[:, at]).astype(BF16)
        d_v = pulled * ngain_ref[:, at] * scale - pull * v
        dy_out[:, at] = d_v * gate
        dz_out[:, at] = (d_v * y * sig * (1.0 + z * (1.0 - sig))).astype(BF16)
        return carry

    lax.fori_loop(0, groups, grad_group, 0)
    for gather in gathers:
        gather.sent()
    for copy in (hidden, cotangent, sums_x):
        copy.wait_send()
    for copy in [store_rows, store_s] + store_normt + store_cott:
        copy.wait()


def in_vmem():
    return pl.BlockSpec(memory_space=pltpu.VMEM)


def in_any():
    return pl.BlockSpec(memory_space=pl.ANY)


def forward_all(
    hidden, cot, small, ws, wz, wo, gain, bias, rate, seg_row, conv_x, conv_bc, skip_lanes, norm_gain, width, inner_total, q
):
    half, depth = hidden.shape
    tokens = 2 * half
    shard, inner = ws.shape
    columns = small.shape[1]
    heads = heads_per_step(inner // width)
    lanes = heads * width
    n = (columns - 128) // 2
    blocks = tokens // q
    shape = jax.ShapeDtypeStruct
    sems = pltpu.SemaphoreType.DMA
    weight, rows = (16, shard, inner), (2, half, depth)
    per_head = shape((tokens, 128), F32)
    outs = pl.pallas_call(
        functools.partial(forward_kernel, q, heads, width, inner_total),
        in_specs=[in_vmem()] * 14,
        out_specs=[in_any()] + [in_vmem()] + [in_any()] * 6 + [in_vmem()] * 11,
        out_shape=[
            shape(rows, BF16), shape((16, shard, columns), BF16),
            shape(weight, BF16), shape(weight, BF16), shape(weight, BF16),
            shape((tokens, inner), F32), shape((16, shard, tokens), BF16), shape((16, shard, tokens), BF16),
            per_head, shape((tokens, columns - 128), F32), per_head, per_head, per_head, per_head,
            shape((blocks, n, inner), F32), shape((tokens, inner), F32), shape((tokens, inner), BF16),
            shape((tokens, inner), BF16), shape((1, inner), F32),
        ],
        scratch_shapes=[sems((2, Gather.COPIES))] * 4 + [sems((2, 3)), sems((11,))]
        + [pltpu.VMEM(rows, BF16)] * 2 + [pltpu.VMEM(weight, BF16)] * 3
        + [
            pltpu.VMEM((tokens, inner), F32), pltpu.VMEM((tokens, depth), BF16), pltpu.VMEM((tokens, inner), F32),
            pltpu.VMEM((tokens, inner), F32), pltpu.VMEM((tokens, inner), F32), pltpu.VMEM((2, tokens, 128), F32),
            pltpu.VMEM((8, tokens), F32), pltpu.VMEM((8, tokens), F32),
            pltpu.VMEM((16, shard, tokens), BF16), pltpu.VMEM((16, shard, tokens), BF16), sems((2, 16)),
        ]
        + forward_scratch(tokens, q, n, lanes),
        compiler_params=pltpu.CompilerParams(
            collective_id=0, has_side_effects=True, vmem_limit_bytes=VMEM_LIMIT
        ),
        name="forward_all",
    )(
        hidden, cot, small, ws, wz, wo, gain, bias, rate, seg_row, conv_x, conv_bc, skip_lanes, norm_gain,
    )
    flat = lambda a: a.reshape((-1, a.shape[-1]))
    return [outs[0]] + [flat(a) for a in outs[1:14]] + list(outs[14:])


class Scatter:
    def __init__(self, here, own, away, from_core, from_y, from_z, core_sems, y_sems, z_sems, free):
        self.free, self.core_slots = free, from_core.shape[0]
        self.here, self.own, self.away = here, own, away
        self.from_core, self.from_y, self.from_z = from_core, from_y, from_z
        self.core_sems, self.y_sems, self.z_sems = core_sems, y_sems, z_sems

    def copy(self, src, dst, sems, i, peer):
        return pltpu.make_async_remote_copy(
            src_ref=src, dst_ref=dst, send_sem=sems[0].at[i], recv_sem=sems[1].at[i], device_id=peer,
            device_id_type=MESH,
        )

    def to_core(self, i):
        slot = i % self.away.shape[0]
        return self.copy(
            self.away.at[slot], self.from_core.at[i % self.core_slots], self.core_sems, i, self.here.other_core()
        )

    def across(self, i):
        return self.copy(
            self.own.at[i, pl.ds(0, 4)], self.from_y.at[i], self.y_sems, i, self.here.across_y()
        )

    def up(self, i, k):
        return self.copy(
            self.own.at[i, 4 + k], self.from_z.at[i, k - 1], self.z_sems, i * 6 + k - 1, self.here.at_z(1)
        )

    def down(self, i, k):
        slot = 3 + k if k < 2 else 0
        return self.copy(
            self.own.at[i, 4 + k], self.from_z.at[i, slot], self.z_sems, i * 6 + 3 + k, self.here.at_z(3)
        )

    def start(self, i, left_ref, right, reuse):
        pieces, rows, tokens = left_ref.shape
        half = pieces // 2
        pl.when(reuse)(lambda: self.to_core(jnp.maximum(i - self.away.shape[0], 0)).wait_send())
        make = lambda at: dot(
            left_ref[at : at + half].reshape(half * rows, tokens), right
        ).astype(BF16).reshape(half, rows, right.shape[1])
        self.away[i % self.away.shape[0]] = make(half)
        pl.when(i >= self.core_slots)(lambda: pl.semaphore_wait(self.free, 1))
        self.to_core(i).start()
        self.own[i] = make(0)

    def to_y(self, i):
        self.to_core(i).wait_recv()
        slot = i % self.core_slots
        add = lambda at: (self.own[i, at].astype(F32) + self.from_core[slot, at].astype(F32)).astype(BF16)
        self.own[i, 0:4] = add(slice(0, 4))
        self.across(i).start()
        self.own[i, 4:8] = add(slice(4, 8))

        @pl.when(i + self.core_slots < self.own.shape[0])
        def _():
            pl.semaphore_signal(
                self.free, inc=1, device_id=self.here.other_core(), device_id_type=MESH
            )

    def local_sum(self, i, k):
        return self.own[i, 4 + k].astype(F32) + self.from_y[i, k].astype(F32)

    def hop(self, i, h):
        z = self.here.z
        if h == 0:
            self.across(i).wait_recv()

        @pl.when(z == h)
        def _():
            for k in range(h + 1, 4):
                total = self.local_sum(i, k)
                if h:
                    self.up(i, k).wait_recv()
                    total = total + self.from_z[i, k - 1].astype(F32)
                self.own[i, 4 + k] = total.astype(BF16)
                self.up(i, k).start()

        @pl.when(z == 3 - h)
        def _():
            for k in range(0, 3 - h):
                total = self.local_sum(i, k)
                if h:
                    self.down(i, k).wait_recv()
                    total = total + self.from_z[i, 3 + k if k < 2 else 0].astype(F32)
                self.own[i, 4 + k] = total.astype(BF16)
                self.down(i, k).start()

    def finish(self, i, store):
        for k in range(4):

            @pl.when(self.here.z == k)
            def _(k=k):
                total = self.local_sum(i, k)
                if k > 0:
                    self.up(i, k).wait_recv()
                    total = total + self.from_z[i, k - 1].astype(F32)
                if k < 3:
                    self.down(i, k).wait_recv()
                    total = total + self.from_z[i, 3 + k if k < 2 else 0].astype(F32)
                store(total)

    def sent(self, i, core):
        z = self.here.z
        pl.when(core)(lambda: self.to_core(i).wait_send())
        self.across(i).wait_send()
        for k in (1, 2, 3):
            pl.when(z < k)(lambda k=k: self.up(i, k).wait_send())
        for k in (0, 1, 2):
            pl.when(z > k)(lambda k=k: self.down(i, k).wait_send())


AWAY_SLOTS, CORE_SLOTS = 3, 6


def backward_kernel(
    q, heads, width,
    s_ref, dy_ref, gated_ref, dz_ref, ws_ref, wz_ref, wo_ref, kx_ref, dsk_ref, st_ref,
    bcraw_ref, kbc_ref, la_ref, dt_ref, msk_ref, segr_ref, dtin_ref, rate_ref,
    normt_ref, cott_ref, small_w_ref, rows_ref, scale_ref, gain_ref, gngain_ref, cot_own_ref,
    block_out, grad_in_out, gwo_out, gwz_out, gws_out, gsm_out, sums_out,
    own, away, from_core, from_y, from_z,
    core_send, core_recv, y_send, y_recv, z_send, z_recv, free, x_sems, sum_sems,
    col, proj, x_send, x_came, sum_own, sum_came, ds_v, gk_v, small_v, low_v, gkbc_v, ghead_v,
    bcc, mnegt, cbt, xs, dxs, dtt, gt, la4, lat4, dt4, dla_acc, ddt_acc, dbc_acc,
):
    here = Here()
    step = pl.program_id(0)
    steps = pl.num_programs(0)
    tokens, lanes = s_ref.shape
    depth = col.shape[1]
    half = tokens // 2
    n2 = bcc.shape[1]
    scatter = Scatter(
        here, own, away, from_core, from_y, from_z, (core_send, core_recv), (y_send, y_recv), (z_send, z_recv), free
    )
    chunks = own.shape[0]
    core_sum = send(sum_own.at[0], sum_came.at[0], sum_sems, 0, here.other_core())
    y_sum = send(sum_own.at[1], sum_came.at[1], sum_sems, 1, here.across_y())
    z_sums = [send(sum_own.at[2], sum_came.at[1 + d], sum_sems, 1 + d, here.at_z(d)) for d in (1, 2, 3)]
    x_part = pl.ds(0, 8)
    x_sum = send(sum_own.at[3, x_part], sum_came.at[5, x_part], sum_sems, 5, here.across_x())
    projected = send(x_send.at[0], x_came.at[0], x_sems, 0, here.across_x())
    pulled = send(x_send.at[1], x_came.at[1], x_sems, 1, here.across_x())

    @pl.when(step == 0)
    def _():
        here.greet()

    scatter.start(3 * step, cott_ref, gated_ref[...], step >= AWAY_SLOTS // 3)
    scatter.start(3 * step + 1, normt_ref, dz_ref[...], step >= AWAY_SLOTS // 3)

    @pl.when(step == 0)
    def _():
        bwd_tables(
            q, bcraw_ref, kbc_ref, msk_ref, segr_ref, bcc, mnegt, cbt, dtt, dbc_acc, dla_acc, ddt_acc
        )
        col[...] = jnp.zeros_like(col)
        proj[...] = jnp.zeros_like(proj)

    @pl.when(step > 0)
    def _():
        scatter.to_y(3 * step - 1)

    scatter.to_y(3 * step)

    def three(first_step, act):
        @pl.when(first_step >= 0)
        def _():
            for kind in range(3):
                act(jnp.maximum(first_step, 0) * 3 + kind)

    def between(i):
        if i == 0:
            scatter.to_y(3 * step + 1)
            three(step - 3, lambda c: scatter.hop(c, 1))

    bwd_group(
        q, heads, width, step, s_ref, dy_ref, kx_ref, la_ref, dt_ref, msk_ref, dsk_ref, st_ref, ds_v, gk_v,
        bcc, mnegt, cbt, xs, dxs, dtt, gt, la4, lat4, dt4, dla_acc, ddt_acc, dbc_acc, between,
    )
    scatter.start(3 * step + 2, normt_ref, ds_v[...], step >= AWAY_SLOTS // 3)
    at_lanes = pl.ds(pl.multiple_of(step * lanes, lanes), lanes)
    sum_own[0, 2:8, at_lanes] = gk_v[0:6, :]

    def column_block(j):
        return pl.ds(pl.multiple_of(j * 256, 256), 256)

    def accumulate(j, carry):
        at = column_block(j)
        col[:, at] += dot(dz_ref[...], wz_ref[at, :], NT) + dot(ds_v[...], ws_ref[at, :], NT)
        proj[:, at] += dot(gated_ref[...], wo_ref[at, :], NT)
        return carry

    lax.fori_loop(0, depth // 256, accumulate, 0)
    three(step - 3, lambda c: scatter.hop(c, 2))
    three(step - 2, lambda c: scatter.hop(c, 0))

    @pl.when(step == steps - 1)
    def _():
        chunk = 32

        def by_chunks(act):
            def one(i, carry):
                at = pl.multiple_of(i * chunk, chunk)
                own_at = pl.multiple_of(here.t * half + i * chunk, chunk)
                away_at = pl.multiple_of((1 - here.t) * half + i * chunk, chunk)
                act(pl.ds(at, chunk), pl.ds(own_at, chunk), pl.ds(away_at, chunk))
                return carry

            lax.fori_loop(0, half // chunk, one, 0)

        def pack_projected(rows, own_rows, away_rows):
            x_send[0, rows, :] = proj[away_rows, :].astype(BF16)

        by_chunks(pack_projected)
        projected.start()
        scatter.to_y(3 * steps - 1)
        small_v[:, n2 + 128 :] = jnp.zeros_like(small_v[:, n2 + 128 :])
        bwd_finish(
            q, bcraw_ref, kbc_ref, dt_ref, msk_ref, dtin_ref, rate_ref, small_v, low_v, gkbc_v, ghead_v,
            bcc, dtt, dla_acc, ddt_acc, dbc_acc,
        )
        for i in range(2):
            scatter.start(3 * steps + i, normt_ref, small_v[:, i * lanes : (i + 1) * lanes], steps > 0)

        def small_part(j, carry):
            at = column_block(j)
            col[:, at] += dot(small_v[:, : n2 + 128], small_w_ref[at, :], NT) + dot(
                low_v[...], small_w_ref[at, 0:n2], NT
            )
            return carry

        lax.fori_loop(0, depth // 256, small_part, 0)
        gain = gain_ref[...]

        def norm_back(i, total):
            rows = pl.ds(pl.multiple_of(i * chunk, chunk), chunk)
            side, at = i // (half // chunk), i % (half // chunk)
            inside = pl.ds(pl.multiple_of(at * chunk, chunk), chunk)
            columns = col[rows, :]
            scale = scale_ref[rows, 0:1]
            unit = rows_ref[side, inside, :].astype(F32) * scale
            grad_unit = columns * gain
            col[rows, :] = scale * (
                grad_unit - unit * jnp.mean(grad_unit * unit, axis=1, keepdims=True)
            )
            return total + jnp.sum(columns * unit, axis=0, keepdims=True)

        prenorm = lax.fori_loop(0, tokens // chunk, norm_back, jnp.zeros((1, depth), F32))

        def pack_pulled(rows, own_rows, away_rows):
            x_send[1, rows, :] = col[away_rows, :].astype(BF16)

        by_chunks(pack_pulled)
        pulled.start()
        sum_own[0, 0:1, :] = prenorm
        sum_own[0, 1:2, :] = jnp.zeros((1, depth), F32)
        for r in range(5):
            sum_own[0, 1:2, r * n2 : (r + 1) * n2] = gkbc_v[r : r + 1, :]
        sum_own[0, 8:9, :] = gngain_ref[...]
        sum_own[0, 9:16, :] = jnp.zeros((7, depth), F32)
        sum_own[0, 9:10, 0:128] = ghead_v[0:1, :]
        sum_own[0, 9:10, 128:256] = ghead_v[1:2, :]
        core_sum.start()
        three(steps - 3, lambda c: scatter.hop(c, 1))
        core_sum.wait_recv()
        sum_own[1] = sum_own[0] + sum_came[0]
        y_sum.start()
        for i in range(2):
            scatter.to_y(3 * steps + i)

        def store_at(kind, g):
            out = (gwo_out, gwz_out, gws_out)[kind]
            at = pl.ds(pl.multiple_of(g * lanes, lanes), lanes)

            def store(total):
                out[:, at] = total

            return store

        def finished(g, carry):
            for kind in range(3):
                scatter.finish(g * 3 + kind, store_at(kind, g))
            return carry

        lax.fori_loop(0, steps - 3, finished, 0)
        three(steps - 3, lambda c: scatter.hop(c, 2))
        three(steps - 2, lambda c: scatter.hop(c, 0))
        three(steps - 2, lambda c: scatter.hop(c, 1))
        finished(steps - 3, 0)
        three(steps - 2, lambda c: scatter.hop(c, 2))
        three(steps - 1, lambda c: scatter.hop(c, 0))
        y_sum.wait_recv()
        sum_own[2] = sum_own[1] + sum_came[1]
        for copy in z_sums:
            copy.start()
        three(steps - 1, lambda c: scatter.hop(c, 1))
        finished(steps - 2, 0)
        projected.wait_recv()

        def put_block_out(rows, own_rows, away_rows):
            block_out[rows, :] = (
                rows_ref[here.t, rows, :].astype(F32) + proj[own_rows, :] + x_came[0, rows, :].astype(F32)
            ).astype(BF16)

        by_chunks(put_block_out)
        for i in range(2):
            scatter.hop(3 * steps + i, 0)
        three(steps - 1, lambda c: scatter.hop(c, 2))
        for copy in z_sums:
            copy.wait_recv()
        sum_own[3] = sum_own[2] + sum_came[2] + sum_came[3] + sum_came[4]
        x_sum.start()
        for i in range(2):
            scatter.hop(3 * steps + i, 1)
        finished(steps - 1, 0)
        for i in range(2):
            scatter.hop(3 * steps + i, 2)
        pulled.wait_recv()

        def put_grad_in(rows, own_rows, away_rows):
            grad_in_out[rows, :] = (
                cot_own_ref[rows, :].astype(F32) + col[own_rows, :] + x_came[1, rows, :].astype(F32)
            ).astype(BF16)

        by_chunks(put_grad_in)
        x_sum.wait_recv()
        sums_out[...] = sum_own[3]
        sums_out[0:2, :] = sum_own[3, 0:2, :] + sum_came[5, 0:2, :]
        for i in range(2):

            def store(total, i=i):
                gsm_out[:, i * lanes : (i + 1) * lanes] = total

            scatter.finish(3 * steps + i, store)

        def all_sent(i, carry):
            scatter.sent(i, i >= chunks - AWAY_SLOTS)
            return carry

        lax.fori_loop(0, chunks, all_sent, 0)
        for copy in [core_sum, y_sum, x_sum, projected, pulled] + z_sums:
            copy.wait_send()


def backward_all(
    s, dy, gated, dz, w_s, w_z, w_out_t, conv_x, skip_lanes, states, prep, conv_bc,
    normt, cott, small, rows, scale, gain, gngain, cot_own, width, q,
):
    tokens, inner = s.shape
    depth = w_s.shape[0]
    half = tokens // 2
    heads = heads_per_step(inner // width)
    lanes = heads * width
    groups = inner // lanes
    n2 = prep["bcraw"].shape[1]
    n, blocks, shard = n2 // 2, tokens // q, depth // 16
    chunks = 3 * groups + 2
    shape = jax.ShapeDtypeStruct
    sems = pltpu.SemaphoreType.DMA
    once = lambda array: pl.BlockSpec(
        array.shape, lambda i: (0,) * array.ndim, pipeline_mode=pl.Buffered(1)
    )
    constants = [
        prep["bcraw"], conv_bc, prep["la"], prep["dt"], prep["masks"], prep["seg_row"], prep["dt_in"], prep["rate"],
        normt, cott, small, rows, scale, gain, gngain, cot_own,
    ]
    out_shape = [
        shape((half, depth), BF16), shape((half, depth), BF16), shape((shard, inner), F32),
        shape((shard, inner), F32), shape((shard, inner), F32), shape((shard, 2 * lanes), F32), shape((16, depth), F32),
    ]
    pieces = lambda count, per: pltpu.VMEM((count, per, shard, lanes), BF16)
    return pl.pallas_call(
        functools.partial(backward_kernel, q, heads, width),
        grid=(groups,),
        in_specs=[lane_block(tokens, lanes)] * 4 + [lane_block(depth, lanes)] * 3
        + [lane_block(5, lanes), lane_block(1, lanes), pl.BlockSpec((blocks, n, lanes), lambda i: (0, 0, i))]
        + [once(array) for array in constants],
        out_specs=[once(array) for array in out_shape],
        out_shape=out_shape,
        scratch_shapes=[pieces(chunks, 8), pieces(AWAY_SLOTS, 8), pieces(CORE_SLOTS, 8), pieces(chunks, 4), pieces(chunks, 5)]
        + [sems((chunks,))] * 4 + [sems((6 * chunks,))] * 2 + [pltpu.SemaphoreType.REGULAR, sems((2, 2)), sems((2, 6))]
        + [
            pltpu.VMEM((tokens, depth), F32), pltpu.VMEM((tokens, depth), F32), pltpu.VMEM((2, half, depth), BF16),
            pltpu.VMEM((2, half, depth), BF16), pltpu.VMEM((4, 16, depth), F32), pltpu.VMEM((6, 16, depth), F32),
            pltpu.VMEM((tokens, lanes), BF16), pltpu.VMEM((8, lanes), F32), pltpu.VMEM((tokens, 2 * lanes), BF16),
            pltpu.VMEM((tokens, n2), BF16), pltpu.VMEM((8, n2), F32), pltpu.VMEM((8, 128), F32),
        ]
        + backward_scratch(tokens, q, n, lanes),
        compiler_params=pltpu.CompilerParams(
            dimension_semantics=("arbitrary",), collective_id=1, has_side_effects=True,
            vmem_limit_bytes=67043328,
        ),
        name="backward_all",
    )(s, dy, gated, dz, w_s, w_z, w_out_t, conv_x, skip_lanes, states, *constants)


def lanes_of(per_head):
    return jnp.pad(per_head, [(0, 0)] * (per_head.ndim - 1) + [(0, 128 - per_head.shape[-1])])


def prepare_plain(normed, small, bias, rate, flat_ids, q):
    tokens = normed.shape[0]
    blocks = tokens // q
    proj = dot(normed, small)
    bc_width = small.shape[1] - 128
    dt_in = proj[:, bc_width:] + bias
    dt = jax.nn.softplus(dt_in)
    lower = jnp.where(jnp.arange(q)[:, None] >= jnp.arange(q)[None, :], 1.0, 0.0)
    la = jnp.einsum("ij,bjh->bih", lower, (dt * rate).reshape(blocks, q, 128), precision=HIGHEST)
    shifted = lambda l: jnp.concatenate([jnp.full((l,), -1, jnp.int32), flat_ids[:-l]])
    by_block = flat_ids.reshape(blocks, q)
    before = jnp.concatenate([jnp.full((1,), -1, jnp.int32), by_block[:-1, -1]])
    carried = (by_block == before[:, None]).reshape(-1)
    run_last = (by_block == by_block[:, -1:]).reshape(-1)
    masks = [flat_ids == shifted(1), flat_ids == shifted(2), flat_ids == shifted(3), carried, run_last, flat_ids]
    return proj[:, :bc_width], dt_in, dt, la.reshape(tokens, 128), lanes_of(jnp.stack(masks, axis=1).astype(F32))


def body(
    dp,
    tp,
    hidden_in,
    prenorm_gain,
    w_zx,
    w_dt,
    w_bc,
    conv_x,
    conv_bc,
    dt_bias,
    a_log,
    d_skip,
    norm_gain,
    w_out,
    seg_ids,
    grad_out,
):
    q = BLOCK_LEN
    staged = dp == 16 and tp == 2
    inner = w_out.shape[0]
    head_count = dt_bias.shape[0]
    width = inner // head_count
    bc_width = w_bc.shape[1]
    shard = w_bc.shape[0]
    depth = hidden_in.shape[1]
    inner_total = inner * tp
    tensor = lax.axis_index("tensor")

    bias = lanes_of(dt_bias)[None, :]
    rate = lanes_of(-jnp.exp(a_log))[None, :]
    small_shard = jnp.concatenate([w_bc, lanes_of(w_dt)], axis=1)
    flat_ids = (seg_ids + seg_ids.shape[1] * lax.broadcasted_iota(jnp.int32, seg_ids.shape, 0)).reshape(-1)
    seg_row = flat_ids.astype(F32)[None, :]
    skip_lanes = jnp.repeat(d_skip, width)[None, :]
    prep = dict(rate=rate, seg_row=seg_row)

    if staged:
        (
            full_rows, small, w_s, w_z, w_out_t, s, normt, cott, scale_in,
            prep["bcraw"], prep["dt_in"], prep["dt"], prep["la"], prep["masks"],
            states, d_y, gated, d_z, grad_norm_gain,
        ) = forward_all(
            hidden_in, grad_out, small_shard, w_zx[:, 1, :], w_zx[:, 0, :], w_out.T,
            prenorm_gain[None, :], bias, rate, seg_row, conv_x, conv_bc, skip_lanes, norm_gain[None, :],
            width, inner_total, q,
        )
        split = lambda array: array.reshape(16, shard, array.shape[1])
        block_out, grad_in, grad_w_out, grad_w_z, grad_w_s, grad_small, sums = backward_all(
            s, d_y, gated, d_z, w_s, w_z, w_out_t, conv_x, skip_lanes, states, prep, conv_bc,
            split(normt), split(cott), small, full_rows, scale_in, prenorm_gain[None, :], grad_norm_gain, grad_out,
            width, q,
        )
        half_of = lambda value: lax.dynamic_slice_in_dim(
            value, tensor * (value.shape[-1] // 2), value.shape[-1] // 2, value.ndim - 1
        )
        bc_sum = grad_small[:, :bc_width]
        bc_half = bc_width // 2
        away_bc = lax.dynamic_slice_in_dim(bc_sum, (1 - tensor) * bc_half, bc_half, 1)
        return (
            block_out,
            grad_in,
            half_of(sums[0]),
            jnp.stack([grad_w_z, grad_w_s], axis=1),
            grad_small[:, bc_width : bc_width + head_count],
            half_of(bc_sum) + lax.ppermute(away_bc, "tensor", [(0, 1), (1, 0)]),
            sums[2:7],
            half_of(sums[1, : 5 * bc_width].reshape(5, bc_width)),
            sums[9, :head_count],
            sums[9, 128 : 128 + head_count],
            jnp.sum(sums[7].reshape(head_count, width), axis=1),
            sums[8],
            grad_w_out.T,
        )
    else:
        over_dp = lambda value: lax.all_gather(value, "dp", axis=0, tiled=True)
        small = over_dp(small_shard)
        w_s, w_z, w_out_t = over_dp(w_zx[:, 1, :]), over_dp(w_zx[:, 0, :]), over_dp(w_out.T)
        rows_float = lax.all_gather(hidden_in, "tensor", axis=0, tiled=True).astype(F32)
        cot_rows = lax.all_gather(grad_out, "tensor", axis=0, tiled=True)
        scale_in = lax.rsqrt(jnp.mean(rows_float * rows_float, axis=1, keepdims=True) + EPS)
        normed = (rows_float * scale_in * prenorm_gain).astype(BF16)
        prep["bcraw"], prep["dt_in"], prep["dt"], prep["la"], prep["masks"] = prepare_plain(
            normed, small, bias, rate, flat_ids, q
        )
        s, y, states = scan_forward(normed, w_s, prep, conv_x, conv_bc, skip_lanes, width, q)
        z = dot(normed, w_z)
        gate_sig = sigmoid(z)
        gate = z * gate_sig
        v = y * gate
        grad_gated = dot(cot_rows, w_out_t)
        scaled_grad = grad_gated * norm_gain
        sums = jnp.stack([jnp.sum(v * v, axis=1), jnp.sum(scaled_grad * v, axis=1)])
        sums = lax.psum(sums, "tensor")
        scale_out = lax.rsqrt(sums[0] / inner_total + EPS)[:, None]
        pull = sums[1][:, None] * scale_out**3 / inner_total
        gated = (v * scale_out * norm_gain).astype(BF16)
        grad_norm_gain = jnp.sum(grad_gated * v * scale_out, axis=0)
        d_v = scaled_grad * scale_out - pull * v
        d_y = d_v * gate
        d_z = (d_v * y * gate_sig * (1.0 + z * (1.0 - gate_sig))).astype(BF16)
    tokens = normed.shape[0]

    d_s, grad_taps, d_small, low_bc, grad_taps_bc, grad_heads = scan_backward(
        s, d_y, prep, conv_x, conv_bc, skip_lanes, states, width, q
    )
    grad_d_skip = jnp.sum(grad_taps[5].reshape(head_count, width), axis=1)

    own_rows = tokens // tp
    rows_of = lambda array, i: lax.dynamic_slice_in_dim(array, i * own_rows, own_rows, 0)
    project = lambda i: dot(rows_of(gated, i), w_out_t, NT)
    prenorm_terms = []

    def grad_rows(i):
        columns = (
            dot(rows_of(d_z, i), w_z, NT)
            + dot(rows_of(d_s, i), w_s, NT)
            + dot(rows_of(d_small, i), small, NT)
            + dot(rows_of(low_bc, i), small[:, :bc_width], NT)
        )
        unit = rows_of(rows_float, i) * rows_of(scale_in, i)
        prenorm_terms.append(jnp.sum(columns * unit, axis=0))
        grad_unit = columns * prenorm_gain
        return rows_of(scale_in, i) * (
            grad_unit - unit * jnp.mean(grad_unit * unit, axis=1, keepdims=True)
        )

    products = [
        dot(cot_rows, gated, TN),
        dot(normed, d_z, TN),
        dot(normed, jnp.concatenate([d_s, d_small], axis=1), TN),
    ]
    every = lambda make: jnp.concatenate([make(i) for i in range(tp)], axis=0)
    onto = lambda value, dim: lax.psum_scatter(value, "tensor", scatter_dimension=dim, tiled=True)
    projected, own_grad = onto(every(project), 0), onto(every(grad_rows), 0)

    pieces = [
        sum(prenorm_terms),
        grad_taps_bc[:5].reshape(-1),
        grad_taps[:5].reshape(-1),
        grad_norm_gain,
        grad_heads[0],
        grad_heads[1],
        lanes_of(grad_d_skip),
    ]
    gap = -(pieces[0].shape[0] + pieces[1].shape[0]) % 1024
    pieces.insert(2, jnp.zeros((gap,), F32))
    x_rows = sum(piece.shape[0] for piece in pieces[:3]) // 128
    flat = jnp.concatenate(pieces)
    flat = jnp.pad(flat, (0, -flat.shape[0] % 1024)).reshape(-1, 128)
    half_of = lambda value: lax.dynamic_slice_in_dim(
        value, tensor * (value.shape[-1] // tp), value.shape[-1] // tp, value.ndim - 1
    )
    grad_w_out, grad_w_z, grad_last = [
        lax.psum_scatter(p, "dp", scatter_dimension=0, tiled=True) for p in products
    ]
    grad_w_bc = onto(grad_last[:, inner : inner + bc_width], 1)
    flat = lax.psum(flat, "dp")
    flat = jnp.concatenate([lax.psum(flat[:x_rows], "tensor"), flat[x_rows:]], axis=0)
    block_out = (hidden_in.astype(F32) + projected).astype(BF16)
    grad_in = (grad_out.astype(F32) + own_grad).astype(BF16)
    grad_w_zx = jnp.stack([grad_w_z, grad_last[:, :inner]], axis=1)
    grad_w_dt = grad_last[:, inner + bc_width : inner + bc_width + head_count]

    flat = flat.reshape(-1)
    at, cut_out = 0, []
    for piece in pieces:
        cut_out.append(flat[at : at + piece.shape[0]])
        at += piece.shape[0]
    return (
        block_out,
        grad_in,
        half_of(cut_out[0]),
        grad_w_zx,
        grad_w_dt,
        grad_w_bc,
        cut_out[3].reshape(5, inner),
        half_of(cut_out[1].reshape(5, bc_width)),
        cut_out[5][:head_count],
        cut_out[6][:head_count],
        cut_out[7][:head_count],
        cut_out[4],
        grad_w_out.T,
    )


def solution(mesh):
    in_specs = (
        P(("dp", "tensor"), None),
        P(),
        P("dp", None, "tensor"),
        P("dp", "tensor"),
        P("dp", None),
        P(None, "tensor"),
        P(),
        P("tensor"),
        P("tensor"),
        P("tensor"),
        P("tensor"),
        P("tensor", "dp"),
        P("dp", None),
        P(("dp", "tensor"), None),
    )
    out_specs = (
        P(("dp", "tensor"), None),
        P(("dp", "tensor"), None),
        P("tensor"),
        P("dp", None, "tensor"),
        P("dp", "tensor"),
        P("dp", "tensor"),
        P(None, "tensor"),
        P(None, "tensor"),
        P("tensor"),
        P("tensor"),
        P("tensor"),
        P("tensor"),
        P("tensor", "dp"),
    )
    return jax.shard_map(
        functools.partial(body, mesh.shape["dp"], mesh.shape["tensor"]),
        mesh=mesh,
        in_specs=in_specs,
        out_specs=out_specs,
        check_vma=False,
    )
```

```python
import functools

import jax
import jax.numpy as jnp
from jax import lax
from jax.experimental import pallas as pl
from jax.experimental.pallas import tpu as pltpu
from jax.sharding import PartitionSpec as P

BLOCK_LEN = 256
EPS = 1e-05
NEG = -1e30
F32 = jnp.float32
BF16 = jnp.bfloat16
HIGHEST = lax.Precision.HIGHEST
VMEM_LIMIT = 60 * 1024 * 1024


def dot(a, b, dims=((1,), (0,)), precision=None):
    return lax.dot_general(a, b, (dims, ((), ())), preferred_element_type=F32, precision=precision)


NN, NT, TN = ((1,), (0,)), ((1,), (1,)), ((0,), (0,))


def sigmoid(w):
    return 1.0 / (1.0 + jnp.exp(-w))


def conv_of(signal, taps, masks):
    out = taps[4:5, :] + taps[3:4, :] * signal
    for back in range(1, 4):
        out = out + taps[3 - back : 4 - back, :] * (
            pltpu.roll(signal, back, 0) * masks[:, back - 1 : back]
        )
    return out


def conv_back(grad, signal, taps, masks):
    rows = signal.shape[0]
    grad_signal = taps[3:4, :] * grad
    tap_rows = [None] * 5
    tap_rows[4] = jnp.sum(grad, axis=0, keepdims=True)
    tap_rows[3] = jnp.sum(grad * signal, axis=0, keepdims=True)
    for back in range(1, 4):
        kept = grad * masks[:, back - 1 : back]
        tap_rows[3 - back] = jnp.sum(kept * pltpu.roll(signal, back, 0), axis=0, keepdims=True)
        grad_signal = grad_signal + taps[3 - back : 4 - back, :] * pltpu.roll(kept, rows - back, 0)
    return grad_signal, tap_rows


def expand(columns, width):
    rows, heads = columns.shape
    lane = lax.broadcasted_iota(jnp.int32, (rows, 2 * width), 1)
    pieces = [
        jnp.where(lane < width, columns[:, h : h + 1], columns[:, h + 1 : h + 2])
        for h in range(0, heads, 2)
    ]
    return pieces[0] if len(pieces) == 1 else jnp.concatenate(pieces, axis=1)


def block_rows(block, size):
    return pl.ds(pl.multiple_of(block * size, size), size)


def head_lanes(array, step, heads):
    return pltpu.roll(array, lax.rem(128 - step * heads, 128), 1)


def block_tables(q, bcraw_ref, kbc_ref, msk_ref, segr_ref, bcc, mneg, cb):
    n = bcc.shape[1] // 2
    c = conv_of(bcraw_ref[...], kbc_ref[...], msk_ref[...])
    bcc[...] = c * sigmoid(c)
    later = lax.broadcasted_iota(jnp.int32, (q, q), 0) >= lax.broadcasted_iota(jnp.int32, (q, q), 1)

    def prepare(b, carry):
        rows = block_rows(b, q)
        same = msk_ref[rows, 5:6] == segr_ref[:, rows].astype(F32)
        mneg[rows, :] = jnp.where(later & same, 0.0, NEG)
        cb[rows, :] = dot(bcc[rows, n:], bcc[rows, :n], NT, HIGHEST)
        return carry

    lax.fori_loop(0, bcc.shape[0] // q, prepare, 0)


def fwd_group(
    q, heads, width, step, at, s, taps, skip, la_ref, dt_ref, msk_ref, s_ref, y_ref, st_ref,
    bcc, mneg, cb, xs, state, la4, lat4, dt4,
):
    tokens = s.shape[0]
    blocks = tokens // q
    n = bcc.shape[1] // 2
    lanes = heads * width
    la_here = head_lanes(la_ref[...], step, heads)
    la4[...] = la_here
    lat4[...] = la_here.T[0:8, :]
    dt4[...] = head_lanes(dt_ref[...], step, heads)
    s_ref[:, at] = s
    c = conv_of(s, taps, msk_ref[...])
    xs[...] = c * sigmoid(c)
    state[...] = jnp.zeros_like(state)
    lane_head = lax.broadcasted_iota(jnp.int32, (q, lanes), 1) // width

    def one_block(b, carry):
        rows = block_rows(b, q)
        x = xs[rows, :]
        la = la4[rows, 0:heads]
        u = x * expand(dt4[rows, 0:heads], width)
        ub = u.astype(BF16)
        enter = expand(jnp.exp(la) * msk_ref[rows, 3:4], width)
        last = expand(jnp.exp(la[q - 1 : q, :] - la) * msk_ref[rows, 4:5], width)
        st = state[...]
        st_ref[b, :, at] = st
        base = mneg[rows, :]
        cb_b = cb[rows, :]
        weights, values = [], []
        for h in range(heads):
            decay = jnp.exp(la[:, h : h + 1] - lat4[h : h + 1, rows] + base)
            weights.append((decay * cb_b).astype(BF16))
            values.append(jnp.where(lane_head == h, ub, jnp.zeros_like(ub)))
        local = dot(jnp.concatenate(weights, axis=1), jnp.concatenate(values, axis=0))
        carried = dot(bcc[rows, n:].astype(BF16), st.astype(BF16))
        y_ref[rows, at] = local + carried * enter + skip * x
        state[...] = st * enter[q - 1 : q, :] + dot(
            bcc[rows, :n].astype(BF16), (u * last).astype(BF16), TN
        )
        return carry

    lax.fori_loop(0, blocks, one_block, 0, unroll=blocks <= 2)


def fwd_kernel(
    q, heads, width,
    nm_ref, w_ref, bcraw_ref, kx_ref, kbc_ref, la_ref, dt_ref, msk_ref, segr_ref, dsk_ref,
    s_ref, y_ref, st_ref,
    bcc, mneg, cb, *scratch,
):
    step = pl.program_id(0)

    @pl.when(step == 0)
    def _():
        block_tables(q, bcraw_ref, kbc_ref, msk_ref, segr_ref, bcc, mneg, cb)

    s = dot(nm_ref[...], w_ref[...])
    fwd_group(
        q, heads, width, step, slice(None), s, kx_ref[...], dsk_ref[...], la_ref, dt_ref, msk_ref,
        s_ref, y_ref, st_ref, bcc, mneg, cb, *scratch,
    )


def bwd_tables(q, bcraw_ref, kbc_ref, msk_ref, segr_ref, bcc, mnegt, cbt, *zeroed):
    n = bcc.shape[1] // 2
    c = conv_of(bcraw_ref[...], kbc_ref[...], msk_ref[...])
    bcc[...] = c * sigmoid(c)
    for ref in zeroed:
        ref[...] = jnp.zeros_like(ref)
    earlier = lax.broadcasted_iota(jnp.int32, (q, q), 0) <= lax.broadcasted_iota(jnp.int32, (q, q), 1)

    def prepare(b, carry):
        rows = block_rows(b, q)
        same = msk_ref[rows, 5:6] == segr_ref[:, rows].astype(F32)
        mnegt[rows, :] = jnp.where(earlier & same, 0.0, NEG)
        cbt[rows, :] = dot(bcc[rows, :n], bcc[rows, n:], NT, HIGHEST)
        return carry

    lax.fori_loop(0, bcc.shape[0] // q, prepare, 0)


def bwd_group(
    q, heads, width, step,
    s_ref, dy_ref, kx_ref, la_ref, dt_ref, msk_ref, dsk_ref, st_ref, ds_ref, gk_ref,
    bcc, mnegt, cbt, xs, dxs, dtt, gt, la4, lat4, dt4, dla_acc, ddt_acc, dbc_acc,
    between=None,
):
    tokens = s_ref.shape[0]
    blocks = tokens // q
    n = bcc.shape[1] // 2
    lanes = heads * width
    la_here = head_lanes(la_ref[...], step, heads)
    la4[...] = la_here
    lat4[...] = la_here.T[0:8, :]
    dt4[...] = head_lanes(dt_ref[...], step, heads)
    c = conv_of(s_ref[...], kx_ref[...], msk_ref[...])
    xs[...] = c * sigmoid(c)
    gt[...] = jnp.zeros_like(gt)
    lane_head = lax.broadcasted_iota(jnp.int32, (q, lanes), 1) // width
    pick = jnp.where(
        lax.broadcasted_iota(jnp.int32, (8, lanes), 1) // width
        == lax.broadcasted_iota(jnp.int32, (8, lanes), 0),
        1.0,
        0.0,
    )
    token_lane = lax.broadcasted_iota(jnp.int32, (1, q), 1)
    col_lane = lax.broadcasted_iota(jnp.int32, (q, 128), 1)

    def one_block(i, carry):
        b = blocks - 1 - i
        rows = block_rows(b, q)
        x = xs[rows, :]
        dy = dy_ref[rows, :]
        la = la4[rows, 0:heads]
        dtx = expand(dt4[rows, 0:heads], width)
        u = x * dtx
        ub, dyb = u.astype(BF16), dy.astype(BF16)
        enter = expand(jnp.exp(la) * msk_ref[rows, 3:4], width)
        last = expand(jnp.exp(la[q - 1 : q, :] - la) * msk_ref[rows, 4:5], width)
        base = mnegt[rows, :]
        cb_b = cbt[rows, :]
        weights, values, row_sums = [], [], []
        d_cb = jnp.zeros((q, q), F32)
        col_sums = jnp.zeros((q, 128), F32)
        for h in range(heads):
            own = lane_head == h
            decay = jnp.exp(lat4[h : h + 1, rows] - la[:, h : h + 1] + base)
            dyh = jnp.where(own, dyb, jnp.zeros_like(dyb))
            pair = dot(ub, dyh, NT)
            weight = decay * cb_b
            d_cb = d_cb + decay * pair
            both = weight * pair
            row_sums.append(jnp.sum(both, axis=0, keepdims=True))
            col_sums = jnp.where(col_lane == h, jnp.sum(both, axis=1, keepdims=True), col_sums)
            weights.append(weight.astype(BF16))
            values.append(dyh)
        dtt[rows, :] += d_cb
        g = gt[...]
        gb16 = g.astype(BF16)
        st = st_ref[b]
        stb = st.astype(BF16)
        c16 = bcc[rows, n:].astype(BF16)
        b16 = bcc[rows, :n].astype(BF16)
        gb = dot(b16, gb16) * last
        du = dot(jnp.concatenate(weights, axis=1), jnp.concatenate(values, axis=0)) + gb
        dye = (dy * enter).astype(BF16)
        from_state = dot(c16, stb) * enter
        dbc_acc[rows, n:] += dot(dye, stb, NT)
        dbc_acc[rows, :n] += dot((u * last).astype(BF16), gb16, NT)
        ug = u * gb
        dla = dot(pick, dy * from_state - ug, NT, HIGHEST)
        ddt = dot(pick, x * du, NT, HIGHEST)
        tail = jnp.sum(ug, axis=0, keepdims=True) + enter[q - 1 : q, :] * jnp.sum(
            g * st, axis=0, keepdims=True
        )
        la_rows = []
        for h in range(heads):
            end = jnp.sum(jnp.where(lane_head[0:1, :] == h, tail, 0.0), axis=1, keepdims=True)
            la_rows.append(
                row_sums[h] + dla[h : h + 1, :] + jnp.where(token_lane == q - 1, end, 0.0)
            )
        dt_rows = [ddt[h : h + 1, :] for h in range(heads)]
        rest = jnp.zeros((128 - 2 * heads, q), F32)
        columns = jnp.concatenate(la_rows + dt_rows + [rest], axis=0).T
        la_part = jnp.where(col_lane < heads, columns, 0.0) - col_sums
        dt_part = jnp.where(col_lane >= heads, columns, 0.0)
        dla_acc[rows, :] += pltpu.roll(la_part, step * heads, 1)
        ddt_acc[rows, :] += pltpu.roll(dt_part, lax.rem(128 + (step - 1) * heads, 128), 1)
        gt[...] = g * enter[q - 1 : q, :] + dot(c16, dye, TN)
        dxs[rows, :] = dtx * du + dsk_ref[...] * dy
        return carry

    if between is None:
        lax.fori_loop(0, blocks, one_block, 0, unroll=blocks <= 2)
    else:
        for i in range(blocks):
            one_block(i, 0)
            between(i)

    s = s_ref[...]
    taps = kx_ref[...]
    masks = msk_ref[...]
    c = conv_of(s, taps, masks)
    sig = sigmoid(c)
    grad = dxs[...] * sig * (1.0 + c * (1.0 - sig))
    d_s, tap_rows = conv_back(grad, s, taps, masks)
    ds_ref[...] = d_s.astype(BF16)
    skip_row = jnp.sum(dy_ref[...] * xs[...], axis=0, keepdims=True)
    gk_ref[...] = jnp.concatenate(
        tap_rows + [skip_row, jnp.zeros_like(skip_row), jnp.zeros_like(skip_row)], axis=0
    )


def bwd_finish(
    q, bcraw_ref, kbc_ref, dt_ref, msk_ref, dtin_ref, rate_ref, small_ref, low_ref, gkbc_ref, ghead_ref,
    bcc, dtt, dla_acc, ddt_acc, dbc_acc,
):
    n = bcc.shape[1] // 2
    upper = jnp.where(
        lax.broadcasted_iota(jnp.int32, (q, q), 0) <= lax.broadcasted_iota(jnp.int32, (q, q), 1), 1.0, 0.0
    )

    def finish(b, carry):
        rows = block_rows(b, q)
        d_cb = dtt[rows, :]
        dbc_acc[rows, :n] += dot(d_cb, bcc[rows, n:], NN, HIGHEST)
        dbc_acc[rows, n:] += dot(d_cb, bcc[rows, :n], TN, HIGHEST)
        dla_acc[rows, :] = dot(upper, dla_acc[rows, :], NN, HIGHEST)
        return carry

    lax.fori_loop(0, bcc.shape[0] // q, finish, 0)
    rate = rate_ref[...]
    d_exponent = dla_acc[...]
    d_raw = (ddt_acc[...] + rate * d_exponent) * sigmoid(dtin_ref[...])
    d_rate = rate * jnp.sum(dt_ref[...] * d_exponent, axis=0, keepdims=True)
    d_bias = jnp.sum(d_raw, axis=0, keepdims=True)
    ghead_ref[...] = jnp.concatenate([d_bias, d_rate, jnp.zeros((6, 128), F32)], axis=0)
    raw = bcraw_ref[...]
    taps = kbc_ref[...]
    masks = msk_ref[...]
    c = conv_of(raw, taps, masks)
    sig = sigmoid(c)
    grad = dbc_acc[...] * sig * (1.0 + c * (1.0 - sig))
    d_bc, rows_bc = conv_back(grad, raw, taps, masks)
    high = d_bc.astype(BF16)
    small_ref[:, : 2 * n] = high
    small_ref[:, 2 * n : 2 * n + 128] = d_raw.astype(BF16)
    low_ref[...] = (d_bc - high.astype(F32)).astype(BF16)
    zero_row = jnp.zeros_like(rows_bc[0])
    gkbc_ref[...] = jnp.concatenate(rows_bc + [zero_row] * 3, axis=0)


def bwd_kernel(
    q, heads, width,
    s_ref, dy_ref, bcraw_ref, kx_ref, kbc_ref, la_ref, dt_ref, msk_ref, segr_ref, dsk_ref, st_ref, dtin_ref, rate_ref,
    ds_ref, gk_ref, small_ref, low_ref, gkbc_ref, ghead_ref,
    bcc, mnegt, cbt, xs, dxs, dtt, gt, la4, lat4, dt4, dla_acc, ddt_acc, dbc_acc,
):
    step = pl.program_id(0)

    @pl.when(step == 0)
    def _():
        bwd_tables(
            q, bcraw_ref, kbc_ref, msk_ref, segr_ref, bcc, mnegt, cbt, dtt, dbc_acc, dla_acc, ddt_acc
        )

    bwd_group(
        q, heads, width, step, s_ref, dy_ref, kx_ref, la_ref, dt_ref, msk_ref, dsk_ref, st_ref, ds_ref, gk_ref,
        bcc, mnegt, cbt, xs, dxs, dtt, gt, la4, lat4, dt4, dla_acc, ddt_acc, dbc_acc,
    )

    @pl.when(step == pl.num_programs(0) - 1)
    def _():
        bwd_finish(
            q, bcraw_ref, kbc_ref, dt_ref, msk_ref, dtin_ref, rate_ref, small_ref, low_ref, gkbc_ref, ghead_ref,
            bcc, dtt, dla_acc, ddt_acc, dbc_acc,
        )


def full(shape):
    return pl.BlockSpec(shape, lambda i: (0,) * len(shape))


def lane_block(rows, lanes):
    return pl.BlockSpec((rows, lanes), lambda i: (0, i))


def heads_per_step(head_count):
    return 4 if head_count % 4 == 0 else 2


def forward_scratch(tokens, q, n, lanes):
    return [
        pltpu.VMEM((tokens, 2 * n), F32), pltpu.VMEM((tokens, q), F32), pltpu.VMEM((tokens, q), F32),
        pltpu.VMEM((tokens, lanes), F32), pltpu.VMEM((n, lanes), F32), pltpu.VMEM((tokens, 128), F32),
        pltpu.VMEM((8, tokens), F32), pltpu.VMEM((tokens, 128), F32),
    ]


def scan_forward(normed, w_s, prep, conv_x, conv_bc, skip_lanes, width, q):
    bcraw, la, dt, masks, seg_row = (prep[k] for k in ("bcraw", "la", "dt", "masks", "seg_row"))
    tokens, depth = normed.shape
    inner = w_s.shape[1]
    head_count = inner // width
    heads = heads_per_step(head_count)
    lanes = heads * width
    n = bcraw.shape[1] // 2
    blocks = tokens // q
    return pl.pallas_call(
        functools.partial(fwd_kernel, q, heads, width),
        grid=(head_count // heads,),
        in_specs=[
            full((tokens, depth)), lane_block(depth, lanes), full((tokens, 2 * n)), lane_block(5, lanes),
            full((5, 2 * n)), full((tokens, 128)), full((tokens, 128)), full((tokens, 128)),
            full((1, tokens)), lane_block(1, lanes),
        ],
        out_specs=[
            lane_block(tokens, lanes), lane_block(tokens, lanes),
            pl.BlockSpec((blocks, n, lanes), lambda i: (0, 0, i)),
        ],
        out_shape=[
            jax.ShapeDtypeStruct((tokens, inner), F32), jax.ShapeDtypeStruct((tokens, inner), F32),
            jax.ShapeDtypeStruct((blocks, n, inner), F32),
        ],
        scratch_shapes=forward_scratch(tokens, q, n, lanes),
        compiler_params=pltpu.CompilerParams(
            dimension_semantics=("arbitrary",), vmem_limit_bytes=VMEM_LIMIT
        ),
        cost_estimate=pl.CostEstimate(
            flops=2 * tokens * inner * (depth + q + 4 * n),
            bytes_accessed=2 * (depth * inner + tokens * depth) + 8 * tokens * inner,
            transcendentals=tokens * q * head_count,
        ),
        name="scan_forward",
    )(normed, w_s, bcraw, conv_x, conv_bc, la, dt, masks, seg_row, skip_lanes)


def backward_scratch(tokens, q, n, lanes):
    return [
        pltpu.VMEM((tokens, 2 * n), F32), pltpu.VMEM((tokens, q), F32), pltpu.VMEM((tokens, q), F32),
        pltpu.VMEM((tokens, lanes), F32), pltpu.VMEM((tokens, lanes), F32), pltpu.VMEM((tokens, q), F32),
        pltpu.VMEM((n, lanes), F32), pltpu.VMEM((tokens, 128), F32), pltpu.VMEM((8, tokens), F32),
        pltpu.VMEM((tokens, 128), F32), pltpu.VMEM((tokens, 128), F32), pltpu.VMEM((tokens, 128), F32),
        pltpu.VMEM((tokens, 2 * n), F32),
    ]


def scan_backward(s, dy, prep, conv_x, conv_bc, skip_lanes, states, width, q):
    bcraw, la, dt, masks, seg_row = (prep[k] for k in ("bcraw", "la", "dt", "masks", "seg_row"))
    tokens, inner = s.shape
    head_count = inner // width
    heads = heads_per_step(head_count)
    lanes = heads * width
    n = bcraw.shape[1] // 2
    blocks = tokens // q
    return pl.pallas_call(
        functools.partial(bwd_kernel, q, heads, width),
        grid=(head_count // heads,),
        in_specs=[
            lane_block(tokens, lanes), lane_block(tokens, lanes), full((tokens, 2 * n)), lane_block(5, lanes),
            full((5, 2 * n)), full((tokens, 128)), full((tokens, 128)), full((tokens, 128)),
            full((1, tokens)), lane_block(1, lanes), pl.BlockSpec((blocks, n, lanes), lambda i: (0, 0, i)),
            full((tokens, 128)), full((1, 128)),
        ],
        out_specs=[
            lane_block(tokens, lanes), lane_block(8, lanes), full((tokens, 2 * n + 128)),
            full((tokens, 2 * n)), full((8, 2 * n)), full((8, 128)),
        ],
        out_shape=[
            jax.ShapeDtypeStruct((tokens, inner), BF16), jax.ShapeDtypeStruct((8, inner), F32),
            jax.ShapeDtypeStruct((tokens, 2 * n + 128), BF16), jax.ShapeDtypeStruct((tokens, 2 * n), BF16),
            jax.ShapeDtypeStruct((8, 2 * n), F32), jax.ShapeDtypeStruct((8, 128), F32),
        ],
        scratch_shapes=backward_scratch(tokens, q, n, lanes),
        compiler_params=pltpu.CompilerParams(
            dimension_semantics=("arbitrary",), vmem_limit_bytes=VMEM_LIMIT
        ),
        cost_estimate=pl.CostEstimate(
            flops=2 * tokens * inner * (8 * q + 8 * n),
            bytes_accessed=12 * tokens * inner,
            transcendentals=tokens * q * head_count,
        ),
        name="scan_backward",
    )(
        s, dy, bcraw, conv_x, conv_bc, la, dt, masks, seg_row, skip_lanes, states, prep["dt_in"], prep["rate"],
    )


MESH = pl.DeviceIdType.MESH


class Here:
    def __init__(self):
        self.me = lax.axis_index("dp")
        self.t = lax.axis_index("tensor")
        self.z = self.me // 4
        self.y = (self.me // 2) % 2
        self.c = self.me % 2

    def slot(self, z, y, c):
        return z * 4 + y * 2 + c

    def z_plus(self, d):
        return (self.z + d) % 4

    def owner(self, k):
        core = self.c if k < 8 else 1 - self.c
        return self.slot(k % 4, 1 - self.y if k % 8 < 4 else self.y, core)

    def at_z(self, d):
        return (self.slot(self.z_plus(d), self.y, self.c), self.t)

    def across_y(self):
        return (self.slot(self.z, 1 - self.y, self.c), self.t)

    def other_core(self):
        return (self.slot(self.z, self.y, 1 - self.c), self.t)

    def across_x(self):
        return (self.me, 1 - self.t)

    def greet(self):
        barrier = pltpu.get_barrier_semaphore()
        for peer in (self.at_z(1), self.at_z(2), self.at_z(3), self.across_y(), self.other_core(), self.across_x()):
            pl.semaphore_signal(barrier, inc=1, device_id=peer, device_id_type=MESH)
        pl.semaphore_wait(barrier, 6)


def send(src, dst, sems, index, peer):
    return pltpu.make_async_remote_copy(
        src_ref=src, dst_ref=dst, send_sem=sems.at[0, index], recv_sem=sems.at[1, index],
        device_id=peer, device_id_type=MESH,
    )


class Gather:
    COPIES = 27

    def __init__(self, here, src, dst, lanes, sems, local_sem):
        self.here, self.dst, self.lanes, self.sems = here, dst, lanes, sems
        self.src = src.at[:, lanes]
        self.local = pltpu.make_async_copy(self.src, self.at(here.me), local_sem)

    def at(self, slot):
        return self.dst.at[slot, :, self.lanes]

    def holds(self, i):
        z = self.here.z
        return z >= 0 if i == 0 else z >= i if i <= 3 else z + i - 3 <= 3

    def slot_of(self, i, far=False):
        here = self.here
        z = here.z - i if i <= 3 else here.z + i - 3
        return here.slot(z, 1 - here.y if far else here.y, here.c)

    def from_here(self, i, far=False):
        return self.src if i == 0 and not far else self.at(self.slot_of(i, far))

    def up(self, d):
        i = d - 1
        return send(self.from_here(i), self.at(self.slot_of(i)), self.sems, i, self.here.at_z(1))

    def down(self, d):
        i = d + 2 if d > 1 else 0
        return send(self.from_here(i), self.at(self.slot_of(i)), self.sems, 2 + d, self.here.at_z(3))

    def across(self, i):
        return send(self.from_here(i), self.at(self.slot_of(i)), self.sems, 6 + i, self.here.across_y())

    def to_core(self, k):
        i, far = k % 7, k >= 7
        src = self.from_here(i, far)
        return send(src, self.at(self.slot_of(i, far)), self.sems, 13 + k, self.here.other_core())

    def sends_up(self, d):
        return (self.here.z < 3) & (self.here.z >= d - 1)

    def sends_down(self, d):
        return (self.here.z > 0) & (self.here.z + d <= 4)

    def start_z(self):
        pl.when(self.sends_up(1))(lambda: self.up(1).start())
        pl.when(self.sends_down(1))(lambda: self.down(1).start())

    def start_y(self):
        self.across(0).start()
        self.to_core(0).start()
        self.local.start()

    def pass_z(self, *hops):
        for d in hops:

            @pl.when(self.holds(d))
            def _(d=d):
                self.up(d).wait_recv()
                if d < 3:
                    pl.when(self.here.z < 3)(lambda: self.up(d + 1).start())
                self.across(d).start()
                self.to_core(d).start()

            @pl.when(self.holds(3 + d))
            def _(d=d):
                self.down(d).wait_recv()
                if d < 3:
                    pl.when(self.here.z > 0)(lambda: self.down(d + 1).start())
                self.across(3 + d).start()
                self.to_core(3 + d).start()

    def pass_y(self):
        for i in range(7):

            @pl.when(self.holds(i))
            def _(i=i):
                self.across(i).wait_recv()
                self.to_core(7 + i).start()

    def arrived(self):
        self.local.wait()
        for k in range(14):
            pl.when(self.holds(k % 7))(lambda k=k: self.to_core(k).wait_recv())

    def sent(self):
        for d in (1, 2, 3):
            pl.when(self.sends_up(d))(lambda d=d: self.up(d).wait_send())
            pl.when(self.sends_down(d))(lambda d=d: self.down(d).wait_send())
        for i in range(7):
            pl.when(self.holds(i))(lambda i=i: self.across(i).wait_send())
        for k in range(14):
            pl.when(self.holds(k % 7))(lambda k=k: self.to_core(k).wait_send())


class GatherAcross:
    COPIES = 27

    def __init__(self, here, src, dst, lanes, sems, local_sem):
        self.here, self.sems, self.lanes, self.dst = here, sems, lanes, dst
        self.src = src.at[:, lanes]
        self.local = pltpu.make_async_copy(self.src, self.at(here.me), local_sem)

    holds = Gather.holds
    sends_up, sends_down = Gather.sends_up, Gather.sends_down

    def at(self, slot):
        return self.dst.at[slot, :, self.lanes]

    def slot_of(self, i, row):
        z = self.here.z - i if i <= 3 else self.here.z + i - 3
        return self.here.slot(z, 1 - self.here.y if row else self.here.y, self.here.c)

    def move(self, i, row, index, peer):
        slot = self.slot_of(i, row)
        src = self.src if i == 0 and not row else self.at(slot)
        return send(src, self.at(slot), self.sems, index, peer)

    def across(self):
        return self.move(0, 0, 0, self.here.across_y())

    def up(self, d, row):
        return self.move(d - 1, row, row * 3 + d, self.here.at_z(1))

    def down(self, d, row):
        return self.move(d + 2 if d > 1 else 0, row, 6 + row * 3 + d, self.here.at_z(3))

    def to_core(self, k):
        return self.move(k % 7, k // 7, 13 + k, self.here.other_core())

    def start_y(self):
        self.across().start()
        self.to_core(0).start()
        self.local.start()

    def start_z(self, row):
        pl.when(self.sends_up(1))(lambda: self.up(1, row).start())
        pl.when(self.sends_down(1))(lambda: self.down(1, row).start())

    def pass_y(self):
        self.across().wait_recv()
        self.start_z(1)
        self.to_core(7).start()

    def pass_z(self, d):
        for row in (0, 1):

            @pl.when(self.holds(d))
            def _(row=row):
                self.up(d, row).wait_recv()
                if d < 3:
                    pl.when(self.here.z < 3)(lambda: self.up(d + 1, row).start())
                self.to_core(row * 7 + d).start()

            @pl.when(self.holds(3 + d))
            def _(row=row):
                self.down(d, row).wait_recv()
                if d < 3:
                    pl.when(self.here.z > 0)(lambda: self.down(d + 1, row).start())
                self.to_core(row * 7 + 3 + d).start()

    def arrived(self):
        self.local.wait()
        for k in range(14):
            pl.when(self.holds(k % 7))(lambda k=k: self.to_core(k).wait_recv())

    def sent(self):
        self.across().wait_send()
        for d in (1, 2, 3):
            for row in (0, 1):
                pl.when(self.sends_up(d))(lambda d=d, row=row: self.up(d, row).wait_send())
                pl.when(self.sends_down(d))(lambda d=d, row=row: self.down(d, row).wait_send())
        for k in range(14):
            pl.when(self.holds(k % 7))(lambda k=k: self.to_core(k).wait_send())


def softplus(w):
    return jnp.maximum(w, 0.0) + jnp.log1p(jnp.exp(-jnp.abs(w)))


def forward_kernel(
    q, heads, width, inner_total,
    hid_ref, cot_ref, small_ref, zx_ref, wo_ref, vec_ref, seg_ref, kx_ref, kbc_ref,
    rows_out, small_out, ws_out, wz_out, wo_out, s_out, normt_out, cott_out,
    scale_hbm, bcraw_hbm, dtin_hbm, dt_hbm, la_hbm, masks_hbm, st_hbm, dy_out, gated_out, dz_out, gngain_out,
    small_sems, ws_sems, wz_sems, wo_sems, wb_sems, x_sems, local_sems,
    rows_v, cot_v, small_v, ws_v, wz_v, wo_v, s_v, normed_v, y_v, z_v, dg_v, sum_v, sum_own, sum_came, normt_v, cott_v,
    dy_v, gated_v, dz_v, t_sems, out_sems,
    scale_out, bcraw_out, dtin_out, dt_out, la_out, masks_out, st_out, keep_sems,
    bcc, mneg, cb, *group_scratch,
):
    here = Here()
    tokens = normed_v.shape[0]
    half = tokens // 2
    inner = y_v.shape[1]
    lanes = heads * width
    groups = inner // lanes
    here.greet()
    hidden = send(hid_ref, rows_v.at[here.t], x_sems, 0, here.across_x())
    cotangent = send(cot_ref, cot_v.at[here.t], x_sems, 1, here.across_x())
    sums_x = send(sum_own, sum_came, x_sems, 2, here.across_x())
    whole, first, second = pl.ds(0, inner), pl.ds(0, inner // 2), pl.ds(inner // 2, inner // 2)
    small = Gather(here, small_ref, small_out, pl.ds(0, small_ref.shape[1]), small_sems, local_sems.at[0])
    ws = Gather(here, zx_ref.at[1], ws_out, whole, ws_sems, local_sems.at[1])
    wz = Gather(here, zx_ref.at[0], wz_out, whole, wz_sems, local_sems.at[2])
    wo = Gather(here, wo_ref, wo_out, first, wo_sems, local_sems.at[3])
    wb = GatherAcross(here, wo_ref, wo_out, second, wb_sems, local_sems.at[12])
    gathers = [small, ws, wz, wo, wb]
    local = lambda src, dst, i: pltpu.make_async_copy(src, dst, local_sems.at[i])
    own_hidden = local(hid_ref, rows_v.at[here.t], 4)
    own_cot = local(cot_ref, cot_v.at[here.t], 5)
    load_ws, load_wz = local(ws_out, ws_v, 6), local(wz_out, wz_v, 7)
    load_wo = local(wo_out.at[:, :, first], wo_v.at[:, :, first], 8)
    load_wb = local(wo_out.at[:, :, second], wo_v.at[:, :, second], 13)
    store_rows, store_s = local(rows_v, rows_out, 9), local(s_v, s_out, 10)
    load_small = local(small_out, small_v, 11)
    keep = lambda src, dst, i: pltpu.make_async_copy(src, dst, keep_sems.at[i])
    keep_scale, keep_masks, keep_st = (
        keep(scale_out, scale_hbm, 0), keep(masks_out, masks_hbm, 1), keep(st_out, st_hbm, 2)
    )
    keep_prep = [
        keep(bcraw_out, bcraw_hbm, 3), keep(dtin_out, dtin_hbm, 4), keep(dt_out, dt_hbm, 5), keep(la_out, la_hbm, 6)
    ]

    def by_piece(src, dst, row):
        return [
            pltpu.make_async_copy(src.at[here.owner(k)], dst.at[k], t_sems.at[row, k]) for k in range(16)
        ]

    store_normt, store_cott = by_piece(normt_v, normt_out, 0), by_piece(cott_v, cott_out, 1)

    def turn(values, at, dst):
        shard_rows = dst.shape[1]
        flipped = values.astype(F32).T.astype(BF16)
        dst[pl.ds(at * (384 // shard_rows), 384 // shard_rows)] = flipped.reshape(
            384 // shard_rows, shard_rows, flipped.shape[1]
        )
    hidden.start()
    for gather in (small, ws):
        gather.start_z()
        gather.start_y()
    cotangent.start()
    own_hidden.start()
    own_cot.start()

    seg = jnp.broadcast_to(seg_ref[...].astype(F32), (128, tokens)).T
    row = lax.broadcasted_iota(jnp.int32, (tokens, 128), 0)
    lane = lax.broadcasted_iota(jnp.int32, (tokens, 128), 1)
    masks = jnp.where(lane == 5, seg, 0.0)
    for back in (1, 2, 3):
        same = (pltpu.roll(seg, back, 0) == seg) & (row >= back)
        masks = jnp.where((lane == back - 1) & same, 1.0, masks)
    for b in range(tokens // q):
        inside = (row >= b * q) & (row < (b + 1) * q)
        if b:
            carried = inside & (seg == seg[b * q - 1 : b * q, :])
            masks = jnp.where((lane == 3) & carried, 1.0, masks)
        run_last = inside & (seg == seg[(b + 1) * q - 1 : (b + 1) * q, :])
        masks = jnp.where((lane == 4) & run_last, 1.0, masks)
    masks_out[...] = masks
    keep_masks.start()

    small.pass_z(1, 2, 3)
    ws.pass_z(1, 2)
    wz.start_z()
    small.pass_y()
    own_hidden.wait()
    hidden.wait_recv()
    store_rows.start()
    gain = vec_ref[0:1, :]
    chunk = 64

    def norm(i, carry):
        side, at = i // (half // chunk), i % (half // chunk)
        rows = pl.ds(pl.multiple_of(at * chunk, chunk), chunk)
        values = rows_v[side, rows, :].astype(F32)
        scale = lax.rsqrt(jnp.mean(values * values, axis=1, keepdims=True) + EPS)
        out_rows = pl.ds(pl.multiple_of(i * chunk, chunk), chunk)
        normed_v[out_rows, :] = (values * scale * gain).astype(BF16)
        scale_out[out_rows, :] = jnp.broadcast_to(scale, (chunk, 128))
        return carry

    lax.fori_loop(0, tokens // chunk, norm, 0)
    keep_scale.start()
    ws.pass_z(3)
    wz.start_y()
    wb.start_y()
    wz.pass_z(1)
    small.arrived()
    load_small.start()
    load_small.wait()
    pieces, shard, columns = small_v.shape
    proj = dot(normed_v[...], small_v[...].reshape(pieces * shard, columns))
    bc_width = columns - 128
    bcraw_out[...] = proj[:, :bc_width]
    dt_in = proj[:, bc_width:] + vec_ref[3:4, 0:128]
    dtin_out[...] = dt_in
    dt = softplus(dt_in)
    dt_out[...] = dt
    lower = jnp.where(
        lax.broadcasted_iota(jnp.int32, (q, q), 0) >= lax.broadcasted_iota(jnp.int32, (q, q), 1), 1.0, 0.0
    )
    exponent = dt * vec_ref[3:4, 128:256]
    for b in range(tokens // q):
        la_out[b * q : (b + 1) * q, :] = dot(lower, exponent[b * q : (b + 1) * q, :], NN, HIGHEST)
    for copy in keep_prep:
        copy.start()
    block_tables(q, bcraw_out, kbc_ref, masks_out, seg_ref, bcc, mneg, cb)
    wz.pass_z(2)
    wo.start_z()
    ws.pass_y()
    ws.arrived()
    load_ws.start()
    load_ws.wait()

    def weight_block(ref, at):
        return ref[:, :, at].reshape(pieces * shard, lanes)

    def lane_range(g):
        return pl.ds(pl.multiple_of(g * lanes, lanes), lanes)

    def scan_group(g, carry):
        @pl.when(g == 0)
        def _():
            wz.pass_z(3)
            wo.start_y()

        pl.when(g == 1)(lambda: wo.pass_z(1))

        @pl.when(g == 2)
        def _():
            wo.pass_z(2)
            wb.start_z(0)
            wb.pass_y()

        @pl.when(g == 4)
        def _():
            wo.pass_z(3)
            wb.pass_z(1)

        at = lane_range(g)
        s = dot(normed_v[...], weight_block(ws_v, at))
        fwd_group(
            q, heads, width, g, at, s, kx_ref[:, at], vec_ref[2:3, at], la_out, dt_out, masks_out,
            s_v, y_v, st_out, bcc, mneg, cb, *group_scratch,
        )
        return carry

    lax.fori_loop(0, groups, scan_group, 0)
    store_s.start()
    keep_st.start()
    wz.pass_y()
    wb.pass_z(2)

    def turn_normed(i, carry):
        turn(normed_v[:, pl.ds(pl.multiple_of(i * 384, 384), 384)], i, normt_v)
        return carry

    lax.fori_loop(0, normed_v.shape[1] // 384, turn_normed, 0)
    for copy in store_normt:
        copy.start()
    wz.arrived()
    load_wz.start()
    own_cot.wait()
    cotangent.wait_recv()

    def turn_cot(i, carry):
        turn(
            cot_v[:, :, pl.ds(pl.multiple_of(i * 384, 384), 384)].reshape(tokens, 384), i, cott_v
        )
        return carry

    lax.fori_loop(0, cot_v.shape[2] // 384, turn_cot, 0)
    for copy in store_cott:
        copy.start()
    sum_v[...] = jnp.zeros_like(sum_v)
    load_wz.wait()

    def gate_group(g, carry):
        at = lane_range(g)
        z = dot(normed_v[...], weight_block(wz_v, at))
        z_v[:, at] = z
        v = y_v[:, at] * (z * sigmoid(z))
        square = v * v
        for piece in range(lanes // 128):
            sum_v[0] += square[:, piece * 128 : (piece + 1) * 128]
        return carry

    lax.fori_loop(0, groups, gate_group, 0)
    wo.pass_y()
    wb.pass_z(3)
    wo.arrived()
    load_wo.start()
    load_wo.wait()

    def pull_group(g, carry):
        at = lane_range(g)
        side = cot_v[...].reshape(tokens, cot_v.shape[2])
        pulled = dot(side, weight_block(wo_v, at))
        dg_v[:, at] = pulled
        z = z_v[:, at]
        product = pulled * vec_ref[1:2, at] * (y_v[:, at] * (z * sigmoid(z)))
        for piece in range(lanes // 128):
            sum_v[1] += product[:, piece * 128 : (piece + 1) * 128]
        return carry

    lax.fori_loop(0, groups // 2, pull_group, 0)
    wb.arrived()
    load_wb.start()
    load_wb.wait()
    lax.fori_loop(groups // 2, groups, pull_group, 0)
    row_of = lambda array: jnp.sum(array.T, axis=0, keepdims=True)
    sum_own[...] = jnp.concatenate(
        [row_of(sum_v[0]), row_of(sum_v[1]), jnp.zeros((6, tokens), F32)], axis=0
    )
    sums_x.start()
    sums_x.wait_recv()
    both = sum_own[...] + sum_came[...]
    scale_row = lax.rsqrt(both[0:1, :] / inner_total + EPS)
    pull_row = both[1:2, :] * (scale_row * scale_row * scale_row) / inner_total
    column_of = lambda array: jnp.broadcast_to(array, (128, tokens)).T
    sum_v[0] = column_of(scale_row)
    sum_v[1] = column_of(pull_row)

    def grad_group(g, carry):
        at = lane_range(g)
        scale, pull = sum_v[0][:, 0:1], sum_v[1][:, 0:1]
        z, y, pulled = z_v[:, at], y_v[:, at], dg_v[:, at]
        sig = sigmoid(z)
        gate = z * sig
        v = y * gate
        unit = v * scale
        gngain_out[:, at] = jnp.sum(pulled * unit, axis=0, keepdims=True)
        gated_v[:, at] = (unit * vec_ref[1:2, at]).astype(BF16)
        d_v = pulled * vec_ref[1:2, at] * scale - pull * v
        dy_v[:, at] = d_v * gate
        dz_v[:, at] = (d_v * y * sig * (1.0 + z * (1.0 - sig))).astype(BF16)
        return carry

    def grad_out_copies(g):
        at = lane_range(g)
        return [
            pltpu.make_async_copy(src.at[:, at], dst.at[:, at], out_sems.at[i, g])
            for i, (src, dst) in enumerate([(dy_v, dy_out), (gated_v, gated_out), (dz_v, dz_out)])
        ]

    def grad_and_store(g, carry):
        grad_group(g, carry)
        for copy in grad_out_copies(g):
            copy.start()
        return carry

    lax.fori_loop(0, groups, grad_and_store, 0)
    for gather in gathers:
        gather.sent()

    def stored(g, carry):
        for copy in grad_out_copies(g):
            copy.wait()
        return carry

    lax.fori_loop(0, groups, stored, 0)
    for copy in (hidden, cotangent, sums_x):
        copy.wait_send()
    for copy in [store_rows, store_s, keep_scale, keep_masks, keep_st] + keep_prep + store_normt + store_cott:
        copy.wait()


def in_vmem():
    return pl.BlockSpec(memory_space=pltpu.VMEM)


def in_any():
    return pl.BlockSpec(memory_space=pl.ANY)


def forward_all(hidden, cot, small, zx, wo, vectors, seg_ids, conv_x, conv_bc, width, inner_total, q):
    half, depth = hidden.shape
    tokens = 2 * half
    shard, inner = zx.shape[1:]
    columns = small.shape[1]
    heads = heads_per_step(inner // width)
    lanes = heads * width
    n = (columns - 128) // 2
    blocks = tokens // q
    shape = jax.ShapeDtypeStruct
    sems = pltpu.SemaphoreType.DMA
    weight, rows = (16, shard, inner), (2, half, depth)
    per_head = shape((tokens, 128), F32)
    outs = pl.pallas_call(
        functools.partial(forward_kernel, q, heads, width, inner_total),
        in_specs=[in_vmem()] * 9,
        out_specs=[in_any()] * 18 + [in_vmem()],
        out_shape=[
            shape(rows, BF16), shape((16, shard, columns), BF16),
            shape(weight, BF16), shape(weight, BF16), shape(weight, BF16),
            shape((tokens, inner), F32), shape((16, shard, tokens), BF16), shape((16, shard, tokens), BF16),
            per_head, shape((tokens, columns - 128), F32), per_head, per_head, per_head, per_head,
            shape((blocks, n, inner), F32), shape((tokens, inner), F32), shape((tokens, inner), BF16),
            shape((tokens, inner), BF16), shape((1, inner), F32),
        ],
        scratch_shapes=[sems((2, Gather.COPIES))] * 5 + [sems((2, 3)), sems((14,))]
        + [pltpu.VMEM(rows, BF16)] * 2 + [pltpu.VMEM((16, shard, columns), BF16)] + [pltpu.VMEM(weight, BF16)] * 3
        + [
            pltpu.VMEM((tokens, inner), F32), pltpu.VMEM((tokens, depth), BF16), pltpu.VMEM((tokens, inner), F32),
            pltpu.VMEM((tokens, inner), F32), pltpu.VMEM((tokens, inner), F32), pltpu.VMEM((2, tokens, 128), F32),
            pltpu.VMEM((8, tokens), F32), pltpu.VMEM((8, tokens), F32),
            pltpu.VMEM((16, shard, tokens), BF16), pltpu.VMEM((16, shard, tokens), BF16),
            pltpu.VMEM((tokens, inner), F32), pltpu.VMEM((tokens, inner), BF16), pltpu.VMEM((tokens, inner), BF16),
            sems((2, 16)), sems((3, inner // lanes)),
            pltpu.VMEM((tokens, 128), F32), pltpu.VMEM((tokens, columns - 128), F32),
        ]
        + [pltpu.VMEM((tokens, 128), F32)] * 4
        + [pltpu.VMEM((blocks, n, inner), F32), sems((7,))]
        + forward_scratch(tokens, q, n, lanes),
        compiler_params=pltpu.CompilerParams(
            collective_id=0, has_side_effects=True, vmem_limit_bytes=VMEM_LIMIT
        ),
        name="forward_all",
    )(hidden, cot, small, zx, wo, vectors, seg_ids, conv_x, conv_bc)
    flat = lambda a: a.reshape((-1, a.shape[-1]))
    return [outs[0]] + [flat(a) for a in outs[1:14]] + list(outs[14:])


class Scatter:
    def __init__(self, here, own, away, from_core, from_y, from_z, core_sems, y_sems, z_sems, free):
        self.free, self.core_slots = free, from_core.shape[0]
        self.here, self.own, self.away = here, own, away
        self.from_core, self.from_y, self.from_z = from_core, from_y, from_z
        self.core_sems, self.y_sems, self.z_sems = core_sems, y_sems, z_sems

    def copy(self, src, dst, sems, i, peer):
        return pltpu.make_async_remote_copy(
            src_ref=src, dst_ref=dst, send_sem=sems[0].at[i], recv_sem=sems[1].at[i], device_id=peer,
            device_id_type=MESH,
        )

    def to_core(self, i):
        slot = i % self.away.shape[0]
        return self.copy(
            self.away.at[slot], self.from_core.at[i % self.core_slots], self.core_sems, i, self.here.other_core()
        )

    def across(self, i):
        return self.copy(
            self.own.at[i, pl.ds(0, 4)], self.from_y.at[i], self.y_sems, i, self.here.across_y()
        )

    def up(self, i, k):
        return self.copy(
            self.own.at[i, 4 + k], self.from_z.at[i, k - 1], self.z_sems, i * 6 + k - 1, self.here.at_z(1)
        )

    def down(self, i, k):
        slot = 3 + k if k < 2 else 0
        return self.copy(
            self.own.at[i, 4 + k], self.from_z.at[i, slot], self.z_sems, i * 6 + 3 + k, self.here.at_z(3)
        )

    def start(self, i, left_ref, right, reuse):
        pieces, rows, tokens = left_ref.shape
        half = pieces // 2
        pl.when(reuse)(lambda: self.to_core(jnp.maximum(i - self.away.shape[0], 0)).wait_send())
        make = lambda at: dot(
            left_ref[at : at + half].reshape(half * rows, tokens), right
        ).astype(BF16).reshape(half, rows, right.shape[1])
        self.away[i % self.away.shape[0]] = make(half)
        pl.when(i >= self.core_slots)(lambda: pl.semaphore_wait(self.free, 1))
        self.to_core(i).start()
        self.own[i] = make(0)

    def to_y(self, i):
        self.to_core(i).wait_recv()
        slot = i % self.core_slots
        add = lambda at: (self.own[i, at].astype(F32) + self.from_core[slot, at].astype(F32)).astype(BF16)
        self.own[i, 0:4] = add(slice(0, 4))
        self.across(i).start()
        self.own[i, 4:8] = add(slice(4, 8))

        @pl.when(i + self.core_slots < self.own.shape[0])
        def _():
            pl.semaphore_signal(
                self.free, inc=1, device_id=self.here.other_core(), device_id_type=MESH
            )

    def local_sum(self, i, k):
        return self.own[i, 4 + k].astype(F32) + self.from_y[i, k].astype(F32)

    def hop(self, i, h):
        z = self.here.z
        if h == 0:
            self.across(i).wait_recv()

        @pl.when(z == h)
        def _():
            for k in range(3, h, -1):
                total = self.local_sum(i, k)
                if h:
                    self.up(i, k).wait_recv()
                    total = total + self.from_z[i, k - 1].astype(F32)
                self.own[i, 4 + k] = total.astype(BF16)
                self.up(i, k).start()

        @pl.when(z == 3 - h)
        def _():
            for k in range(0, 3 - h):
                total = self.local_sum(i, k)
                if h:
                    self.down(i, k).wait_recv()
                    total = total + self.from_z[i, 3 + k if k < 2 else 0].astype(F32)
                self.own[i, 4 + k] = total.astype(BF16)
                self.down(i, k).start()

    def finish(self, i, store):
        for k in range(4):

            @pl.when(self.here.z == k)
            def _(k=k):
                total = self.local_sum(i, k)
                if k > 0:
                    self.up(i, k).wait_recv()
                    total = total + self.from_z[i, k - 1].astype(F32)
                if k < 3:
                    self.down(i, k).wait_recv()
                    total = total + self.from_z[i, 3 + k if k < 2 else 0].astype(F32)
                store(total)

    def sent(self, i, core):
        z = self.here.z
        pl.when(core)(lambda: self.to_core(i).wait_send())
        self.across(i).wait_send()
        for k in (1, 2, 3):
            pl.when(z < k)(lambda k=k: self.up(i, k).wait_send())
        for k in (0, 1, 2):
            pl.when(z > k)(lambda k=k: self.down(i, k).wait_send())


AWAY_SLOTS, CORE_SLOTS = 3, 6


def backward_kernel(
    q, heads, width,
    s_ref, dy_ref, ws_ref, wz_ref, wo_ref, kx_ref, veclanes_ref, st_ref,
    kbc_ref, segr_ref, vec_ref, gngain_ref,
    bcraw_hbm, la_hbm, dt_hbm, msk_hbm, normt_hbm, cott_hbm, gated_hbm, dz_hbm,
    dtin_hbm, small_w_hbm, rows_hbm, scale_hbm, cot_own_hbm,
    block_hbm, grad_in_hbm, gwo_hbm, gzx_hbm, gbc_hbm, gdt_hbm, sums_hbm,
    own, away, from_core, from_y, from_z,
    core_send, core_recv, y_send, y_recv, z_send, z_recv, free, x_sems, sum_sems,
    col, proj, x_send, x_came, sum_own, sum_came, ds_v, gk_v, small_v, low_v, gkbc_v, ghead_v,
    bcraw_ref, la_ref, dt_ref, msk_ref, normt_ref, cott_ref, gated_ref, dz_ref,
    dtin_ref, small_w_ref, rows_ref, scale_ref, cot_own_ref, load_sems,
    block_out, grad_in_out, gwo_out, gzx_out, gbc_out, gdt_out, sums_out, store_sems,
    bcc, mnegt, cbt, xs, dxs, dtt, gt, la4, lat4, dt4, dla_acc, ddt_acc, dbc_acc,
):
    here = Here()
    step = pl.program_id(0)
    tokens, lanes = s_ref.shape
    depth = col.shape[1]
    steps = gwo_out.shape[1] // lanes
    rate_ref, gain_ref = vec_ref.at[pl.ds(3, 1), pl.ds(128, 128)], vec_ref.at[pl.ds(0, 1)]
    dsk_ref = veclanes_ref.at[pl.ds(2, 1)]
    half = tokens // 2
    n2 = bcc.shape[1]
    scatter = Scatter(
        here, own, away, from_core, from_y, from_z, (core_send, core_recv), (y_send, y_recv), (z_send, z_recv), free
    )
    chunks = own.shape[0]
    core_sum = send(sum_own.at[0], sum_came.at[0], sum_sems, 0, here.other_core())
    y_sum = send(sum_own.at[1], sum_came.at[1], sum_sems, 1, here.across_y())
    z_sums = [send(sum_own.at[2], sum_came.at[1 + d], sum_sems, 1 + d, here.at_z(d)) for d in (1, 2, 3)]
    x_part = pl.ds(0, 8)
    x_sum = send(sum_own.at[3, x_part], sum_came.at[5, x_part], sum_sems, 5, here.across_x())
    pulled = send(x_send.at[1], x_came.at[1], x_sems, 0, here.across_x())

    def projected(g):
        at = pl.ds(pl.multiple_of(g * 256, 256), 256)
        return send(x_send.at[0, :, at], x_came.at[0, :, at], x_sems, 1 + g, here.across_x())

    load = lambda src, dst, i: pltpu.make_async_copy(src, dst, load_sems.at[i])
    loads = [
        load(src, dst, i)
        for i, (src, dst) in enumerate(
            [
                (gated_hbm, gated_ref), (cott_hbm, cott_ref), (dz_hbm, dz_ref), (normt_hbm, normt_ref),
                (bcraw_hbm, bcraw_ref), (la_hbm, la_ref), (dt_hbm, dt_ref), (msk_hbm, msk_ref),
                (dtin_hbm, dtin_ref), (small_w_hbm, small_w_ref), (rows_hbm, rows_ref), (scale_hbm, scale_ref),
                (cot_own_hbm, cot_own_ref),
            ]
        )
    ]
    stores = [
        pltpu.make_async_copy(src, dst, store_sems.at[i])
        for i, (src, dst) in enumerate(
            [
                (block_out, block_hbm), (grad_in_out, grad_in_hbm), (gwo_out, gwo_hbm), (gzx_out, gzx_hbm),
                (gbc_out, gbc_hbm), (gdt_out, gdt_hbm), (sums_out, sums_hbm),
            ]
        )
    ]
    at_lanes = pl.ds(pl.multiple_of(step * lanes, lanes), lanes)

    @pl.when(step == 0)
    def _():
        for copy in loads:
            copy.start()
        here.greet()
        for copy in loads[:8]:
            copy.wait()

    scatter.start(3 * step, cott_ref, gated_ref[:, at_lanes], step >= AWAY_SLOTS // 3)
    scatter.start(3 * step + 1, normt_ref, dz_ref[:, at_lanes], step >= AWAY_SLOTS // 3)

    @pl.when(step == 0)
    def _():
        bwd_tables(
            q, bcraw_ref, kbc_ref, msk_ref, segr_ref, bcc, mnegt, cbt, dtt, dbc_acc, dla_acc, ddt_acc
        )
        col[...] = jnp.zeros_like(col)

    def store_at(kind, g):
        out = gwo_out if kind == 0 else gzx_out.at[kind - 1]
        at = pl.ds(pl.multiple_of(g * lanes, lanes), lanes)

        def store(total):
            out[:, at] = total

        return store

    def small_store(i):
        def store(total):
            (gbc_out, gdt_out)[i][...] = total

        return store

    def tick(base, j):
        drain = isinstance(base, int)
        for back, act in ((8, None), (7, 2), (5, 1), (3, 0)):
            kind, turn = (j - back) % 3, (j - back) // 3
            g = base + turn
            if drain:
                c = 3 * g + kind
                if c >= chunks:
                    continue
                if act is None:
                    scatter.finish(c, small_store(c - (chunks - 2)) if c >= chunks - 2 else store_at(kind, g))
                else:
                    scatter.hop(c, act)
            else:

                @pl.when(g >= 0)
                def _(act=act, kind=kind, g=jnp.maximum(g, 0)):
                    if act is None:
                        scatter.finish(3 * g + kind, store_at(kind, g))
                    else:
                        scatter.hop(3 * g + kind, act)

    scatter.to_y(3 * step)
    tick(step, 0)
    own_half = pl.ds(pl.multiple_of(here.t * half, half), half)
    away_half = pl.ds(pl.multiple_of((1 - here.t) * half, half), half)
    at_columns = pl.ds(pl.multiple_of(step * 256, 256), 256)
    x_send[0, :, at_columns] = dot(gated_ref[away_half, :], wo_ref[...], NT).astype(BF16)
    projected(step).start()
    proj[:, at_columns] = dot(gated_ref[own_half, :], wo_ref[...], NT)
    col[:, at_columns] += dot(dz_ref[...], wz_ref[...], NT)

    def between(i):
        if i == 0:
            scatter.to_y(3 * step + 1)
            tick(step, 1)

    bwd_group(
        q, heads, width, step, s_ref, dy_ref, kx_ref, la_ref, dt_ref, msk_ref, dsk_ref, st_ref, ds_v, gk_v,
        bcc, mnegt, cbt, xs, dxs, dtt, gt, la4, lat4, dt4, dla_acc, ddt_acc, dbc_acc, between,
    )
    scatter.start(3 * step + 2, normt_ref, ds_v[...], step >= AWAY_SLOTS // 3)
    sum_own[0, 2:8, at_lanes] = gk_v[0:6, :]

    def column_block(j):
        return pl.ds(pl.multiple_of(j * 256, 256), 256)

    def accumulate(j, carry):
        at = column_block(j)
        col[:, at] += dot(ds_v[...], ws_ref[at, :], NT)
        return carry

    lax.fori_loop(0, depth // 256, accumulate, 0)
    scatter.to_y(3 * step + 2)
    tick(step, 2)

    @pl.when(step == steps - 1)
    def _():
        chunk = 32

        def by_chunks(act):
            def one(i, carry):
                at = pl.multiple_of(i * chunk, chunk)
                own_at = pl.multiple_of(here.t * half + i * chunk, chunk)
                away_at = pl.multiple_of((1 - here.t) * half + i * chunk, chunk)
                act(pl.ds(at, chunk), pl.ds(own_at, chunk), pl.ds(away_at, chunk))
                return carry

            lax.fori_loop(0, half // chunk, one, 0)

        for copy in loads[8:]:
            copy.wait()
        small_v[:, n2 + 128 :] = jnp.zeros_like(small_v[:, n2 + 128 :])
        bwd_finish(
            q, bcraw_ref, kbc_ref, dt_ref, msk_ref, dtin_ref, rate_ref, small_v, low_v, gkbc_v, ghead_v,
            bcc, dtt, dla_acc, ddt_acc, dbc_acc,
        )
        for i in range(2):
            scatter.start(3 * steps + i, normt_ref, small_v[:, i * lanes : (i + 1) * lanes], steps > 0)
        tick(steps, 0)
        for i in range(2):
            scatter.to_y(3 * steps + i)

        def small_part(j, carry):
            at = column_block(j)
            col[:, at] += dot(small_v[:, : n2 + 128], small_w_ref[at, :], NT) + dot(
                low_v[...], small_w_ref[at, 0:n2], NT
            )
            return carry

        lax.fori_loop(0, depth // 256, small_part, 0)
        tick(steps, 1)
        gain = gain_ref[...]

        def norm_back(side, store):
            def one(i, total):
                inside = pl.ds(pl.multiple_of(i * chunk, chunk), chunk)
                rows = pl.ds(pl.multiple_of(side * half + i * chunk, chunk), chunk)
                columns = col[rows, :]
                scale = scale_ref[rows, 0:1]
                unit = rows_ref[side, inside, :].astype(F32) * scale
                grad_unit = columns * gain
                store(
                    rows, inside,
                    scale * (grad_unit - unit * jnp.mean(grad_unit * unit, axis=1, keepdims=True)),
                )
                return total + jnp.sum(columns * unit, axis=0, keepdims=True)

            return one

        def to_send(rows, inside, value):
            x_send[1, inside, :] = value.astype(BF16)

        def to_keep(rows, inside, value):
            col[rows, :] = value

        prenorm = lax.fori_loop(
            0, half // chunk, norm_back(1 - here.t, to_send), jnp.zeros((1, depth), F32)
        )
        pulled.start()
        prenorm = lax.fori_loop(0, half // chunk, norm_back(here.t, to_keep), prenorm)
        sum_own[0, 0:1, :] = prenorm
        sum_own[0, 1:2, :] = jnp.zeros((1, depth), F32)
        for r in range(5):
            sum_own[0, 1:2, r * n2 : (r + 1) * n2] = gkbc_v[r : r + 1, :]
        sum_own[0, 8:9, :] = gngain_ref[...]
        sum_own[0, 9:16, :] = jnp.zeros((7, depth), F32)
        sum_own[0, 9:10, 0:128] = ghead_v[0:1, :]
        sum_own[0, 9:10, 128:256] = ghead_v[1:2, :]
        head_of = lax.broadcasted_iota(jnp.int32, (128, depth), 1) // width
        pick = jnp.where(head_of == lax.broadcasted_iota(jnp.int32, (128, depth), 0), 1.0, 0.0)
        sum_own[0, 9:10, 256:384] = dot(sum_own[0, 0:8, :], pick, NT, HIGHEST)[7:8, :]
        core_sum.start()
        tick(steps, 2)
        core_sum.wait_recv()
        sum_own[1] = sum_own[0] + sum_came[0]
        y_sum.start()
        tick(steps, 3)
        tick(steps, 4)
        y_sum.wait_recv()
        sum_own[2] = sum_own[1] + sum_came[1]
        for copy in z_sums:
            copy.start()
        tick(steps, 5)
        tick(steps, 6)
        for copy in z_sums:
            copy.wait_recv()
        sum_own[3] = sum_own[2] + sum_came[2] + sum_came[3] + sum_came[4]
        x_sum.start()
        tick(steps, 7)
        tick(steps, 8)

        def arrived_projected(g, carry):
            projected(g).wait_recv()
            return carry

        lax.fori_loop(0, steps, arrived_projected, 0)

        def put_block_out(rows, own_rows, away_rows):
            block_out[rows, :] = (
                rows_ref[here.t, rows, :].astype(F32) + proj[rows, :] + x_came[0, rows, :].astype(F32)
            ).astype(BF16)

        by_chunks(put_block_out)
        stores[0].start()
        pulled.wait_recv()

        def put_grad_in(rows, own_rows, away_rows):
            grad_in_out[rows, :] = (
                cot_own_ref[rows, :].astype(F32) + col[own_rows, :] + x_came[1, rows, :].astype(F32)
            ).astype(BF16)

        by_chunks(put_grad_in)
        stores[1].start()
        for copy in stores[2:5]:
            copy.start()
        x_sum.wait_recv()
        sums_out[...] = sum_own[3]
        sums_out[0:2, :] = sum_own[3, 0:2, :] + sum_came[5, 0:2, :]
        stores[6].start()
        tick(steps, 9)
        stores[5].start()

        def all_sent(i, carry):
            scatter.sent(i, i >= chunks - AWAY_SLOTS)
            return carry

        lax.fori_loop(0, chunks, all_sent, 0)

        def sent_projected(g, carry):
            projected(g).wait_send()
            return carry

        lax.fori_loop(0, steps, sent_projected, 0)
        for copy in [core_sum, y_sum, x_sum, pulled] + z_sums:
            copy.wait_send()
        for copy in stores:
            copy.wait()


def backward_all(
    s, dy, gated, dz, w_s, w_z, w_out_t, conv_x, vectors, states, prep, conv_bc,
    normt, cott, small, rows, scale, seg_ids, gngain, cot_own, width, q,
):
    tokens, inner = s.shape
    depth = w_s.shape[0]
    half = tokens // 2
    heads = heads_per_step(inner // width)
    lanes = heads * width
    groups = inner // lanes
    n2 = prep["bcraw"].shape[1]
    n, blocks, shard = n2 // 2, tokens // q, depth // 16
    chunks = 3 * groups + 2
    shape = jax.ShapeDtypeStruct
    sems = pltpu.SemaphoreType.DMA
    once = lambda array: pl.BlockSpec(
        array.shape, lambda i: (0,) * array.ndim, pipeline_mode=pl.Buffered(1)
    )
    constants = [conv_bc, seg_ids, vectors, gngain]
    loaded = [
        prep["bcraw"], prep["la"], prep["dt"], prep["masks"], normt, cott, gated, dz,
        prep["dt_in"], small, rows, scale, cot_own,
    ]
    like = lambda array: pltpu.VMEM(array.shape, array.dtype)
    row_block = pl.BlockSpec((depth // groups, inner), lambda i: (i, 0))
    out_shape = [
        shape((half, depth), BF16), shape((half, depth), BF16), shape((shard, inner), F32),
        shape((2, shard, inner), F32), shape((shard, lanes), F32), shape((shard, lanes), F32), shape((16, depth), F32),
    ]
    pieces = lambda count, per: pltpu.VMEM((count, per, shard, lanes), BF16)
    return pl.pallas_call(
        functools.partial(backward_kernel, q, heads, width),
        grid=(groups,),
        in_specs=[lane_block(tokens, lanes)] * 2 + [lane_block(depth, lanes), row_block, row_block]
        + [lane_block(5, lanes), lane_block(8, lanes), pl.BlockSpec((blocks, n, lanes), lambda i: (0, 0, i))]
        + [once(array) for array in constants] + [in_any()] * len(loaded),
        out_specs=[in_any()] * len(out_shape),
        out_shape=out_shape,
        scratch_shapes=[pieces(chunks, 8), pieces(AWAY_SLOTS, 8), pieces(CORE_SLOTS, 8), pieces(chunks, 4), pieces(chunks, 5)]
        + [sems((chunks,))] * 4 + [sems((6 * chunks,))] * 2 + [pltpu.SemaphoreType.REGULAR, sems((2, 1 + groups)), sems((2, 6))]
        + [
            pltpu.VMEM((tokens, depth), F32), pltpu.VMEM((half, depth), F32), pltpu.VMEM((2, half, depth), BF16),
            pltpu.VMEM((2, half, depth), BF16), pltpu.VMEM((4, 16, depth), F32), pltpu.VMEM((6, 16, depth), F32),
            pltpu.VMEM((tokens, lanes), BF16), pltpu.VMEM((8, lanes), F32), pltpu.VMEM((tokens, 2 * lanes), BF16),
            pltpu.VMEM((tokens, n2), BF16), pltpu.VMEM((8, n2), F32), pltpu.VMEM((8, 128), F32),
        ]
        + [like(array) for array in loaded] + [sems((len(loaded),))]
        + [like(array) for array in out_shape] + [sems((len(out_shape),))]
        + backward_scratch(tokens, q, n, lanes),
        compiler_params=pltpu.CompilerParams(
            dimension_semantics=("arbitrary",), collective_id=1, has_side_effects=True,
            vmem_limit_bytes=67043328,
        ),
        name="backward_all",
    )(s, dy, w_s, w_z, w_out_t, conv_x, vectors, states, *constants, *loaded)


def lanes_of(per_head):
    return jnp.pad(per_head, [(0, 0)] * (per_head.ndim - 1) + [(0, 128 - per_head.shape[-1])])


def prepare_plain(normed, small, bias, rate, flat_ids, q):
    tokens = normed.shape[0]
    blocks = tokens // q
    proj = dot(normed, small)
    bc_width = small.shape[1] - 128
    dt_in = proj[:, bc_width:] + bias
    dt = jax.nn.softplus(dt_in)
    lower = jnp.where(jnp.arange(q)[:, None] >= jnp.arange(q)[None, :], 1.0, 0.0)
    la = jnp.einsum("ij,bjh->bih", lower, (dt * rate).reshape(blocks, q, 128), precision=HIGHEST)
    shifted = lambda l: jnp.concatenate([jnp.full((l,), -1, jnp.int32), flat_ids[:-l]])
    by_block = flat_ids.reshape(blocks, q)
    before = jnp.concatenate([jnp.full((1,), -1, jnp.int32), by_block[:-1, -1]])
    carried = (by_block == before[:, None]).reshape(-1)
    run_last = (by_block == by_block[:, -1:]).reshape(-1)
    masks = [flat_ids == shifted(1), flat_ids == shifted(2), flat_ids == shifted(3), carried, run_last, flat_ids]
    return proj[:, :bc_width], dt_in, dt, la.reshape(tokens, 128), lanes_of(jnp.stack(masks, axis=1).astype(F32))


def body(
    dp,
    tp,
    hidden_in,
    prenorm_gain,
    w_zx,
    w_dt,
    w_bc,
    conv_x,
    conv_bc,
    dt_bias,
    a_log,
    d_skip,
    norm_gain,
    w_out,
    seg_ids,
    grad_out,
):
    q = BLOCK_LEN
    staged = dp == 16 and tp == 2 and seg_ids.shape[0] == 1 and hidden_in.shape[1] == w_out.shape[0]
    inner = w_out.shape[0]
    head_count = dt_bias.shape[0]
    width = inner // head_count
    bc_width = w_bc.shape[1]
    shard = w_bc.shape[0]
    depth = hidden_in.shape[1]
    inner_total = inner * tp
    tensor = lax.axis_index("tensor")

    bias = lanes_of(dt_bias)[None, :]
    rate = lanes_of(-jnp.exp(a_log))[None, :]
    small_shard = jnp.concatenate([w_bc, lanes_of(w_dt)], axis=1)
    flat_ids = (seg_ids + seg_ids.shape[1] * lax.broadcasted_iota(jnp.int32, seg_ids.shape, 0)).reshape(-1)
    seg_row = flat_ids.astype(F32)[None, :]
    skip_lanes = jnp.repeat(d_skip, width)[None, :]
    prep = dict(rate=rate, seg_row=seg_row)

    if staged:
        heads_row = jnp.concatenate([bias[0], rate[0], jnp.zeros((inner - 256,), F32)])
        vectors = jnp.stack([prenorm_gain, norm_gain, skip_lanes[0], heads_row] + [jnp.zeros_like(heads_row)] * 4)
        (
            full_rows, small, w_s, w_z, w_out_t, s, normt, cott, scale_in,
            prep["bcraw"], prep["dt_in"], prep["dt"], prep["la"], prep["masks"],
            states, d_y, gated, d_z, grad_norm_gain,
        ) = forward_all(
            hidden_in, grad_out, small_shard, w_zx.transpose(1, 0, 2), w_out.T, vectors, seg_ids, conv_x, conv_bc,
            width, inner_total, q,
        )
        split = lambda array: array.reshape(16, shard, array.shape[1])
        block_out, grad_in, grad_w_out, grad_w_zx, bc_sum, grad_dt, sums = backward_all(
            s, d_y, gated, d_z, w_s, w_z, w_out_t, conv_x, vectors, states, prep, conv_bc,
            split(normt), split(cott), small, full_rows, scale_in, seg_ids, grad_norm_gain, grad_out,
            width, q,
        )
        half_of = lambda value: lax.dynamic_slice_in_dim(
            value, tensor * (value.shape[-1] // 2), value.shape[-1] // 2, value.ndim - 1
        )
        bc_half = bc_width // 2
        away_bc = lax.dynamic_slice_in_dim(bc_sum, (1 - tensor) * bc_half, bc_half, 1)
        return (
            block_out,
            grad_in,
            half_of(sums[0]),
            grad_w_zx.transpose(1, 0, 2),
            grad_dt[:, :head_count],
            half_of(bc_sum) + lax.ppermute(away_bc, "tensor", [(0, 1), (1, 0)]),
            sums[2:7],
            half_of(sums[1, : 5 * bc_width].reshape(5, bc_width)),
            sums[9, :head_count],
            sums[9, 128 : 128 + head_count],
            sums[9, 256 : 256 + head_count],
            sums[8],
            grad_w_out.T,
        )
    else:
        over_dp = lambda value: lax.all_gather(value, "dp", axis=0, tiled=True)
        small = over_dp(small_shard)
        w_s, w_z, w_out_t = over_dp(w_zx[:, 1, :]), over_dp(w_zx[:, 0, :]), over_dp(w_out.T)
        rows_float = lax.all_gather(hidden_in, "tensor", axis=0, tiled=True).astype(F32)
        cot_rows = lax.all_gather(grad_out, "tensor", axis=0, tiled=True)
        scale_in = lax.rsqrt(jnp.mean(rows_float * rows_float, axis=1, keepdims=True) + EPS)
        normed = (rows_float * scale_in * prenorm_gain).astype(BF16)
        prep["bcraw"], prep["dt_in"], prep["dt"], prep["la"], prep["masks"] = prepare_plain(
            normed, small, bias, rate, flat_ids, q
        )
        s, y, states = scan_forward(normed, w_s, prep, conv_x, conv_bc, skip_lanes, width, q)
        z = dot(normed, w_z)
        gate_sig = sigmoid(z)
        gate = z * gate_sig
        v = y * gate
        grad_gated = dot(cot_rows, w_out_t)
        scaled_grad = grad_gated * norm_gain
        sums = jnp.stack([jnp.sum(v * v, axis=1), jnp.sum(scaled_grad * v, axis=1)])
        sums = lax.psum(sums, "tensor")
        scale_out = lax.rsqrt(sums[0] / inner_total + EPS)[:, None]
        pull = sums[1][:, None] * scale_out**3 / inner_total
        gated = (v * scale_out * norm_gain).astype(BF16)
        grad_norm_gain = jnp.sum(grad_gated * v * scale_out, axis=0)
        d_v = scaled_grad * scale_out - pull * v
        d_y = d_v * gate
        d_z = (d_v * y * gate_sig * (1.0 + z * (1.0 - gate_sig))).astype(BF16)
    tokens = normed.shape[0]

    d_s, grad_taps, d_small, low_bc, grad_taps_bc, grad_heads = scan_backward(
        s, d_y, prep, conv_x, conv_bc, skip_lanes, states, width, q
    )
    grad_d_skip = jnp.sum(grad_taps[5].reshape(head_count, width), axis=1)

    own_rows = tokens // tp
    rows_of = lambda array, i: lax.dynamic_slice_in_dim(array, i * own_rows, own_rows, 0)
    project = lambda i: dot(rows_of(gated, i), w_out_t, NT)
    prenorm_terms = []

    def grad_rows(i):
        columns = (
            dot(rows_of(d_z, i), w_z, NT)
            + dot(rows_of(d_s, i), w_s, NT)
            + dot(rows_of(d_small, i), small, NT)
            + dot(rows_of(low_bc, i), small[:, :bc_width], NT)
        )
        unit = rows_of(rows_float, i) * rows_of(scale_in, i)
        prenorm_terms.append(jnp.sum(columns * unit, axis=0))
        grad_unit = columns * prenorm_gain
        return rows_of(scale_in, i) * (
            grad_unit - unit * jnp.mean(grad_unit * unit, axis=1, keepdims=True)
        )

    products = [
        dot(cot_rows, gated, TN),
        dot(normed, d_z, TN),
        dot(normed, jnp.concatenate([d_s, d_small], axis=1), TN),
    ]
    every = lambda make: jnp.concatenate([make(i) for i in range(tp)], axis=0)
    onto = lambda value, dim: lax.psum_scatter(value, "tensor", scatter_dimension=dim, tiled=True)
    projected, own_grad = onto(every(project), 0), onto(every(grad_rows), 0)

    pieces = [
        sum(prenorm_terms),
        grad_taps_bc[:5].reshape(-1),
        grad_taps[:5].reshape(-1),
        grad_norm_gain,
        grad_heads[0],
        grad_heads[1],
        lanes_of(grad_d_skip),
    ]
    gap = -(pieces[0].shape[0] + pieces[1].shape[0]) % 1024
    pieces.insert(2, jnp.zeros((gap,), F32))
    x_rows = sum(piece.shape[0] for piece in pieces[:3]) // 128
    flat = jnp.concatenate(pieces)
    flat = jnp.pad(flat, (0, -flat.shape[0] % 1024)).reshape(-1, 128)
    half_of = lambda value: lax.dynamic_slice_in_dim(
        value, tensor * (value.shape[-1] // tp), value.shape[-1] // tp, value.ndim - 1
    )
    grad_w_out, grad_w_z, grad_last = [
        lax.psum_scatter(p, "dp", scatter_dimension=0, tiled=True) for p in products
    ]
    grad_w_bc = onto(grad_last[:, inner : inner + bc_width], 1)
    flat = lax.psum(flat, "dp")
    flat = jnp.concatenate([lax.psum(flat[:x_rows], "tensor"), flat[x_rows:]], axis=0)
    block_out = (hidden_in.astype(F32) + projected).astype(BF16)
    grad_in = (grad_out.astype(F32) + own_grad).astype(BF16)
    grad_w_zx = jnp.stack([grad_w_z, grad_last[:, :inner]], axis=1)
    grad_w_dt = grad_last[:, inner + bc_width : inner + bc_width + head_count]

    flat = flat.reshape(-1)
    at, cut_out = 0, []
    for piece in pieces:
        cut_out.append(flat[at : at + piece.shape[0]])
        at += piece.shape[0]
    return (
        block_out,
        grad_in,
        half_of(cut_out[0]),
        grad_w_zx,
        grad_w_dt,
        grad_w_bc,
        cut_out[3].reshape(5, inner),
        half_of(cut_out[1].reshape(5, bc_width)),
        cut_out[5][:head_count],
        cut_out[6][:head_count],
        cut_out[7][:head_count],
        cut_out[4],
        grad_w_out.T,
    )


def solution(mesh):
    in_specs = (
        P(("dp", "tensor"), None),
        P(),
        P("dp", None, "tensor"),
        P("dp", "tensor"),
        P("dp", None),
        P(None, "tensor"),
        P(),
        P("tensor"),
        P("tensor"),
        P("tensor"),
        P("tensor"),
        P("tensor", "dp"),
        P("dp", None),
        P(("dp", "tensor"), None),
    )
    out_specs = (
        P(("dp", "tensor"), None),
        P(("dp", "tensor"), None),
        P("tensor"),
        P("dp", None, "tensor"),
        P("dp", "tensor"),
        P("dp", "tensor"),
        P(None, "tensor"),
        P(None, "tensor"),
        P("tensor"),
        P("tensor"),
        P("tensor"),
        P("tensor"),
        P("tensor", "dp"),
    )
    return jax.shard_map(
        functools.partial(body, mesh.shape["dp"], mesh.shape["tensor"]),
        mesh=mesh,
        in_specs=in_specs,
        out_specs=out_specs,
        check_vma=False,
    )
```

```python
import functools

import jax
import jax.numpy as jnp
from jax import lax
from jax.experimental import pallas as pl
from jax.experimental.pallas import tpu as pltpu
from jax.sharding import PartitionSpec as P

BLOCK_LEN = 256
EPS = 1e-05
NEG = -1e30
F32 = jnp.float32
BF16 = jnp.bfloat16
HIGHEST = lax.Precision.HIGHEST
VMEM_LIMIT = 60 * 1024 * 1024


def dot(a, b, dims=((1,), (0,)), precision=None):
    return lax.dot_general(a, b, (dims, ((), ())), preferred_element_type=F32, precision=precision)


NN, NT, TN = ((1,), (0,)), ((1,), (1,)), ((0,), (0,))


def sigmoid(w):
    return 1.0 / (1.0 + jnp.exp(-w))


def conv_of(signal, taps, masks):
    out = taps[4:5, :] + taps[3:4, :] * signal
    for back in range(1, 4):
        out = out + taps[3 - back : 4 - back, :] * (
            pltpu.roll(signal, back, 0) * masks[:, back - 1 : back]
        )
    return out


def conv_back(grad, signal, taps, masks):
    rows = signal.shape[0]
    grad_signal = taps[3:4, :] * grad
    tap_rows = [None] * 5
    tap_rows[4] = jnp.sum(grad, axis=0, keepdims=True)
    tap_rows[3] = jnp.sum(grad * signal, axis=0, keepdims=True)
    for back in range(1, 4):
        kept = grad * masks[:, back - 1 : back]
        tap_rows[3 - back] = jnp.sum(kept * pltpu.roll(signal, back, 0), axis=0, keepdims=True)
        grad_signal = grad_signal + taps[3 - back : 4 - back, :] * pltpu.roll(kept, rows - back, 0)
    return grad_signal, tap_rows


def expand(columns, width):
    rows, heads = columns.shape
    lane = lax.broadcasted_iota(jnp.int32, (rows, 2 * width), 1)
    pieces = [
        jnp.where(lane < width, columns[:, h : h + 1], columns[:, h + 1 : h + 2])
        for h in range(0, heads, 2)
    ]
    return pieces[0] if len(pieces) == 1 else jnp.concatenate(pieces, axis=1)


def block_rows(block, size):
    return pl.ds(pl.multiple_of(block * size, size), size)


def head_lanes(array, step, heads):
    return pltpu.roll(array, lax.rem(128 - step * heads, 128), 1)


def block_tables(q, bcraw_ref, kbc_ref, msk_ref, segr_ref, bcc, mneg, cb):
    n = bcc.shape[1] // 2
    c = conv_of(bcraw_ref[...], kbc_ref[...], msk_ref[...])
    bcc[...] = c * sigmoid(c)
    later = lax.broadcasted_iota(jnp.int32, (q, q), 0) >= lax.broadcasted_iota(jnp.int32, (q, q), 1)

    def prepare(b, carry):
        rows = block_rows(b, q)
        same = msk_ref[rows, 5:6] == segr_ref[:, rows].astype(F32)
        mneg[rows, :] = jnp.where(later & same, 0.0, NEG)
        cb[rows, :] = dot(bcc[rows, n:], bcc[rows, :n], NT, HIGHEST)
        return carry

    lax.fori_loop(0, bcc.shape[0] // q, prepare, 0)


def fwd_group(
    q, heads, width, step, at, s, taps, skip, la_ref, dt_ref, msk_ref, s_ref, y_ref, st_ref,
    bcc, mneg, cb, xs, state, la4, lat4, dt4,
):
    tokens = s.shape[0]
    blocks = tokens // q
    n = bcc.shape[1] // 2
    lanes = heads * width
    la_here = head_lanes(la_ref[...], step, heads)
    la4[...] = la_here
    lat4[...] = la_here.T[0:8, :]
    dt4[...] = head_lanes(dt_ref[...], step, heads)
    s_ref[:, at] = s
    c = conv_of(s, taps, msk_ref[...])
    xs[...] = c * sigmoid(c)
    state[...] = jnp.zeros_like(state)
    lane_head = lax.broadcasted_iota(jnp.int32, (q, lanes), 1) // width

    def one_block(b, carry):
        rows = block_rows(b, q)
        x = xs[rows, :]
        la = la4[rows, 0:heads]
        u = x * expand(dt4[rows, 0:heads], width)
        ub = u.astype(BF16)
        enter = expand(jnp.exp(la) * msk_ref[rows, 3:4], width)
        last = expand(jnp.exp(la[q - 1 : q, :] - la) * msk_ref[rows, 4:5], width)
        st = state[...]
        st_ref[b, :, at] = st
        base = mneg[rows, :]
        cb_b = cb[rows, :]
        weights, values = [], []
        for h in range(heads):
            decay = jnp.exp(la[:, h : h + 1] - lat4[h : h + 1, rows] + base)
            weights.append((decay * cb_b).astype(BF16))
            values.append(jnp.where(lane_head == h, ub, jnp.zeros_like(ub)))
        local = dot(jnp.concatenate(weights, axis=1), jnp.concatenate(values, axis=0))
        carried = dot(bcc[rows, n:].astype(BF16), st.astype(BF16))
        y_ref[rows, at] = local + carried * enter + skip * x
        state[...] = st * enter[q - 1 : q, :] + dot(
            bcc[rows, :n].astype(BF16), (u * last).astype(BF16), TN
        )
        return carry

    lax.fori_loop(0, blocks, one_block, 0, unroll=blocks <= 2)


def fwd_kernel(
    q, heads, width,
    nm_ref, w_ref, bcraw_ref, kx_ref, kbc_ref, la_ref, dt_ref, msk_ref, segr_ref, dsk_ref,
    s_ref, y_ref, st_ref,
    bcc, mneg, cb, *scratch,
):
    step = pl.program_id(0)

    @pl.when(step == 0)
    def _():
        block_tables(q, bcraw_ref, kbc_ref, msk_ref, segr_ref, bcc, mneg, cb)

    s = dot(nm_ref[...], w_ref[...])
    fwd_group(
        q, heads, width, step, slice(None), s, kx_ref[...], dsk_ref[...], la_ref, dt_ref, msk_ref,
        s_ref, y_ref, st_ref, bcc, mneg, cb, *scratch,
    )


def bwd_tables(q, bcraw_ref, kbc_ref, msk_ref, segr_ref, bcc, mnegt, cbt, *zeroed):
    n = bcc.shape[1] // 2
    c = conv_of(bcraw_ref[...], kbc_ref[...], msk_ref[...])
    bcc[...] = c * sigmoid(c)
    for ref in zeroed:
        ref[...] = jnp.zeros_like(ref)
    earlier = lax.broadcasted_iota(jnp.int32, (q, q), 0) <= lax.broadcasted_iota(jnp.int32, (q, q), 1)

    def prepare(b, carry):
        rows = block_rows(b, q)
        same = msk_ref[rows, 5:6] == segr_ref[:, rows].astype(F32)
        mnegt[rows, :] = jnp.where(earlier & same, 0.0, NEG)
        cbt[rows, :] = dot(bcc[rows, :n], bcc[rows, n:], NT, HIGHEST)
        return carry

    lax.fori_loop(0, bcc.shape[0] // q, prepare, 0)


def bwd_group(
    q, heads, width, step,
    s_ref, dy_ref, kx_ref, la_ref, dt_ref, msk_ref, dsk_ref, st_ref, ds_ref, gk_ref,
    bcc, mnegt, cbt, xs, dxs, dtt, gt, la4, lat4, dt4, dla_acc, ddt_acc, dbc_acc,
    between=None,
):
    tokens = s_ref.shape[0]
    blocks = tokens // q
    n = bcc.shape[1] // 2
    lanes = heads * width
    la_here = head_lanes(la_ref[...], step, heads)
    la4[...] = la_here
    lat4[...] = la_here.T[0:8, :]
    dt4[...] = head_lanes(dt_ref[...], step, heads)
    c = conv_of(s_ref[...], kx_ref[...], msk_ref[...])
    xs[...] = c * sigmoid(c)
    gt[...] = jnp.zeros_like(gt)
    lane_head = lax.broadcasted_iota(jnp.int32, (q, lanes), 1) // width
    pick = jnp.where(
        lax.broadcasted_iota(jnp.int32, (8, lanes), 1) // width
        == lax.broadcasted_iota(jnp.int32, (8, lanes), 0),
        1.0,
        0.0,
    )
    token_lane = lax.broadcasted_iota(jnp.int32, (1, q), 1)
    col_lane = lax.broadcasted_iota(jnp.int32, (q, 128), 1)

    def one_block(i, carry):
        b = blocks - 1 - i
        rows = block_rows(b, q)
        x = xs[rows, :]
        dy = dy_ref[rows, :]
        la = la4[rows, 0:heads]
        dtx = expand(dt4[rows, 0:heads], width)
        u = x * dtx
        ub, dyb = u.astype(BF16), dy.astype(BF16)
        enter = expand(jnp.exp(la) * msk_ref[rows, 3:4], width)
        last = expand(jnp.exp(la[q - 1 : q, :] - la) * msk_ref[rows, 4:5], width)
        base = mnegt[rows, :]
        cb_b = cbt[rows, :]
        weights, values, row_sums = [], [], []
        d_cb = jnp.zeros((q, q), F32)
        col_sums = jnp.zeros((q, 128), F32)
        for h in range(heads):
            own = lane_head == h
            decay = jnp.exp(lat4[h : h + 1, rows] - la[:, h : h + 1] + base)
            dyh = jnp.where(own, dyb, jnp.zeros_like(dyb))
            pair = dot(ub, dyh, NT)
            weight = decay * cb_b
            d_cb = d_cb + decay * pair
            both = weight * pair
            row_sums.append(jnp.sum(both, axis=0, keepdims=True))
            col_sums = jnp.where(col_lane == h, jnp.sum(both, axis=1, keepdims=True), col_sums)
            weights.append(weight.astype(BF16))
            values.append(dyh)
        dtt[rows, :] += d_cb
        g = gt[...]
        gb16 = g.astype(BF16)
        st = st_ref[b]
        stb = st.astype(BF16)
        c16 = bcc[rows, n:].astype(BF16)
        b16 = bcc[rows, :n].astype(BF16)
        gb = dot(b16, gb16) * last
        du = dot(jnp.concatenate(weights, axis=1), jnp.concatenate(values, axis=0)) + gb
        dye = (dy * enter).astype(BF16)
        from_state = dot(c16, stb) * enter
        dbc_acc[rows, n:] += dot(dye, stb, NT)
        dbc_acc[rows, :n] += dot((u * last).astype(BF16), gb16, NT)
        ug = u * gb
        dla = dot(pick, dy * from_state - ug, NT, HIGHEST)
        ddt = dot(pick, x * du, NT, HIGHEST)
        tail = jnp.sum(ug, axis=0, keepdims=True) + enter[q - 1 : q, :] * jnp.sum(
            g * st, axis=0, keepdims=True
        )
        la_rows = []
        for h in range(heads):
            end = jnp.sum(jnp.where(lane_head[0:1, :] == h, tail, 0.0), axis=1, keepdims=True)
            la_rows.append(
                row_sums[h] + dla[h : h + 1, :] + jnp.where(token_lane == q - 1, end, 0.0)
            )
        dt_rows = [ddt[h : h + 1, :] for h in range(heads)]
        rest = jnp.zeros((128 - 2 * heads, q), F32)
        columns = jnp.concatenate(la_rows + dt_rows + [rest], axis=0).T
        la_part = jnp.where(col_lane < heads, columns, 0.0) - col_sums
        dt_part = jnp.where(col_lane >= heads, columns, 0.0)
        dla_acc[rows, :] += pltpu.roll(la_part, step * heads, 1)
        ddt_acc[rows, :] += pltpu.roll(dt_part, lax.rem(128 + (step - 1) * heads, 128), 1)
        gt[...] = g * enter[q - 1 : q, :] + dot(c16, dye, TN)
        dxs[rows, :] = dtx * du + dsk_ref[...] * dy
        return carry

    if between is None:
        lax.fori_loop(0, blocks, one_block, 0, unroll=blocks <= 2)
    else:
        for i in range(blocks):
            one_block(i, 0)
            between(i)

    s = s_ref[...]
    taps = kx_ref[...]
    masks = msk_ref[...]
    c = conv_of(s, taps, masks)
    sig = sigmoid(c)
    grad = dxs[...] * sig * (1.0 + c * (1.0 - sig))
    d_s, tap_rows = conv_back(grad, s, taps, masks)
    ds_ref[...] = d_s.astype(BF16)
    skip_row = jnp.sum(dy_ref[...] * xs[...], axis=0, keepdims=True)
    gk_ref[...] = jnp.concatenate(
        tap_rows + [skip_row, jnp.zeros_like(skip_row), jnp.zeros_like(skip_row)], axis=0
    )


def bwd_finish(
    q, bcraw_ref, kbc_ref, dt_ref, msk_ref, dtin_ref, rate_ref, small_ref, low_ref, gkbc_ref, ghead_ref,
    bcc, dtt, dla_acc, ddt_acc, dbc_acc,
):
    n = bcc.shape[1] // 2
    upper = jnp.where(
        lax.broadcasted_iota(jnp.int32, (q, q), 0) <= lax.broadcasted_iota(jnp.int32, (q, q), 1), 1.0, 0.0
    )

    def finish(b, carry):
        rows = block_rows(b, q)
        d_cb = dtt[rows, :]
        dbc_acc[rows, :n] += dot(d_cb, bcc[rows, n:], NN, HIGHEST)
        dbc_acc[rows, n:] += dot(d_cb, bcc[rows, :n], TN, HIGHEST)
        dla_acc[rows, :] = dot(upper, dla_acc[rows, :], NN, HIGHEST)
        return carry

    lax.fori_loop(0, bcc.shape[0] // q, finish, 0)
    rate = rate_ref[...]
    d_exponent = dla_acc[...]
    d_raw = (ddt_acc[...] + rate * d_exponent) * sigmoid(dtin_ref[...])
    d_rate = rate * jnp.sum(dt_ref[...] * d_exponent, axis=0, keepdims=True)
    d_bias = jnp.sum(d_raw, axis=0, keepdims=True)
    ghead_ref[...] = jnp.concatenate([d_bias, d_rate, jnp.zeros((6, 128), F32)], axis=0)
    raw = bcraw_ref[...]
    taps = kbc_ref[...]
    masks = msk_ref[...]
    c = conv_of(raw, taps, masks)
    sig = sigmoid(c)
    grad = dbc_acc[...] * sig * (1.0 + c * (1.0 - sig))
    d_bc, rows_bc = conv_back(grad, raw, taps, masks)
    high = d_bc.astype(BF16)
    small_ref[:, : 2 * n] = high
    small_ref[:, 2 * n : 2 * n + 128] = d_raw.astype(BF16)
    low_ref[...] = (d_bc - high.astype(F32)).astype(BF16)
    zero_row = jnp.zeros_like(rows_bc[0])
    gkbc_ref[...] = jnp.concatenate(rows_bc + [zero_row] * 3, axis=0)


def bwd_kernel(
    q, heads, width,
    s_ref, dy_ref, bcraw_ref, kx_ref, kbc_ref, la_ref, dt_ref, msk_ref, segr_ref, dsk_ref, st_ref, dtin_ref, rate_ref,
    ds_ref, gk_ref, small_ref, low_ref, gkbc_ref, ghead_ref,
    bcc, mnegt, cbt, xs, dxs, dtt, gt, la4, lat4, dt4, dla_acc, ddt_acc, dbc_acc,
):
    step = pl.program_id(0)

    @pl.when(step == 0)
    def _():
        bwd_tables(
            q, bcraw_ref, kbc_ref, msk_ref, segr_ref, bcc, mnegt, cbt, dtt, dbc_acc, dla_acc, ddt_acc
        )

    bwd_group(
        q, heads, width, step, s_ref, dy_ref, kx_ref, la_ref, dt_ref, msk_ref, dsk_ref, st_ref, ds_ref, gk_ref,
        bcc, mnegt, cbt, xs, dxs, dtt, gt, la4, lat4, dt4, dla_acc, ddt_acc, dbc_acc,
    )

    @pl.when(step == pl.num_programs(0) - 1)
    def _():
        bwd_finish(
            q, bcraw_ref, kbc_ref, dt_ref, msk_ref, dtin_ref, rate_ref, small_ref, low_ref, gkbc_ref, ghead_ref,
            bcc, dtt, dla_acc, ddt_acc, dbc_acc,
        )


def full(shape):
    return pl.BlockSpec(shape, lambda i: (0,) * len(shape))


def lane_block(rows, lanes):
    return pl.BlockSpec((rows, lanes), lambda i: (0, i))


def heads_per_step(head_count):
    return 4 if head_count % 4 == 0 else 2


def forward_scratch(tokens, q, n, lanes):
    return [
        pltpu.VMEM((tokens, 2 * n), F32), pltpu.VMEM((tokens, q), F32), pltpu.VMEM((tokens, q), F32),
        pltpu.VMEM((tokens, lanes), F32), pltpu.VMEM((n, lanes), F32), pltpu.VMEM((tokens, 128), F32),
        pltpu.VMEM((8, tokens), F32), pltpu.VMEM((tokens, 128), F32),
    ]


def scan_forward(normed, w_s, prep, conv_x, conv_bc, skip_lanes, width, q):
    bcraw, la, dt, masks, seg_row = (prep[k] for k in ("bcraw", "la", "dt", "masks", "seg_row"))
    tokens, depth = normed.shape
    inner = w_s.shape[1]
    head_count = inner // width
    heads = heads_per_step(head_count)
    lanes = heads * width
    n = bcraw.shape[1] // 2
    blocks = tokens // q
    return pl.pallas_call(
        functools.partial(fwd_kernel, q, heads, width),
        grid=(head_count // heads,),
        in_specs=[
            full((tokens, depth)), lane_block(depth, lanes), full((tokens, 2 * n)), lane_block(5, lanes),
            full((5, 2 * n)), full((tokens, 128)), full((tokens, 128)), full((tokens, 128)),
            full((1, tokens)), lane_block(1, lanes),
        ],
        out_specs=[
            lane_block(tokens, lanes), lane_block(tokens, lanes),
            pl.BlockSpec((blocks, n, lanes), lambda i: (0, 0, i)),
        ],
        out_shape=[
            jax.ShapeDtypeStruct((tokens, inner), F32), jax.ShapeDtypeStruct((tokens, inner), F32),
            jax.ShapeDtypeStruct((blocks, n, inner), F32),
        ],
        scratch_shapes=forward_scratch(tokens, q, n, lanes),
        compiler_params=pltpu.CompilerParams(
            dimension_semantics=("arbitrary",), vmem_limit_bytes=VMEM_LIMIT
        ),
        cost_estimate=pl.CostEstimate(
            flops=2 * tokens * inner * (depth + q + 4 * n),
            bytes_accessed=2 * (depth * inner + tokens * depth) + 8 * tokens * inner,
            transcendentals=tokens * q * head_count,
        ),
        name="scan_forward",
    )(normed, w_s, bcraw, conv_x, conv_bc, la, dt, masks, seg_row, skip_lanes)


def backward_scratch(tokens, q, n, lanes):
    return [
        pltpu.VMEM((tokens, 2 * n), F32), pltpu.VMEM((tokens, q), F32), pltpu.VMEM((tokens, q), F32),
        pltpu.VMEM((tokens, lanes), F32), pltpu.VMEM((tokens, lanes), F32), pltpu.VMEM((tokens, q), F32),
        pltpu.VMEM((n, lanes), F32), pltpu.VMEM((tokens, 128), F32), pltpu.VMEM((8, tokens), F32),
        pltpu.VMEM((tokens, 128), F32), pltpu.VMEM((tokens, 128), F32), pltpu.VMEM((tokens, 128), F32),
        pltpu.VMEM((tokens, 2 * n), F32),
    ]


def scan_backward(s, dy, prep, conv_x, conv_bc, skip_lanes, states, width, q):
    bcraw, la, dt, masks, seg_row = (prep[k] for k in ("bcraw", "la", "dt", "masks", "seg_row"))
    tokens, inner = s.shape
    head_count = inner // width
    heads = heads_per_step(head_count)
    lanes = heads * width
    n = bcraw.shape[1] // 2
    blocks = tokens // q
    return pl.pallas_call(
        functools.partial(bwd_kernel, q, heads, width),
        grid=(head_count // heads,),
        in_specs=[
            lane_block(tokens, lanes), lane_block(tokens, lanes), full((tokens, 2 * n)), lane_block(5, lanes),
            full((5, 2 * n)), full((tokens, 128)), full((tokens, 128)), full((tokens, 128)),
            full((1, tokens)), lane_block(1, lanes), pl.BlockSpec((blocks, n, lanes), lambda i: (0, 0, i)),
            full((tokens, 128)), full((1, 128)),
        ],
        out_specs=[
            lane_block(tokens, lanes), lane_block(8, lanes), full((tokens, 2 * n + 128)),
            full((tokens, 2 * n)), full((8, 2 * n)), full((8, 128)),
        ],
        out_shape=[
            jax.ShapeDtypeStruct((tokens, inner), BF16), jax.ShapeDtypeStruct((8, inner), F32),
            jax.ShapeDtypeStruct((tokens, 2 * n + 128), BF16), jax.ShapeDtypeStruct((tokens, 2 * n), BF16),
            jax.ShapeDtypeStruct((8, 2 * n), F32), jax.ShapeDtypeStruct((8, 128), F32),
        ],
        scratch_shapes=backward_scratch(tokens, q, n, lanes),
        compiler_params=pltpu.CompilerParams(
            dimension_semantics=("arbitrary",), vmem_limit_bytes=VMEM_LIMIT
        ),
        cost_estimate=pl.CostEstimate(
            flops=2 * tokens * inner * (8 * q + 8 * n),
            bytes_accessed=12 * tokens * inner,
            transcendentals=tokens * q * head_count,
        ),
        name="scan_backward",
    )(
        s, dy, bcraw, conv_x, conv_bc, la, dt, masks, seg_row, skip_lanes, states, prep["dt_in"], prep["rate"],
    )


MESH = pl.DeviceIdType.MESH


class Here:
    def __init__(self):
        self.me = lax.axis_index("dp")
        self.t = lax.axis_index("tensor")
        self.z = self.me // 4
        self.y = (self.me // 2) % 2
        self.c = self.me % 2

    def slot(self, z, y, c):
        return z * 4 + y * 2 + c

    def z_plus(self, d):
        return (self.z + d) % 4

    def owner(self, k):
        core = self.c if k < 8 else 1 - self.c
        return self.slot(k % 4, 1 - self.y if k % 8 < 4 else self.y, core)

    def at_z(self, d):
        return (self.slot(self.z_plus(d), self.y, self.c), self.t)

    def across_y(self):
        return (self.slot(self.z, 1 - self.y, self.c), self.t)

    def other_core(self):
        return (self.slot(self.z, self.y, 1 - self.c), self.t)

    def across_x(self):
        return (self.me, 1 - self.t)

    def greet(self):
        barrier = pltpu.get_barrier_semaphore()
        for peer in (self.at_z(1), self.at_z(2), self.at_z(3), self.across_y(), self.other_core(), self.across_x()):
            pl.semaphore_signal(barrier, inc=1, device_id=peer, device_id_type=MESH)
        pl.semaphore_wait(barrier, 6)


def send(src, dst, sems, index, peer):
    return pltpu.make_async_remote_copy(
        src_ref=src, dst_ref=dst, send_sem=sems.at[0, index], recv_sem=sems.at[1, index],
        device_id=peer, device_id_type=MESH,
    )


class Gather:
    COPIES = 27

    def __init__(self, here, src, dst, lanes, sems, local_sem):
        self.here, self.dst, self.lanes, self.sems = here, dst, lanes, sems
        self.src = src.at[:, lanes]
        self.local = pltpu.make_async_copy(self.src, self.at(here.me), local_sem)

    def at(self, slot):
        return self.dst.at[slot, :, self.lanes]

    def holds(self, i):
        z = self.here.z
        return z >= 0 if i == 0 else z >= i if i <= 3 else z + i - 3 <= 3

    def slot_of(self, i, far=False):
        here = self.here
        z = here.z - i if i <= 3 else here.z + i - 3
        return here.slot(z, 1 - here.y if far else here.y, here.c)

    def from_here(self, i, far=False):
        return self.src if i == 0 and not far else self.at(self.slot_of(i, far))

    def up(self, d):
        i = d - 1
        return send(self.from_here(i), self.at(self.slot_of(i)), self.sems, i, self.here.at_z(1))

    def down(self, d):
        i = d + 2 if d > 1 else 0
        return send(self.from_here(i), self.at(self.slot_of(i)), self.sems, 2 + d, self.here.at_z(3))

    def across(self, i):
        return send(self.from_here(i), self.at(self.slot_of(i)), self.sems, 6 + i, self.here.across_y())

    def to_core(self, k):
        i, far = k % 7, k >= 7
        src = self.from_here(i, far)
        return send(src, self.at(self.slot_of(i, far)), self.sems, 13 + k, self.here.other_core())

    def sends_up(self, d):
        return (self.here.z < 3) & (self.here.z >= d - 1)

    def sends_down(self, d):
        return (self.here.z > 0) & (self.here.z + d <= 4)

    def start_z(self):
        pl.when(self.sends_up(1))(lambda: self.up(1).start())
        pl.when(self.sends_down(1))(lambda: self.down(1).start())

    def start_y(self):
        self.across(0).start()
        self.to_core(0).start()
        self.local.start()

    def pass_z(self, *hops):
        for d in hops:

            @pl.when(self.holds(d))
            def _(d=d):
                self.up(d).wait_recv()
                if d < 3:
                    pl.when(self.here.z < 3)(lambda: self.up(d + 1).start())
                self.across(d).start()
                self.to_core(d).start()

            @pl.when(self.holds(3 + d))
            def _(d=d):
                self.down(d).wait_recv()
                if d < 3:
                    pl.when(self.here.z > 0)(lambda: self.down(d + 1).start())
                self.across(3 + d).start()
                self.to_core(3 + d).start()

    def pass_y(self):
        for i in range(7):

            @pl.when(self.holds(i))
            def _(i=i):
                self.across(i).wait_recv()
                self.to_core(7 + i).start()

    def arrived(self):
        self.local.wait()
        for k in range(14):
            pl.when(self.holds(k % 7))(lambda k=k: self.to_core(k).wait_recv())

    def sent(self):
        for d in (1, 2, 3):
            pl.when(self.sends_up(d))(lambda d=d: self.up(d).wait_send())
            pl.when(self.sends_down(d))(lambda d=d: self.down(d).wait_send())
        for i in range(7):
            pl.when(self.holds(i))(lambda i=i: self.across(i).wait_send())
        for k in range(14):
            pl.when(self.holds(k % 7))(lambda k=k: self.to_core(k).wait_send())


class GatherAcross:
    COPIES = 27

    def __init__(self, here, src, dst, lanes, sems, local_sem):
        self.here, self.sems, self.lanes, self.dst = here, sems, lanes, dst
        self.src = src.at[:, lanes]
        self.local = pltpu.make_async_copy(self.src, self.at(here.me), local_sem)

    holds = Gather.holds
    sends_up, sends_down = Gather.sends_up, Gather.sends_down

    def at(self, slot):
        return self.dst.at[slot, :, self.lanes]

    def slot_of(self, i, row):
        z = self.here.z - i if i <= 3 else self.here.z + i - 3
        return self.here.slot(z, 1 - self.here.y if row else self.here.y, self.here.c)

    def move(self, i, row, index, peer):
        slot = self.slot_of(i, row)
        src = self.src if i == 0 and not row else self.at(slot)
        return send(src, self.at(slot), self.sems, index, peer)

    def across(self):
        return self.move(0, 0, 0, self.here.across_y())

    def up(self, d, row):
        return self.move(d - 1, row, row * 3 + d, self.here.at_z(1))

    def down(self, d, row):
        return self.move(d + 2 if d > 1 else 0, row, 6 + row * 3 + d, self.here.at_z(3))

    def to_core(self, k):
        return self.move(k % 7, k // 7, 13 + k, self.here.other_core())

    def start_y(self):
        self.across().start()
        self.to_core(0).start()
        self.local.start()

    def start_z(self, row):
        pl.when(self.sends_up(1))(lambda: self.up(1, row).start())
        pl.when(self.sends_down(1))(lambda: self.down(1, row).start())

    def pass_y(self):
        self.across().wait_recv()
        self.start_z(1)
        self.to_core(7).start()

    def pass_z(self, d):
        for row in (0, 1):

            @pl.when(self.holds(d))
            def _(row=row):
                self.up(d, row).wait_recv()
                if d < 3:
                    pl.when(self.here.z < 3)(lambda: self.up(d + 1, row).start())
                self.to_core(row * 7 + d).start()

            @pl.when(self.holds(3 + d))
            def _(row=row):
                self.down(d, row).wait_recv()
                if d < 3:
                    pl.when(self.here.z > 0)(lambda: self.down(d + 1, row).start())
                self.to_core(row * 7 + 3 + d).start()

    def arrived(self):
        self.local.wait()
        for k in range(14):
            pl.when(self.holds(k % 7))(lambda k=k: self.to_core(k).wait_recv())

    def sent(self):
        self.across().wait_send()
        for d in (1, 2, 3):
            for row in (0, 1):
                pl.when(self.sends_up(d))(lambda d=d, row=row: self.up(d, row).wait_send())
                pl.when(self.sends_down(d))(lambda d=d, row=row: self.down(d, row).wait_send())
        for k in range(14):
            pl.when(self.holds(k % 7))(lambda k=k: self.to_core(k).wait_send())


def softplus(w):
    return jnp.maximum(w, 0.0) + jnp.log1p(jnp.exp(-jnp.abs(w)))


def forward_kernel(
    q, heads, width, inner_total,
    hid_ref, cot_ref, bc_ref, dt_t_ref, zx_ref, wo_ref, gain_in, ngain_in, heads_in, seg_ref, kx_ref, kbc_ref,
    rows_out, small_out, ws_out, wz_out, wo_out, s_out, normt_out, cott_out,
    scale_hbm, bcraw_hbm, dtin_hbm, dt_hbm, la_hbm, masks_hbm, st_hbm, dy_out, gated_out, dz_out, gngain_out, vec_ref,
    small_sems, ws_sems, wz_sems, wo_sems, wb_sems, x_sems, local_sems,
    rows_v, cot_v, small_v, ws_v, wz_v, wo_v, s_v, normed_v, y_v, z_v, dg_v, sum_v, sum_own, sum_came, normt_v, cott_v,
    dy_v, gated_v, dz_v, t_sems, out_sems,
    scale_out, bcraw_out, dtin_out, dt_out, la_out, masks_out, st_out, keep_sems, small_ref, square,
    bcc, mneg, cb, *group_scratch,
):
    here = Here()
    tokens = normed_v.shape[0]
    half = tokens // 2
    inner = y_v.shape[1]
    lanes = heads * width
    groups = inner // lanes
    here.greet()
    hidden = send(hid_ref, rows_v.at[here.t], x_sems, 0, here.across_x())
    cotangent = send(cot_ref, cot_v.at[here.t], x_sems, 1, here.across_x())
    sums_x = send(sum_own, sum_came, x_sems, 2, here.across_x())
    whole, first, second = pl.ds(0, inner), pl.ds(0, inner // 2), pl.ds(inner // 2, inner // 2)
    small = Gather(here, small_ref, small_v, pl.ds(0, small_ref.shape[1]), small_sems, local_sems.at[0])
    ws = Gather(here, zx_ref.at[1], ws_v, whole, ws_sems, local_sems.at[1])
    wz = Gather(here, zx_ref.at[0], wz_v, whole, wz_sems, local_sems.at[2])
    wo = Gather(here, wo_ref, wo_v, first, wo_sems, local_sems.at[3])
    wb = GatherAcross(here, wo_ref, wo_v, second, wb_sems, local_sems.at[12])
    gathers = [small, ws, wz, wo, wb]
    local = lambda src, dst, i: pltpu.make_async_copy(src, dst, local_sems.at[i])
    own_hidden = local(hid_ref, rows_v.at[here.t], 4)
    own_cot = local(cot_ref, cot_v.at[here.t], 5)
    store_ws, store_wz = local(ws_v, ws_out, 6), local(wz_v, wz_out, 7)
    store_wo = local(wo_v.at[:, :, first], wo_out.at[:, :, first], 8)
    store_wb = local(wo_v.at[:, :, second], wo_out.at[:, :, second], 13)
    store_rows, store_s = local(rows_v, rows_out, 9), local(s_v, s_out, 10)
    store_small = local(small_v, small_out, 11)
    keep = lambda src, dst, i: pltpu.make_async_copy(src, dst, keep_sems.at[i])
    keep_scale, keep_masks, keep_st = (
        keep(scale_out, scale_hbm, 0), keep(masks_out, masks_hbm, 1), keep(st_out, st_hbm, 2)
    )
    keep_prep = [
        keep(bcraw_out, bcraw_hbm, 3), keep(dtin_out, dtin_hbm, 4), keep(dt_out, dt_hbm, 5), keep(la_out, la_hbm, 6)
    ]

    def by_piece(src, dst, row):
        return [
            pltpu.make_async_copy(src.at[here.owner(k)], dst.at[k], t_sems.at[row, k]) for k in range(16)
        ]

    store_normt, store_cott = by_piece(normt_v, normt_out, 0), by_piece(cott_v, cott_out, 1)

    def turn(values, at, dst):
        shard_rows = dst.shape[1]
        flipped = values.astype(F32).T.astype(BF16)
        dst[pl.ds(at * (384 // shard_rows), 384 // shard_rows)] = flipped.reshape(
            384 // shard_rows, shard_rows, flipped.shape[1]
        )
    hidden.start()
    n_heads, shard_rows = dt_t_ref.shape
    square[...] = jnp.zeros_like(square)
    square[0:n_heads, 0:shard_rows] = dt_t_ref[...].astype(F32)
    bc_columns = bc_ref.shape[1]
    small_ref[:, 0:bc_columns] = bc_ref[...]
    small_ref[:, bc_columns : bc_columns + 128] = square[...].T[0:shard_rows, :].astype(BF16)
    vec_ref[...] = jnp.zeros_like(vec_ref)
    vec_ref[0:1, :] = gain_in[...]
    vec_ref[1:2, :] = ngain_in[...]
    head_of = lax.broadcasted_iota(jnp.int32, (128, inner), 1) // width
    spread = jnp.where(head_of == lax.broadcasted_iota(jnp.int32, (128, inner), 0), 1.0, 0.0)
    per_head = jnp.concatenate([heads_in[2:3, :], jnp.zeros((7, 128), F32)], axis=0)
    vec_ref[2:3, :] = dot(per_head, spread, NN, HIGHEST)[0:1, :]
    vec_ref[3:4, 0:128] = heads_in[0:1, :]
    vec_ref[3:4, 128:256] = -jnp.exp(heads_in[1:2, :])
    for gather in (small, ws):
        gather.start_z()
        gather.start_y()
    cotangent.start()
    own_hidden.start()
    own_cot.start()

    seg = jnp.broadcast_to(seg_ref[...].astype(F32), (128, tokens)).T
    row = lax.broadcasted_iota(jnp.int32, (tokens, 128), 0)
    lane = lax.broadcasted_iota(jnp.int32, (tokens, 128), 1)
    masks = jnp.where(lane == 5, seg, 0.0)
    for back in (1, 2, 3):
        same = (pltpu.roll(seg, back, 0) == seg) & (row >= back)
        masks = jnp.where((lane == back - 1) & same, 1.0, masks)
    for b in range(tokens // q):
        inside = (row >= b * q) & (row < (b + 1) * q)
        if b:
            carried = inside & (seg == seg[b * q - 1 : b * q, :])
            masks = jnp.where((lane == 3) & carried, 1.0, masks)
        run_last = inside & (seg == seg[(b + 1) * q - 1 : (b + 1) * q, :])
        masks = jnp.where((lane == 4) & run_last, 1.0, masks)
    masks_out[...] = masks
    keep_masks.start()

    small.pass_z(1, 2, 3)
    ws.pass_z(1, 2)
    wz.start_z()
    small.pass_y()
    own_hidden.wait()
    hidden.wait_recv()
    store_rows.start()
    gain = vec_ref[0:1, :]
    chunk = 64

    def norm(i, carry):
        side, at = i // (half // chunk), i % (half // chunk)
        rows = pl.ds(pl.multiple_of(at * chunk, chunk), chunk)
        values = rows_v[side, rows, :].astype(F32)
        scale = lax.rsqrt(jnp.mean(values * values, axis=1, keepdims=True) + EPS)
        out_rows = pl.ds(pl.multiple_of(i * chunk, chunk), chunk)
        normed_v[out_rows, :] = (values * scale * gain).astype(BF16)
        scale_out[out_rows, :] = jnp.broadcast_to(scale, (chunk, 128))
        return carry

    lax.fori_loop(0, tokens // chunk, norm, 0)
    keep_scale.start()
    ws.pass_z(3)
    wz.start_y()
    wb.start_y()
    wz.pass_z(1)
    small.arrived()
    store_small.start()
    pieces, shard, columns = small_v.shape
    proj = dot(normed_v[...], small_v[...].reshape(pieces * shard, columns))
    bc_width = columns - 128
    bcraw_out[...] = proj[:, :bc_width]
    dt_in = proj[:, bc_width:] + vec_ref[3:4, 0:128]
    dtin_out[...] = dt_in
    dt = softplus(dt_in)
    dt_out[...] = dt
    lower = jnp.where(
        lax.broadcasted_iota(jnp.int32, (q, q), 0) >= lax.broadcasted_iota(jnp.int32, (q, q), 1), 1.0, 0.0
    )
    exponent = dt * vec_ref[3:4, 128:256]
    for b in range(tokens // q):
        la_out[b * q : (b + 1) * q, :] = dot(lower, exponent[b * q : (b + 1) * q, :], NN, HIGHEST)
    for copy in keep_prep:
        copy.start()
    block_tables(q, bcraw_out, kbc_ref, masks_out, seg_ref, bcc, mneg, cb)
    wz.pass_z(2)
    wo.start_z()
    ws.pass_y()
    ws.arrived()
    store_ws.start()

    def weight_block(ref, at):
        return ref[:, :, at].reshape(pieces * shard, lanes)

    def lane_range(g):
        return pl.ds(pl.multiple_of(g * lanes, lanes), lanes)

    def scan_group(g, carry):
        @pl.when(g == 0)
        def _():
            wz.pass_z(3)
            wo.start_y()

        pl.when(g == 1)(lambda: wo.pass_z(1))

        @pl.when(g == 2)
        def _():
            wo.pass_z(2)
            wb.start_z(0)
            wb.pass_y()

        @pl.when(g == 4)
        def _():
            wo.pass_z(3)
            wb.pass_z(1)

        at = lane_range(g)
        s = dot(normed_v[...], weight_block(ws_v, at))
        fwd_group(
            q, heads, width, g, at, s, kx_ref[:, at], vec_ref[2:3, at], la_out, dt_out, masks_out,
            s_v, y_v, st_out, bcc, mneg, cb, *group_scratch,
        )
        return carry

    lax.fori_loop(0, groups, scan_group, 0)
    store_s.start()
    keep_st.start()
    wz.pass_y()
    wb.pass_z(2)

    def turn_normed(i, carry):
        turn(normed_v[:, pl.ds(pl.multiple_of(i * 384, 384), 384)], i, normt_v)
        return carry

    lax.fori_loop(0, normed_v.shape[1] // 384, turn_normed, 0)
    for copy in store_normt:
        copy.start()
    wz.arrived()
    store_wz.start()
    own_cot.wait()
    cotangent.wait_recv()

    def turn_cot(i, carry):
        turn(
            cot_v[:, :, pl.ds(pl.multiple_of(i * 384, 384), 384)].reshape(tokens, 384), i, cott_v
        )
        return carry

    lax.fori_loop(0, cot_v.shape[2] // 384, turn_cot, 0)
    for copy in store_cott:
        copy.start()
    sum_v[...] = jnp.zeros_like(sum_v)

    def gate_group(g, carry):
        at = lane_range(g)
        z = dot(normed_v[...], weight_block(wz_v, at))
        z_v[:, at] = z
        v = y_v[:, at] * (z * sigmoid(z))
        square = v * v
        for piece in range(lanes // 128):
            sum_v[0] += square[:, piece * 128 : (piece + 1) * 128]
        return carry

    lax.fori_loop(0, groups, gate_group, 0)
    wo.pass_y()
    wb.pass_z(3)
    wo.arrived()
    store_wo.start()

    def pull_group(g, carry):
        at = lane_range(g)
        side = cot_v[...].reshape(tokens, cot_v.shape[2])
        pulled = dot(side, weight_block(wo_v, at))
        dg_v[:, at] = pulled
        z = z_v[:, at]
        product = pulled * vec_ref[1:2, at] * (y_v[:, at] * (z * sigmoid(z)))
        for piece in range(lanes // 128):
            sum_v[1] += product[:, piece * 128 : (piece + 1) * 128]
        return carry

    lax.fori_loop(0, groups // 2, pull_group, 0)
    wb.arrived()
    store_wb.start()
    lax.fori_loop(groups // 2, groups, pull_group, 0)
    row_of = lambda array: jnp.sum(array.T, axis=0, keepdims=True)
    sum_own[...] = jnp.concatenate(
        [row_of(sum_v[0]), row_of(sum_v[1]), jnp.zeros((6, tokens), F32)], axis=0
    )
    sums_x.start()
    sums_x.wait_recv()
    both = sum_own[...] + sum_came[...]
    scale_row = lax.rsqrt(both[0:1, :] / inner_total + EPS)
    pull_row = both[1:2, :] * (scale_row * scale_row * scale_row) / inner_total
    column_of = lambda array: jnp.broadcast_to(array, (128, tokens)).T
    sum_v[0] = column_of(scale_row)
    sum_v[1] = column_of(pull_row)

    def grad_group(g, carry):
        at = lane_range(g)
        scale, pull = sum_v[0][:, 0:1], sum_v[1][:, 0:1]
        z, y, pulled = z_v[:, at], y_v[:, at], dg_v[:, at]
        sig = sigmoid(z)
        gate = z * sig
        v = y * gate
        unit = v * scale
        gngain_out[:, at] = jnp.sum(pulled * unit, axis=0, keepdims=True)
        gated_v[:, at] = (unit * vec_ref[1:2, at]).astype(BF16)
        d_v = pulled * vec_ref[1:2, at] * scale - pull * v
        dy_v[:, at] = d_v * gate
        dz_v[:, at] = (d_v * y * sig * (1.0 + z * (1.0 - sig))).astype(BF16)
        return carry

    def grad_out_copies(g):
        at = lane_range(g)
        return [
            pltpu.make_async_copy(src.at[:, at], dst.at[:, at], out_sems.at[i, g])
            for i, (src, dst) in enumerate([(dy_v, dy_out), (gated_v, gated_out), (dz_v, dz_out)])
        ]

    def grad_and_store(g, carry):
        grad_group(g, carry)
        for copy in grad_out_copies(g):
            copy.start()
        return carry

    lax.fori_loop(0, groups, grad_and_store, 0)
    for gather in gathers:
        gather.sent()

    def stored(g, carry):
        for copy in grad_out_copies(g):
            copy.wait()
        return carry

    lax.fori_loop(0, groups, stored, 0)
    for copy in (hidden, cotangent, sums_x):
        copy.wait_send()
    for copy in [store_rows, store_s, store_ws, store_wz, store_wo, store_wb, store_small, keep_scale, keep_masks, keep_st] + keep_prep + store_normt + store_cott:
        copy.wait()


def in_vmem():
    return pl.BlockSpec(memory_space=pltpu.VMEM)


def in_any():
    return pl.BlockSpec(memory_space=pl.ANY)


def forward_all(hidden, cot, bc, dt_t, zx, wo, gain, ngain, heads_in, seg_ids, conv_x, conv_bc, width, inner_total, q):
    half, depth = hidden.shape
    tokens = 2 * half
    shard, inner = zx.shape[1:]
    columns = bc.shape[1] + 128
    heads = heads_per_step(inner // width)
    lanes = heads * width
    n = (columns - 128) // 2
    blocks = tokens // q
    shape = jax.ShapeDtypeStruct
    sems = pltpu.SemaphoreType.DMA
    weight, rows = (16, shard, inner), (2, half, depth)
    per_head = shape((tokens, 128), F32)
    outs = pl.pallas_call(
        functools.partial(forward_kernel, q, heads, width, inner_total),
        in_specs=[in_vmem()] * 12,
        out_specs=[in_any()] * 18 + [in_vmem()] * 2,
        out_shape=[
            shape(rows, BF16), shape((16, shard, columns), BF16),
            shape(weight, BF16), shape(weight, BF16), shape(weight, BF16),
            shape((tokens, inner), F32), shape((16, shard, tokens), BF16), shape((16, shard, tokens), BF16),
            per_head, shape((tokens, columns - 128), F32), per_head, per_head, per_head, per_head,
            shape((blocks, n, inner), F32), shape((tokens, inner), F32), shape((tokens, inner), BF16),
            shape((tokens, inner), BF16), shape((1, inner), F32), shape((8, inner), F32),
        ],
        scratch_shapes=[sems((2, Gather.COPIES))] * 5 + [sems((2, 3)), sems((14,))]
        + [pltpu.VMEM(rows, BF16)] * 2 + [pltpu.VMEM((16, shard, columns), BF16)] + [pltpu.VMEM(weight, BF16)] * 3
        + [
            pltpu.VMEM((tokens, inner), F32), pltpu.VMEM((tokens, depth), BF16), pltpu.VMEM((tokens, inner), F32),
            pltpu.VMEM((tokens, inner), F32), pltpu.VMEM((tokens, inner), F32), pltpu.VMEM((2, tokens, 128), F32),
            pltpu.VMEM((8, tokens), F32), pltpu.VMEM((8, tokens), F32),
            pltpu.VMEM((16, shard, tokens), BF16), pltpu.VMEM((16, shard, tokens), BF16),
            pltpu.VMEM((tokens, inner), F32), pltpu.VMEM((tokens, inner), BF16), pltpu.VMEM((tokens, inner), BF16),
            sems((2, 16)), sems((3, inner // lanes)),
            pltpu.VMEM((tokens, 128), F32), pltpu.VMEM((tokens, columns - 128), F32),
        ]
        + [pltpu.VMEM((tokens, 128), F32)] * 4
        + [pltpu.VMEM((blocks, n, inner), F32), sems((7,)), pltpu.VMEM((shard, columns), BF16), pltpu.VMEM((128, 128), F32)]
        + forward_scratch(tokens, q, n, lanes),
        compiler_params=pltpu.CompilerParams(
            collective_id=0, has_side_effects=True, vmem_limit_bytes=VMEM_LIMIT
        ),
        name="forward_all",
    )(hidden, cot, bc, dt_t, zx, wo, gain, ngain, heads_in, seg_ids, conv_x, conv_bc)
    flat = lambda a: a.reshape((-1, a.shape[-1]))
    return [outs[0]] + [flat(a) for a in outs[1:14]] + list(outs[14:])


class Scatter:
    def __init__(self, here, own, away, from_core, from_y, from_z, core_sems, y_sems, z_sems, free):
        self.free, self.core_slots = free, from_core.shape[0]
        self.here, self.own, self.away = here, own, away
        self.from_core, self.from_y, self.from_z = from_core, from_y, from_z
        self.core_sems, self.y_sems, self.z_sems = core_sems, y_sems, z_sems

    def copy(self, src, dst, sems, i, peer):
        return pltpu.make_async_remote_copy(
            src_ref=src, dst_ref=dst, send_sem=sems[0].at[i], recv_sem=sems[1].at[i], device_id=peer,
            device_id_type=MESH,
        )

    def to_core(self, i):
        slot = i % self.away.shape[0]
        return self.copy(
            self.away.at[slot], self.from_core.at[i % self.core_slots], self.core_sems, i, self.here.other_core()
        )

    def across(self, i):
        return self.copy(
            self.own.at[i, pl.ds(0, 4)], self.from_y.at[i], self.y_sems, i, self.here.across_y()
        )

    def up(self, i, k):
        return self.copy(
            self.own.at[i, 4 + k], self.from_z.at[i, k - 1], self.z_sems, i * 6 + k - 1, self.here.at_z(1)
        )

    def down(self, i, k):
        slot = 3 + k if k < 2 else 0
        return self.copy(
            self.own.at[i, 4 + k], self.from_z.at[i, slot], self.z_sems, i * 6 + 3 + k, self.here.at_z(3)
        )

    def start(self, i, left_ref, right, reuse):
        pieces, rows, tokens = left_ref.shape
        half = pieces // 2
        pl.when(reuse)(lambda: self.to_core(jnp.maximum(i - self.away.shape[0], 0)).wait_send())
        make = lambda at: dot(
            left_ref[at : at + half].reshape(half * rows, tokens), right
        ).astype(BF16).reshape(half, rows, right.shape[1])
        self.away[i % self.away.shape[0]] = make(half)
        pl.when(i >= self.core_slots)(lambda: pl.semaphore_wait(self.free, 1))
        self.to_core(i).start()
        self.own[i] = make(0)

    def to_y(self, i):
        self.to_core(i).wait_recv()
        slot = i % self.core_slots
        add = lambda at: (self.own[i, at].astype(F32) + self.from_core[slot, at].astype(F32)).astype(BF16)
        self.own[i, 0:4] = add(slice(0, 4))
        self.across(i).start()
        self.own[i, 4:8] = add(slice(4, 8))

        @pl.when(i + self.core_slots < self.own.shape[0])
        def _():
            pl.semaphore_signal(
                self.free, inc=1, device_id=self.here.other_core(), device_id_type=MESH
            )

    def local_sum(self, i, k):
        return self.own[i, 4 + k].astype(F32) + self.from_y[i, k].astype(F32)

    def hop(self, i, h):
        z = self.here.z
        if h == 0:
            self.across(i).wait_recv()

        @pl.when(z == h)
        def _():
            for k in range(3, h, -1):
                total = self.local_sum(i, k)
                if h:
                    self.up(i, k).wait_recv()
                    total = total + self.from_z[i, k - 1].astype(F32)
                self.own[i, 4 + k] = total.astype(BF16)
                self.up(i, k).start()

        @pl.when(z == 3 - h)
        def _():
            for k in range(0, 3 - h):
                total = self.local_sum(i, k)
                if h:
                    self.down(i, k).wait_recv()
                    total = total + self.from_z[i, 3 + k if k < 2 else 0].astype(F32)
                self.own[i, 4 + k] = total.astype(BF16)
                self.down(i, k).start()

    def finish(self, i, store):
        for k in range(4):

            @pl.when(self.here.z == k)
            def _(k=k):
                total = self.local_sum(i, k)
                if k > 0:
                    self.up(i, k).wait_recv()
                    total = total + self.from_z[i, k - 1].astype(F32)
                if k < 3:
                    self.down(i, k).wait_recv()
                    total = total + self.from_z[i, 3 + k if k < 2 else 0].astype(F32)
                store(total)

    def sent(self, i, core):
        z = self.here.z
        pl.when(core)(lambda: self.to_core(i).wait_send())
        self.across(i).wait_send()
        for k in (1, 2, 3):
            pl.when(z < k)(lambda k=k: self.up(i, k).wait_send())
        for k in (0, 1, 2):
            pl.when(z > k)(lambda k=k: self.down(i, k).wait_send())


AWAY_SLOTS, CORE_SLOTS = 3, 6


def backward_kernel(
    q, heads, width,
    s_ref, dy_ref, ws_ref, wz_ref, wo_ref, kx_ref, veclanes_ref, st_ref,
    kbc_ref, segr_ref, vec_ref, gngain_ref,
    bcraw_hbm, la_hbm, dt_hbm, msk_hbm, normt_hbm, cott_hbm, gated_hbm, dz_hbm,
    dtin_hbm, small_w_hbm, rows_hbm, scale_hbm, cot_own_hbm,
    block_hbm, grad_in_hbm, gwo_hbm, gzx_hbm, gbc_hbm, gdt_hbm, sums_hbm,
    own, away, from_core, from_y, from_z,
    core_send, core_recv, y_send, y_recv, z_send, z_recv, free, x_sems, sum_sems,
    col, proj, x_send, x_came, sum_own, sum_came, ds_v, gk_v, small_v, low_v, gkbc_v, ghead_v,
    bcraw_ref, la_ref, dt_ref, msk_ref, normt_ref, cott_ref, gated_ref, dz_ref,
    dtin_ref, small_w_ref, rows_ref, scale_ref, cot_own_ref, load_sems,
    block_out, grad_in_out, gwo_out, gzx_out, gbc_out, gdt_out, sums_out, store_sems,
    bcc, mnegt, cbt, xs, dxs, dtt, gt, la4, lat4, dt4, dla_acc, ddt_acc, dbc_acc,
):
    here = Here()
    step = pl.program_id(0)
    tokens, lanes = s_ref.shape
    depth = col.shape[1]
    steps = gwo_out.shape[1] // lanes
    rate_ref, gain_ref = vec_ref.at[pl.ds(3, 1), pl.ds(128, 128)], vec_ref.at[pl.ds(0, 1)]
    dsk_ref = veclanes_ref.at[pl.ds(2, 1)]
    half = tokens // 2
    n2 = bcc.shape[1]
    scatter = Scatter(
        here, own, away, from_core, from_y, from_z, (core_send, core_recv), (y_send, y_recv), (z_send, z_recv), free
    )
    chunks = own.shape[0]
    core_sum = send(sum_own.at[0], sum_came.at[0], sum_sems, 0, here.other_core())
    y_sum = send(sum_own.at[1], sum_came.at[1], sum_sems, 1, here.across_y())
    z_sums = [send(sum_own.at[2], sum_came.at[1 + d], sum_sems, 1 + d, here.at_z(d)) for d in (1, 2, 3)]
    x_part = pl.ds(0, 8)
    x_sum = send(sum_own.at[3, x_part], sum_came.at[5, x_part], sum_sems, 5, here.across_x())
    pulled = send(x_send.at[1], x_came.at[1], x_sems, 0, here.across_x())

    def projected(g):
        at = pl.ds(pl.multiple_of(g * 256, 256), 256)
        return send(x_send.at[0, :, at], x_came.at[0, :, at], x_sems, 1 + g, here.across_x())

    load = lambda src, dst, i: pltpu.make_async_copy(src, dst, load_sems.at[i])
    loads = [
        load(src, dst, i)
        for i, (src, dst) in enumerate(
            [
                (gated_hbm, gated_ref), (cott_hbm, cott_ref), (dz_hbm, dz_ref), (normt_hbm, normt_ref),
                (bcraw_hbm, bcraw_ref), (la_hbm, la_ref), (dt_hbm, dt_ref), (msk_hbm, msk_ref),
                (dtin_hbm, dtin_ref), (small_w_hbm, small_w_ref), (rows_hbm, rows_ref), (scale_hbm, scale_ref),
                (cot_own_hbm, cot_own_ref),
            ]
        )
    ]
    stores = [
        pltpu.make_async_copy(src, dst, store_sems.at[i])
        for i, (src, dst) in enumerate(
            [
                (block_out, block_hbm), (grad_in_out, grad_in_hbm), (gwo_out, gwo_hbm), (gzx_out, gzx_hbm),
                (gbc_out, gbc_hbm), (gdt_out, gdt_hbm), (sums_out, sums_hbm),
            ]
        )
    ]
    at_lanes = pl.ds(pl.multiple_of(step * lanes, lanes), lanes)

    @pl.when(step == 0)
    def _():
        for copy in loads:
            copy.start()
        here.greet()
        for copy in loads[:8]:
            copy.wait()

    scatter.start(3 * step, cott_ref, gated_ref[:, at_lanes], step >= AWAY_SLOTS // 3)
    scatter.start(3 * step + 1, normt_ref, dz_ref[:, at_lanes], step >= AWAY_SLOTS // 3)

    @pl.when(step == 0)
    def _():
        bwd_tables(
            q, bcraw_ref, kbc_ref, msk_ref, segr_ref, bcc, mnegt, cbt, dtt, dbc_acc, dla_acc, ddt_acc
        )
        col[...] = jnp.zeros_like(col)

    def store_at(kind, g):
        at = pl.ds(pl.multiple_of(g * lanes, lanes), lanes)

        def store(total):
            if kind == 0:
                gwo_out[:, at] = total
            else:
                gzx_out[:, kind - 1, at] = total

        return store

    def small_store(i):
        def store(total):
            if i == 0:
                gbc_out[...] = total
            else:
                rest = jnp.zeros((128 - total.shape[0], 128), F32)
                gdt_out[...] = jnp.concatenate([total[:, 0:128], rest], axis=0).T[:, 0 : total.shape[0]]

        return store

    def tick(base, j):
        drain = isinstance(base, int)
        for back, act in ((8, None), (7, 2), (5, 1), (3, 0)):
            kind, turn = (j - back) % 3, (j - back) // 3
            g = base + turn
            if drain:
                c = 3 * g + kind
                if c >= chunks:
                    continue
                if act is None:
                    scatter.finish(c, small_store(c - (chunks - 2)) if c >= chunks - 2 else store_at(kind, g))
                else:
                    scatter.hop(c, act)
            else:

                @pl.when(g >= 0)
                def _(act=act, kind=kind, g=jnp.maximum(g, 0)):
                    if act is None:
                        scatter.finish(3 * g + kind, store_at(kind, g))
                    else:
                        scatter.hop(3 * g + kind, act)

    scatter.to_y(3 * step)
    tick(step, 0)
    own_half = pl.ds(pl.multiple_of(here.t * half, half), half)
    away_half = pl.ds(pl.multiple_of((1 - here.t) * half, half), half)
    at_columns = pl.ds(pl.multiple_of(step * 256, 256), 256)
    x_send[0, :, at_columns] = dot(gated_ref[away_half, :], wo_ref[...], NT).astype(BF16)
    projected(step).start()
    proj[:, at_columns] = dot(gated_ref[own_half, :], wo_ref[...], NT)
    col[:, at_columns] += dot(dz_ref[...], wz_ref[...], NT)

    def between(i):
        if i == 0:
            scatter.to_y(3 * step + 1)
            tick(step, 1)

    bwd_group(
        q, heads, width, step, s_ref, dy_ref, kx_ref, la_ref, dt_ref, msk_ref, dsk_ref, st_ref, ds_v, gk_v,
        bcc, mnegt, cbt, xs, dxs, dtt, gt, la4, lat4, dt4, dla_acc, ddt_acc, dbc_acc, between,
    )
    scatter.start(3 * step + 2, normt_ref, ds_v[...], step >= AWAY_SLOTS // 3)
    sum_own[0, 2:8, at_lanes] = gk_v[0:6, :]

    def column_block(j):
        return pl.ds(pl.multiple_of(j * 256, 256), 256)

    def accumulate(j, carry):
        at = column_block(j)
        col[:, at] += dot(ds_v[...], ws_ref[at, :], NT)
        return carry

    lax.fori_loop(0, depth // 256, accumulate, 0)
    scatter.to_y(3 * step + 2)
    tick(step, 2)

    @pl.when(step == steps - 1)
    def _():
        chunk = 32

        def by_chunks(act):
            def one(i, carry):
                at = pl.multiple_of(i * chunk, chunk)
                own_at = pl.multiple_of(here.t * half + i * chunk, chunk)
                away_at = pl.multiple_of((1 - here.t) * half + i * chunk, chunk)
                act(pl.ds(at, chunk), pl.ds(own_at, chunk), pl.ds(away_at, chunk))
                return carry

            lax.fori_loop(0, half // chunk, one, 0)

        for copy in loads[8:]:
            copy.wait()
        small_v[:, n2 + 128 :] = jnp.zeros_like(small_v[:, n2 + 128 :])
        bwd_finish(
            q, bcraw_ref, kbc_ref, dt_ref, msk_ref, dtin_ref, rate_ref, small_v, low_v, gkbc_v, ghead_v,
            bcc, dtt, dla_acc, ddt_acc, dbc_acc,
        )
        for i in range(2):
            scatter.start(3 * steps + i, normt_ref, small_v[:, i * lanes : (i + 1) * lanes], steps > 0)
        tick(steps, 0)
        for i in range(2):
            scatter.to_y(3 * steps + i)

        def small_part(j, carry):
            at = column_block(j)
            col[:, at] += dot(small_v[:, : n2 + 128], small_w_ref[at, :], NT) + dot(
                low_v[...], small_w_ref[at, 0:n2], NT
            )
            return carry

        lax.fori_loop(0, depth // 256, small_part, 0)
        tick(steps, 1)
        gain = gain_ref[...]

        def norm_back(side, store):
            def one(i, total):
                inside = pl.ds(pl.multiple_of(i * chunk, chunk), chunk)
                rows = pl.ds(pl.multiple_of(side * half + i * chunk, chunk), chunk)
                columns = col[rows, :]
                scale = scale_ref[rows, 0:1]
                unit = rows_ref[side, inside, :].astype(F32) * scale
                grad_unit = columns * gain
                store(
                    rows, inside,
                    scale * (grad_unit - unit * jnp.mean(grad_unit * unit, axis=1, keepdims=True)),
                )
                return total + jnp.sum(columns * unit, axis=0, keepdims=True)

            return one

        def to_send(rows, inside, value):
            x_send[1, inside, :] = value.astype(BF16)

        def to_keep(rows, inside, value):
            col[rows, :] = value

        prenorm = lax.fori_loop(
            0, half // chunk, norm_back(1 - here.t, to_send), jnp.zeros((1, depth), F32)
        )
        pulled.start()
        prenorm = lax.fori_loop(0, half // chunk, norm_back(here.t, to_keep), prenorm)
        sum_own[0, 0:1, :] = prenorm
        sum_own[0, 1:2, :] = jnp.zeros((1, depth), F32)
        for r in range(5):
            sum_own[0, 1:2, r * n2 : (r + 1) * n2] = gkbc_v[r : r + 1, :]
        sum_own[0, 8:9, :] = gngain_ref[...]
        sum_own[0, 9:16, :] = jnp.zeros((7, depth), F32)
        sum_own[0, 9:10, 0:128] = ghead_v[0:1, :]
        sum_own[0, 9:10, 128:256] = ghead_v[1:2, :]
        head_of = lax.broadcasted_iota(jnp.int32, (128, depth), 1) // width
        pick = jnp.where(head_of == lax.broadcasted_iota(jnp.int32, (128, depth), 0), 1.0, 0.0)
        sum_own[0, 9:10, 256:384] = dot(sum_own[0, 0:8, :], pick, NT, HIGHEST)[7:8, :]
        core_sum.start()
        tick(steps, 2)
        core_sum.wait_recv()
        sum_own[1] = sum_own[0] + sum_came[0]
        y_sum.start()
        tick(steps, 3)
        tick(steps, 4)
        y_sum.wait_recv()
        sum_own[2] = sum_own[1] + sum_came[1]
        for copy in z_sums:
            copy.start()
        tick(steps, 5)
        tick(steps, 6)
        for copy in z_sums:
            copy.wait_recv()
        sum_own[3] = sum_own[2] + sum_came[2] + sum_came[3] + sum_came[4]
        x_sum.start()
        tick(steps, 7)
        tick(steps, 8)

        def arrived_projected(g, carry):
            projected(g).wait_recv()
            return carry

        lax.fori_loop(0, steps, arrived_projected, 0)

        def put_block_out(rows, own_rows, away_rows):
            block_out[rows, :] = (
                rows_ref[here.t, rows, :].astype(F32) + proj[rows, :] + x_came[0, rows, :].astype(F32)
            ).astype(BF16)

        by_chunks(put_block_out)
        stores[0].start()
        pulled.wait_recv()

        def put_grad_in(rows, own_rows, away_rows):
            grad_in_out[rows, :] = (
                cot_own_ref[rows, :].astype(F32) + col[own_rows, :] + x_came[1, rows, :].astype(F32)
            ).astype(BF16)

        by_chunks(put_grad_in)
        stores[1].start()
        for copy in stores[2:5]:
            copy.start()
        x_sum.wait_recv()
        sums_out[...] = sum_own[3]
        sums_out[0:2, :] = sum_own[3, 0:2, :] + sum_came[5, 0:2, :]
        stores[6].start()
        tick(steps, 9)
        stores[5].start()

        def all_sent(i, carry):
            scatter.sent(i, i >= chunks - AWAY_SLOTS)
            return carry

        lax.fori_loop(0, chunks, all_sent, 0)

        def sent_projected(g, carry):
            projected(g).wait_send()
            return carry

        lax.fori_loop(0, steps, sent_projected, 0)
        for copy in [core_sum, y_sum, x_sum, pulled] + z_sums:
            copy.wait_send()
        for copy in stores:
            copy.wait()


def backward_all(
    s, dy, gated, dz, w_s, w_z, w_out_t, conv_x, vectors, states, prep, conv_bc,
    normt, cott, small, rows, scale, seg_ids, gngain, cot_own, width, q,
):
    tokens, inner = s.shape
    depth = w_s.shape[0]
    half = tokens // 2
    heads = heads_per_step(inner // width)
    lanes = heads * width
    groups = inner // lanes
    n2 = prep["bcraw"].shape[1]
    n, blocks, shard = n2 // 2, tokens // q, depth // 16
    chunks = 3 * groups + 2
    shape = jax.ShapeDtypeStruct
    sems = pltpu.SemaphoreType.DMA
    once = lambda array: pl.BlockSpec(
        array.shape, lambda i: (0,) * array.ndim, pipeline_mode=pl.Buffered(1)
    )
    constants = [conv_bc, seg_ids, vectors, gngain]
    loaded = [
        prep["bcraw"], prep["la"], prep["dt"], prep["masks"], normt, cott, gated, dz,
        prep["dt_in"], small, rows, scale, cot_own,
    ]
    like = lambda array: pltpu.VMEM(array.shape, array.dtype)
    row_block = pl.BlockSpec((depth // groups, inner), lambda i: (i, 0))
    out_shape = [
        shape((half, depth), BF16), shape((half, depth), BF16), shape((shard, inner), F32),
        shape((shard, 2, inner), F32), shape((shard, lanes), F32), shape((128, shard), F32), shape((16, depth), F32),
    ]
    pieces = lambda count, per: pltpu.VMEM((count, per, shard, lanes), BF16)
    return pl.pallas_call(
        functools.partial(backward_kernel, q, heads, width),
        grid=(groups,),
        in_specs=[lane_block(tokens, lanes)] * 2 + [lane_block(depth, lanes), row_block, row_block]
        + [lane_block(5, lanes), lane_block(8, lanes), pl.BlockSpec((blocks, n, lanes), lambda i: (0, 0, i))]
        + [once(array) for array in constants] + [in_any()] * len(loaded),
        out_specs=[in_any()] * len(out_shape),
        out_shape=out_shape,
        scratch_shapes=[pieces(chunks, 8), pieces(AWAY_SLOTS, 8), pieces(CORE_SLOTS, 8), pieces(chunks, 4), pieces(chunks, 5)]
        + [sems((chunks,))] * 4 + [sems((6 * chunks,))] * 2 + [pltpu.SemaphoreType.REGULAR, sems((2, 1 + groups)), sems((2, 6))]
        + [
            pltpu.VMEM((tokens, depth), F32), pltpu.VMEM((half, depth), F32), pltpu.VMEM((2, half, depth), BF16),
            pltpu.VMEM((2, half, depth), BF16), pltpu.VMEM((4, 16, depth), F32), pltpu.VMEM((6, 16, depth), F32),
            pltpu.VMEM((tokens, lanes), BF16), pltpu.VMEM((8, lanes), F32), pltpu.VMEM((tokens, 2 * lanes), BF16),
            pltpu.VMEM((tokens, n2), BF16), pltpu.VMEM((8, n2), F32), pltpu.VMEM((8, 128), F32),
        ]
        + [like(array) for array in loaded] + [sems((len(loaded),))]
        + [like(array) for array in out_shape] + [sems((len(out_shape),))]
        + backward_scratch(tokens, q, n, lanes),
        compiler_params=pltpu.CompilerParams(
            dimension_semantics=("arbitrary",), collective_id=1, has_side_effects=True,
            vmem_limit_bytes=67043328,
        ),
        name="backward_all",
    )(s, dy, w_s, w_z, w_out_t, conv_x, vectors, states, *constants, *loaded)


def lanes_of(per_head):
    return jnp.pad(per_head, [(0, 0)] * (per_head.ndim - 1) + [(0, 128 - per_head.shape[-1])])


def prepare_plain(normed, small, bias, rate, flat_ids, q):
    tokens = normed.shape[0]
    blocks = tokens // q
    proj = dot(normed, small)
    bc_width = small.shape[1] - 128
    dt_in = proj[:, bc_width:] + bias
    dt = jax.nn.softplus(dt_in)
    lower = jnp.where(jnp.arange(q)[:, None] >= jnp.arange(q)[None, :], 1.0, 0.0)
    la = jnp.einsum("ij,bjh->bih", lower, (dt * rate).reshape(blocks, q, 128), precision=HIGHEST)
    shifted = lambda l: jnp.concatenate([jnp.full((l,), -1, jnp.int32), flat_ids[:-l]])
    by_block = flat_ids.reshape(blocks, q)
    before = jnp.concatenate([jnp.full((1,), -1, jnp.int32), by_block[:-1, -1]])
    carried = (by_block == before[:, None]).reshape(-1)
    run_last = (by_block == by_block[:, -1:]).reshape(-1)
    masks = [flat_ids == shifted(1), flat_ids == shifted(2), flat_ids == shifted(3), carried, run_last, flat_ids]
    return proj[:, :bc_width], dt_in, dt, la.reshape(tokens, 128), lanes_of(jnp.stack(masks, axis=1).astype(F32))


def body(
    dp,
    tp,
    hidden_in,
    prenorm_gain,
    w_zx,
    w_dt,
    w_bc,
    conv_x,
    conv_bc,
    dt_bias,
    a_log,
    d_skip,
    norm_gain,
    w_out,
    seg_ids,
    grad_out,
):
    q = BLOCK_LEN
    staged = dp == 16 and tp == 2 and seg_ids.shape[0] == 1 and hidden_in.shape[1] == w_out.shape[0]
    inner = w_out.shape[0]
    head_count = dt_bias.shape[0]
    width = inner // head_count
    bc_width = w_bc.shape[1]
    shard = w_bc.shape[0]
    depth = hidden_in.shape[1]
    inner_total = inner * tp
    tensor = lax.axis_index("tensor")

    bias = lanes_of(dt_bias)[None, :]
    rate = lanes_of(-jnp.exp(a_log))[None, :]
    small_shard = jnp.concatenate([w_bc, lanes_of(w_dt)], axis=1)
    flat_ids = (seg_ids + seg_ids.shape[1] * lax.broadcasted_iota(jnp.int32, seg_ids.shape, 0)).reshape(-1)
    seg_row = flat_ids.astype(F32)[None, :]
    skip_lanes = jnp.repeat(d_skip, width)[None, :]
    prep = dict(rate=rate, seg_row=seg_row)

    if staged:
        heads_in = lanes_of(jnp.stack([dt_bias, a_log, d_skip]))
        (
            full_rows, small, w_s, w_z, w_out_t, s, normt, cott, scale_in,
            prep["bcraw"], prep["dt_in"], prep["dt"], prep["la"], prep["masks"],
            states, d_y, gated, d_z, grad_norm_gain, vectors,
        ) = forward_all(
            hidden_in, grad_out, w_bc, w_dt.T, w_zx.transpose(1, 0, 2), w_out.T, prenorm_gain[None, :], norm_gain[None, :],
            heads_in, seg_ids, conv_x, conv_bc,
            width, inner_total, q,
        )
        split = lambda array: array.reshape(16, shard, array.shape[1])
        block_out, grad_in, grad_w_out, grad_w_zx, bc_sum, grad_dt, sums = backward_all(
            s, d_y, gated, d_z, w_s, w_z, w_out_t, conv_x, vectors, states, prep, conv_bc,
            split(normt), split(cott), small, full_rows, scale_in, seg_ids, grad_norm_gain, grad_out,
            width, q,
        )
        half_of = lambda value: lax.dynamic_slice_in_dim(
            value, tensor * (value.shape[-1] // 2), value.shape[-1] // 2, value.ndim - 1
        )
        bc_half = bc_width // 2
        away_bc = lax.dynamic_slice_in_dim(bc_sum, (1 - tensor) * bc_half, bc_half, 1)
        return (
            block_out,
            grad_in,
            half_of(sums[0]),
            grad_w_zx,
            grad_dt[:head_count].T,
            half_of(bc_sum) + lax.ppermute(away_bc, "tensor", [(0, 1), (1, 0)]),
            sums[2:7],
            half_of(sums[1, : 5 * bc_width].reshape(5, bc_width)),
            sums[9, :head_count],
            sums[9, 128 : 128 + head_count],
            sums[9, 256 : 256 + head_count],
            sums[8],
            grad_w_out.T,
        )
    else:
        over_dp = lambda value: lax.all_gather(value, "dp", axis=0, tiled=True)
        small = over_dp(small_shard)
        w_s, w_z, w_out_t = over_dp(w_zx[:, 1, :]), over_dp(w_zx[:, 0, :]), over_dp(w_out.T)
        rows_float = lax.all_gather(hidden_in, "tensor", axis=0, tiled=True).astype(F32)
        cot_rows = lax.all_gather(grad_out, "tensor", axis=0, tiled=True)
        scale_in = lax.rsqrt(jnp.mean(rows_float * rows_float, axis=1, keepdims=True) + EPS)
        normed = (rows_float * scale_in * prenorm_gain).astype(BF16)
        prep["bcraw"], prep["dt_in"], prep["dt"], prep["la"], prep["masks"] = prepare_plain(
            normed, small, bias, rate, flat_ids, q
        )
        s, y, states = scan_forward(normed, w_s, prep, conv_x, conv_bc, skip_lanes, width, q)
        z = dot(normed, w_z)
        gate_sig = sigmoid(z)
        gate = z * gate_sig
        v = y * gate
        grad_gated = dot(cot_rows, w_out_t)
        scaled_grad = grad_gated * norm_gain
        sums = jnp.stack([jnp.sum(v * v, axis=1), jnp.sum(scaled_grad * v, axis=1)])
        sums = lax.psum(sums, "tensor")
        scale_out = lax.rsqrt(sums[0] / inner_total + EPS)[:, None]
        pull = sums[1][:, None] * scale_out**3 / inner_total
        gated = (v * scale_out * norm_gain).astype(BF16)
        grad_norm_gain = jnp.sum(grad_gated * v * scale_out, axis=0)
        d_v = scaled_grad * scale_out - pull * v
        d_y = d_v * gate
        d_z = (d_v * y * gate_sig * (1.0 + z * (1.0 - gate_sig))).astype(BF16)
    tokens = normed.shape[0]

    d_s, grad_taps, d_small, low_bc, grad_taps_bc, grad_heads = scan_backward(
        s, d_y, prep, conv_x, conv_bc, skip_lanes, states, width, q
    )
    grad_d_skip = jnp.sum(grad_taps[5].reshape(head_count, width), axis=1)

    own_rows = tokens // tp
    rows_of = lambda array, i: lax.dynamic_slice_in_dim(array, i * own_rows, own_rows, 0)
    project = lambda i: dot(rows_of(gated, i), w_out_t, NT)
    prenorm_terms = []

    def grad_rows(i):
        columns = (
            dot(rows_of(d_z, i), w_z, NT)
            + dot(rows_of(d_s, i), w_s, NT)
            + dot(rows_of(d_small, i), small, NT)
            + dot(rows_of(low_bc, i), small[:, :bc_width], NT)
        )
        unit = rows_of(rows_float, i) * rows_of(scale_in, i)
        prenorm_terms.append(jnp.sum(columns * unit, axis=0))
        grad_unit = columns * prenorm_gain
        return rows_of(scale_in, i) * (
            grad_unit - unit * jnp.mean(grad_unit * unit, axis=1, keepdims=True)
        )

    products = [
        dot(cot_rows, gated, TN),
        dot(normed, d_z, TN),
        dot(normed, jnp.concatenate([d_s, d_small], axis=1), TN),
    ]
    every = lambda make: jnp.concatenate([make(i) for i in range(tp)], axis=0)
    onto = lambda value, dim: lax.psum_scatter(value, "tensor", scatter_dimension=dim, tiled=True)
    projected, own_grad = onto(every(project), 0), onto(every(grad_rows), 0)

    pieces = [
        sum(prenorm_terms),
        grad_taps_bc[:5].reshape(-1),
        grad_taps[:5].reshape(-1),
        grad_norm_gain,
        grad_heads[0],
        grad_heads[1],
        lanes_of(grad_d_skip),
    ]
    gap = -(pieces[0].shape[0] + pieces[1].shape[0]) % 1024
    pieces.insert(2, jnp.zeros((gap,), F32))
    x_rows = sum(piece.shape[0] for piece in pieces[:3]) // 128
    flat = jnp.concatenate(pieces)
    flat = jnp.pad(flat, (0, -flat.shape[0] % 1024)).reshape(-1, 128)
    half_of = lambda value: lax.dynamic_slice_in_dim(
        value, tensor * (value.shape[-1] // tp), value.shape[-1] // tp, value.ndim - 1
    )
    grad_w_out, grad_w_z, grad_last = [
        lax.psum_scatter(p, "dp", scatter_dimension=0, tiled=True) for p in products
    ]
    grad_w_bc = onto(grad_last[:, inner : inner + bc_width], 1)
    flat = lax.psum(flat, "dp")
    flat = jnp.concatenate([lax.psum(flat[:x_rows], "tensor"), flat[x_rows:]], axis=0)
    block_out = (hidden_in.astype(F32) + projected).astype(BF16)
    grad_in = (grad_out.astype(F32) + own_grad).astype(BF16)
    grad_w_zx = jnp.stack([grad_w_z, grad_last[:, :inner]], axis=1)
    grad_w_dt = grad_last[:, inner + bc_width : inner + bc_width + head_count]

    flat = flat.reshape(-1)
    at, cut_out = 0, []
    for piece in pieces:
        cut_out.append(flat[at : at + piece.shape[0]])
        at += piece.shape[0]
    return (
        block_out,
        grad_in,
        half_of(cut_out[0]),
        grad_w_zx,
        grad_w_dt,
        grad_w_bc,
        cut_out[3].reshape(5, inner),
        half_of(cut_out[1].reshape(5, bc_width)),
        cut_out[5][:head_count],
        cut_out[6][:head_count],
        cut_out[7][:head_count],
        cut_out[4],
        grad_w_out.T,
    )


def solution(mesh):
    in_specs = (
        P(("dp", "tensor"), None),
        P(),
        P("dp", None, "tensor"),
        P("dp", "tensor"),
        P("dp", None),
        P(None, "tensor"),
        P(),
        P("tensor"),
        P("tensor"),
        P("tensor"),
        P("tensor"),
        P("tensor", "dp"),
        P("dp", None),
        P(("dp", "tensor"), None),
    )
    out_specs = (
        P(("dp", "tensor"), None),
        P(("dp", "tensor"), None),
        P("tensor"),
        P("dp", None, "tensor"),
        P("dp", "tensor"),
        P("dp", "tensor"),
        P(None, "tensor"),
        P(None, "tensor"),
        P("tensor"),
        P("tensor"),
        P("tensor"),
        P("tensor"),
        P("tensor", "dp"),
    )
    return jax.shard_map(
        functools.partial(body, mesh.shape["dp"], mesh.shape["tensor"]),
        mesh=mesh,
        in_specs=in_specs,
        out_specs=out_specs,
        check_vma=False,
    )
```

```python
import functools

import jax
import jax.numpy as jnp
from jax import lax
from jax.experimental import pallas as pl
from jax.experimental.pallas import tpu as pltpu
from jax.sharding import PartitionSpec as P

BLOCK_LEN = 256
EPS = 1e-05
NEG = -1e30
F32 = jnp.float32
BF16 = jnp.bfloat16
HIGHEST = lax.Precision.HIGHEST
VMEM_LIMIT = 60 * 1024 * 1024


def dot(a, b, dims=((1,), (0,)), precision=None):
    return lax.dot_general(a, b, (dims, ((), ())), preferred_element_type=F32, precision=precision)


NN, NT, TN = ((1,), (0,)), ((1,), (1,)), ((0,), (0,))


def sigmoid(w):
    return 1.0 / (1.0 + jnp.exp(-w))


def conv_of(signal, taps, masks):
    out = taps[4:5, :] + taps[3:4, :] * signal
    for back in range(1, 4):
        out = out + taps[3 - back : 4 - back, :] * (
            pltpu.roll(signal, back, 0) * masks[:, back - 1 : back]
        )
    return out


def conv_back(grad, signal, taps, masks):
    rows = signal.shape[0]
    grad_signal = taps[3:4, :] * grad
    tap_rows = [None] * 5
    tap_rows[4] = jnp.sum(grad, axis=0, keepdims=True)
    tap_rows[3] = jnp.sum(grad * signal, axis=0, keepdims=True)
    for back in range(1, 4):
        kept = grad * masks[:, back - 1 : back]
        tap_rows[3 - back] = jnp.sum(kept * pltpu.roll(signal, back, 0), axis=0, keepdims=True)
        grad_signal = grad_signal + taps[3 - back : 4 - back, :] * pltpu.roll(kept, rows - back, 0)
    return grad_signal, tap_rows


def exact_dot(values, picks):
    high = values.astype(BF16)
    low = (values - high.astype(F32)).astype(BF16)
    return dot(high, picks) + dot(low, picks)


def head_picks(lanes, width):
    head = lax.broadcasted_iota(jnp.int32, (lanes, 128), 0) // width
    return jnp.where(head == lax.broadcasted_iota(jnp.int32, (lanes, 128), 1), 1.0, 0.0).astype(BF16)


def expand(columns, width):
    rows, heads = columns.shape
    lane = lax.broadcasted_iota(jnp.int32, (rows, 2 * width), 1)
    pieces = [
        jnp.where(lane < width, columns[:, h : h + 1], columns[:, h + 1 : h + 2])
        for h in range(0, heads, 2)
    ]
    return pieces[0] if len(pieces) == 1 else jnp.concatenate(pieces, axis=1)


def block_rows(block, size):
    return pl.ds(pl.multiple_of(block * size, size), size)


def head_lanes(array, step, heads):
    return pltpu.roll(array, lax.rem(128 - step * heads, 128), 1)


def block_tables(q, bcraw_ref, kbc_ref, msk_ref, segr_ref, bcc, mneg, cb):
    n = bcc.shape[1] // 2
    c = conv_of(bcraw_ref[...], kbc_ref[...], msk_ref[...])
    bcc[...] = c * sigmoid(c)
    later = lax.broadcasted_iota(jnp.int32, (q, q), 0) >= lax.broadcasted_iota(jnp.int32, (q, q), 1)

    def prepare(b, carry):
        rows = block_rows(b, q)
        same = msk_ref[rows, 5:6] == segr_ref[:, rows].astype(F32)
        mneg[rows, :] = jnp.where(later & same, 0.0, NEG)
        cb[rows, :] = dot(bcc[rows, n:], bcc[rows, :n], NT, HIGHEST)
        return carry

    lax.fori_loop(0, bcc.shape[0] // q, prepare, 0)


def fwd_group(
    q, heads, width, step, at, s, taps, skip, la_ref, dt_ref, msk_ref, s_ref, y_ref, st_ref,
    bcc, mneg, cb, xs, state, la4, lat4, dt4,
):
    tokens = s.shape[0]
    blocks = tokens // q
    n = bcc.shape[1] // 2
    lanes = heads * width
    la_here = head_lanes(la_ref[...], step, heads)
    la4[...] = la_here
    lat4[...] = la_here.T[0:8, :]
    dt4[...] = head_lanes(dt_ref[...], step, heads)
    s_ref[:, at] = s
    c = conv_of(s, taps, msk_ref[...])
    xs[...] = c * sigmoid(c)
    state[...] = jnp.zeros_like(state)
    lane_head = lax.broadcasted_iota(jnp.int32, (q, lanes), 1) // width

    def one_block(b, carry):
        rows = block_rows(b, q)
        x = xs[rows, :]
        la = la4[rows, 0:heads]
        u = x * expand(dt4[rows, 0:heads], width)
        ub = u.astype(BF16)
        enter = expand(jnp.exp(la) * msk_ref[rows, 3:4], width)
        last = expand(jnp.exp(la[q - 1 : q, :] - la) * msk_ref[rows, 4:5], width)
        st = state[...]
        st_ref[b, :, at] = st
        base = mneg[rows, :]
        cb_b = cb[rows, :]
        weights, values = [], []
        for h in range(heads):
            decay = jnp.exp(la[:, h : h + 1] - lat4[h : h + 1, rows] + base)
            weights.append((decay * cb_b).astype(BF16))
            values.append(jnp.where(lane_head == h, ub, jnp.zeros_like(ub)))
        local = dot(jnp.concatenate(weights, axis=1), jnp.concatenate(values, axis=0))
        carried = dot(bcc[rows, n:].astype(BF16), st.astype(BF16))
        y_ref[rows, at] = local + carried * enter + skip * x
        state[...] = st * enter[q - 1 : q, :] + dot(
            bcc[rows, :n].astype(BF16), (u * last).astype(BF16), TN
        )
        return carry

    lax.fori_loop(0, blocks, one_block, 0, unroll=blocks <= 2)


def fwd_kernel(
    q, heads, width,
    nm_ref, w_ref, bcraw_ref, kx_ref, kbc_ref, la_ref, dt_ref, msk_ref, segr_ref, dsk_ref,
    s_ref, y_ref, st_ref,
    bcc, mneg, cb, *scratch,
):
    step = pl.program_id(0)

    @pl.when(step == 0)
    def _():
        block_tables(q, bcraw_ref, kbc_ref, msk_ref, segr_ref, bcc, mneg, cb)

    s = dot(nm_ref[...], w_ref[...])
    fwd_group(
        q, heads, width, step, slice(None), s, kx_ref[...], dsk_ref[...], la_ref, dt_ref, msk_ref,
        s_ref, y_ref, st_ref, bcc, mneg, cb, *scratch,
    )


def bwd_tables(q, bcraw_ref, kbc_ref, msk_ref, segr_ref, bcc, mnegt, cbt, *zeroed):
    n = bcc.shape[1] // 2
    c = conv_of(bcraw_ref[...], kbc_ref[...], msk_ref[...])
    bcc[...] = c * sigmoid(c)
    for ref in zeroed:
        ref[...] = jnp.zeros_like(ref)
    earlier = lax.broadcasted_iota(jnp.int32, (q, q), 0) <= lax.broadcasted_iota(jnp.int32, (q, q), 1)

    def prepare(b, carry):
        rows = block_rows(b, q)
        same = msk_ref[rows, 5:6] == segr_ref[:, rows].astype(F32)
        mnegt[rows, :] = jnp.where(earlier & same, 0.0, NEG)
        cbt[rows, :] = dot(bcc[rows, :n], bcc[rows, n:], NT, HIGHEST)
        return carry

    lax.fori_loop(0, bcc.shape[0] // q, prepare, 0)


def bwd_group(
    q, heads, width, step,
    s_ref, dy_ref, kx_ref, la_ref, dt_ref, msk_ref, dsk_ref, st_ref, ds_ref, gk_ref,
    bcc, mnegt, cbt, xs, dxs, dtt, gt, la4, lat4, dt4, dla_acc, ddt_acc, dbc_acc,
    between=None,
):
    tokens = s_ref.shape[0]
    blocks = tokens // q
    n = bcc.shape[1] // 2
    lanes = heads * width
    la_here = head_lanes(la_ref[...], step, heads)
    la4[...] = la_here
    lat4[...] = la_here.T[0:8, :]
    dt4[...] = head_lanes(dt_ref[...], step, heads)
    c = conv_of(s_ref[...], kx_ref[...], msk_ref[...])
    xs[...] = c * sigmoid(c)
    gt[...] = jnp.zeros_like(gt)
    lane_head = lax.broadcasted_iota(jnp.int32, (q, lanes), 1) // width
    picks = head_picks(lanes, width)
    token_lane = lax.broadcasted_iota(jnp.int32, (1, q), 1)
    col_lane = lax.broadcasted_iota(jnp.int32, (q, 128), 1)

    def one_block(i, carry):
        b = blocks - 1 - i
        rows = block_rows(b, q)
        x = xs[rows, :]
        dy = dy_ref[rows, :]
        la = la4[rows, 0:heads]
        dtx = expand(dt4[rows, 0:heads], width)
        u = x * dtx
        ub, dyb = u.astype(BF16), dy.astype(BF16)
        enter = expand(jnp.exp(la) * msk_ref[rows, 3:4], width)
        last = expand(jnp.exp(la[q - 1 : q, :] - la) * msk_ref[rows, 4:5], width)
        base = mnegt[rows, :]
        cb_b = cbt[rows, :]
        weights, values, row_sums = [], [], []
        d_cb = jnp.zeros((q, q), F32)
        col_sums = jnp.zeros((q, 128), F32)
        for h in range(heads):
            own = lane_head == h
            decay = jnp.exp(lat4[h : h + 1, rows] - la[:, h : h + 1] + base)
            dyh = jnp.where(own, dyb, jnp.zeros_like(dyb))
            pair = dot(ub, dyh, NT)
            weight = decay * cb_b
            d_cb = d_cb + decay * pair
            both = weight * pair
            row_sums.append(jnp.sum(both, axis=0, keepdims=True))
            col_sums = jnp.where(col_lane == h, jnp.sum(both, axis=1, keepdims=True), col_sums)
            weights.append(weight.astype(BF16))
            values.append(dyh)
        dtt[rows, :] += d_cb
        g = gt[...]
        gb16 = g.astype(BF16)
        st = st_ref[b]
        stb = st.astype(BF16)
        c16 = bcc[rows, n:].astype(BF16)
        b16 = bcc[rows, :n].astype(BF16)
        gb = dot(b16, gb16) * last
        du = dot(jnp.concatenate(weights, axis=1), jnp.concatenate(values, axis=0)) + gb
        dye = (dy * enter).astype(BF16)
        from_state = dot(c16, stb) * enter
        dbc_acc[rows, n:] += dot(dye, stb, NT)
        dbc_acc[rows, :n] += dot((u * last).astype(BF16), gb16, NT)
        ug = u * gb
        tail = jnp.sum(ug, axis=0, keepdims=True) + enter[q - 1 : q, :] * jnp.sum(
            g * st, axis=0, keepdims=True
        )
        la_rows = []
        for h in range(heads):
            end = jnp.sum(jnp.where(lane_head[0:1, :] == h, tail, 0.0), axis=1, keepdims=True)
            la_rows.append(row_sums[h] + jnp.where(token_lane == q - 1, end, 0.0))
        rest = jnp.zeros((128 - heads, q), F32)
        columns = jnp.concatenate(la_rows + [rest], axis=0).T
        la_part = columns + exact_dot(dy * from_state - ug, picks) - col_sums
        dla_acc[rows, :] += pltpu.roll(la_part, step * heads, 1)
        ddt_acc[rows, :] += pltpu.roll(exact_dot(x * du, picks), step * heads, 1)
        gt[...] = g * enter[q - 1 : q, :] + dot(c16, dye, TN)
        dxs[rows, :] = dtx * du + dsk_ref[...] * dy
        return carry

    if between is None:
        lax.fori_loop(0, blocks, one_block, 0, unroll=blocks <= 2)
    else:
        for i in range(blocks):
            one_block(i, 0)
            between(i)

    s = s_ref[...]
    taps = kx_ref[...]
    masks = msk_ref[...]
    c = conv_of(s, taps, masks)
    sig = sigmoid(c)
    grad = dxs[...] * sig * (1.0 + c * (1.0 - sig))
    d_s, tap_rows = conv_back(grad, s, taps, masks)
    ds_ref[...] = d_s.astype(BF16)
    skip_row = jnp.sum(dy_ref[...] * xs[...], axis=0, keepdims=True)
    gk_ref[...] = jnp.concatenate(
        tap_rows + [skip_row, jnp.zeros_like(skip_row), jnp.zeros_like(skip_row)], axis=0
    )


def bwd_finish(
    q, bcraw_ref, kbc_ref, dt_ref, msk_ref, dtin_ref, rate_ref, small_ref, low_ref, gkbc_ref, ghead_ref,
    bcc, dtt, dla_acc, ddt_acc, dbc_acc,
):
    n = bcc.shape[1] // 2
    upper = jnp.where(
        lax.broadcasted_iota(jnp.int32, (q, q), 0) <= lax.broadcasted_iota(jnp.int32, (q, q), 1), 1.0, 0.0
    ).astype(BF16)

    def finish(b, carry):
        rows = block_rows(b, q)
        d_cb = dtt[rows, :]
        high = d_cb.astype(BF16)
        low = (d_cb - high.astype(F32)).astype(BF16)
        c_part, b_part = bcc[rows, n:], bcc[rows, :n]
        c_high, b_high = c_part.astype(BF16), b_part.astype(BF16)
        c_low = (c_part - c_high.astype(F32)).astype(BF16)
        b_low = (b_part - b_high.astype(F32)).astype(BF16)
        dbc_acc[rows, :n] += dot(high, c_high) + dot(low, c_high) + dot(high, c_low)
        dbc_acc[rows, n:] += dot(high, b_high, TN) + dot(low, b_high, TN) + dot(high, b_low, TN)
        terms = dla_acc[rows, :]
        high = terms.astype(BF16)
        rest = terms - high.astype(F32)
        middle = rest.astype(BF16)
        low = (rest - middle.astype(F32)).astype(BF16)
        dla_acc[rows, :] = dot(upper, high) + dot(upper, middle) + dot(upper, low)
        return carry

    lax.fori_loop(0, bcc.shape[0] // q, finish, 0)
    rate = rate_ref[...]
    d_exponent = dla_acc[...]
    d_raw = (ddt_acc[...] + rate * d_exponent) * sigmoid(dtin_ref[...])
    d_rate = rate * jnp.sum(dt_ref[...] * d_exponent, axis=0, keepdims=True)
    d_bias = jnp.sum(d_raw, axis=0, keepdims=True)
    ghead_ref[...] = jnp.concatenate([d_bias, d_rate, jnp.zeros((6, 128), F32)], axis=0)
    raw = bcraw_ref[...]
    taps = kbc_ref[...]
    masks = msk_ref[...]
    c = conv_of(raw, taps, masks)
    sig = sigmoid(c)
    grad = dbc_acc[...] * sig * (1.0 + c * (1.0 - sig))
    d_bc, rows_bc = conv_back(grad, raw, taps, masks)
    high = d_bc.astype(BF16)
    small_ref[:, : 2 * n] = high
    small_ref[:, 2 * n : 2 * n + 128] = d_raw.astype(BF16)
    low_ref[...] = (d_bc - high.astype(F32)).astype(BF16)
    zero_row = jnp.zeros_like(rows_bc[0])
    gkbc_ref[...] = jnp.concatenate(rows_bc + [zero_row] * 3, axis=0)


def bwd_kernel(
    q, heads, width,
    s_ref, dy_ref, bcraw_ref, kx_ref, kbc_ref, la_ref, dt_ref, msk_ref, segr_ref, dsk_ref, st_ref, dtin_ref, rate_ref,
    ds_ref, gk_ref, small_ref, low_ref, gkbc_ref, ghead_ref,
    bcc, mnegt, cbt, xs, dxs, dtt, gt, la4, lat4, dt4, dla_acc, ddt_acc, dbc_acc,
):
    step = pl.program_id(0)

    @pl.when(step == 0)
    def _():
        bwd_tables(
            q, bcraw_ref, kbc_ref, msk_ref, segr_ref, bcc, mnegt, cbt, dtt, dbc_acc, dla_acc, ddt_acc
        )

    bwd_group(
        q, heads, width, step, s_ref, dy_ref, kx_ref, la_ref, dt_ref, msk_ref, dsk_ref, st_ref, ds_ref, gk_ref,
        bcc, mnegt, cbt, xs, dxs, dtt, gt, la4, lat4, dt4, dla_acc, ddt_acc, dbc_acc,
    )

    @pl.when(step == pl.num_programs(0) - 1)
    def _():
        bwd_finish(
            q, bcraw_ref, kbc_ref, dt_ref, msk_ref, dtin_ref, rate_ref, small_ref, low_ref, gkbc_ref, ghead_ref,
            bcc, dtt, dla_acc, ddt_acc, dbc_acc,
        )


def full(shape):
    return pl.BlockSpec(shape, lambda i: (0,) * len(shape))


def lane_block(rows, lanes):
    return pl.BlockSpec((rows, lanes), lambda i: (0, i))


def heads_per_step(head_count):
    return 4 if head_count % 4 == 0 else 2


def forward_scratch(tokens, q, n, lanes):
    return [
        pltpu.VMEM((tokens, 2 * n), F32), pltpu.VMEM((tokens, q), F32), pltpu.VMEM((tokens, q), F32),
        pltpu.VMEM((tokens, lanes), F32), pltpu.VMEM((n, lanes), F32), pltpu.VMEM((tokens, 128), F32),
        pltpu.VMEM((8, tokens), F32), pltpu.VMEM((tokens, 128), F32),
    ]


def scan_forward(normed, w_s, prep, conv_x, conv_bc, skip_lanes, width, q):
    bcraw, la, dt, masks, seg_row = (prep[k] for k in ("bcraw", "la", "dt", "masks", "seg_row"))
    tokens, depth = normed.shape
    inner = w_s.shape[1]
    head_count = inner // width
    heads = heads_per_step(head_count)
    lanes = heads * width
    n = bcraw.shape[1] // 2
    blocks = tokens // q
    return pl.pallas_call(
        functools.partial(fwd_kernel, q, heads, width),
        grid=(head_count // heads,),
        in_specs=[
            full((tokens, depth)), lane_block(depth, lanes), full((tokens, 2 * n)), lane_block(5, lanes),
            full((5, 2 * n)), full((tokens, 128)), full((tokens, 128)), full((tokens, 128)),
            full((1, tokens)), lane_block(1, lanes),
        ],
        out_specs=[
            lane_block(tokens, lanes), lane_block(tokens, lanes),
            pl.BlockSpec((blocks, n, lanes), lambda i: (0, 0, i)),
        ],
        out_shape=[
            jax.ShapeDtypeStruct((tokens, inner), F32), jax.ShapeDtypeStruct((tokens, inner), F32),
            jax.ShapeDtypeStruct((blocks, n, inner), F32),
        ],
        scratch_shapes=forward_scratch(tokens, q, n, lanes),
        compiler_params=pltpu.CompilerParams(
            dimension_semantics=("arbitrary",), vmem_limit_bytes=VMEM_LIMIT
        ),
        cost_estimate=pl.CostEstimate(
            flops=2 * tokens * inner * (depth + q + 4 * n),
            bytes_accessed=2 * (depth * inner + tokens * depth) + 8 * tokens * inner,
            transcendentals=tokens * q * head_count,
        ),
        name="scan_forward",
    )(normed, w_s, bcraw, conv_x, conv_bc, la, dt, masks, seg_row, skip_lanes)


def backward_scratch(tokens, q, n, lanes):
    return [
        pltpu.VMEM((tokens, 2 * n), F32), pltpu.VMEM((tokens, q), F32), pltpu.VMEM((tokens, q), F32),
        pltpu.VMEM((tokens, lanes), F32), pltpu.VMEM((tokens, lanes), F32), pltpu.VMEM((tokens, q), F32),
        pltpu.VMEM((n, lanes), F32), pltpu.VMEM((tokens, 128), F32), pltpu.VMEM((8, tokens), F32),
        pltpu.VMEM((tokens, 128), F32), pltpu.VMEM((tokens, 128), F32), pltpu.VMEM((tokens, 128), F32),
        pltpu.VMEM((tokens, 2 * n), F32),
    ]


def scan_backward(s, dy, prep, conv_x, conv_bc, skip_lanes, states, width, q):
    bcraw, la, dt, masks, seg_row = (prep[k] for k in ("bcraw", "la", "dt", "masks", "seg_row"))
    tokens, inner = s.shape
    head_count = inner // width
    heads = heads_per_step(head_count)
    lanes = heads * width
    n = bcraw.shape[1] // 2
    blocks = tokens // q
    return pl.pallas_call(
        functools.partial(bwd_kernel, q, heads, width),
        grid=(head_count // heads,),
        in_specs=[
            lane_block(tokens, lanes), lane_block(tokens, lanes), full((tokens, 2 * n)), lane_block(5, lanes),
            full((5, 2 * n)), full((tokens, 128)), full((tokens, 128)), full((tokens, 128)),
            full((1, tokens)), lane_block(1, lanes), pl.BlockSpec((blocks, n, lanes), lambda i: (0, 0, i)),
            full((tokens, 128)), full((1, 128)),
        ],
        out_specs=[
            lane_block(tokens, lanes), lane_block(8, lanes), full((tokens, 2 * n + 128)),
            full((tokens, 2 * n)), full((8, 2 * n)), full((8, 128)),
        ],
        out_shape=[
            jax.ShapeDtypeStruct((tokens, inner), BF16), jax.ShapeDtypeStruct((8, inner), F32),
            jax.ShapeDtypeStruct((tokens, 2 * n + 128), BF16), jax.ShapeDtypeStruct((tokens, 2 * n), BF16),
            jax.ShapeDtypeStruct((8, 2 * n), F32), jax.ShapeDtypeStruct((8, 128), F32),
        ],
        scratch_shapes=backward_scratch(tokens, q, n, lanes),
        compiler_params=pltpu.CompilerParams(
            dimension_semantics=("arbitrary",), vmem_limit_bytes=VMEM_LIMIT
        ),
        cost_estimate=pl.CostEstimate(
            flops=2 * tokens * inner * (8 * q + 8 * n),
            bytes_accessed=12 * tokens * inner,
            transcendentals=tokens * q * head_count,
        ),
        name="scan_backward",
    )(
        s, dy, bcraw, conv_x, conv_bc, la, dt, masks, seg_row, skip_lanes, states, prep["dt_in"], prep["rate"],
    )


MESH = pl.DeviceIdType.MESH


class Here:
    def __init__(self):
        self.me = lax.axis_index("dp")
        self.t = lax.axis_index("tensor")
        self.z = self.me // 4
        self.y = (self.me // 2) % 2
        self.c = self.me % 2

    def slot(self, z, y, c):
        return z * 4 + y * 2 + c

    def z_plus(self, d):
        return (self.z + d) % 4

    def owner(self, k):
        core = self.c if k < 8 else 1 - self.c
        return self.slot(k % 4, 1 - self.y if k % 8 < 4 else self.y, core)

    def at_z(self, d):
        return (self.slot(self.z_plus(d), self.y, self.c), self.t)

    def across_y(self):
        return (self.slot(self.z, 1 - self.y, self.c), self.t)

    def other_core(self):
        return (self.slot(self.z, self.y, 1 - self.c), self.t)

    def across_x(self):
        return (self.me, 1 - self.t)

    def greet(self):
        barrier = pltpu.get_barrier_semaphore()
        for peer in (self.at_z(1), self.at_z(2), self.at_z(3), self.across_y(), self.other_core(), self.across_x()):
            pl.semaphore_signal(barrier, inc=1, device_id=peer, device_id_type=MESH)
        pl.semaphore_wait(barrier, 6)


def send(src, dst, sems, index, peer):
    return pltpu.make_async_remote_copy(
        src_ref=src, dst_ref=dst, send_sem=sems.at[0, index], recv_sem=sems.at[1, index],
        device_id=peer, device_id_type=MESH,
    )


class Gather:
    COPIES = 27

    def __init__(self, here, src, dst, lanes, sems, local_sem):
        self.here, self.dst, self.lanes, self.sems = here, dst, lanes, sems
        self.src = src.at[:, lanes]
        self.local = pltpu.make_async_copy(self.src, self.at(here.me), local_sem)

    def at(self, slot):
        return self.dst.at[slot, :, self.lanes]

    def holds(self, i):
        z = self.here.z
        return z >= 0 if i == 0 else z >= i if i <= 3 else z + i - 3 <= 3

    def slot_of(self, i, far=False):
        here = self.here
        z = here.z - i if i <= 3 else here.z + i - 3
        return here.slot(z, 1 - here.y if far else here.y, here.c)

    def from_here(self, i, far=False):
        return self.src if i == 0 and not far else self.at(self.slot_of(i, far))

    def up(self, d):
        i = d - 1
        return send(self.from_here(i), self.at(self.slot_of(i)), self.sems, i, self.here.at_z(1))

    def down(self, d):
        i = d + 2 if d > 1 else 0
        return send(self.from_here(i), self.at(self.slot_of(i)), self.sems, 2 + d, self.here.at_z(3))

    def across(self, i):
        return send(self.from_here(i), self.at(self.slot_of(i)), self.sems, 6 + i, self.here.across_y())

    def to_core(self, k):
        i, far = k % 7, k >= 7
        src = self.from_here(i, far)
        return send(src, self.at(self.slot_of(i, far)), self.sems, 13 + k, self.here.other_core())

    def sends_up(self, d):
        return (self.here.z < 3) & (self.here.z >= d - 1)

    def sends_down(self, d):
        return (self.here.z > 0) & (self.here.z + d <= 4)

    def start_z(self):
        pl.when(self.sends_up(1))(lambda: self.up(1).start())
        pl.when(self.sends_down(1))(lambda: self.down(1).start())

    def start_y(self):
        self.across(0).start()
        self.to_core(0).start()
        self.local.start()

    def pass_z(self, *hops):
        for d in hops:

            @pl.when(self.holds(d))
            def _(d=d):
                self.up(d).wait_recv()
                if d < 3:
                    pl.when(self.here.z < 3)(lambda: self.up(d + 1).start())
                self.across(d).start()
                self.to_core(d).start()

            @pl.when(self.holds(3 + d))
            def _(d=d):
                self.down(d).wait_recv()
                if d < 3:
                    pl.when(self.here.z > 0)(lambda: self.down(d + 1).start())
                self.across(3 + d).start()
                self.to_core(3 + d).start()

    def pass_y(self):
        for i in range(7):

            @pl.when(self.holds(i))
            def _(i=i):
                self.across(i).wait_recv()
                self.to_core(7 + i).start()

    def arrived(self):
        self.local.wait()
        for k in range(14):
            pl.when(self.holds(k % 7))(lambda k=k: self.to_core(k).wait_recv())

    def sent(self):
        for d in (1, 2, 3):
            pl.when(self.sends_up(d))(lambda d=d: self.up(d).wait_send())
            pl.when(self.sends_down(d))(lambda d=d: self.down(d).wait_send())
        for i in range(7):
            pl.when(self.holds(i))(lambda i=i: self.across(i).wait_send())
        for k in range(14):
            pl.when(self.holds(k % 7))(lambda k=k: self.to_core(k).wait_send())


class GatherAcross:
    COPIES = 27

    def __init__(self, here, src, dst, lanes, sems, local_sem):
        self.here, self.sems, self.lanes, self.dst = here, sems, lanes, dst
        self.src = src.at[:, lanes]
        self.local = pltpu.make_async_copy(self.src, self.at(here.me), local_sem)

    holds = Gather.holds
    sends_up, sends_down = Gather.sends_up, Gather.sends_down

    def at(self, slot):
        return self.dst.at[slot, :, self.lanes]

    def slot_of(self, i, row):
        z = self.here.z - i if i <= 3 else self.here.z + i - 3
        return self.here.slot(z, 1 - self.here.y if row else self.here.y, self.here.c)

    def move(self, i, row, index, peer):
        slot = self.slot_of(i, row)
        src = self.src if i == 0 and not row else self.at(slot)
        return send(src, self.at(slot), self.sems, index, peer)

    def across(self):
        return self.move(0, 0, 0, self.here.across_y())

    def up(self, d, row):
        return self.move(d - 1, row, row * 3 + d, self.here.at_z(1))

    def down(self, d, row):
        return self.move(d + 2 if d > 1 else 0, row, 6 + row * 3 + d, self.here.at_z(3))

    def to_core(self, k):
        return self.move(k % 7, k // 7, 13 + k, self.here.other_core())

    def start_y(self):
        self.across().start()
        self.to_core(0).start()
        self.local.start()

    def start_z(self, row):
        pl.when(self.sends_up(1))(lambda: self.up(1, row).start())
        pl.when(self.sends_down(1))(lambda: self.down(1, row).start())

    def pass_y(self):
        self.across().wait_recv()
        self.start_z(1)
        self.to_core(7).start()

    def pass_z(self, d):
        for row in (0, 1):

            @pl.when(self.holds(d))
            def _(row=row):
                self.up(d, row).wait_recv()
                if d < 3:
                    pl.when(self.here.z < 3)(lambda: self.up(d + 1, row).start())
                self.to_core(row * 7 + d).start()

            @pl.when(self.holds(3 + d))
            def _(row=row):
                self.down(d, row).wait_recv()
                if d < 3:
                    pl.when(self.here.z > 0)(lambda: self.down(d + 1, row).start())
                self.to_core(row * 7 + 3 + d).start()

    def arrived(self):
        self.local.wait()
        for k in range(14):
            pl.when(self.holds(k % 7))(lambda k=k: self.to_core(k).wait_recv())

    def sent(self):
        self.across().wait_send()
        for d in (1, 2, 3):
            for row in (0, 1):
                pl.when(self.sends_up(d))(lambda d=d, row=row: self.up(d, row).wait_send())
                pl.when(self.sends_down(d))(lambda d=d, row=row: self.down(d, row).wait_send())
        for k in range(14):
            pl.when(self.holds(k % 7))(lambda k=k: self.to_core(k).wait_send())


def softplus(w):
    return jnp.maximum(w, 0.0) + jnp.log1p(jnp.exp(-jnp.abs(w)))


def forward_kernel(
    q, heads, width, inner_total,
    hid_ref, cot_ref, bc_ref, dt_t_ref, zx_ref, wo_ref, gain_in, ngain_in, heads_in, seg_ref, kx_ref, kbc_ref,
    rows_out, small_out, ws_out, wz_out, wo_out, s_out, normt_out, cott_out,
    scale_hbm, bcraw_hbm, dtin_hbm, dt_hbm, la_hbm, masks_hbm, st_hbm, dy_out, gated_out, dz_out, gngain_out, vec_ref,
    small_sems, ws_sems, wz_sems, wo_sems, wb_sems, x_sems, local_sems,
    rows_v, cot_v, small_v, ws_v, wz_v, wo_v, s_v, normed_v, y_v, z_v, dg_v, sum_v, sum_own, sum_came, normt_v, cott_v,
    dy_v, gated_v, dz_v, t_sems, out_sems,
    scale_out, bcraw_out, dtin_out, dt_out, la_out, masks_out, st_out, keep_sems, small_ref, square,
    bcc, mneg, cb, *group_scratch,
):
    here = Here()
    tokens = normed_v.shape[0]
    half = tokens // 2
    inner = y_v.shape[1]
    lanes = heads * width
    groups = inner // lanes
    here.greet()
    hidden = send(hid_ref, rows_v.at[here.t], x_sems, 0, here.across_x())
    cotangent = send(cot_ref, cot_v.at[here.t], x_sems, 1, here.across_x())
    sums_x = send(sum_own, sum_came, x_sems, 2, here.across_x())
    whole, first, second = pl.ds(0, inner), pl.ds(0, inner // 2), pl.ds(inner // 2, inner // 2)
    small = Gather(here, small_ref, small_v, pl.ds(0, small_ref.shape[1]), small_sems, local_sems.at[0])
    ws = Gather(here, zx_ref.at[1], ws_v, whole, ws_sems, local_sems.at[1])
    wz = Gather(here, zx_ref.at[0], wz_v, whole, wz_sems, local_sems.at[2])
    wo = Gather(here, wo_ref, wo_v, first, wo_sems, local_sems.at[3])
    wb = GatherAcross(here, wo_ref, wo_v, second, wb_sems, local_sems.at[12])
    gathers = [small, ws, wz, wo, wb]
    local = lambda src, dst, i: pltpu.make_async_copy(src, dst, local_sems.at[i])
    own_hidden = local(hid_ref, rows_v.at[here.t], 4)
    own_cot = local(cot_ref, cot_v.at[here.t], 5)
    store_ws, store_wz = local(ws_v, ws_out, 6), local(wz_v, wz_out, 7)
    store_wo = local(wo_v.at[:, :, first], wo_out.at[:, :, first], 8)
    store_wb = local(wo_v.at[:, :, second], wo_out.at[:, :, second], 13)
    store_rows, store_s = local(rows_v, rows_out, 9), local(s_v, s_out, 10)
    store_small = local(small_v, small_out, 11)
    keep = lambda src, dst, i: pltpu.make_async_copy(src, dst, keep_sems.at[i])
    keep_scale, keep_masks, keep_st = (
        keep(scale_out, scale_hbm, 0), keep(masks_out, masks_hbm, 1), keep(st_out, st_hbm, 2)
    )
    keep_prep = [
        keep(bcraw_out, bcraw_hbm, 3), keep(dtin_out, dtin_hbm, 4), keep(dt_out, dt_hbm, 5), keep(la_out, la_hbm, 6)
    ]

    def by_piece(src, dst, row):
        return [
            pltpu.make_async_copy(src.at[here.owner(k)], dst.at[k], t_sems.at[row, k]) for k in range(16)
        ]

    store_normt, store_cott = by_piece(normt_v, normt_out, 0), by_piece(cott_v, cott_out, 1)

    def turn(values, at, dst):
        shard_rows = dst.shape[1]
        flipped = values.astype(F32).T.astype(BF16)
        dst[pl.ds(at * (384 // shard_rows), 384 // shard_rows)] = flipped.reshape(
            384 // shard_rows, shard_rows, flipped.shape[1]
        )
    hidden.start()
    n_heads, shard_rows = dt_t_ref.shape
    square[...] = jnp.zeros_like(square)
    square[0:n_heads, 0:shard_rows] = dt_t_ref[...].astype(F32)
    bc_columns = bc_ref.shape[1]
    small_ref[:, 0:bc_columns] = bc_ref[...]
    small_ref[:, bc_columns : bc_columns + 128] = square[...].T[0:shard_rows, :].astype(BF16)
    vec_ref[...] = jnp.zeros_like(vec_ref)
    vec_ref[0:1, :] = gain_in[...]
    vec_ref[1:2, :] = ngain_in[...]
    head_of = lax.broadcasted_iota(jnp.int32, (128, inner), 1) // width
    spread = jnp.where(head_of == lax.broadcasted_iota(jnp.int32, (128, inner), 0), 1.0, 0.0)
    per_head = jnp.concatenate([heads_in[2:3, :], jnp.zeros((7, 128), F32)], axis=0)
    vec_ref[2:3, :] = dot(per_head, spread, NN, HIGHEST)[0:1, :]
    vec_ref[3:4, 0:128] = heads_in[0:1, :]
    vec_ref[3:4, 128:256] = -jnp.exp(heads_in[1:2, :])
    for gather in (small, ws):
        gather.start_z()
        gather.start_y()
    cotangent.start()
    own_hidden.start()
    own_cot.start()

    seg = jnp.broadcast_to(seg_ref[...].astype(F32), (128, tokens)).T
    row = lax.broadcasted_iota(jnp.int32, (tokens, 128), 0)
    lane = lax.broadcasted_iota(jnp.int32, (tokens, 128), 1)
    masks = jnp.where(lane == 5, seg, 0.0)
    for back in (1, 2, 3):
        same = (pltpu.roll(seg, back, 0) == seg) & (row >= back)
        masks = jnp.where((lane == back - 1) & same, 1.0, masks)
    for b in range(tokens // q):
        inside = (row >= b * q) & (row < (b + 1) * q)
        if b:
            carried = inside & (seg == seg[b * q - 1 : b * q, :])
            masks = jnp.where((lane == 3) & carried, 1.0, masks)
        run_last = inside & (seg == seg[(b + 1) * q - 1 : (b + 1) * q, :])
        masks = jnp.where((lane == 4) & run_last, 1.0, masks)
    masks_out[...] = masks
    keep_masks.start()

    small.pass_z(1, 2, 3)
    ws.pass_z(1, 2)
    wz.start_z()
    small.pass_y()
    own_hidden.wait()
    hidden.wait_recv()
    store_rows.start()
    gain = vec_ref[0:1, :]
    chunk = 64

    def norm(i, carry):
        side, at = i // (half // chunk), i % (half // chunk)
        rows = pl.ds(pl.multiple_of(at * chunk, chunk), chunk)
        values = rows_v[side, rows, :].astype(F32)
        scale = lax.rsqrt(jnp.mean(values * values, axis=1, keepdims=True) + EPS)
        out_rows = pl.ds(pl.multiple_of(i * chunk, chunk), chunk)
        normed_v[out_rows, :] = (values * scale * gain).astype(BF16)
        scale_out[out_rows, :] = jnp.broadcast_to(scale, (chunk, 128))
        return carry

    lax.fori_loop(0, tokens // chunk, norm, 0)
    keep_scale.start()
    ws.pass_z(3)
    wz.start_y()
    wb.start_y()
    wz.pass_z(1)
    small.arrived()
    store_small.start()
    pieces, shard, columns = small_v.shape
    proj = dot(normed_v[...], small_v[...].reshape(pieces * shard, columns))
    bc_width = columns - 128
    bcraw_out[...] = proj[:, :bc_width]
    dt_in = proj[:, bc_width:] + vec_ref[3:4, 0:128]
    dtin_out[...] = dt_in
    dt = softplus(dt_in)
    dt_out[...] = dt
    lower = jnp.where(
        lax.broadcasted_iota(jnp.int32, (q, q), 0) >= lax.broadcasted_iota(jnp.int32, (q, q), 1), 1.0, 0.0
    )
    exponent = dt * vec_ref[3:4, 128:256]
    for b in range(tokens // q):
        la_out[b * q : (b + 1) * q, :] = dot(lower, exponent[b * q : (b + 1) * q, :], NN, HIGHEST)
    for copy in keep_prep:
        copy.start()
    block_tables(q, bcraw_out, kbc_ref, masks_out, seg_ref, bcc, mneg, cb)
    wz.pass_z(2)
    wo.start_z()
    ws.pass_y()
    ws.arrived()
    store_ws.start()

    def weight_block(ref, at):
        return ref[:, :, at].reshape(pieces * shard, lanes)

    def lane_range(g):
        return pl.ds(pl.multiple_of(g * lanes, lanes), lanes)

    def scan_group(g, carry):
        @pl.when(g == 0)
        def _():
            wz.pass_z(3)
            wo.start_y()

        pl.when(g == 1)(lambda: wo.pass_z(1))

        @pl.when(g == 2)
        def _():
            wo.pass_z(2)
            wb.start_z(0)
            wb.pass_y()

        @pl.when(g == 4)
        def _():
            wo.pass_z(3)
            wb.pass_z(1)

        at = lane_range(g)
        s = dot(normed_v[...], weight_block(ws_v, at))
        fwd_group(
            q, heads, width, g, at, s, kx_ref[:, at], vec_ref[2:3, at], la_out, dt_out, masks_out,
            s_v, y_v, st_out, bcc, mneg, cb, *group_scratch,
        )
        return carry

    lax.fori_loop(0, groups, scan_group, 0)
    store_s.start()
    keep_st.start()
    wz.pass_y()
    wb.pass_z(2)

    def turn_normed(i, carry):
        turn(normed_v[:, pl.ds(pl.multiple_of(i * 384, 384), 384)], i, normt_v)
        return carry

    lax.fori_loop(0, normed_v.shape[1] // 384, turn_normed, 0)
    for copy in store_normt:
        copy.start()
    wz.arrived()
    store_wz.start()
    own_cot.wait()
    cotangent.wait_recv()

    def turn_cot(i, carry):
        turn(
            cot_v[:, :, pl.ds(pl.multiple_of(i * 384, 384), 384)].reshape(tokens, 384), i, cott_v
        )
        return carry

    lax.fori_loop(0, cot_v.shape[2] // 384, turn_cot, 0)
    for copy in store_cott:
        copy.start()
    sum_v[...] = jnp.zeros_like(sum_v)

    def gate_group(g, carry):
        at = lane_range(g)
        z = dot(normed_v[...], weight_block(wz_v, at))
        z_v[:, at] = z
        v = y_v[:, at] * (z * sigmoid(z))
        square = v * v
        for piece in range(lanes // 128):
            sum_v[0] += square[:, piece * 128 : (piece + 1) * 128]
        return carry

    lax.fori_loop(0, groups, gate_group, 0)
    wo.pass_y()
    wb.pass_z(3)
    wo.arrived()
    store_wo.start()

    def pull_group(g, carry):
        at = lane_range(g)
        side = cot_v[...].reshape(tokens, cot_v.shape[2])
        pulled = dot(side, weight_block(wo_v, at))
        dg_v[:, at] = pulled
        z = z_v[:, at]
        product = pulled * vec_ref[1:2, at] * (y_v[:, at] * (z * sigmoid(z)))
        for piece in range(lanes // 128):
            sum_v[1] += product[:, piece * 128 : (piece + 1) * 128]
        return carry

    lax.fori_loop(0, groups // 2, pull_group, 0)
    wb.arrived()
    store_wb.start()
    lax.fori_loop(groups // 2, groups, pull_group, 0)
    row_of = lambda array: jnp.sum(array.T, axis=0, keepdims=True)
    sum_own[...] = jnp.concatenate(
        [row_of(sum_v[0]), row_of(sum_v[1]), jnp.zeros((6, tokens), F32)], axis=0
    )
    sums_x.start()
    sums_x.wait_recv()
    both = sum_own[...] + sum_came[...]
    scale_row = lax.rsqrt(both[0:1, :] / inner_total + EPS)
    pull_row = both[1:2, :] * (scale_row * scale_row * scale_row) / inner_total
    column_of = lambda array: jnp.broadcast_to(array, (128, tokens)).T
    sum_v[0] = column_of(scale_row)
    sum_v[1] = column_of(pull_row)

    def grad_group(g, carry):
        at = lane_range(g)
        scale, pull = sum_v[0][:, 0:1], sum_v[1][:, 0:1]
        z, y, pulled = z_v[:, at], y_v[:, at], dg_v[:, at]
        sig = sigmoid(z)
        gate = z * sig
        v = y * gate
        unit = v * scale
        gngain_out[:, at] = jnp.sum(pulled * unit, axis=0, keepdims=True)
        gated_v[:, at] = (unit * vec_ref[1:2, at]).astype(BF16)
        d_v = pulled * vec_ref[1:2, at] * scale - pull * v
        dy_v[:, at] = d_v * gate
        dz_v[:, at] = (d_v * y * sig * (1.0 + z * (1.0 - sig))).astype(BF16)
        return carry

    def grad_out_copies(g):
        at = lane_range(g)
        return [
            pltpu.make_async_copy(src.at[:, at], dst.at[:, at], out_sems.at[i, g])
            for i, (src, dst) in enumerate([(dy_v, dy_out), (gated_v, gated_out), (dz_v, dz_out)])
        ]

    def grad_and_store(g, carry):
        grad_group(g, carry)
        for copy in grad_out_copies(g):
            copy.start()
        return carry

    lax.fori_loop(0, groups, grad_and_store, 0)
    for gather in gathers:
        gather.sent()

    def stored(g, carry):
        for copy in grad_out_copies(g):
            copy.wait()
        return carry

    lax.fori_loop(0, groups, stored, 0)
    for copy in (hidden, cotangent, sums_x):
        copy.wait_send()
    for copy in [store_rows, store_s, store_ws, store_wz, store_wo, store_wb, store_small, keep_scale, keep_masks, keep_st] + keep_prep + store_normt + store_cott:
        copy.wait()


def in_vmem():
    return pl.BlockSpec(memory_space=pltpu.VMEM)


def in_any():
    return pl.BlockSpec(memory_space=pl.ANY)


def forward_all(hidden, cot, bc, dt_t, zx, wo, gain, ngain, heads_in, seg_ids, conv_x, conv_bc, width, inner_total, q):
    half, depth = hidden.shape
    tokens = 2 * half
    shard, inner = zx.shape[1:]
    columns = bc.shape[1] + 128
    heads = heads_per_step(inner // width)
    lanes = heads * width
    n = (columns - 128) // 2
    blocks = tokens // q
    shape = jax.ShapeDtypeStruct
    sems = pltpu.SemaphoreType.DMA
    weight, rows = (16, shard, inner), (2, half, depth)
    per_head = shape((tokens, 128), F32)
    outs = pl.pallas_call(
        functools.partial(forward_kernel, q, heads, width, inner_total),
        in_specs=[in_vmem()] * 12,
        out_specs=[in_any()] * 18 + [in_vmem()] * 2,
        out_shape=[
            shape(rows, BF16), shape((16, shard, columns), BF16),
            shape(weight, BF16), shape(weight, BF16), shape(weight, BF16),
            shape((tokens, inner), F32), shape((16, shard, tokens), BF16), shape((16, shard, tokens), BF16),
            per_head, shape((tokens, columns - 128), F32), per_head, per_head, per_head, per_head,
            shape((blocks, n, inner), F32), shape((tokens, inner), F32), shape((tokens, inner), BF16),
            shape((tokens, inner), BF16), shape((1, inner), F32), shape((8, inner), F32),
        ],
        scratch_shapes=[sems((2, Gather.COPIES))] * 5 + [sems((2, 3)), sems((14,))]
        + [pltpu.VMEM(rows, BF16)] * 2 + [pltpu.VMEM((16, shard, columns), BF16)] + [pltpu.VMEM(weight, BF16)] * 3
        + [
            pltpu.VMEM((tokens, inner), F32), pltpu.VMEM((tokens, depth), BF16), pltpu.VMEM((tokens, inner), F32),
            pltpu.VMEM((tokens, inner), F32), pltpu.VMEM((tokens, inner), F32), pltpu.VMEM((2, tokens, 128), F32),
            pltpu.VMEM((8, tokens), F32), pltpu.VMEM((8, tokens), F32),
            pltpu.VMEM((16, shard, tokens), BF16), pltpu.VMEM((16, shard, tokens), BF16),
            pltpu.VMEM((tokens, inner), F32), pltpu.VMEM((tokens, inner), BF16), pltpu.VMEM((tokens, inner), BF16),
            sems((2, 16)), sems((3, inner // lanes)),
            pltpu.VMEM((tokens, 128), F32), pltpu.VMEM((tokens, columns - 128), F32),
        ]
        + [pltpu.VMEM((tokens, 128), F32)] * 4
        + [pltpu.VMEM((blocks, n, inner), F32), sems((7,)), pltpu.VMEM((shard, columns), BF16), pltpu.VMEM((128, 128), F32)]
        + forward_scratch(tokens, q, n, lanes),
        compiler_params=pltpu.CompilerParams(
            collective_id=0, has_side_effects=True, vmem_limit_bytes=VMEM_LIMIT
        ),
        name="forward_all",
    )(hidden, cot, bc, dt_t, zx, wo, gain, ngain, heads_in, seg_ids, conv_x, conv_bc)
    flat = lambda a: a.reshape((-1, a.shape[-1]))
    return [outs[0]] + [flat(a) for a in outs[1:14]] + list(outs[14:])


class Scatter:
    def __init__(self, here, own, away, from_core, from_y, from_z, core_sems, y_sems, z_sems, free):
        self.free, self.core_slots = free, from_core.shape[0]
        self.here, self.own, self.away = here, own, away
        self.from_core, self.from_y, self.from_z = from_core, from_y, from_z
        self.core_sems, self.y_sems, self.z_sems = core_sems, y_sems, z_sems

    def copy(self, src, dst, sems, i, peer):
        return pltpu.make_async_remote_copy(
            src_ref=src, dst_ref=dst, send_sem=sems[0].at[i], recv_sem=sems[1].at[i], device_id=peer,
            device_id_type=MESH,
        )

    def to_core(self, i):
        slot = i % self.away.shape[0]
        return self.copy(
            self.away.at[slot], self.from_core.at[i % self.core_slots], self.core_sems, i, self.here.other_core()
        )

    def across(self, i):
        return self.copy(
            self.own.at[i, pl.ds(0, 4)], self.from_y.at[i], self.y_sems, i, self.here.across_y()
        )

    def up(self, i, k):
        return self.copy(
            self.own.at[i, 4 + k], self.from_z.at[i, k - 1], self.z_sems, i * 6 + k - 1, self.here.at_z(1)
        )

    def down(self, i, k):
        slot = 3 + k if k < 2 else 0
        return self.copy(
            self.own.at[i, 4 + k], self.from_z.at[i, slot], self.z_sems, i * 6 + 3 + k, self.here.at_z(3)
        )

    def start(self, i, left_ref, right, reuse):
        pieces, rows, tokens = left_ref.shape
        half = pieces // 2
        pl.when(reuse)(lambda: self.to_core(jnp.maximum(i - self.away.shape[0], 0)).wait_send())
        make = lambda at: dot(
            left_ref[at : at + half].reshape(half * rows, tokens), right
        ).astype(BF16).reshape(half, rows, right.shape[1])
        self.away[i % self.away.shape[0]] = make(half)
        pl.when(i >= self.core_slots)(lambda: pl.semaphore_wait(self.free, 1))
        self.to_core(i).start()
        self.own[i] = make(0)

    def to_y(self, i):
        self.to_core(i).wait_recv()
        slot = i % self.core_slots
        add = lambda at: (self.own[i, at].astype(F32) + self.from_core[slot, at].astype(F32)).astype(BF16)
        self.own[i, 0:4] = add(slice(0, 4))
        self.across(i).start()
        self.own[i, 4:8] = add(slice(4, 8))

        @pl.when(i + self.core_slots < self.own.shape[0])
        def _():
            pl.semaphore_signal(
                self.free, inc=1, device_id=self.here.other_core(), device_id_type=MESH
            )

    def local_sum(self, i, k):
        return self.own[i, 4 + k].astype(F32) + self.from_y[i, k].astype(F32)

    def hop(self, i, h):
        z = self.here.z
        if h == 0:
            self.across(i).wait_recv()

        @pl.when(z == h)
        def _():
            for k in range(3, h, -1):
                total = self.local_sum(i, k)
                if h:
                    self.up(i, k).wait_recv()
                    total = total + self.from_z[i, k - 1].astype(F32)
                self.own[i, 4 + k] = total.astype(BF16)
                self.up(i, k).start()

        @pl.when(z == 3 - h)
        def _():
            for k in range(0, 3 - h):
                total = self.local_sum(i, k)
                if h:
                    self.down(i, k).wait_recv()
                    total = total + self.from_z[i, 3 + k if k < 2 else 0].astype(F32)
                self.own[i, 4 + k] = total.astype(BF16)
                self.down(i, k).start()

    def finish(self, i, store):
        for k in range(4):

            @pl.when(self.here.z == k)
            def _(k=k):
                total = self.local_sum(i, k)
                if k > 0:
                    self.up(i, k).wait_recv()
                    total = total + self.from_z[i, k - 1].astype(F32)
                if k < 3:
                    self.down(i, k).wait_recv()
                    total = total + self.from_z[i, 3 + k if k < 2 else 0].astype(F32)
                store(total)

    def sent(self, i, core):
        z = self.here.z
        pl.when(core)(lambda: self.to_core(i).wait_send())
        self.across(i).wait_send()
        for k in (1, 2, 3):
            pl.when(z < k)(lambda k=k: self.up(i, k).wait_send())
        for k in (0, 1, 2):
            pl.when(z > k)(lambda k=k: self.down(i, k).wait_send())


AWAY_SLOTS, CORE_SLOTS = 3, 6


def backward_kernel(
    q, heads, width,
    s_ref, dy_ref, ws_ref, wz_ref, wo_ref, kx_ref, veclanes_ref, st_ref,
    kbc_ref, segr_ref, vec_ref, gngain_ref,
    bcraw_hbm, la_hbm, dt_hbm, msk_hbm, normt_hbm, cott_hbm, gated_hbm, dz_hbm,
    dtin_hbm, small_w_hbm, rows_hbm, scale_hbm, cot_own_hbm,
    block_hbm, grad_in_hbm, gwo_hbm, gzx_hbm, gbc_hbm, gdt_hbm, sums_hbm,
    own, away, from_core, from_y, from_z,
    core_send, core_recv, y_send, y_recv, z_send, z_recv, free, x_sems, sum_sems,
    col, proj, x_send, x_came, sum_own, sum_came, ds_v, gk_v, small_v, low_v, gkbc_v, ghead_v,
    bcraw_ref, la_ref, dt_ref, msk_ref, normt_ref, cott_ref, gated_ref, dz_ref,
    dtin_ref, small_w_ref, rows_ref, scale_ref, cot_own_ref, load_sems,
    block_out, grad_in_out, gwo_out, gzx_out, gbc_out, gdt_out, sums_out, store_sems,
    bcc, mnegt, cbt, xs, dxs, dtt, gt, la4, lat4, dt4, dla_acc, ddt_acc, dbc_acc,
):
    here = Here()
    step = pl.program_id(0)
    tokens, lanes = s_ref.shape
    depth = col.shape[1]
    steps = gwo_out.shape[1] // lanes
    rate_ref, gain_ref = vec_ref.at[pl.ds(3, 1), pl.ds(128, 128)], vec_ref.at[pl.ds(0, 1)]
    dsk_ref = veclanes_ref.at[pl.ds(2, 1)]
    half = tokens // 2
    n2 = bcc.shape[1]
    scatter = Scatter(
        here, own, away, from_core, from_y, from_z, (core_send, core_recv), (y_send, y_recv), (z_send, z_recv), free
    )
    chunks = own.shape[0]
    late, early = 0, 1
    span = lambda part: pl.ds(8 * part, 8)

    def sum_copy(part, level, came, index, peer):
        return send(
            sum_own.at[level, span(part)], sum_came.at[came, span(part)], sum_sems, index + 6 * part, peer
        )

    core_sum = {part: sum_copy(part, 0, 0, 0, here.other_core()) for part in (late, early)}
    y_sum = {part: sum_copy(part, 1, 1, 1, here.across_y()) for part in (late, early)}
    z_sums = {
        part: [sum_copy(part, 2, 1 + d, 1 + d, here.at_z(d)) for d in (1, 2, 3)] for part in (late, early)
    }
    x_sum = sum_copy(late, 3, 5, 5, here.across_x())

    def sum_to_y(part):
        core_sum[part].wait_recv()
        sum_own[1, span(part)] = sum_own[0, span(part)] + sum_came[0, span(part)]
        y_sum[part].start()

    def sum_to_z(part):
        y_sum[part].wait_recv()
        sum_own[2, span(part)] = sum_own[1, span(part)] + sum_came[1, span(part)]
        for copy in z_sums[part]:
            copy.start()

    def sum_done(part):
        for copy in z_sums[part]:
            copy.wait_recv()
        sum_own[3, span(part)] = (
            sum_own[2, span(part)] + sum_came[2, span(part)] + sum_came[3, span(part)] + sum_came[4, span(part)]
        )

    pulled = send(x_send.at[1], x_came.at[1], x_sems, 0, here.across_x())

    def projected(g):
        at = pl.ds(pl.multiple_of(g * 256, 256), 256)
        return send(x_send.at[0, :, at], x_came.at[0, :, at], x_sems, 1 + g, here.across_x())

    load = lambda src, dst, i: pltpu.make_async_copy(src, dst, load_sems.at[i])
    loads = [
        load(src, dst, i)
        for i, (src, dst) in enumerate(
            [
                (gated_hbm, gated_ref), (cott_hbm, cott_ref), (dz_hbm, dz_ref), (normt_hbm, normt_ref),
                (bcraw_hbm, bcraw_ref), (la_hbm, la_ref), (dt_hbm, dt_ref), (msk_hbm, msk_ref),
                (dtin_hbm, dtin_ref), (small_w_hbm, small_w_ref), (rows_hbm, rows_ref), (scale_hbm, scale_ref),
                (cot_own_hbm, cot_own_ref),
            ]
        )
    ]
    stores = [
        pltpu.make_async_copy(src, dst, store_sems.at[i])
        for i, (src, dst) in enumerate(
            [
                (block_out, block_hbm), (grad_in_out, grad_in_hbm), (gwo_out, gwo_hbm), (gzx_out, gzx_hbm),
                (gbc_out, gbc_hbm), (gdt_out, gdt_hbm), (sums_out, sums_hbm),
            ]
        )
    ]
    at_lanes = pl.ds(pl.multiple_of(step * lanes, lanes), lanes)

    @pl.when(step == 0)
    def _():
        for copy in loads:
            copy.start()
        here.greet()
        for copy in loads[:8]:
            copy.wait()

    scatter.start(3 * step, cott_ref, gated_ref[:, at_lanes], step >= AWAY_SLOTS // 3)
    scatter.start(3 * step + 1, normt_ref, dz_ref[:, at_lanes], step >= AWAY_SLOTS // 3)

    @pl.when(step == 0)
    def _():
        bwd_tables(
            q, bcraw_ref, kbc_ref, msk_ref, segr_ref, bcc, mnegt, cbt, dtt, dbc_acc, dla_acc, ddt_acc
        )
        col[...] = jnp.zeros_like(col)

    def store_at(kind, g):
        at = pl.ds(pl.multiple_of(g * lanes, lanes), lanes)

        def store(total):
            if kind == 0:
                gwo_out[:, at] = total
            else:
                gzx_out[:, kind - 1, at] = total

        return store

    def small_store(i):
        def store(total):
            if i == 0:
                gbc_out[...] = total
            else:
                rest = jnp.zeros((128 - total.shape[0], 128), F32)
                gdt_out[...] = jnp.concatenate([total[:, 0:128], rest], axis=0).T[:, 0 : total.shape[0]]

        return store

    def tick(base, j):
        drain = isinstance(base, int)
        for back, act in ((8, None), (7, 2), (5, 1), (3, 0)):
            kind, turn = (j - back) % 3, (j - back) // 3
            g = base + turn
            if drain:
                c = 3 * g + kind
                if c >= chunks:
                    continue
                if act is None:
                    scatter.finish(c, small_store(c - (chunks - 2)) if c >= chunks - 2 else store_at(kind, g))
                else:
                    scatter.hop(c, act)
            else:

                @pl.when(g >= 0)
                def _(act=act, kind=kind, g=jnp.maximum(g, 0)):
                    if act is None:
                        scatter.finish(3 * g + kind, store_at(kind, g))
                    else:
                        scatter.hop(3 * g + kind, act)

    scatter.to_y(3 * step)
    tick(step, 0)
    own_half = pl.ds(pl.multiple_of(here.t * half, half), half)
    away_half = pl.ds(pl.multiple_of((1 - here.t) * half, half), half)
    at_columns = pl.ds(pl.multiple_of(step * 256, 256), 256)
    x_send[0, :, at_columns] = dot(gated_ref[away_half, :], wo_ref[...], NT).astype(BF16)
    projected(step).start()
    proj[:, at_columns] = dot(gated_ref[own_half, :], wo_ref[...], NT)
    col[:, at_columns] += dot(dz_ref[...], wz_ref[...], NT)

    def between(i):
        if i == 0:
            scatter.to_y(3 * step + 1)
            tick(step, 1)

    bwd_group(
        q, heads, width, step, s_ref, dy_ref, kx_ref, la_ref, dt_ref, msk_ref, dsk_ref, st_ref, ds_v, gk_v,
        bcc, mnegt, cbt, xs, dxs, dtt, gt, la4, lat4, dt4, dla_acc, ddt_acc, dbc_acc, between,
    )
    scatter.start(3 * step + 2, normt_ref, ds_v[...], step >= AWAY_SLOTS // 3)
    sum_own[0, 8:14, at_lanes] = gk_v[0:6, :]

    def column_block(j):
        return pl.ds(pl.multiple_of(j * 256, 256), 256)

    def accumulate(j, carry):
        at = column_block(j)
        col[:, at] += dot(ds_v[...], ws_ref[at, :], NT)
        return carry

    lax.fori_loop(0, depth // 256, accumulate, 0)
    scatter.to_y(3 * step + 2)
    tick(step, 2)

    @pl.when(step == steps - 1)
    def _():
        chunk = 32

        def by_chunks(act):
            def one(i, carry):
                at = pl.multiple_of(i * chunk, chunk)
                own_at = pl.multiple_of(here.t * half + i * chunk, chunk)
                away_at = pl.multiple_of((1 - here.t) * half + i * chunk, chunk)
                act(pl.ds(at, chunk), pl.ds(own_at, chunk), pl.ds(away_at, chunk))
                return carry

            lax.fori_loop(0, half // chunk, one, 0)

        for copy in loads[8:]:
            copy.wait()
        sum_own[0, 14:15, :] = gngain_ref[...]
        sum_own[0, 15:16, :] = jnp.zeros((1, depth), F32)
        core_sum[early].start()
        small_v[:, n2 + 128 :] = jnp.zeros_like(small_v[:, n2 + 128 :])
        bwd_finish(
            q, bcraw_ref, kbc_ref, dt_ref, msk_ref, dtin_ref, rate_ref, small_v, low_v, gkbc_v, ghead_v,
            bcc, dtt, dla_acc, ddt_acc, dbc_acc,
        )
        for i in range(2):
            scatter.start(3 * steps + i, normt_ref, small_v[:, i * lanes : (i + 1) * lanes], steps > 0)
        sum_to_y(early)
        tick(steps, 0)
        for i in range(2):
            scatter.to_y(3 * steps + i)

        def small_part(j, carry):
            at = column_block(j)
            col[:, at] += dot(small_v[:, : n2 + 128], small_w_ref[at, :], NT)
            return carry

        lax.fori_loop(0, depth // 256, small_part, 0)
        tick(steps, 1)
        sum_to_z(early)
        gain = gain_ref[...]

        def norm_back(side, store):
            def one(i, total):
                inside = pl.ds(pl.multiple_of(i * chunk, chunk), chunk)
                rows = pl.ds(pl.multiple_of(side * half + i * chunk, chunk), chunk)
                columns = col[rows, :]
                scale = scale_ref[rows, 0:1]
                unit = rows_ref[side, inside, :].astype(F32) * scale
                grad_unit = columns * gain
                store(
                    rows, inside,
                    scale * (grad_unit - unit * jnp.mean(grad_unit * unit, axis=1, keepdims=True)),
                )
                return total + jnp.sum(columns * unit, axis=0, keepdims=True)

            return one

        def to_send(rows, inside, value):
            x_send[1, inside, :] = value.astype(BF16)

        def to_keep(rows, inside, value):
            col[rows, :] = value

        prenorm = lax.fori_loop(
            0, half // chunk, norm_back(1 - here.t, to_send), jnp.zeros((1, depth), F32)
        )
        pulled.start()
        prenorm = lax.fori_loop(0, half // chunk, norm_back(here.t, to_keep), prenorm)
        sum_own[0, span(late)] = jnp.zeros((8, depth), F32)
        sum_own[0, 0:1, :] = prenorm
        for r in range(5):
            sum_own[0, 1:2, r * n2 : (r + 1) * n2] = gkbc_v[r : r + 1, :]
        sum_own[0, 2:3, 0:128] = ghead_v[0:1, :]
        sum_own[0, 2:3, 128:256] = ghead_v[1:2, :]
        sum_own[0, 2:3, 256:384] = exact_dot(sum_own[0, span(early)], head_picks(depth, width))[5:6, :]
        core_sum[late].start()
        tick(steps, 2)
        sum_to_y(late)
        sum_done(early)
        tick(steps, 3)
        tick(steps, 4)
        sum_to_z(late)
        tick(steps, 5)
        tick(steps, 6)
        tick(steps, 7)
        sum_done(late)
        x_sum.start()
        tick(steps, 8)

        def arrived_projected(g, carry):
            projected(g).wait_recv()
            return carry

        lax.fori_loop(0, steps, arrived_projected, 0)

        def put_block_out(rows, own_rows, away_rows):
            block_out[rows, :] = (
                rows_ref[here.t, rows, :].astype(F32) + proj[rows, :] + x_came[0, rows, :].astype(F32)
            ).astype(BF16)

        by_chunks(put_block_out)
        stores[0].start()
        pulled.wait_recv()

        def put_grad_in(rows, own_rows, away_rows):
            grad_in_out[rows, :] = (
                cot_own_ref[rows, :].astype(F32) + col[own_rows, :] + x_came[1, rows, :].astype(F32)
            ).astype(BF16)

        by_chunks(put_grad_in)
        stores[1].start()
        for copy in stores[2:5]:
            copy.start()
        x_sum.wait_recv()
        sums_out[...] = sum_own[3]
        sums_out[0:2, :] = sum_own[3, 0:2, :] + sum_came[5, 0:2, :]
        stores[6].start()
        tick(steps, 9)
        stores[5].start()

        def all_sent(i, carry):
            scatter.sent(i, i >= chunks - AWAY_SLOTS)
            return carry

        lax.fori_loop(0, chunks, all_sent, 0)

        def sent_projected(g, carry):
            projected(g).wait_send()
            return carry

        lax.fori_loop(0, steps, sent_projected, 0)
        for part in (late, early):
            for copy in [core_sum[part], y_sum[part]] + z_sums[part]:
                copy.wait_send()
        for copy in (x_sum, pulled):
            copy.wait_send()
        for copy in stores:
            copy.wait()


def backward_all(
    s, dy, gated, dz, w_s, w_z, w_out_t, conv_x, vectors, states, prep, conv_bc,
    normt, cott, small, rows, scale, seg_ids, gngain, cot_own, width, q,
):
    tokens, inner = s.shape
    depth = w_s.shape[0]
    half = tokens // 2
    heads = heads_per_step(inner // width)
    lanes = heads * width
    groups = inner // lanes
    n2 = prep["bcraw"].shape[1]
    n, blocks, shard = n2 // 2, tokens // q, depth // 16
    chunks = 3 * groups + 2
    shape = jax.ShapeDtypeStruct
    sems = pltpu.SemaphoreType.DMA
    once = lambda array: pl.BlockSpec(
        array.shape, lambda i: (0,) * array.ndim, pipeline_mode=pl.Buffered(1)
    )
    constants = [conv_bc, seg_ids, vectors, gngain]
    loaded = [
        prep["bcraw"], prep["la"], prep["dt"], prep["masks"], normt, cott, gated, dz,
        prep["dt_in"], small, rows, scale, cot_own,
    ]
    like = lambda array: pltpu.VMEM(array.shape, array.dtype)
    row_block = pl.BlockSpec((depth // groups, inner), lambda i: (i, 0))
    out_shape = [
        shape((half, depth), BF16), shape((half, depth), BF16), shape((shard, inner), F32),
        shape((shard, 2, inner), F32), shape((shard, lanes), F32), shape((128, shard), F32), shape((16, depth), F32),
    ]
    pieces = lambda count, per: pltpu.VMEM((count, per, shard, lanes), BF16)
    return pl.pallas_call(
        functools.partial(backward_kernel, q, heads, width),
        grid=(groups,),
        in_specs=[lane_block(tokens, lanes)] * 2 + [lane_block(depth, lanes), row_block, row_block]
        + [lane_block(5, lanes), lane_block(8, lanes), pl.BlockSpec((blocks, n, lanes), lambda i: (0, 0, i))]
        + [once(array) for array in constants] + [in_any()] * len(loaded),
        out_specs=[in_any()] * len(out_shape),
        out_shape=out_shape,
        scratch_shapes=[pieces(chunks, 8), pieces(AWAY_SLOTS, 8), pieces(CORE_SLOTS, 8), pieces(chunks, 4), pieces(chunks, 5)]
        + [sems((chunks,))] * 4 + [sems((6 * chunks,))] * 2 + [pltpu.SemaphoreType.REGULAR, sems((2, 1 + groups)), sems((2, 12))]
        + [
            pltpu.VMEM((tokens, depth), F32), pltpu.VMEM((half, depth), F32), pltpu.VMEM((2, half, depth), BF16),
            pltpu.VMEM((2, half, depth), BF16), pltpu.VMEM((4, 16, depth), F32), pltpu.VMEM((6, 16, depth), F32),
            pltpu.VMEM((tokens, lanes), BF16), pltpu.VMEM((8, lanes), F32), pltpu.VMEM((tokens, 2 * lanes), BF16),
            pltpu.VMEM((tokens, n2), BF16), pltpu.VMEM((8, n2), F32), pltpu.VMEM((8, 128), F32),
        ]
        + [like(array) for array in loaded] + [sems((len(loaded),))]
        + [like(array) for array in out_shape] + [sems((len(out_shape),))]
        + backward_scratch(tokens, q, n, lanes),
        compiler_params=pltpu.CompilerParams(
            dimension_semantics=("arbitrary",), collective_id=1, has_side_effects=True,
            vmem_limit_bytes=67043328,
        ),
        name="backward_all",
    )(s, dy, w_s, w_z, w_out_t, conv_x, vectors, states, *constants, *loaded)


def lanes_of(per_head):
    return jnp.pad(per_head, [(0, 0)] * (per_head.ndim - 1) + [(0, 128 - per_head.shape[-1])])


def prepare_plain(normed, small, bias, rate, flat_ids, q):
    tokens = normed.shape[0]
    blocks = tokens // q
    proj = dot(normed, small)
    bc_width = small.shape[1] - 128
    dt_in = proj[:, bc_width:] + bias
    dt = jax.nn.softplus(dt_in)
    lower = jnp.where(jnp.arange(q)[:, None] >= jnp.arange(q)[None, :], 1.0, 0.0)
    la = jnp.einsum("ij,bjh->bih", lower, (dt * rate).reshape(blocks, q, 128), precision=HIGHEST)
    shifted = lambda l: jnp.concatenate([jnp.full((l,), -1, jnp.int32), flat_ids[:-l]])
    by_block = flat_ids.reshape(blocks, q)
    before = jnp.concatenate([jnp.full((1,), -1, jnp.int32), by_block[:-1, -1]])
    carried = (by_block == before[:, None]).reshape(-1)
    run_last = (by_block == by_block[:, -1:]).reshape(-1)
    masks = [flat_ids == shifted(1), flat_ids == shifted(2), flat_ids == shifted(3), carried, run_last, flat_ids]
    return proj[:, :bc_width], dt_in, dt, la.reshape(tokens, 128), lanes_of(jnp.stack(masks, axis=1).astype(F32))


def body(
    dp,
    tp,
    hidden_in,
    prenorm_gain,
    w_zx,
    w_dt,
    w_bc,
    conv_x,
    conv_bc,
    dt_bias,
    a_log,
    d_skip,
    norm_gain,
    w_out,
    seg_ids,
    grad_out,
):
    q = BLOCK_LEN
    staged = dp == 16 and tp == 2 and seg_ids.shape[0] == 1 and hidden_in.shape[1] == w_out.shape[0]
    inner = w_out.shape[0]
    head_count = dt_bias.shape[0]
    width = inner // head_count
    bc_width = w_bc.shape[1]
    shard = w_bc.shape[0]
    depth = hidden_in.shape[1]
    inner_total = inner * tp
    tensor = lax.axis_index("tensor")

    bias = lanes_of(dt_bias)[None, :]
    rate = lanes_of(-jnp.exp(a_log))[None, :]
    small_shard = jnp.concatenate([w_bc, lanes_of(w_dt)], axis=1)
    flat_ids = (seg_ids + seg_ids.shape[1] * lax.broadcasted_iota(jnp.int32, seg_ids.shape, 0)).reshape(-1)
    seg_row = flat_ids.astype(F32)[None, :]
    skip_lanes = jnp.repeat(d_skip, width)[None, :]
    prep = dict(rate=rate, seg_row=seg_row)

    if staged:
        heads_in = lanes_of(jnp.stack([dt_bias, a_log, d_skip]))
        (
            full_rows, small, w_s, w_z, w_out_t, s, normt, cott, scale_in,
            prep["bcraw"], prep["dt_in"], prep["dt"], prep["la"], prep["masks"],
            states, d_y, gated, d_z, grad_norm_gain, vectors,
        ) = forward_all(
            hidden_in, grad_out, w_bc, w_dt.T, w_zx.transpose(1, 0, 2), w_out.T, prenorm_gain[None, :], norm_gain[None, :],
            heads_in, seg_ids, conv_x, conv_bc,
            width, inner_total, q,
        )
        split = lambda array: array.reshape(16, shard, array.shape[1])
        block_out, grad_in, grad_w_out, grad_w_zx, bc_sum, grad_dt, sums = backward_all(
            s, d_y, gated, d_z, w_s, w_z, w_out_t, conv_x, vectors, states, prep, conv_bc,
            split(normt), split(cott), small, full_rows, scale_in, seg_ids, grad_norm_gain, grad_out,
            width, q,
        )
        half_of = lambda value: lax.dynamic_slice_in_dim(
            value, tensor * (value.shape[-1] // 2), value.shape[-1] // 2, value.ndim - 1
        )
        bc_half = bc_width // 2
        away_bc = lax.dynamic_slice_in_dim(bc_sum, (1 - tensor) * bc_half, bc_half, 1)
        return (
            block_out,
            grad_in,
            half_of(sums[0]),
            grad_w_zx,
            grad_dt[:head_count].T,
            half_of(bc_sum) + lax.ppermute(away_bc, "tensor", [(0, 1), (1, 0)]),
            sums[8:13],
            half_of(sums[1, : 5 * bc_width].reshape(5, bc_width)),
            sums[2, :head_count],
            sums[2, 128 : 128 + head_count],
            sums[2, 256 : 256 + head_count],
            sums[14],
            grad_w_out.T,
        )
    else:
        over_dp = lambda value: lax.all_gather(value, "dp", axis=0, tiled=True)
        small = over_dp(small_shard)
        w_s, w_z, w_out_t = over_dp(w_zx[:, 1, :]), over_dp(w_zx[:, 0, :]), over_dp(w_out.T)
        rows_float = lax.all_gather(hidden_in, "tensor", axis=0, tiled=True).astype(F32)
        cot_rows = lax.all_gather(grad_out, "tensor", axis=0, tiled=True)
        scale_in = lax.rsqrt(jnp.mean(rows_float * rows_float, axis=1, keepdims=True) + EPS)
        normed = (rows_float * scale_in * prenorm_gain).astype(BF16)
        prep["bcraw"], prep["dt_in"], prep["dt"], prep["la"], prep["masks"] = prepare_plain(
            normed, small, bias, rate, flat_ids, q
        )
        s, y, states = scan_forward(normed, w_s, prep, conv_x, conv_bc, skip_lanes, width, q)
        z = dot(normed, w_z)
        gate_sig = sigmoid(z)
        gate = z * gate_sig
        v = y * gate
        grad_gated = dot(cot_rows, w_out_t)
        scaled_grad = grad_gated * norm_gain
        sums = jnp.stack([jnp.sum(v * v, axis=1), jnp.sum(scaled_grad * v, axis=1)])
        sums = lax.psum(sums, "tensor")
        scale_out = lax.rsqrt(sums[0] / inner_total + EPS)[:, None]
        pull = sums[1][:, None] * scale_out**3 / inner_total
        gated = (v * scale_out * norm_gain).astype(BF16)
        grad_norm_gain = jnp.sum(grad_gated * v * scale_out, axis=0)
        d_v = scaled_grad * scale_out - pull * v
        d_y = d_v * gate
        d_z = (d_v * y * gate_sig * (1.0 + z * (1.0 - gate_sig))).astype(BF16)
    tokens = normed.shape[0]

    d_s, grad_taps, d_small, low_bc, grad_taps_bc, grad_heads = scan_backward(
        s, d_y, prep, conv_x, conv_bc, skip_lanes, states, width, q
    )
    grad_d_skip = jnp.sum(grad_taps[5].reshape(head_count, width), axis=1)

    own_rows = tokens // tp
    rows_of = lambda array, i: lax.dynamic_slice_in_dim(array, i * own_rows, own_rows, 0)
    project = lambda i: dot(rows_of(gated, i), w_out_t, NT)
    prenorm_terms = []

    def grad_rows(i):
        columns = (
            dot(rows_of(d_z, i), w_z, NT)
            + dot(rows_of(d_s, i), w_s, NT)
            + dot(rows_of(d_small, i), small, NT)
            + dot(rows_of(low_bc, i), small[:, :bc_width], NT)
        )
        unit = rows_of(rows_float, i) * rows_of(scale_in, i)
        prenorm_terms.append(jnp.sum(columns * unit, axis=0))
        grad_unit = columns * prenorm_gain
        return rows_of(scale_in, i) * (
            grad_unit - unit * jnp.mean(grad_unit * unit, axis=1, keepdims=True)
        )

    products = [
        dot(cot_rows, gated, TN),
        dot(normed, d_z, TN),
        dot(normed, jnp.concatenate([d_s, d_small], axis=1), TN),
    ]
    every = lambda make: jnp.concatenate([make(i) for i in range(tp)], axis=0)
    onto = lambda value, dim: lax.psum_scatter(value, "tensor", scatter_dimension=dim, tiled=True)
    projected, own_grad = onto(every(project), 0), onto(every(grad_rows), 0)

    pieces = [
        sum(prenorm_terms),
        grad_taps_bc[:5].reshape(-1),
        grad_taps[:5].reshape(-1),
        grad_norm_gain,
        grad_heads[0],
        grad_heads[1],
        lanes_of(grad_d_skip),
    ]
    gap = -(pieces[0].shape[0] + pieces[1].shape[0]) % 1024
    pieces.insert(2, jnp.zeros((gap,), F32))
    x_rows = sum(piece.shape[0] for piece in pieces[:3]) // 128
    flat = jnp.concatenate(pieces)
    flat = jnp.pad(flat, (0, -flat.shape[0] % 1024)).reshape(-1, 128)
    half_of = lambda value: lax.dynamic_slice_in_dim(
        value, tensor * (value.shape[-1] // tp), value.shape[-1] // tp, value.ndim - 1
    )
    grad_w_out, grad_w_z, grad_last = [
        lax.psum_scatter(p, "dp", scatter_dimension=0, tiled=True) for p in products
    ]
    grad_w_bc = onto(grad_last[:, inner : inner + bc_width], 1)
    flat = lax.psum(flat, "dp")
    flat = jnp.concatenate([lax.psum(flat[:x_rows], "tensor"), flat[x_rows:]], axis=0)
    block_out = (hidden_in.astype(F32) + projected).astype(BF16)
    grad_in = (grad_out.astype(F32) + own_grad).astype(BF16)
    grad_w_zx = jnp.stack([grad_w_z, grad_last[:, :inner]], axis=1)
    grad_w_dt = grad_last[:, inner + bc_width : inner + bc_width + head_count]

    flat = flat.reshape(-1)
    at, cut_out = 0, []
    for piece in pieces:
        cut_out.append(flat[at : at + piece.shape[0]])
        at += piece.shape[0]
    return (
        block_out,
        grad_in,
        half_of(cut_out[0]),
        grad_w_zx,
        grad_w_dt,
        grad_w_bc,
        cut_out[3].reshape(5, inner),
        half_of(cut_out[1].reshape(5, bc_width)),
        cut_out[5][:head_count],
        cut_out[6][:head_count],
        cut_out[7][:head_count],
        cut_out[4],
        grad_w_out.T,
    )


def solution(mesh):
    in_specs = (
        P(("dp", "tensor"), None),
        P(),
        P("dp", None, "tensor"),
        P("dp", "tensor"),
        P("dp", None),
        P(None, "tensor"),
        P(),
        P("tensor"),
        P("tensor"),
        P("tensor"),
        P("tensor"),
        P("tensor", "dp"),
        P("dp", None),
        P(("dp", "tensor"), None),
    )
    out_specs = (
        P(("dp", "tensor"), None),
        P(("dp", "tensor"), None),
        P("tensor"),
        P("dp", None, "tensor"),
        P("dp", "tensor"),
        P("dp", "tensor"),
        P(None, "tensor"),
        P(None, "tensor"),
        P("tensor"),
        P("tensor"),
        P("tensor"),
        P("tensor"),
        P("tensor", "dp"),
    )
    return jax.shard_map(
        functools.partial(body, mesh.shape["dp"], mesh.shape["tensor"]),
        mesh=mesh,
        in_specs=in_specs,
        out_specs=out_specs,
        check_vma=False,
    )
```
